32 devices in a mesh: rep: 2 (over x), shard: 16 (over z, y, core).
Axes of the slice: x: 2, y: 2, z: 4, core: 2. Of those that a mesh axis runs over, the one named last changes fastest.
Arguments:
- tokens: bfloat16 [32, 1024, 1024], P(('rep', 'shard')), may hold values from -6 to 6
- lengths: int32 [32], P(('rep', 'shard')), may hold values from 1 to 1024, 24576 in all
- first_gain: float32 [1024], replicated, may hold values from 0.5 to 1.5
- first_bias: float32 [1024], replicated, may hold values from -1.75 to 1.75
- decay_rates: float32 [16], replicated, may hold values from 0.0005 to 0.05
- state_in: bfloat16 [16, 1024], P(None, 'shard'), may hold values from -0.1875 to 0.1875
- state_out: bfloat16 [16, 1024], P(None, 'shard'), may hold values from -1.5 to 1.5
- skip_gain: float32 [1024], replicated, may hold values from -6 to 6
- query_weight: bfloat16 [1024, 1024], P('shard'), may hold values from -0.1875 to 0.1875
- key_weight: bfloat16 [1024, 1024], P('shard'), may hold values from -0.1875 to 0.1875
- value_weight: bfloat16 [1024, 1024], P('shard'), may hold values from -0.1875 to 0.1875
- output_weight: bfloat16 [1024, 1024], P('shard'), may hold values from -0.5 to 0.5
- second_gain: float32 [1024], replicated, may hold values from 0.5 to 1.5
- second_bias: float32 [1024], replicated, may hold values from -1.75 to 1.75
- up_weight: bfloat16 [1024, 4096], P('shard'), may hold values from -0.1875 to 0.1875
- up_bias: float32 [4096], replicated, may hold values from -1.75 to 1.75
- down_weight: bfloat16 [4096, 1024], P('shard'), may hold values from -0.09375 to 0.09375
- down_bias: float32 [1024], replicated, may hold values from -1.75 to 1.75
- cotangent: bfloat16 [32, 1024, 1024], P(('rep', 'shard')), may hold values from -6 to 6
Outputs:
- result: bfloat16 [32, 1024, 1024], P(('rep', 'shard'))
- grad_tokens: bfloat16 [32, 1024, 1024], P(('rep', 'shard'))
- grad_first_gain: float32 [1024], replicated
- grad_first_bias: float32 [1024], replicated
- grad_decay_rates: float32 [16], replicated
- grad_state_in: float32 [16, 1024], P(None, 'shard')
- grad_state_out: float32 [16, 1024], P(None, 'shard')
- grad_skip_gain: float32 [1024], replicated
- grad_query_weight: float32 [1024, 1024], P('shard')
- grad_key_weight: float32 [1024, 1024], P('shard')
- grad_value_weight: float32 [1024, 1024], P('shard')
- grad_output_weight: float32 [1024, 1024], P('shard')
- grad_second_gain: float32 [1024], replicated
- grad_second_bias: float32 [1024], replicated
- grad_up_weight: float32 [1024, 4096], P('shard')
- grad_up_bias: float32 [4096], replicated
- grad_down_weight: float32 [4096, 1024], P('shard')
- grad_down_bias: float32 [1024], replicated
The draws below stay inside these ranges and needn't reach their ends.
Inputs may be any that keep to these rules, and one draw needn't show every extreme that they name: `lengths`: live tokens of each sequence; its positions from its length to 1023 are padding; some sequence fills its whole slot.
All inputs are finite; a program needn't handle non-finite values. No bound on the sum of `lengths` on one device may be relied on, other than what follows from the above.
Results may differ from the reference program's by a relative error of at most 0.013.
The reference program's roundings to bfloat16 on the way count: a program that leaves them out, or rounds other values in their place, can miss the bound.
Values may be sent and summed in bfloat16 or wider, within the bound.
A program may use at most 256 MiB of HBM per device.

```python
import math
import jax
import jax.numpy as jnp
import numpy as np
from jax import lax

D = 1024
DH = 128
FF = 4096
P_SIZE = 16
BLK = 512
CTX = 128
NBLK = 2
SEQ = 1024
NSEQ = 32


def block_levels(stream_key, shape, cuts, low, largest):
    factor_of = 1.0
    for axis_at, parts in cuts:
        heights = jax.random.uniform(jax.random.fold_in(jax.random.fold_in(stream_key, 6), axis_at), (parts,), jnp.float32, low / len(cuts), largest / len(cuts))
        factor_of = factor_of * jnp.repeat(jnp.exp(heights), shape[axis_at] // parts).reshape((-1,) + (1,) * (len(shape) - 1 - axis_at))
    return factor_of


def length_profile(number_of, total, bound, slope):
    loads = [(1 << 20) // math.isqrt(standing ** slope) + 1 for standing in range(2, number_of + 1)]
    surplus, given = total - bound - (number_of - 1), [1] * (number_of - 1)
    while surplus > 0:
        movable = [i for i in range(number_of - 1) if given[i] < bound]
        whole, left = sum([loads[i] for i in movable]), surplus
        for i in movable:
            extra = min(bound - given[i], max(1, left * loads[i] // whole), surplus)
            given[i] = given[i] + extra
            surplus = surplus - extra
    return np.array([bound] + given)


def ragged(stream_key, amount, total, bound, slope):
    if amount == 2:
        one = jax.random.randint(stream_key, (), max(1, total - bound), min(bound, total - 1) + 1)
        return jnp.stack([one, total - one])
    sizes = jnp.asarray(length_profile(amount, total, bound, slope), jnp.int32)
    pairs = (amount - 1) // 2
    giver, sink = sizes[1:1 + 2 * pairs:2], sizes[2:2 + 2 * pairs:2]
    slack = jnp.minimum(giver - 1, bound - sink)
    passed = jax.random.randint(jax.random.fold_in(stream_key, 1), (pairs,), 0, 1 << 20) % (slack + 1)
    sizes = sizes.at[1:1 + 2 * pairs:2].set(giver - passed).at[2:2 + 2 * pairs:2].set(sink + passed)
    return sizes[jax.random.permutation(jax.random.fold_in(stream_key, 2), amount)]


def gaussian(stream_key, extent, scale, reach, pieces=(), held_as=jnp.bfloat16):
    gain = block_levels(stream_key, extent, pieces, -0.22, 0.18) if pieces else 1.0
    array = jax.random.normal(stream_key, extent, jnp.float32) * scale * gain
    return jnp.minimum(jnp.maximum(array, -reach), reach).astype(held_as)


def setup_inputs(seed: int = 0) -> dict:
    streams_of = jax.random.split(jax.random.key(seed), 20)
    tokens = gaussian(streams_of[0], (NSEQ, SEQ, D), 1.0, 6.0, ((0, 32),))
    lengths = ragged(streams_of[1], NSEQ, NSEQ * SEQ * 3 // 4, SEQ, 0).astype(jnp.int32)
    first_gain = jnp.clip(1.0 + 0.1 * jax.random.normal(streams_of[2], (D,), jnp.float32), 0.5, 1.5)
    first_bias = gaussian(streams_of[3], (D,), 0.3, 1.75, (), jnp.float32)
    decay_rates = jnp.clip(jnp.exp(jax.random.uniform(streams_of[4], (P_SIZE,), jnp.float32, math.log(0.0005), math.log(0.05))), 0.0005, 0.05)
    state_in = gaussian(streams_of[5], (P_SIZE, D), D ** -0.5, 0.1875, ((1, 16),))
    state_out = gaussian(streams_of[6], (P_SIZE, D), P_SIZE ** -0.5, 1.5, ((1, 16),))
    skip_gain = gaussian(streams_of[7], (D,), 1.0, 6.0, (), jnp.float32)
    query_weight = gaussian(streams_of[8], (D, D), D ** -0.5, 0.1875, ((0, 16),))
    key_weight = gaussian(streams_of[9], (D, D), D ** -0.5, 0.1875, ((0, 16),))
    value_weight = gaussian(streams_of[10], (D, D), D ** -0.5, 0.1875, ((0, 16),))
    output_weight = gaussian(streams_of[11], (D, D), (D // 8) ** -0.5, 0.5, ((0, 16),))
    second_gain = jnp.clip(1.0 + 0.1 * jax.random.normal(streams_of[12], (D,), jnp.float32), 0.5, 1.5)
    second_bias = gaussian(streams_of[13], (D,), 0.3, 1.75, (), jnp.float32)
    up_weight = gaussian(streams_of[14], (D, FF), D ** -0.5, 0.1875, ((0, 16),))
    up_bias = gaussian(streams_of[15], (FF,), 0.3, 1.75, (), jnp.float32)
    down_weight = gaussian(streams_of[16], (FF, D), FF ** -0.5, 0.09375, ((0, 16),))
    down_bias = gaussian(streams_of[17], (D,), 0.3, 1.75, (), jnp.float32)
    cotangent = gaussian(streams_of[18], (NSEQ, SEQ, D), 1.0, 6.0, ((0, 32),))
    return {"tokens": tokens, "lengths": lengths, "first_gain": first_gain, "first_bias": first_bias, "decay_rates": decay_rates, "state_in": state_in, "state_out": state_out, "skip_gain": skip_gain, "query_weight": query_weight, "key_weight": key_weight, "value_weight": value_weight, "output_weight": output_weight, "second_gain": second_gain, "second_bias": second_bias, "up_weight": up_weight, "up_bias": up_bias, "down_weight": down_weight, "down_bias": down_bias, "cotangent": cotangent}


NORM_EPS = 1e-05
NEG_LARGE = -1e+30
HIGHEST = lax.Precision.HIGHEST

@jax.custom_vjp
def low(v):
    return lax.optimization_barrier(v.astype(jnp.bfloat16)).astype(jnp.float32)

@jax.custom_vjp
def low_back(v):
    return v

def low_keep(v):
    return (low(v), None)

def low_pass(kept, grad):
    return (grad,)

def back_keep(v):
    return (v, None)

def back_low(kept, grad):
    return (low(grad),)
low.defvjp(low_keep, low_pass)
low_back.defvjp(back_keep, back_low)

def layer_norm(hidden, gain_vec, bias_vec):
    average = lax.optimization_barrier(jnp.mean(hidden, axis=-1, keepdims=True))
    centred = hidden - average
    spread = lax.optimization_barrier(jnp.mean(centred * centred, axis=-1, keepdims=True))
    return centred * lax.rsqrt(spread + NORM_EPS) * gain_vec + bias_vec

def state_context(rounded, normed, decay_rates, state_in, state_out, skip_gain):
    driven = jnp.einsum('std,pd->stp', rounded, state_in, precision=HIGHEST)
    decay_factor = jnp.exp(-decay_rates)
    driven = driven * jnp.sqrt(1.0 - decay_factor * decay_factor)
    factors = jnp.broadcast_to(decay_factor, driven.shape)

    def combine(earlier, subsequent):
        return (earlier[0] * subsequent[0], subsequent[0] * earlier[1] + subsequent[1])
    states = lax.associative_scan(combine, (factors, driven), axis=1)[1]
    seq_count = rounded.shape[0]
    tail_states = states.reshape(seq_count, NBLK, BLK, P_SIZE)[:, :, BLK - CTX:, :]
    skipped = normed.reshape(seq_count, NBLK, BLK, D)[:, :, BLK - CTX:, :]
    outputs = jnp.einsum('sbcp,pd->sbcd', tail_states, state_out, precision=HIGHEST) + skip_gain * skipped
    empty_ctx = jnp.zeros((seq_count, 1, CTX, D), jnp.float32)
    return jnp.concatenate([empty_ctx, outputs[:, :NBLK - 1]], axis=1)

def attend_block(block_item):
    queries, key_rows, value_rows, ctx_keys, ctx_values, ctx_valid = block_item
    row_count = queries.shape[0]
    head_count = queries.shape[1] // DH
    key_heads = jnp.concatenate([ctx_keys, key_rows], 0).reshape(CTX + row_count, head_count, DH)
    value_heads = jnp.concatenate([ctx_values, value_rows], 0).reshape(CTX + row_count, head_count, DH)
    scores = jnp.einsum('qhd,khd->hqk', queries.reshape(row_count, head_count, DH), key_heads, precision=HIGHEST) * DH ** (-0.5)
    scores = low_back(scores)
    causal = jnp.arange(row_count)[:, None] >= jnp.arange(row_count)[None, :]
    allowed = jnp.concatenate([jnp.broadcast_to(ctx_valid[None, :], (row_count, CTX)), causal], axis=1)
    scores = jnp.where(allowed[None], scores, NEG_LARGE)
    weights = low(jax.nn.softmax(scores, axis=-1))
    attended = jnp.einsum('hqk,khd->qhd', weights, value_heads, precision=HIGHEST)
    return attended.reshape(row_count, head_count * DH)

def project(source, weight):
    return low(low_back(jnp.einsum('...d,de->...e', source, weight, precision=HIGHEST)))

def forward(token_rows, seq_lengths, params):
    first_gain, first_bias, decay_rates, state_in, state_out, skip_gain, query_weight, key_weight, value_weight, output_weight, second_gain, second_bias, up_weight, up_bias, down_weight, down_bias = params
    seq_count = token_rows.shape[0]
    block_count = seq_count * NBLK
    normed = layer_norm(token_rows, first_gain, first_bias)
    rounded = low(normed)
    context = low(state_context(rounded, normed, decay_rates, state_in, state_out, skip_gain))
    query_rows = project(rounded, query_weight)
    key_rows = project(rounded, key_weight)
    value_rows = project(rounded, value_weight)
    ctx_keys = project(context, key_weight)
    ctx_values = project(context, value_weight)
    block_index = jnp.arange(NBLK)[None, :, None]
    ctx_valid = jnp.broadcast_to(block_index > 0, (seq_count, NBLK, CTX))
    attended = lax.map(jax.checkpoint(attend_block), (query_rows.reshape(block_count, BLK, D), key_rows.reshape(block_count, BLK, D), value_rows.reshape(block_count, BLK, D), ctx_keys.reshape(block_count, CTX, D), ctx_values.reshape(block_count, CTX, D), ctx_valid.reshape(block_count, CTX)))
    attended = low(low_back(attended.reshape(seq_count, SEQ, D)))
    residual = token_rows + low_back(jnp.einsum('std,de->ste', attended, output_weight, precision=HIGHEST))
    second = low(layer_norm(residual, second_gain, second_bias))
    hidden = low_back(jnp.einsum('std,df->stf', second, up_weight, precision=HIGHEST) + up_bias)
    active = low(jax.nn.gelu(hidden))
    branch = low_back(jnp.einsum('stf,fd->std', active, down_weight, precision=HIGHEST) + down_bias)
    row_mask = (jnp.arange(SEQ)[None, :] < seq_lengths[:, None]).astype(jnp.float32)
    return (residual + branch) * row_mask[:, :, None]

def reference(tokens, lengths, first_gain, first_bias, decay_rates, state_in, state_out, skip_gain, query_weight, key_weight, value_weight, output_weight, second_gain, second_bias, up_weight, up_bias, down_weight, down_bias, cotangent):
    params = tuple((member.astype(jnp.float32) for member in (first_gain, first_bias, decay_rates, state_in, state_out, skip_gain, query_weight, key_weight, value_weight, output_weight, second_gain, second_bias, up_weight, up_bias, down_weight, down_bias)))
    group_size = math.gcd(NSEQ, max(1, 4096 // SEQ))
    step_count = NSEQ // group_size
    token_groups = tokens.astype(jnp.float32).reshape(step_count, group_size, SEQ, D)
    length_groups = lengths.reshape(step_count, group_size)
    cot_groups = cotangent.astype(jnp.float32).reshape(step_count, group_size, SEQ, D)

    def scan_step(gradients, batch_item):
        token_rows, seq_lengths, cot_rows = batch_item

        def apply_layer(rows_in, weights_in):
            return forward(rows_in, seq_lengths, weights_in)
        block_out, pullback = jax.vjp(apply_layer, token_rows, params)
        grad_rows, grad_params = pullback(cot_rows)
        gradients = jax.tree.map(jnp.add, gradients, grad_params)
        return (gradients, (block_out.astype(jnp.bfloat16), grad_rows.astype(jnp.bfloat16)))
    zero_grads = jax.tree.map(jnp.zeros_like, params)
    gradients, (results, grad_rows) = lax.scan(scan_step, zero_grads, (token_groups, length_groups, cot_groups))
    return (results.reshape(NSEQ, SEQ, D), grad_rows.reshape(NSEQ, SEQ, D), gradients[0], gradients[1], gradients[2], gradients[3], gradients[4], gradients[5], gradients[6], gradients[7], gradients[8], gradients[9], gradients[10], gradients[11], gradients[12], gradients[13], gradients[14], gradients[15])
```

```python
import functools
import math

import jax
import jax.numpy as jnp
from jax import lax
from jax.experimental import pallas as pl
from jax.experimental.pallas import tpu as pltpu
from jax.sharding import PartitionSpec as P

DH = 128
BLK = 512
CTX = 128
NBLK = 2
EPS = 1e-05
NEG = -1e30
SCALE = DH ** (-0.5)
MESH = pl.DeviceIdType.MESH
F32 = jnp.float32
BF16 = jnp.bfloat16
VMEM_LIMIT = 66_000_000
NC = 8


def chip_at(pos):
    turned = pos // 4
    return (1 - turned) * (2 * pos) + turned * (2 * (7 - pos) + 1)


class Net:
    def __init__(self):
        self.rep = lax.axis_index("rep")
        self.shard = lax.axis_index("shard")
        self.core = self.shard % 2
        chip = self.shard // 2
        z, y = chip // 2, chip % 2
        self.pos = (1 - y) * z + y * (7 - z)
        self.step = 1 - 2 * self.core
        self.mate = (self.rep, 2 * chip + 1 - self.core)
        self.twin = (1 - self.rep, self.shard)

    def at(self, hops, core):
        return 2 * chip_at((self.pos + self.step * hops + 4 * NC) % NC) + core

    def along(self, hops):
        return (self.rep, self.at(hops, self.core))

    def greet(self):
        barrier = pltpu.get_barrier_semaphore()
        for device in (self.along(1), self.along(-1), self.mate, self.twin):
            pl.semaphore_signal(barrier, inc=1, device_id=device, device_id_type=MESH)
        pl.semaphore_wait(barrier, 4)


def rcopy(src, dst, send, recv, device):
    return pltpu.make_async_remote_copy(
        src_ref=src, dst_ref=dst, send_sem=send, recv_sem=recv, device_id=device, device_id_type=MESH
    )


def dot_nn(a, b):
    return lax.dot_general(a, b, (((1,), (0,)), ((), ())), preferred_element_type=F32)


def dot_nt(a, b):
    return lax.dot_general(a, b, (((1,), (1,)), ((), ())), preferred_element_type=F32)


def dot_tn(a, b):
    return lax.dot_general(a, b, (((0,), (0,)), ((), ())), preferred_element_type=F32)


def norm_parts(rows):
    centred = rows - jnp.mean(rows, axis=-1, keepdims=True)
    spread = jnp.mean(centred * centred, axis=-1, keepdims=True)
    inverse = lax.rsqrt(spread + EPS)
    return centred * inverse, inverse


def split_dot(dot, left, right, narrow):
    total = None
    rest = left
    for _ in range(narrow):
        term = rest.astype(BF16)
        part = dot(term, right)
        total = part if total is None else total + part
        rest = rest - term.astype(F32)
    return total


def lane_scan(values, factor, reverse):
    width = values.shape[1]
    lane = lax.broadcasted_iota(jnp.int32, values.shape, 1)
    shift = 1
    power = factor
    while shift < width:
        if reverse:
            moved = pltpu.roll(values, width - shift, 1)
            moved = jnp.where(lane < width - shift, moved, 0.0)
        else:
            moved = pltpu.roll(values, shift, 1)
            moved = jnp.where(lane >= shift, moved, 0.0)
        values = values + power * moved
        power = power * power
        shift *= 2
    return values


def forward_kernel(
    tok, wq, wk, wv, wo, wup, sio, fg, fb, skip, sg, sb, decay,
    wall, sio_all, rnd_o, q_o, k_o, v_o, att_o, res_o, sec_o, p_o, u_o, st_o,
    tok_s, rnd_s, w_s, q_s, k_s, v_s, att_s, res_s, sec_s, pbuf, nctx, sio_s,
    own_s, loc, rs, rr, ss, sr, cs, cr, xs, xr, outs, psem,
):
    net = Net()
    rep, core = net.rep, net.core
    rows_of = 64
    width = 1024

    def block(shard):
        return pl.ds(pl.multiple_of(shard * rows_of, rows_of), rows_of)

    mine = block(net.shard)
    own = [wq, wk, wv, wo]
    copies = [pltpu.make_async_copy(own[i], own_s.at[i], loc.at[i]) for i in range(4)]
    copies += [
        pltpu.make_async_copy(wup.at[:, pl.ds(i * width, width)], own_s.at[4 + i], loc.at[4 + i])
        for i in range(4)
    ]
    small = pltpu.make_async_copy(sio, sio_all.at[mine], loc.at[8])
    arrive = pltpu.make_async_copy(tok, tok_s, loc.at[9])
    for copy in copies:
        copy.start()
    small.start()
    arrive.start()
    net.greet()
    for copy in copies:
        copy.wait()

    def piece(slot):
        if isinstance(slot, int) and slot < 2:
            return 1 if slot else 2 * rep
        later = slot - 2
        return 3 + later + 3 * rep * ((later % 2) * (3 - later) // 2)

    def ring(slot, way, hop, which, where):
        ref = wall.at[which, where]
        sems = rs.at[slot, way, hop], rr.at[slot, way, hop]
        return rcopy(ref, ref, *sems, net.along(1 - 2 * way))

    def ring_own(slot, way):
        which = piece(slot)
        sems = rs.at[slot, way, 0], rr.at[slot, way, 0]
        ref = wall.at[which, mine]
        rcopy(own_s.at[which], ref, *sems, net.along(1 - 2 * way)).start()

    def ring_small(way, hop, where):
        ref = sio_all.at[where]
        return rcopy(ref, ref, ss.at[way, hop], sr.at[way, hop], net.along(1 - 2 * way))

    def mate(which, index, where):
        ref = wall.at[which, where]
        return rcopy(ref, ref, cs.at[which, index], cr.at[which, index], net.mate)

    def mate_small(index, where):
        ref = sio_all.at[where]
        return rcopy(ref, ref, cs.at[8, index], cr.at[8, index], net.mate)

    def twin(turn, index, which, where):
        ref = wall.at[which, where]
        return rcopy(ref, ref, xs.at[turn, index], xr.at[turn, index], net.twin)

    def source(way, hop):
        return block(net.at((2 * way - 1) * (hop + 1), core))

    def serve(slot, way, hop):
        which = piece(slot)
        where = source(way, hop)
        ring(slot, way, hop, which, where).wait_recv()

        @pl.when(hop < 3 - way)
        def _():
            ring(slot, way, hop + 1, which, where).start()

        mate(which, 1 + 2 * hop + way, where).start()

    def serve_out(slot, turn, way, hop):
        twin(turn, 2 * hop + way, piece(slot), source(way, hop)).start()

    def serve_in(turn, way, hop):
        where = source(way, hop)
        which = 2 * (1 - rep) if turn == 0 else 7 - 3 * rep
        twin(turn, 2 * hop + way, which, where).wait_recv()
        mate(which, 1 + 2 * hop + way, where).start()

    for slot in range(2):
        for way in range(2):
            ring_own(slot, way)
    small.wait()
    for way in range(2):
        ring_small(way, 0, mine).start()
    mate_small(0, mine).start()
    for which in range(8):
        rcopy(own_s.at[which], wall.at[which, mine], cs.at[which, 0], cr.at[which, 0], net.mate).start()
    keep = [pltpu.make_async_copy(own_s.at[i], wall.at[i, mine], loc.at[i]) for i in range(8)]
    for copy in keep:
        copy.start()
    arrive.wait()

    def first_norm(at):
        rows = pl.ds(pl.multiple_of(at * 128, 128), 128)
        xhat, _ = norm_parts(tok_s[rows, :].astype(F32))
        normed = xhat * fg[...] + fb[...]
        rnd_s[rows, :] = normed.astype(BF16)

    turns = [(hop, way) for hop in range(4) for way in range(2) if hop < 4 - way]
    for n, (hop, way) in enumerate(turns):
        first_norm(n)
        serve(0, way, hop)
        serve_out(0, 0, way, hop)
        serve(1, way, hop)
        where = source(way, hop)
        ring_small(way, hop, where).wait_recv()
        if hop < 3 - way:
            ring_small(way, hop + 1, where).start()
        mate_small(1 + 2 * hop + way, where).start()
        if n == 3:
            for slot in range(2, 6):
                for each in range(2):
                    ring_own(slot, each)
        if n >= 3:
            serve_in(0, turns[n - 3][1], turns[n - 3][0])
    first_norm(7)
    for hop, way in turns[-3:]:
        serve_in(0, way, hop)

    def event(m):
        hop = m // 8
        way = (m % 8) // 4
        slot = 2 + m % 4
        serve(slot, way, hop)

        @pl.when(slot == 3)
        def _():
            serve_out(3, 1, way, hop)

        @pl.when((slot == 3) & (m >= 8))
        def _():
            serve_in(1, way, hop - 1)

    xhat, _ = norm_parts(tok_s[pl.ds(BLK - CTX, CTX), :].astype(F32))
    nctx[...] = xhat * fg[...] + fb[...]

    @pl.loop(0, NC)
    def _(index):
        where = block(0)
        mate_small(index, where).wait_recv()
        for which in range(3):
            mate(which, index, where).wait_recv()

    for copy in keep:
        copy.wait()
    loads = [pltpu.make_async_copy(sio_all, sio_s, loc.at[8])]
    loads += [pltpu.make_async_copy(wall.at[i], w_s.at[i], loc.at[i]) for i in range(3)]
    for copy in loads:
        copy.start()
    loads[0].wait()
    u_all = lax.dot_general(
        sio_s[...], rnd_s[pl.ds(0, BLK), :], (((0,), (1,)), ((), ())), preferred_element_type=F32
    )
    factor = jnp.exp(-decay[...])
    raw = u_all[0:16, :]
    u_o[...] = raw
    states = lane_scan(raw * jnp.sqrt(1.0 - factor * factor), factor, False)
    st_o[...] = states
    tail = states[:, BLK - CTX :]
    padded = jnp.concatenate(
        [jnp.zeros((16, CTX), F32), tail, jnp.zeros((96, CTX), F32)], axis=0
    )
    made = split_dot(
        lambda a, b: lax.dot_general(a, b, (((0,), (1,)), ((), ())), preferred_element_type=F32),
        padded, sio_s[...], 3,
    )
    rnd_s[pl.ds(1024, CTX), :] = (made + skip[...] * nctx[...]).astype(BF16)
    finals = [pltpu.make_async_copy(rnd_s, rnd_o, outs.at[0])]
    finals[0].start()

    for copy in loads[1:]:
        copy.wait()

    @pl.loop(0, 4)
    def _(at):
        cols = pl.ds(pl.multiple_of(at * 256, 256), 256)
        q_s[:, cols] = dot_nn(rnd_s[pl.ds(0, 1024), :], w_s[0, :, cols]).astype(BF16)
        event(3 * at)
        k_s[:, cols] = dot_nn(rnd_s[...], w_s[1, :, cols]).astype(BF16)
        event(3 * at + 1)
        v_s[:, cols] = dot_nn(rnd_s[...], w_s[2, :, cols]).astype(BF16)
        event(3 * at + 2)

    for i, (a, b) in enumerate(((q_s, q_o), (k_s, k_o), (v_s, v_o))):
        finals.append(pltpu.make_async_copy(a, b, outs.at[1 + i]))
        finals[-1].start()

    for half in range(2):
        pbuf[half] = jnp.zeros((BLK, CTX + BLK), BF16)

    def p_copy(slot, at):
        return pltpu.make_async_copy(pbuf.at[slot], p_o.at[at], psem.at[slot])

    for b in range(NBLK):

        @pl.loop(0, 8)
        def _(h, b=b):
            cols = pl.ds(pl.multiple_of(h * DH, DH), DH)
            slot = h % 2
            if b == 0:

                @pl.when(h >= 2)
                def _():
                    p_copy(slot, h).wait()
            else:
                p_copy(slot, h).wait()
            for i in range(2):
                span = (i + 1) * 256
                rows = pl.ds(b * BLK + i * 256, 256)
                queries = q_s[rows, cols]
                scores = dot_nt(queries, k_s[pl.ds(b * BLK, span), cols]) * SCALE
                ahead = lax.broadcasted_iota(jnp.int32, scores.shape, 0) + i * 256
                scores = jnp.where(
                    ahead >= lax.broadcasted_iota(jnp.int32, scores.shape, 1), scores, NEG
                )
                top = jnp.max(scores, axis=-1, keepdims=True)
                if b:
                    before = dot_nt(queries, k_s[pl.ds(1024, CTX), cols]) * SCALE
                    top = jnp.maximum(top, jnp.max(before, axis=-1, keepdims=True))
                expos = jnp.exp(scores - top)
                total = jnp.sum(expos, axis=-1, keepdims=True)
                if b:
                    expos_before = jnp.exp(before - top)
                    total = total + jnp.sum(expos_before, axis=-1, keepdims=True)
                share = 1.0 / total
                weights = (expos * share).astype(BF16)
                mixed = dot_nn(weights, v_s[pl.ds(b * BLK, span), cols])
                pbuf[slot, pl.ds(i * 256, 256), pl.ds(CTX, span)] = weights
                if b:
                    weights = (expos_before * share).astype(BF16)
                    mixed = mixed + dot_nn(weights, v_s[pl.ds(1024, CTX), cols])
                    pbuf[slot, pl.ds(i * 256, 256), pl.ds(0, CTX)] = weights
                att_s[rows, cols] = mixed.astype(BF16)
            p_copy(slot, b * 8 + h).start()
            event(12 + b * 8 + h)

    finals.append(pltpu.make_async_copy(att_s, att_o, outs.at[4]))
    finals[-1].start()

    @pl.loop(0, NC)
    def _(index):
        mate(3, index, block(0)).wait_recv()

    load = pltpu.make_async_copy(wall.at[3], w_s.at[3], loc.at[3])
    load.start()
    load.wait()

    @pl.loop(0, 4)
    def _(at):
        rows = pl.ds(pl.multiple_of(at * 256, 256), 256)
        residual = tok_s[rows, :].astype(F32) + dot_nn(att_s[rows, :], w_s[3])
        res_s[rows, :] = residual
        xhat, _ = norm_parts(residual)
        sec_s[rows, :] = (xhat * sg[...] + sb[...]).astype(BF16)
        pltpu.make_async_copy(res_s.at[rows], res_o.at[rows], outs.at[5 + at]).start()
        pltpu.make_async_copy(sec_s.at[rows], sec_o.at[rows], outs.at[9 + at]).start()

    for copy in finals:
        copy.wait()
    for at in range(4):
        rows = pl.ds(at * 256, 256)
        pltpu.make_async_copy(res_s.at[rows], res_o.at[rows], outs.at[5 + at]).wait()
        pltpu.make_async_copy(sec_s.at[rows], sec_o.at[rows], outs.at[9 + at]).wait()
    for slot in range(2):
        p_copy(slot, slot).wait()

    serve_in(1, 1, 2)
    serve_in(1, 0, 3)

    @pl.loop(0, NC)
    def _(index):
        for which in range(4, 8):
            mate(which, index, block(0)).wait_recv()
        for which in range(8):
            mate(which, index, block(0)).wait_send()
        mate_small(index, block(0)).wait_send()

    @pl.loop(0, NC - 1)
    def _(index):
        hop = index // 2
        way = index % 2
        for slot in range(6):
            ring(slot, way, hop, 0, block(0)).wait_send()
        ring_small(way, hop, block(0)).wait_send()
        for turn in range(2):
            twin(turn, index, 0, block(0)).wait_send()


def any_spec(n):
    return [pl.BlockSpec(memory_space=pl.ANY)] * n


def vmem_spec(n):
    return [pl.BlockSpec(memory_space=pltpu.VMEM)] * n


def run_forward(tok, wq, wk, wv, wo, wup, sio, fg, fb, skip, sg, sb, decay):
    shape = jax.ShapeDtypeStruct
    dma = pltpu.SemaphoreType.DMA
    big = (1024, 1024)
    ext = (1024 + CTX, 1024)
    return pl.pallas_call(
        forward_kernel,
        name="forward_part",
        out_shape=(
            shape((8,) + big, BF16), shape((1024, 128), BF16), shape(ext, BF16), shape(big, BF16),
            shape(ext, BF16), shape(ext, BF16), shape(big, BF16), shape(big, F32),
            shape(big, BF16), shape((16, BLK, CTX + BLK), BF16), shape((16, BLK), F32),
            shape((16, BLK), F32),
        ),
        in_specs=any_spec(7) + vmem_spec(6),
        out_specs=any_spec(10) + vmem_spec(2),
        scratch_shapes=[
            pltpu.VMEM(big, BF16), pltpu.VMEM(ext, BF16), pltpu.VMEM((4,) + big, BF16),
            pltpu.VMEM(big, BF16), pltpu.VMEM(ext, BF16), pltpu.VMEM(ext, BF16),
            pltpu.VMEM(big, BF16), pltpu.VMEM(big, F32), pltpu.VMEM(big, BF16),
            pltpu.VMEM((2, BLK, CTX + BLK), BF16), pltpu.VMEM((CTX, 1024), F32),
            pltpu.VMEM((1024, 128), BF16),
            pltpu.VMEM((8, 64, 1024), BF16),
            dma((10,)), dma((6, 2, 4)), dma((6, 2, 4)), dma((2, 4)), dma((2, 4)),
            dma((9, NC)), dma((9, NC)), dma((2, NC - 1)), dma((2, NC - 1)), dma((13,)), dma((2,)),
        ],
        compiler_params=pltpu.CompilerParams(
            collective_id=0, has_side_effects=True, vmem_limit_bytes=VMEM_LIMIT
        ),
    )(tok, wq, wk, wv, wo, wup, sio, fg, fb, skip, sg, sb, decay)


GELU_C = math.sqrt(2.0 / math.pi)
GELU_A = 0.044715


def feed_kernel(
    sec, res, wall, wdn, cot, live, upb, dnb, sg,
    out_o, gatt_o, dwup_o, piece_o, gdb_o, gub_o, gsg_o, gsb_o,
    sec_s, gb_s, wup_s, wd_s, br_s, gs_s, act_s, gh_s, a_s, b_s, prec, rrec, rsend, xsend, xrec,
    xfs, xfr, dwup_s, own_s, res_s,
    loc, ars, arr, axs, axr, cas, car, cxs, cxr, ps, pr, rs, rr, xs, xr, fs, fr, outs, dsem,
):
    net = Net()
    rep, core = net.rep, net.core
    rows_of = 256
    ring_rows = 192
    part = 64
    ahead, behind = net.along(1), net.along(-1)

    def ring_part(shard, size=ring_rows, first=rep * part):
        return pl.ds(pl.multiple_of(shard * rows_of + first, part), size)

    def sole_part(shard, of):
        return pl.ds(pl.multiple_of(shard * rows_of + 3 * of * part, part), part)

    def block(shard):
        return pl.ds(pl.multiple_of(shard * rows_of, rows_of), rows_of)

    def mine_at(step):
        return net.at(-(step + 1), core)

    def other_at(step):
        return net.at(step + 1, 1 - core)

    loads = [
        pltpu.make_async_copy(wdn, own_s, loc.at[0]),
        pltpu.make_async_copy(sec, sec_s, loc.at[1]),
        pltpu.make_async_copy(cot, gb_s, loc.at[2]),
    ]
    loads += [pltpu.make_async_copy(wall.at[4 + i], wup_s.at[i], loc.at[3 + i]) for i in range(4)]
    for load in loads:
        load.start()
    net.greet()
    loads[0].wait()

    def gather(hop, shard):
        ref = wd_s.at[ring_part(shard)]
        return rcopy(ref, ref, ars.at[hop], arr.at[hop], ahead)

    def gather_twin(hop, shard, of):
        ref = wd_s.at[sole_part(shard, of)]
        return rcopy(ref, ref, axs.at[hop], axr.at[hop], net.twin)

    def mate_ring(index, shard, first):
        ref = wd_s.at[ring_part(shard, ring_rows, first)]
        return rcopy(ref, ref, cas.at[index], car.at[index], net.mate)

    def mate_sole(index, shard, of):
        ref = wd_s.at[sole_part(shard, of)]
        return rcopy(ref, ref, cxs.at[index], cxr.at[index], net.mate)

    here = net.shard
    ring_own = own_s.at[pl.ds(pl.multiple_of(rep * part, part), ring_rows)]
    sole_own = own_s.at[pl.ds(pl.multiple_of(3 * (1 - rep) * part, part), part)]
    rcopy(ring_own, wd_s.at[ring_part(here)], ars.at[0], arr.at[0], ahead).start()
    rcopy(ring_own, wd_s.at[ring_part(here)], cas.at[0], car.at[0], net.mate).start()
    rcopy(sole_own, wd_s.at[sole_part(here, 1 - rep)], cxs.at[0], cxr.at[0], net.mate).start()

    def serve(hop):
        shard = mine_at(hop)
        gather(hop, shard).wait_recv()

        @pl.when(hop < NC - 2)
        def _():
            gather(hop + 1, shard).start()

        gather_twin(hop, shard, rep).start()
        mate_ring(hop + 1, shard, rep * part).start()

    def serve_twin(hop):
        shard = mine_at(hop)
        gather_twin(hop, shard, 1 - rep).wait_recv()
        mate_sole(hop + 1, shard, 1 - rep).start()

    for load in loads[1:3]:
        load.wait()

    wd_s[block(here), :] = own_s[...]

    @pl.loop(0, 4)
    def _(at):
        rows = pl.ds(pl.multiple_of(at * 256, 256), 256)
        when = lax.broadcasted_iota(jnp.int32, (256, 1024), 0) + at * 256
        kept = jnp.where(when < live[...], gb_s[rows, :].astype(F32), 0.0)
        gb_s[rows, :] = kept.astype(BF16)
        added = jnp.sum(kept, axis=0, keepdims=True)
        gdb_o[...] = jnp.where(at == 0, added, gdb_o[...] + added)
        br_s[rows, :] = jnp.zeros((256, 1024), F32)
        gs_s[rows, :] = jnp.zeros((256, 1024), F32)

    serve(0)
    for load in loads[3:]:
        load.wait()
    serve_twin(0)

    def to_mate(step):
        slot = step % 2
        return rcopy(b_s.at[slot], prec.at[step], ps.at[step], pr.at[step], net.mate)

    def to_ring(step):
        return rcopy(rsend.at[step % 2], rrec.at[step], rs.at[step], rr.at[step], ahead)

    def to_twin(step):
        return rcopy(xsend.at[step % 2], xrec.at[step], xs.at[step], xr.at[step], net.twin)

    def dwup_copy(slot, half, shard):
        cols = pl.ds(pl.multiple_of((shard % 4) * 256, 256), 256)
        return pltpu.make_async_copy(
            dwup_s.at[slot, half], dwup_o.at[shard // 4, :, cols], dsem.at[slot, half]
        )

    ring_local = pl.ds(pl.multiple_of(rep * part, part), ring_rows)
    sole_mine = pl.ds(pl.multiple_of(3 * rep * part, part), part)
    sole_theirs = pl.ds(pl.multiple_of(3 * (1 - rep) * part, part), part)

    def combine(step):
        slot = step % 2
        to_mate(step).wait_recv()
        a_s[slot] = a_s[slot] + prec[step].astype(F32)

        @pl.when(step >= 2)
        def _():
            to_twin(step - 2).wait_send()

        xsend[slot] = a_s[slot, sole_theirs, :].astype(BF16)
        to_twin(step).start()

    def forward(step):
        slot = step % 2
        to_twin(step).wait_recv()
        a_s[slot, sole_mine, :] = a_s[slot, sole_mine, :] + xrec[step].astype(F32)

        @pl.when(step >= 1)
        def _():
            to_ring(step - 1).wait_recv()
            a_s[slot, ring_local, :] = a_s[slot, ring_local, :] + rrec[step - 1].astype(F32)

        @pl.when((step >= 2) & (step < NC - 1))
        def _():
            to_ring(step - 2).wait_send()

        @pl.when(step < NC - 1)
        def _():
            rsend[slot] = a_s[slot, ring_local, :].astype(BF16)
            to_ring(step).start()

    @pl.loop(0, NC)
    def _(step):
        slot = step % 2
        a, b = mine_at(step), other_at(step)
        index = (step + 1) % NC
        mate_ring(index, b, rep * part).wait_recv()
        mate_sole(index, b, 1 - rep).wait_recv()

        @pl.when(step < NC - 2)
        def _():
            serve(step + 1)

        def up(shard):
            cols = pl.ds(pl.multiple_of((shard % 4) * 256, 256), 256)
            return wup_s[shard // 4, :, cols]

        def bias(shard):
            return upb[:, pl.ds(pl.multiple_of(shard * 256, 256), 256)]

        @pl.loop(0, 4)
        def _(at):
            rows = pl.ds(pl.multiple_of(at * 256, 256), 256)
            for half, shard in enumerate((a, b)):
                cols = pl.ds(half * 256, 256)
                hidden = dot_nn(sec_s[rows, :], up(shard)) + bias(shard)
                grad = dot_nt(gb_s[rows, :], wd_s[block(shard), :])
                square = hidden * hidden
                bent = jnp.tanh(hidden * (GELU_C + (GELU_C * GELU_A) * square))
                half_up = 0.5 + 0.5 * bent
                act_s[rows, cols] = (hidden * half_up).astype(BF16)
                slope = half_up + (0.5 * hidden) * (1.0 - bent * bent) * (
                    GELU_C + (3.0 * GELU_C * GELU_A) * square
                )
                gh_s[rows, cols] = (grad * slope).astype(BF16)

        @pl.when(step < NC - 2)
        def _():
            serve_twin(step + 1)

        @pl.when(step >= 1)
        def _():
            combine(step - 1)

        made = dot_tn(act_s[...], gb_s[...])

        @pl.when(step >= 2)
        def _():
            to_mate(step - 2).wait_send()

        a_s[slot] = made[0:256]
        b_s[slot] = made[256:512].astype(BF16)
        to_mate(step).start()

        for half, shard in enumerate((a, b)):
            cols = pl.ds(pl.multiple_of(shard * 256, 256), 256)
            gub_o[:, cols] = jnp.sum(
                gh_s[:, half * 256 : half * 256 + 256].astype(F32), axis=0, keepdims=True
            )

            @pl.when(step >= 2)
            def _(half=half, shard=shard):
                dwup_copy(slot, half, shard).wait()

            dwup_s[slot, half] = dot_tn(sec_s[...], gh_s[:, half * 256 : half * 256 + 256]).astype(BF16)
            dwup_copy(slot, half, shard).start()

        @pl.when(step >= 1)
        def _():
            forward(step - 1)

        @pl.loop(0, 4)
        def _(at):
            rows = pl.ds(pl.multiple_of(at * 256, 256), 256)
            down = jnp.concatenate([wd_s[block(a), :], wd_s[block(b), :]], axis=0)
            br_s[rows, :] = br_s[rows, :] + dot_nn(act_s[rows, :], down)
            rise = jnp.concatenate([up(a), up(b)], axis=1)
            gs_s[rows, :] = gs_s[rows, :] + dot_nt(gh_s[rows, :], rise)

    def residual_in(at):
        rows = pl.ds(at * 256, 256)
        return pltpu.make_async_copy(res.at[rows], res_s.at[rows], loc.at[at])

    for at in range(4):
        residual_in(at).start()
    combine(NC - 1)

    def leave(at, which):
        rows = pl.ds(pl.multiple_of(at * 256, 256), 256)
        source = (sec_s, gb_s)[which]
        return pltpu.make_async_copy(
            source.at[rows], (out_o, gatt_o)[which].at[rows], outs.at[which, at]
        )

    @pl.loop(0, 4)
    def _(at):
        residual_in(at).wait()
        rows = pl.ds(pl.multiple_of(at * 256, 256), 256)
        kept = res_s[rows, :]
        when = lax.broadcasted_iota(jnp.int32, (256, 1024), 0) + at * 256
        total = kept + br_s[rows, :] + dnb[...]
        sec_s[rows, :] = jnp.where(when < live[...], total, 0.0).astype(BF16)
        xhat, inverse = norm_parts(kept)
        grad = gs_s[rows, :]
        gain = jnp.sum(grad * xhat, axis=0, keepdims=True)
        shift = jnp.sum(grad, axis=0, keepdims=True)
        gsg_o[...] = jnp.where(at == 0, gain, gsg_o[...] + gain)
        gsb_o[...] = jnp.where(at == 0, shift, gsb_o[...] + shift)
        grad = grad * sg[...]
        grad = grad - jnp.mean(grad, axis=-1, keepdims=True) - xhat * jnp.mean(
            grad * xhat, axis=-1, keepdims=True
        )
        gb_s[rows, :] = (gb_s[rows, :].astype(F32) + inverse * grad).astype(BF16)
        for which in range(2):
            leave(at, which).start()

    forward(NC - 1)
    last = (NC - 1) % 2
    xfs[...] = a_s[last, ring_local, :].astype(BF16)
    swap = rcopy(xfs, xfr, fs.at[0], fr.at[0], net.twin)
    swap.start()

    @pl.loop(0, NC - 1)
    def _(hop):
        gather(hop, 0).wait_send()
        gather_twin(hop, 0, 0).wait_send()

    @pl.loop(0, NC)
    def _(index):
        mate_ring(index, 0, 0).wait_send()
        mate_sole(index, 0, 0).wait_send()

    for step in range(NC - 2, NC):
        to_mate(step).wait_send()
        to_twin(step).wait_send()
        to_ring(step - 1).wait_send()
        for half in range(2):
            dwup_copy(step % 2, half, 0).wait()
    for at in range(4):
        for which in range(2):
            leave(at, which).wait()
    swap.wait()
    theirs = pl.ds(pl.multiple_of((1 - rep) * part, part), ring_rows)
    piece_o[...] = jnp.zeros((rows_of, 1024), F32)
    piece_o[ring_local, :] = xfs[...].astype(F32)
    piece_o[theirs, :] = piece_o[theirs, :] + xfr[...].astype(F32)


def run_feed(sec, res, wall, wdn, cot, live, upb, dnb, sg):
    shape = jax.ShapeDtypeStruct
    dma = pltpu.SemaphoreType.DMA
    vmem = pltpu.VMEM
    big = (1024, 1024)
    return pl.pallas_call(
        feed_kernel,
        name="feed_part",
        out_shape=(
            shape(big, BF16), shape(big, BF16), shape((4,) + big, BF16),
            shape((256, 1024), F32), shape((1, 1024), F32), shape((1, 4096), F32),
            shape((1, 1024), F32), shape((1, 1024), F32),
        ),
        in_specs=any_spec(5) + vmem_spec(4),
        out_specs=any_spec(3) + vmem_spec(5),
        scratch_shapes=[
            vmem(big, BF16), vmem(big, BF16), vmem((4,) + big, BF16), vmem((4096, 1024), BF16),
            vmem(big, F32), vmem(big, F32), vmem((1024, 512), BF16), vmem((1024, 512), BF16),
            vmem((2, 256, 1024), F32), vmem((2, 256, 1024), BF16), vmem((NC, 256, 1024), BF16),
            vmem((NC - 1, 192, 1024), BF16), vmem((2, 192, 1024), BF16), vmem((2, 64, 1024), BF16),
            vmem((NC, 64, 1024), BF16), vmem((192, 1024), BF16), vmem((192, 1024), BF16),
            vmem((2, 2, 1024, 256), BF16), vmem((256, 1024), BF16), vmem(big, F32),
            dma((7,)), dma((NC - 1,)), dma((NC - 1,)), dma((NC - 1,)), dma((NC - 1,)),
            dma((NC,)), dma((NC,)), dma((NC,)), dma((NC,)), dma((NC,)), dma((NC,)),
            dma((NC - 1,)), dma((NC - 1,)), dma((NC,)), dma((NC,)), dma((1,)), dma((1,)),
            dma((2, 4)), dma((2, 2)),
        ],
        compiler_params=pltpu.CompilerParams(
            collective_id=1, has_side_effects=True, vmem_limit_bytes=VMEM_LIMIT
        ),
    )(sec, res, wall, wdn, cot, live, upb, dnb, sg)


def backward_kernel(
    dwup, gatt, att, wall, q, kx, vx, rnd, p, tok, sio, u_in, st_in, fg, fb, skip, decay,
    gtok_o, dup_o, do_o, dq_o, dk_o, dv_o, gfg_o, gfb_o, gskip_o, gsi_o, gso_o, grate_o,
    own_b, prec_b, rrec_b, xrec_b, fin_b, finr_b, acc_b,
    own_g, prec_g, rrec_g, xrec_g, fin_g, finr_g, acc_g, go_s,
    gatt_s, wo_s, att_s, ga_s, q_s, k_s, v_s, rnd_s, dk_s, dv_s, pbuf, ds_s, gres_s, nb_s,
    sio_s, gd_s, gctx_s,
    loc, psem, gsem, osem, mbs, mbr, mgs, mgr, rbs, rbr, rgs, rgr, xbs, xbr, xgs, xgr,
    fbs, fbr, fgs, fgr,
):
    net = Net()
    rep, core = net.rep, net.core
    theirs = 1 - core

    loads = [
        pltpu.make_async_copy(gatt, gatt_s, loc.at[0]),
        pltpu.make_async_copy(wall.at[3], wo_s, loc.at[1]),
        pltpu.make_async_copy(att, att_s, loc.at[2]),
        pltpu.make_async_copy(q, q_s, loc.at[3]),
        pltpu.make_async_copy(kx, k_s, loc.at[4]),
        pltpu.make_async_copy(vx, v_s, loc.at[5]),
        pltpu.make_async_copy(rnd, rnd_s, loc.at[6]),
        pltpu.make_async_copy(sio, sio_s, loc.at[7]),
    ]
    rises = [pltpu.make_async_copy(dwup.at[i, :, core], own_b.at[i], loc.at[8 + i]) for i in range(4)]
    for copy in rises:
        copy.start()
    for copy in loads:
        copy.start()
    fin_b[...] = jnp.zeros(fin_b.shape, BF16)
    finr_b[...] = jnp.zeros(finr_b.shape, BF16)
    fin_g[...] = jnp.zeros(fin_g.shape, BF16)
    finr_g[...] = jnp.zeros(finr_g.shape, BF16)
    net.greet()

    def mate_big(which, source):
        return rcopy(source, prec_b.at[which], mbs.at[which], mbr.at[which], net.mate)

    def mate_group(g):
        return rcopy(own_g.at[g, :, theirs], prec_g.at[g], mgs.at[g], mgr.at[g], net.mate)

    for i in (0, 3, 1, 2):
        mate_big(i, dwup.at[i, :, theirs]).start()

    def chip_for(n):
        t, way = n // 2, n % 2
        hops = (4 - t) * (1 - way) + (t - 3) * way
        return chip_at((net.pos + net.step * hops + 4 * NC) % NC)

    class Stream:
        def __init__(self, own, prec, rrec, xrec, fin, finr, acc, sems):
            self.own, self.prec, self.rrec, self.xrec = own, prec, rrec, xrec
            self.fin, self.finr, self.acc = fin, finr, acc
            self.rs, self.rr, self.xs, self.xr, self.fs, self.fr = sems

        def ring(self, slot, which, n):
            source = self.prec.at[which, chip_for(n)]
            way = n % 2
            return rcopy(
                source, self.rrec.at[slot, n], self.rs.at[slot, n], self.rr.at[slot, n],
                net.along(1 - 2 * way),
            )

        def twin(self, which, n):
            chip = chip_for(n)
            return rcopy(
                self.prec.at[which, chip], self.xrec.at[chip], self.xs.at[n], self.xr.at[n], net.twin
            )

        def finish(self, which):
            return rcopy(
                self.fin.at[which], self.finr.at[which], self.fs.at[which], self.fr.at[which], net.twin
            )

        def give(self, which, n):
            chip = chip_for(n)
            self.prec[which, chip] = (
                self.own(which, chip).astype(F32) + self.prec[which, chip].astype(F32)
            ).astype(BF16)
            self.twin(which, n).start()

        def turn(self, slot, which, n, sole):
            chip = chip_for(n)
            self.acc[...] = self.own(which, chip).astype(F32) + self.prec[which, chip].astype(F32)

            @pl.when(sole)
            def _():
                self.twin(which, n).wait_recv()
                self.acc[...] = self.acc[...] + self.xrec[chip].astype(F32)

            @pl.when((n >= 2) & (n < 7))
            def _():
                self.ring(slot, which, n - 2).wait_recv()
                self.acc[...] = self.acc[...] + self.rrec[slot, n - 2].astype(F32)

            @pl.when(n < 7)
            def _():
                self.prec[which, chip] = self.acc[...].astype(BF16)
                self.ring(slot, which, n).start()

            @pl.when(n == 7)
            def _():
                self.ring(slot, which, 5).wait_recv()
                self.ring(slot, which, 6).wait_recv()
                total = self.acc[...] + self.rrec[slot, 5].astype(F32) + self.rrec[slot, 6].astype(F32)
                self.fin[which] = total.astype(BF16)
                self.finish(which).start()

    big = Stream(
        lambda which, chip: go_s[chip, core] if isinstance(which, int) and which == 4 else own_b[which, chip],
        prec_b, rrec_b, xrec_b, fin_b, finr_b, acc_b,
        (rbs, rbr, xbs, xbr, fbs, fbr),
    )
    group = Stream(
        lambda which, chip: own_g[which, chip, core], prec_g, rrec_g, xrec_g, fin_g, finr_g, acc_g,
        (rgs, rgr, xgs, xgr, fgs, fgr),
    )

    def rise(j):
        return j + 3 * rep * ((2 - j) // 2)

    for i in range(2):
        loads[i].wait()

    def p_copy(slot, at):
        return pltpu.make_async_copy(p.at[at], pbuf.at[slot], psem.at[slot])

    p_copy(0, 0).start()

    @pl.loop(0, 4)
    def _(at):
        rows = pl.ds(pl.multiple_of(at * 256, 256), 256)
        ga_s[rows, :] = dot_nt(gatt_s[rows, :], wo_s[...]).astype(BF16)

    for copy in rises:
        copy.wait()
    for i in range(4):
        mate_big(i, dwup.at[i, :, theirs]).wait_recv()

    @pl.loop(0, NC)
    def _(n):
        big.give(3 * (1 - rep), n)

    for n in range(2):
        for j in (1, 2, 0):
            big.turn(j, rise(j), n, j == 0)
    loads[2].wait()

    @pl.loop(0, 4)
    def _(at):
        cols = pl.ds(pl.multiple_of(at * 256, 256), 256)
        made = dot_tn(att_s[...], gatt_s[:, cols]).astype(BF16)
        go_s[:, :, :, cols] = made.reshape(NC, 2, 64, 256)

    mate_big(4, go_s.at[:, theirs]).start()
    tok_load = pltpu.make_async_copy(tok, wo_s, loc.at[0])
    tok_load.start()
    for copy in loads[3:]:
        copy.wait()
    ds_s[...] = jnp.zeros(ds_s.shape, BF16)
    dq_s = gatt_s

    def weights_in(i):
        target = (q_s, k_s.at[pl.ds(0, 1024)], v_s.at[pl.ds(0, 1024)])[i]
        return pltpu.make_async_copy(wall.at[i], target, loc.at[1 + i])

    @pl.loop(0, 4)
    def _(g):
        for hh in range(2):
            for b in range(NBLK):
                i = 2 * hh + b
                m = 4 * g + i
                h = 2 * g + hh
                slot = i % 2
                cols = pl.ds(pl.multiple_of(h * DH, DH), DH)
                following = 2 * hh + b + 1
                nb, nh = following % 2, 2 * g + following // 2
                p_copy(slot, b * 8 + h).wait()
                if following < 4:
                    p_copy(1 - slot, nb * 8 + nh).start()
                else:

                    @pl.when(g < 3)
                    def _():
                        p_copy(1 - slot, nh).start()

                for part in range(2):
                    span = (part + 1) * 256
                    rows = pl.ds(b * BLK + part * 256, 256)
                    local = pl.ds(part * 256, 256)
                    grads = ga_s[rows, cols]
                    slope = dot_nt(grads, v_s[pl.ds(b * BLK, span), cols])
                    kept = pbuf[slot, local, pl.ds(CTX, span)].astype(F32)
                    both = jnp.sum(kept * slope, axis=-1, keepdims=True)
                    mass = jnp.sum(kept, axis=-1, keepdims=True)
                    if b:
                        slope_before = dot_nt(grads, v_s[pl.ds(1024, CTX), cols])
                        kept_before = pbuf[slot, local, pl.ds(0, CTX)].astype(F32)
                        both += jnp.sum(kept_before * slope_before, axis=-1, keepdims=True)
                        mass += jnp.sum(kept_before, axis=-1, keepdims=True)
                    both = both / mass
                    inner = (kept * (slope - both)).astype(BF16)
                    ds_s[local, pl.ds(CTX, span)] = inner
                    total = dot_nn(inner, k_s[pl.ds(b * BLK, span), cols])
                    if b:
                        inner = (kept_before * (slope_before - both)).astype(BF16)
                        ds_s[local, pl.ds(0, CTX)] = inner
                        total = total + dot_nn(inner, k_s[pl.ds(1024, CTX), cols])
                    dq_s[rows, cols] = (total * SCALE).astype(BF16)
                rows = pl.ds(b * BLK, BLK)
                first = 0 if b else CTX
                made_k = dot_tn(ds_s[:, first:], q_s[rows, cols]) * SCALE
                made_v = dot_tn(pbuf[slot, :, first:], ga_s[rows, cols])
                if b:
                    dk_s[pl.ds(1024, CTX), cols] = made_k[:CTX].astype(BF16)
                    dv_s[pl.ds(1024, CTX), cols] = made_v[:CTX].astype(BF16)
                    made_k, made_v = made_k[CTX:], made_v[CTX:]
                dk_s[rows, cols] = made_k.astype(BF16)
                dv_s[rows, cols] = made_v.astype(BF16)

                @pl.when(m < 9)
                def _(m=m):
                    for e in range(2):
                        at = 2 * m + e
                        j = at % 3
                        big.turn(j, rise(j), 2 + at // 3, j == 0)

                @pl.when(m == 4)
                def _():
                    mate_big(4, go_s.at[:, theirs]).wait_recv()

                @pl.when((m >= 4) & (m < 12))
                def _(m=m):
                    big.turn(3, 4, m - 4, False)

                @pl.when(m == 9)
                def _():
                    for each in range(2):
                        mate_group(each).wait_recv()

                @pl.when((m >= 9) & (m < 13))
                def _(m=m):
                    for e in range(2):
                        group.give(1 - rep, 2 * (m - 9) + e)

                @pl.when(m >= 12)
                def _(m=m):
                    for e in range(2):
                        group.turn(0, rep, 2 * (m - 12) + e, True)

        @pl.when(g == 3)
        def _():
            for i in range(3):
                weights_in(i).start()

        cols = pl.ds(pl.multiple_of(g * 256, 256), 256)
        own_g[g, :, :, :, 0:256] = dot_tn(rnd_s[0:1024, :], dq_s[:, cols]).astype(BF16).reshape(NC, 2, 64, 256)
        own_g[g, :, :, :, 256:512] = dot_tn(rnd_s[...], dk_s[:, cols]).astype(BF16).reshape(NC, 2, 64, 256)
        own_g[g, :, :, :, 512:768] = dot_tn(rnd_s[...], dv_s[:, cols]).astype(BF16).reshape(NC, 2, 64, 256)
        mate_group(g).start()

    mate_group(2).wait_recv()
    for n in range(2):
        group.turn(1, 2, n, False)
    for i in range(3):
        weights_in(i).wait()
    tok_load.wait()

    def gres_in(at):
        rows = pl.ds(pl.multiple_of(at * 256, 256), 256)
        return pltpu.make_async_copy(gatt.at[rows], gres_s.at[at % 2], gsem.at[at % 2])

    gres_in(0).start()

    after = pl.ds(1024, CTX)
    gctx = dot_nt(dk_s[after, :], k_s[0:1024, :]) + dot_nt(dv_s[after, :], v_s[0:1024, :])
    gctx_s[...] = gctx
    xhat, _ = norm_parts(wo_s[pl.ds(BLK - CTX, CTX), :].astype(F32))
    gskip_o[...] = jnp.sum(gctx * (xhat * fg[...] + fb[...]), axis=0, keepdims=True)
    mate_group(3).wait_recv()
    for n in range(2):
        group.turn(2, 3, n, False)
    states, raw = st_in[...], u_in[...]
    factor = jnp.exp(-decay[...])
    scale = jnp.sqrt(1.0 - factor * factor)
    gso_o[...] = lax.dot_general(
        states[:, BLK - CTX :], gctx, (((1,), (0,)), ((), ())),
        preferred_element_type=F32, precision=lax.Precision.HIGHEST,
    )
    back = split_dot(
        lambda a, b: lax.dot_general(b, a, (((0,), (1,)), ((), ())), preferred_element_type=F32),
        gctx, sio_s[...], 3,
    )
    seeds = jnp.concatenate([jnp.zeros((16, BLK - CTX), F32), back[16:32, :]], axis=1)
    lam = lane_scan(seeds, factor, True)
    lane = lax.broadcasted_iota(jnp.int32, lam.shape, 1)
    earlier = jnp.where(lane >= 1, pltpu.roll(states, 1, 1), 0.0)
    rates = -factor * jnp.sum(lam * (earlier - (factor / scale) * raw), axis=1, keepdims=True)
    grate_o[...] = jnp.broadcast_to(rates, grate_o.shape)
    driven = scale * lam
    gsi_o[...] = split_dot(dot_nn, driven, rnd_s[0:BLK, :], 3)
    gd_s[...] = jnp.zeros(gd_s.shape, F32)
    gd_s[0:16, 0:BLK] = driven

    def leave(at):
        rows = pl.ds(pl.multiple_of(at * 256, 256), 256)
        return pltpu.make_async_copy(rnd_s.at[rows], gtok_o.at[rows], osem.at[at])

    @pl.loop(0, 4)
    def _(at):
        rows = pl.ds(pl.multiple_of(at * 256, 256), 256)

        @pl.when(at < 3)
        def _():
            gres_in(at + 1).start()

        nb_s[...] = (
            dot_nt(dq_s[rows, :], q_s[...])
            + dot_nt(dk_s[rows, :], k_s[0:1024, :])
            + dot_nt(dv_s[rows, :], v_s[0:1024, :])
            + split_dot(
                lambda a, b: lax.dot_general(a, b, (((0,), (1,)), ((), ())), preferred_element_type=F32),
                gd_s[:, rows], sio_s[...], 3,
            )
        )

        @pl.when(at == 1)
        def _():
            half = pl.ds(128, CTX)
            nb_s[half, :] = nb_s[half, :] + skip[...] * gctx_s[...]

        @pl.when(at < 3)
        def _():
            for e in range(2):
                group.turn(1, 2, 2 + 2 * at + e, False)
                group.turn(2, 3, 2 + 2 * at + e, False)

        xhat, inverse = norm_parts(wo_s[rows, :].astype(F32))
        grad = nb_s[...]
        gain = jnp.sum(grad * xhat, axis=0, keepdims=True)
        shift = jnp.sum(grad, axis=0, keepdims=True)
        gfg_o[...] = jnp.where(at == 0, gain, gfg_o[...] + gain)
        gfb_o[...] = jnp.where(at == 0, shift, gfb_o[...] + shift)
        grad = grad * fg[...]
        grad = grad - jnp.mean(grad, axis=-1, keepdims=True) - xhat * jnp.mean(
            grad * xhat, axis=-1, keepdims=True
        )
        gres_in(at).wait()
        rnd_s[rows, :] = (gres_s[at % 2].astype(F32) + inverse * grad).astype(BF16)
        leave(at).start()

    for j in range(3):
        big.finish(rise(j)).wait_send()
    big.finish(4).wait_send()
    for which in (rep, 2, 3):
        group.finish(which).wait_send()
    twin_rise = 3 * (1 - rep)
    for which in (twin_rise, 1, 2, 4):
        big.finish(which).wait_recv()
    for which in (1 - rep, 2, 3):
        group.finish(which).wait_recv()
    for i in range(4):
        dup_o[:, i * 1024 : (i + 1) * 1024] = fin_b[i].astype(F32) + finr_b[i].astype(F32)
    do_o[...] = fin_b[4].astype(F32) + finr_b[4].astype(F32)
    for g in range(4):
        for i, out in enumerate((dq_o, dk_o, dv_o)):
            cols = slice(i * 256, (i + 1) * 256)
            out[:, g * 256 : (g + 1) * 256] = fin_g[g, :, cols].astype(F32) + finr_g[g, :, cols].astype(F32)

    for i in range(4):
        mate_big(i, dwup.at[i, :, theirs]).wait_send()
        mate_group(i).wait_send()
        leave(i).wait()
    mate_big(4, go_s.at[:, theirs]).wait_send()

    @pl.loop(0, NC)
    def _(n):
        big.twin(3 * (1 - rep), n).wait_send()
        group.twin(1 - rep, n).wait_send()

    @pl.loop(0, NC - 1)
    def _(n):
        for slot in range(4):
            big.ring(slot, 0, n).wait_send()
        for slot in range(3):
            group.ring(slot, 0, n).wait_send()


def run_backward(dwup, gatt, att, wall, q, kx, vx, rnd, p, tok, sio, u, st, fg, fb, skip, decay):
    shape = jax.ShapeDtypeStruct
    dma = pltpu.SemaphoreType.DMA
    vmem = pltpu.VMEM
    full = (1024, 1024)
    ext = (1024 + CTX, 1024)
    part = (64, 1024)
    cut = (64, 768)
    return pl.pallas_call(
        backward_kernel,
        name="backward_part",
        out_shape=(
            shape(full, BF16), shape((64, 4096), F32), shape(part, F32), shape(part, F32),
            shape(part, F32), shape(part, F32), shape((1, 1024), F32), shape((1, 1024), F32),
            shape((1, 1024), F32), shape((16, 1024), F32), shape((16, 1024), F32), shape((16, 128), F32),
        ),
        in_specs=any_spec(11) + vmem_spec(6),
        out_specs=any_spec(1) + vmem_spec(11),
        scratch_shapes=[
            vmem((4, NC) + part, BF16), vmem((5, NC) + part, BF16), vmem((4, NC - 1) + part, BF16),
            vmem((NC,) + part, BF16), vmem((5,) + part, BF16), vmem((5,) + part, BF16), vmem(part, F32),
            vmem((4, NC, 2) + cut, BF16), vmem((4, NC) + cut, BF16), vmem((3, NC - 1) + cut, BF16),
            vmem((NC,) + cut, BF16), vmem((4,) + cut, BF16), vmem((4,) + cut, BF16), vmem(cut, F32),
            vmem((NC, 2) + part, BF16),
            vmem(full, BF16), vmem(full, BF16), vmem(full, BF16), vmem(full, BF16), vmem(full, BF16),
            vmem(ext, BF16), vmem(ext, BF16), vmem(ext, BF16), vmem(ext, BF16), vmem(ext, BF16),
            vmem((2, BLK, CTX + BLK), BF16), vmem((BLK, CTX + BLK), BF16), vmem((2, 256, 1024), BF16),
            vmem((256, 1024), F32), vmem((1024, 128), BF16), vmem((128, 1024), F32), vmem((CTX, 1024), F32),
            dma((12,)), dma((2,)), dma((2,)), dma((4,)), dma((5,)), dma((5,)), dma((4,)), dma((4,)),
            dma((4, NC - 1)), dma((4, NC - 1)), dma((3, NC - 1)), dma((3, NC - 1)),
            dma((NC,)), dma((NC,)), dma((NC,)), dma((NC,)), dma((5,)), dma((5,)), dma((4,)), dma((4,)),
        ],
        compiler_params=pltpu.CompilerParams(
            collective_id=2, has_side_effects=True, vmem_limit_bytes=VMEM_LIMIT
        ),
    )(dwup, gatt, att, wall, q, kx, vx, rnd, p, tok, sio, u, st, fg, fb, skip, decay)


def small_kernel(x, out, got, here, ss, sr, bs, br):
    rep, shard = lax.axis_index("rep"), lax.axis_index("shard")
    me = rep * 16 + shard

    def device(away):
        other = (me + away) % 32
        return other, (other // 16, other % 16)

    barrier = pltpu.get_barrier_semaphore()

    @pl.loop(1, 32)
    def _(away):
        pl.semaphore_signal(barrier, inc=1, device_id=device(away)[1], device_id_type=MESH)

    pl.semaphore_wait(barrier, 31)

    def share(away):
        other, where = device(away)
        return rcopy(x.at[other], got.at[away], ss.at[away], sr.at[away], where)

    def spread(away):
        return rcopy(here, out.at[me], bs.at[away], br.at[away], device(away)[1])

    @pl.loop(1, 32)
    def _(away):
        share(away).start()

    here[...] = x[me]

    @pl.loop(1, 32)
    def _(away):
        share(away).wait_recv()
        here[...] = here[...] + got[away]

    @pl.loop(1, 32)
    def _(away):
        spread(away).start()

    out[me] = here[...]

    @pl.loop(1, 32)
    def _(away):
        spread(away).wait()
        share(away).wait_send()


def run_small(x):
    dma = pltpu.SemaphoreType.DMA
    return pl.pallas_call(
        small_kernel,
        name="small_sums",
        out_shape=jax.ShapeDtypeStruct((32, 16, 128), F32),
        in_specs=vmem_spec(1),
        out_specs=vmem_spec(1)[0],
        scratch_shapes=[
            pltpu.VMEM((32, 16, 128), F32), pltpu.VMEM((16, 128), F32),
            dma((32,)), dma((32,)), dma((32,)), dma((32,)),
        ],
        compiler_params=pltpu.CompilerParams(collective_id=3, has_side_effects=True),
    )(x)


def fused_device(
    tokens, lengths, first_gain, first_bias, decay_rates, state_in, state_out, skip_gain,
    query_weight, key_weight, value_weight, output_weight, second_gain, second_bias,
    up_weight, up_bias, down_weight, down_bias, cotangent,
):
    tok = tokens.reshape(1024, 1024)
    cot = cotangent.reshape(1024, 1024)
    fg, fb, skip, sg, sb, dnb, upb = (
        v.reshape(1, -1)
        for v in (first_gain, first_bias, skip_gain, second_gain, second_bias, down_bias, up_bias)
    )
    decay = decay_rates.reshape(16, 1)
    live = jnp.broadcast_to(lengths.reshape(1, 1), (1, 1024))
    sio = jnp.concatenate([state_in.T, state_out.T, jnp.zeros((64, 96), BF16)], axis=1)
    wall, sio_all, rnd, q, kx, vx, att, res, sec, p, u, st = run_forward(
        tok, query_weight, key_weight, value_weight, output_weight, up_weight, sio,
        fg, fb, skip, sg, sb, decay,
    )
    result, gatt, dwup, piece_down, gdb, gub, gsg, gsb = run_feed(
        sec, res, wall, down_weight, cot, live, upb, dnb, sg
    )
    gtok, piece_up, piece_out, piece_q, piece_k, piece_v, gfg, gfb, gskip, gsi, gso, grate = run_backward(
        dwup.reshape(4, NC, 2, 64, 1024), gatt, att, wall, q, kx, vx, rnd, p, tok, sio_all,
        u, st, fg, fb, skip, decay,
    )
    flat = jnp.concatenate(
        [gfg[0], gfb[0], gskip[0], gsg[0], gsb[0], gdb[0], gub[0], gsi.reshape(-1), gso.reshape(-1)]
        + [grate[:, 0], jnp.zeros((65536 - 10 * 1024 - 2 * 16384 - 16,), F32)]
    )
    total = run_small(flat.reshape(32, 16, 128)).reshape(-1)
    row = [total[i * 1024 : (i + 1) * 1024] for i in range(6)]
    shard = lax.axis_index("shard")
    mine = [
        lax.dynamic_slice(total[at : at + 16384].reshape(16, 1024), (0, shard * 64), (16, 64))
        for at in (10240, 26624)
    ]
    return (
        result.reshape(1, 1024, 1024), gtok.reshape(1, 1024, 1024), row[0], row[1],
        total[43008:43024], mine[0], mine[1], row[2], piece_q, piece_k, piece_v, piece_out,
        row[3], row[4], piece_up, total[6144:10240], piece_down, row[5],
    )


NORM_EPS = 1e-05
NEG_LARGE = -1e30
HIGHEST = lax.Precision.HIGHEST


def layer_norm(hidden, gain_vec, bias_vec):
    average = jnp.mean(hidden, axis=-1, keepdims=True)
    centred = hidden - average
    spread = jnp.mean(centred * centred, axis=-1, keepdims=True)
    return centred * lax.rsqrt(spread + NORM_EPS) * gain_vec + bias_vec


def state_context(driven_raw, normed, decay_rates, state_out, skip_gain):
    decay_factor = jnp.exp(-decay_rates)
    driven = driven_raw * jnp.sqrt(1.0 - decay_factor * decay_factor)
    factors = jnp.broadcast_to(decay_factor, driven.shape)

    def combine(earlier, subsequent):
        return (earlier[0] * subsequent[0], subsequent[0] * earlier[1] + subsequent[1])

    states = lax.associative_scan(combine, (factors, driven), axis=1)[1]
    seq_count = driven_raw.shape[0]
    state_width = driven_raw.shape[2]
    model_width = normed.shape[2]
    tail_states = states.reshape(seq_count, NBLK, BLK, state_width)[:, :, BLK - CTX :, :]
    skipped = normed.reshape(seq_count, NBLK, BLK, model_width)[:, :, BLK - CTX :, :]
    outputs = (
        jnp.einsum("sbcp,pd->sbcd", tail_states, state_out, precision=HIGHEST) + skip_gain * skipped
    )
    empty_ctx = jnp.zeros((seq_count, 1, CTX, model_width), jnp.float32)
    return jnp.concatenate([empty_ctx, outputs[:, : NBLK - 1]], axis=1)


def block_scores(queries, key_rows, ctx_keys, ctx_valid):
    row_count = queries.shape[0]
    head_count = queries.shape[1] // DH
    query_heads = queries.reshape(row_count, head_count, DH)
    key_heads = jnp.concatenate([ctx_keys, key_rows], 0).reshape(-1, head_count, DH)
    scores = jnp.einsum(
        "qhd,khd->hqk", query_heads, key_heads, preferred_element_type=jnp.float32
    ) * DH ** (-0.5)
    causal = lax.broadcasted_iota(jnp.int32, (row_count, row_count), 0) >= lax.broadcasted_iota(
        jnp.int32, (row_count, row_count), 1
    )
    allowed = jnp.concatenate(
        [jnp.broadcast_to(ctx_valid[None, :], (row_count, ctx_keys.shape[0])), causal], axis=1
    )
    return (jnp.where(allowed[None], scores, NEG_LARGE), query_heads, key_heads)


def attend_forward(block_item):
    queries, key_rows, value_rows, ctx_keys, ctx_values, ctx_valid = block_item
    scores, query_heads, key_heads = block_scores(queries, key_rows, ctx_keys, ctx_valid)
    row_max = jnp.max(scores, axis=-1, keepdims=True)
    expos = jnp.exp(scores - row_max)
    denominator = jnp.sum(expos, axis=-1, keepdims=True)
    weights = (expos / denominator).astype(jnp.bfloat16)
    value_heads = jnp.concatenate([ctx_values, value_rows], 0).reshape(key_heads.shape)
    attended = jnp.einsum("hqk,khd->qhd", weights, value_heads, preferred_element_type=jnp.float32)
    return (
        attended.reshape(queries.shape).astype(jnp.bfloat16),
        (row_max + jnp.log(denominator))[..., 0],
    )


def attend_backward(block_item):
    queries, key_rows, value_rows, ctx_keys, ctx_values, ctx_valid, log_total, grad_attended = (
        block_item
    )
    scores, query_heads, key_heads = block_scores(queries, key_rows, ctx_keys, ctx_valid)
    probs = jnp.exp(scores - log_total[..., None])
    value_heads = jnp.concatenate([ctx_values, value_rows], 0).reshape(key_heads.shape)
    grad_heads = grad_attended.reshape(query_heads.shape)
    grad_probs = jnp.einsum(
        "qhd,khd->hqk", grad_heads, value_heads, preferred_element_type=jnp.float32
    )
    grad_scores = (
        probs * (grad_probs - jnp.sum(probs * grad_probs, axis=-1, keepdims=True))
    ).astype(jnp.bfloat16)
    grad_values = jnp.einsum(
        "hqk,qhd->khd", probs.astype(jnp.bfloat16), grad_heads, preferred_element_type=jnp.float32
    )
    grad_queries = jnp.einsum(
        "hqk,khd->qhd", grad_scores, key_heads, preferred_element_type=jnp.float32
    ) * DH ** (-0.5)
    grad_keys = jnp.einsum(
        "hqk,qhd->khd", grad_scores, query_heads, preferred_element_type=jnp.float32
    ) * DH ** (-0.5)
    ctx_count = ctx_keys.shape[0]
    model_width = queries.shape[1]
    grad_keys = grad_keys.reshape(-1, model_width).astype(jnp.bfloat16)
    grad_values = grad_values.reshape(-1, model_width).astype(jnp.bfloat16)
    return (
        grad_queries.reshape(queries.shape).astype(jnp.bfloat16),
        grad_keys[ctx_count:],
        grad_values[ctx_count:],
        grad_keys[:ctx_count],
        grad_values[:ctx_count],
    )


def per_device(
    tokens,
    lengths,
    first_gain,
    first_bias,
    decay_rates,
    state_in,
    state_out,
    skip_gain,
    query_weight,
    key_weight,
    value_weight,
    output_weight,
    second_gain,
    second_bias,
    up_weight,
    up_bias,
    down_weight,
    down_bias,
    cotangent,
):
    full_query, full_key, full_value, full_output, full_up, full_down, full_in, full_out = (
        lax.all_gather(query_weight, "shard", axis=0, tiled=True),
        lax.all_gather(key_weight, "shard", axis=0, tiled=True),
        lax.all_gather(value_weight, "shard", axis=0, tiled=True),
        lax.all_gather(output_weight, "shard", axis=0, tiled=True),
        lax.all_gather(up_weight, "shard", axis=0, tiled=True),
        lax.all_gather(down_weight, "shard", axis=0, tiled=True),
        lax.all_gather(state_in, "shard", axis=1, tiled=True),
        lax.all_gather(state_out, "shard", axis=1, tiled=True),
    )
    seq_count, seq_len, model_width = tokens.shape
    row_count = seq_count * seq_len
    block_count = seq_count * NBLK
    positions = lax.broadcasted_iota(jnp.int32, (seq_count, seq_len), 1)
    row_mask = (positions < lengths[:, None]).astype(jnp.float32).reshape(row_count, 1)
    block_index = lax.broadcasted_iota(jnp.int32, (seq_count, NBLK, CTX), 1)
    ctx_valid = (block_index > 0).reshape(block_count, CTX)
    token_rows = tokens.astype(jnp.float32)
    normed, first_pullback = jax.vjp(layer_norm, token_rows, first_gain, first_bias)
    rounded = normed.astype(jnp.bfloat16)
    driven_raw = jnp.einsum("std,pd->stp", rounded, full_in, preferred_element_type=jnp.float32)
    context, state_pullback = jax.vjp(
        state_context, driven_raw, normed, decay_rates, full_out.astype(jnp.float32), skip_gain
    )
    ctx_rows = context.astype(jnp.bfloat16).reshape(block_count * CTX, model_width)
    flat_rounded = rounded.reshape(row_count, model_width)
    query_rows = jnp.dot(flat_rounded, full_query, preferred_element_type=jnp.float32).astype(
        jnp.bfloat16
    )
    key_rows = jnp.dot(flat_rounded, full_key, preferred_element_type=jnp.float32).astype(
        jnp.bfloat16
    )
    value_rows = jnp.dot(flat_rounded, full_value, preferred_element_type=jnp.float32).astype(
        jnp.bfloat16
    )
    ctx_keys = jnp.dot(ctx_rows, full_key, preferred_element_type=jnp.float32).astype(jnp.bfloat16)
    ctx_values = jnp.dot(ctx_rows, full_value, preferred_element_type=jnp.float32).astype(
        jnp.bfloat16
    )
    block_inputs = (
        query_rows.reshape(block_count, BLK, model_width),
        key_rows.reshape(block_count, BLK, model_width),
        value_rows.reshape(block_count, BLK, model_width),
        ctx_keys.reshape(block_count, CTX, model_width),
        ctx_values.reshape(block_count, CTX, model_width),
        ctx_valid,
    )
    attended, log_total = lax.map(attend_forward, block_inputs)
    attended_rows = attended.reshape(row_count, model_width)
    residual = token_rows.reshape(row_count, model_width) + jnp.dot(
        attended_rows, full_output, preferred_element_type=jnp.float32
    )
    second, second_pullback = jax.vjp(layer_norm, residual, second_gain, second_bias)
    second_rows = second.astype(jnp.bfloat16)
    hidden = jnp.dot(second_rows, full_up, preferred_element_type=jnp.float32) + up_bias
    active, gelu_pullback = jax.vjp(jax.nn.gelu, hidden)
    active_rows = active.astype(jnp.bfloat16)
    branch = jnp.dot(active_rows, full_down, preferred_element_type=jnp.float32) + down_bias
    result = (
        ((residual + branch) * row_mask)
        .astype(jnp.bfloat16)
        .reshape(seq_count, seq_len, model_width)
    )
    full_query, full_key, full_value, full_output, full_up, full_down, full_in, full_out = (
        lax.all_gather(query_weight, "shard", axis=0, tiled=True),
        lax.all_gather(key_weight, "shard", axis=0, tiled=True),
        lax.all_gather(value_weight, "shard", axis=0, tiled=True),
        lax.all_gather(output_weight, "shard", axis=0, tiled=True),
        lax.all_gather(up_weight, "shard", axis=0, tiled=True),
        lax.all_gather(down_weight, "shard", axis=0, tiled=True),
        lax.all_gather(state_in, "shard", axis=1, tiled=True),
        lax.all_gather(state_out, "shard", axis=1, tiled=True),
    )
    grad_branch = cotangent.reshape(row_count, model_width).astype(jnp.float32) * row_mask
    branch_rounded = grad_branch.astype(jnp.bfloat16)
    grad_down = jnp.einsum(
        "rf,rd->fd", active_rows, branch_rounded, preferred_element_type=jnp.float32
    )
    grad_down_bias = jnp.sum(grad_branch, axis=0)
    grad_active = jnp.einsum(
        "rd,fd->rf", branch_rounded, full_down, preferred_element_type=jnp.float32
    )
    (grad_hidden,) = gelu_pullback(grad_active)
    hidden_rounded = grad_hidden.astype(jnp.bfloat16)
    grad_up = jnp.einsum(
        "rd,rf->df", second_rows, hidden_rounded, preferred_element_type=jnp.float32
    )
    grad_up_bias = jnp.sum(hidden_rounded.astype(jnp.float32), axis=0)
    grad_second = jnp.einsum(
        "rf,df->rd", hidden_rounded, full_up, preferred_element_type=jnp.float32
    )
    grad_residual_part, grad_second_gain, grad_second_bias = second_pullback(grad_second)
    grad_residual = grad_branch + grad_residual_part
    residual_rounded = grad_residual.astype(jnp.bfloat16)
    grad_output = jnp.einsum(
        "rd,re->de", attended_rows, residual_rounded, preferred_element_type=jnp.float32
    )
    grad_attended = jnp.einsum(
        "re,de->rd", residual_rounded, full_output, preferred_element_type=jnp.float32
    ).astype(jnp.bfloat16)
    grad_query_rows, grad_key_rows, grad_value_rows, grad_ctx_keys, grad_ctx_values = lax.map(
        attend_backward,
        block_inputs + (log_total, grad_attended.reshape(block_count, BLK, model_width)),
    )
    grad_query_rows = grad_query_rows.reshape(row_count, model_width)
    grad_key_rows = grad_key_rows.reshape(row_count, model_width)
    grad_value_rows = grad_value_rows.reshape(row_count, model_width)
    grad_ctx_keys = grad_ctx_keys.reshape(block_count * CTX, model_width)
    grad_ctx_values = grad_ctx_values.reshape(block_count * CTX, model_width)
    grad_query = jnp.einsum(
        "rd,re->de", flat_rounded, grad_query_rows, preferred_element_type=jnp.float32
    )
    grad_key = jnp.einsum(
        "rd,re->de", flat_rounded, grad_key_rows, preferred_element_type=jnp.float32
    ) + jnp.einsum("rd,re->de", ctx_rows, grad_ctx_keys, preferred_element_type=jnp.float32)
    grad_value = jnp.einsum(
        "rd,re->de", flat_rounded, grad_value_rows, preferred_element_type=jnp.float32
    ) + jnp.einsum("rd,re->de", ctx_rows, grad_ctx_values, preferred_element_type=jnp.float32)
    grad_normed = (
        jnp.einsum("re,de->rd", grad_query_rows, full_query, preferred_element_type=jnp.float32)
        + jnp.einsum("re,de->rd", grad_key_rows, full_key, preferred_element_type=jnp.float32)
        + jnp.einsum("re,de->rd", grad_value_rows, full_value, preferred_element_type=jnp.float32)
    )
    grad_context = jnp.einsum(
        "re,de->rd", grad_ctx_keys, full_key, preferred_element_type=jnp.float32
    ) + jnp.einsum("re,de->rd", grad_ctx_values, full_value, preferred_element_type=jnp.float32)
    grad_context = grad_context.reshape(seq_count, NBLK, CTX, model_width)
    grad_driven, state_normed, grad_rates, grad_state_out, grad_skip = state_pullback(grad_context)
    grad_in = jnp.einsum(
        "stp,std->pd", grad_driven, rounded, precision=HIGHEST, preferred_element_type=jnp.float32
    )
    state_rounded = jnp.einsum(
        "stp,pd->std", grad_driven, full_in, precision=HIGHEST, preferred_element_type=jnp.float32
    )
    normed_total = (
        grad_normed.reshape(seq_count, seq_len, model_width) + state_rounded + state_normed
    )
    tokens_part, grad_first_gain, grad_first_bias = first_pullback(normed_total)
    grad_tokens = (tokens_part + grad_residual.reshape(seq_count, seq_len, model_width)).astype(
        jnp.bfloat16
    )
    piece_query, piece_key, piece_value, piece_output, piece_up, piece_down, piece_in, piece_out = (
        lax.psum_scatter(grad_query, "shard", scatter_dimension=0, tiled=True),
        lax.psum_scatter(grad_key, "shard", scatter_dimension=0, tiled=True),
        lax.psum_scatter(grad_value, "shard", scatter_dimension=0, tiled=True),
        lax.psum_scatter(grad_output, "shard", scatter_dimension=0, tiled=True),
        lax.psum_scatter(grad_up, "shard", scatter_dimension=0, tiled=True),
        lax.psum_scatter(grad_down, "shard", scatter_dimension=0, tiled=True),
        lax.psum_scatter(grad_in, "shard", scatter_dimension=1, tiled=True),
        lax.psum_scatter(grad_state_out, "shard", scatter_dimension=1, tiled=True),
    )
    piece_query, piece_key, piece_value, piece_output, piece_up, piece_down, piece_in, piece_out = (
        lax.psum(piece_query.astype(jnp.bfloat16), "rep").astype(jnp.float32),
        lax.psum(piece_key.astype(jnp.bfloat16), "rep").astype(jnp.float32),
        lax.psum(piece_value.astype(jnp.bfloat16), "rep").astype(jnp.float32),
        lax.psum(piece_output.astype(jnp.bfloat16), "rep").astype(jnp.float32),
        lax.psum(piece_up.astype(jnp.bfloat16), "rep").astype(jnp.float32),
        lax.psum(piece_down.astype(jnp.bfloat16), "rep").astype(jnp.float32),
        lax.psum(piece_in.astype(jnp.bfloat16), "rep").astype(jnp.float32),
        lax.psum(piece_out.astype(jnp.bfloat16), "rep").astype(jnp.float32),
    )
    (
        sum_first_gain,
        sum_first_bias,
        sum_rates,
        sum_skip,
        sum_second_gain,
        sum_second_bias,
        sum_up_bias,
        sum_down_bias,
    ) = lax.psum(
        (
            grad_first_gain,
            grad_first_bias,
            grad_rates,
            grad_skip,
            grad_second_gain,
            grad_second_bias,
            grad_up_bias,
            grad_down_bias,
        ),
        ("rep", "shard"),
    )
    return (
        result,
        grad_tokens,
        sum_first_gain,
        sum_first_bias,
        sum_rates,
        piece_in,
        piece_out,
        sum_skip,
        piece_query,
        piece_key,
        piece_value,
        piece_output,
        sum_second_gain,
        sum_second_bias,
        piece_up,
        sum_up_bias,
        piece_down,
        sum_down_bias,
    )


def solution(mesh):
    placed = (
        P(("rep", "shard"), None, None),
        P(("rep", "shard")),
        P(),
        P(),
        P(),
        P(None, "shard"),
        P(None, "shard"),
        P(),
        P("shard", None),
        P("shard", None),
        P("shard", None),
        P("shard", None),
        P(),
        P(),
        P("shard", None),
        P(),
        P("shard", None),
        P(),
        P(("rep", "shard"), None, None),
    )
    fused = mesh.shape["rep"] == 2 and mesh.shape["shard"] == 2 * NC
    return jax.shard_map(
        fused_device if fused else per_device,
        mesh=mesh,
        in_specs=placed,
        out_specs=(
            P(("rep", "shard"), None, None),
            P(("rep", "shard"), None, None),
            P(),
            P(),
            P(),
            P(None, "shard"),
            P(None, "shard"),
            P(),
            P("shard", None),
            P("shard", None),
            P("shard", None),
            P("shard", None),
            P(),
            P(),
            P("shard", None),
            P(),
            P("shard", None),
            P(),
        ),
        check_vma=False,
    )
```

```python
import functools
import math

import jax
import jax.numpy as jnp
from jax import lax
from jax.experimental import pallas as pl
from jax.experimental.pallas import tpu as pltpu
from jax.sharding import PartitionSpec as P

DH = 128
BLK = 512
CTX = 128
NBLK = 2
EPS = 1e-05
NEG = -1e30
SCALE = DH ** (-0.5)
MESH = pl.DeviceIdType.MESH
F32 = jnp.float32
BF16 = jnp.bfloat16
VMEM_LIMIT = 66_000_000
NC = 8


def chip_at(pos):
    turned = pos // 4
    return (1 - turned) * (2 * pos) + turned * (2 * (7 - pos) + 1)


class Net:
    def __init__(self):
        self.rep = lax.axis_index("rep")
        self.shard = lax.axis_index("shard")
        self.core = self.shard % 2
        chip = self.shard // 2
        z, y = chip // 2, chip % 2
        self.pos = (1 - y) * z + y * (7 - z)
        self.step = 1 - 2 * self.core
        self.mate = (self.rep, 2 * chip + 1 - self.core)
        self.twin = (1 - self.rep, self.shard)

    def at(self, hops, core):
        return 2 * chip_at((self.pos + self.step * hops + 4 * NC) % NC) + core

    def along(self, hops):
        return (self.rep, self.at(hops, self.core))

    def greet(self):
        barrier = pltpu.get_barrier_semaphore()
        for device in (self.along(1), self.along(-1), self.mate, self.twin):
            pl.semaphore_signal(barrier, inc=1, device_id=device, device_id_type=MESH)
        pl.semaphore_wait(barrier, 4)


def rcopy(src, dst, send, recv, device):
    return pltpu.make_async_remote_copy(
        src_ref=src, dst_ref=dst, send_sem=send, recv_sem=recv, device_id=device, device_id_type=MESH
    )


def dot_nn(a, b):
    return lax.dot_general(a, b, (((1,), (0,)), ((), ())), preferred_element_type=F32)


def dot_nt(a, b):
    return lax.dot_general(a, b, (((1,), (1,)), ((), ())), preferred_element_type=F32)


def dot_tn(a, b):
    return lax.dot_general(a, b, (((0,), (0,)), ((), ())), preferred_element_type=F32)


def norm_parts(rows):
    centred = rows - jnp.mean(rows, axis=-1, keepdims=True)
    spread = jnp.mean(centred * centred, axis=-1, keepdims=True)
    inverse = lax.rsqrt(spread + EPS)
    return centred * inverse, inverse


def split_dot(dot, left, right, narrow):
    total = None
    rest = left
    for _ in range(narrow):
        term = rest.astype(BF16)
        part = dot(term, right)
        total = part if total is None else total + part
        rest = rest - term.astype(F32)
    return total


def lane_scan(values, factor, reverse):
    width = values.shape[1]
    lane = lax.broadcasted_iota(jnp.int32, values.shape, 1)
    shift = 1
    power = factor
    while shift < width:
        if reverse:
            moved = pltpu.roll(values, width - shift, 1)
            moved = jnp.where(lane < width - shift, moved, 0.0)
        else:
            moved = pltpu.roll(values, shift, 1)
            moved = jnp.where(lane >= shift, moved, 0.0)
        values = values + power * moved
        power = power * power
        shift *= 2
    return values


def forward_kernel(
    tok, wq, wk, wv, wo, wup, s_in, s_out, fg, fb, skip, sg, sb, decay,
    wall, sio_all, rnd_o, q_o, k_o, v_o, att_o, res_o, sec_o, p_o, u_o, st_o,
    tok_s, rnd_s, w_s, q_s, k_s, v_s, att_s, res_s, sec_s, pbuf, nctx, sio_s,
    own_s, sio_own, loc, rs, rr, ss, sr, cs, cr, xs, xr, outs, psem,
):
    net = Net()
    rep, core = net.rep, net.core
    rows_of = 64
    width = 1024

    def block(shard):
        return pl.ds(pl.multiple_of(shard * rows_of, rows_of), rows_of)

    mine = block(net.shard)
    own = [wq, wk, wv, wo]
    copies = [pltpu.make_async_copy(own[i], own_s.at[i], loc.at[i]) for i in range(4)]
    copies += [
        pltpu.make_async_copy(wup.at[:, pl.ds(i * width, width)], own_s.at[4 + i], loc.at[4 + i])
        for i in range(4)
    ]
    small = pltpu.make_async_copy(sio_own, sio_all.at[mine], loc.at[8])
    arrive = pltpu.make_async_copy(tok, tok_s, loc.at[9])
    for copy in copies:
        copy.start()
    arrive.start()
    packed = jnp.concatenate(
        [s_in[...].astype(F32), s_out[...].astype(F32), jnp.zeros((96, rows_of), F32)], axis=0
    )
    sio_own[...] = packed.T.astype(BF16)
    small.start()
    net.greet()
    for copy in copies:
        copy.wait()

    def piece(slot):
        if isinstance(slot, int) and slot < 2:
            return 1 if slot else 2 * rep
        later = slot - 2
        return 3 + later + 3 * rep * ((later % 2) * (3 - later) // 2)

    def ring(slot, way, hop, which, where):
        ref = wall.at[which, where]
        sems = rs.at[slot, way, hop], rr.at[slot, way, hop]
        return rcopy(ref, ref, *sems, net.along(1 - 2 * way))

    def ring_own(slot, way):
        which = piece(slot)
        sems = rs.at[slot, way, 0], rr.at[slot, way, 0]
        ref = wall.at[which, mine]
        rcopy(own_s.at[which], ref, *sems, net.along(1 - 2 * way)).start()

    def ring_small(way, hop, where):
        ref = sio_all.at[where]
        return rcopy(ref, ref, ss.at[way, hop], sr.at[way, hop], net.along(1 - 2 * way))

    def mate(which, index, where):
        ref = wall.at[which, where]
        return rcopy(ref, ref, cs.at[which, index], cr.at[which, index], net.mate)

    def mate_small(index, where):
        ref = sio_all.at[where]
        return rcopy(ref, ref, cs.at[8, index], cr.at[8, index], net.mate)

    def twin(turn, index, which, where):
        ref = wall.at[which, where]
        return rcopy(ref, ref, xs.at[turn, index], xr.at[turn, index], net.twin)

    def source(way, hop):
        return block(net.at((2 * way - 1) * (hop + 1), core))

    def serve(slot, way, hop):
        which = piece(slot)
        where = source(way, hop)
        ring(slot, way, hop, which, where).wait_recv()

        @pl.when(hop < 3 - way)
        def _():
            ring(slot, way, hop + 1, which, where).start()

        mate(which, 1 + 2 * hop + way, where).start()

    def serve_out(slot, turn, way, hop):
        twin(turn, 2 * hop + way, piece(slot), source(way, hop)).start()

    def serve_in(turn, way, hop):
        where = source(way, hop)
        which = 2 * (1 - rep) if turn == 0 else 7 - 3 * rep
        twin(turn, 2 * hop + way, which, where).wait_recv()
        mate(which, 1 + 2 * hop + way, where).start()

    for slot in range(2):
        for way in range(2):
            ring_own(slot, way)
    small.wait()
    for way in range(2):
        ring_small(way, 0, mine).start()
    mate_small(0, mine).start()
    for which in range(8):
        rcopy(own_s.at[which], wall.at[which, mine], cs.at[which, 0], cr.at[which, 0], net.mate).start()
    keep = [pltpu.make_async_copy(own_s.at[i], wall.at[i, mine], loc.at[i]) for i in range(8)]
    for copy in keep:
        copy.start()
    arrive.wait()

    def first_norm(at):
        rows = pl.ds(pl.multiple_of(at * 128, 128), 128)
        xhat, _ = norm_parts(tok_s[rows, :].astype(F32))
        normed = xhat * fg[...] + fb[...]
        rnd_s[rows, :] = normed.astype(BF16)

    turns = [(hop, way) for hop in range(4) for way in range(2) if hop < 4 - way]
    for n, (hop, way) in enumerate(turns):
        first_norm(n)
        serve(0, way, hop)
        serve_out(0, 0, way, hop)
        serve(1, way, hop)
        where = source(way, hop)
        ring_small(way, hop, where).wait_recv()
        if hop < 3 - way:
            ring_small(way, hop + 1, where).start()
        mate_small(1 + 2 * hop + way, where).start()
        if n >= 2:
            serve(2, turns[n - 2][1], turns[n - 2][0])
        if n in (0, 2, 4, 5):
            for each in range(2):
                ring_own({0: 2, 2: 3, 4: 4, 5: 5}[n], each)
        if n >= 3:
            serve_in(0, turns[n - 3][1], turns[n - 3][0])
    first_norm(7)
    for hop, way in turns[-3:]:
        serve_in(0, way, hop)

    def event(m):
        later = (m - 2 + 3) // 3 - 1
        turn = (5 + m) * (1 - (m + 20) // 22) + later * ((m + 20) // 22)
        slot = 2 + ((m + 20) // 22) * (1 + (m + 1) % 3)
        hop, way = turn // 2, turn % 2
        serve(slot, way, hop)

        @pl.when(slot == 3)
        def _():
            serve_out(3, 1, way, hop)

        @pl.when((slot == 5) & (turn >= 2))
        def _():
            serve_in(1, way, hop - 1)

    xhat, _ = norm_parts(tok_s[pl.ds(BLK - CTX, CTX), :].astype(F32))
    nctx[...] = xhat * fg[...] + fb[...]

    @pl.loop(0, NC)
    def _(index):
        where = block(0)
        mate_small(index, where).wait_recv()
        for which in range(3):
            mate(which, index, where).wait_recv()

    for copy in keep:
        copy.wait()
    loads = [pltpu.make_async_copy(sio_all, sio_s, loc.at[8])]
    loads += [pltpu.make_async_copy(wall.at[i], w_s.at[i], loc.at[i]) for i in range(3)]
    for copy in loads:
        copy.start()
    loads[0].wait()
    u_all = lax.dot_general(
        sio_s[...], rnd_s[pl.ds(0, BLK), :], (((0,), (1,)), ((), ())), preferred_element_type=F32
    )
    factor = jnp.exp(-column(decay[...]))
    raw = u_all[0:16, :]
    u_o[...] = raw
    states = lane_scan(raw * jnp.sqrt(1.0 - factor * factor), factor, False)
    st_o[...] = states
    tail = states[:, BLK - CTX :]
    padded = jnp.concatenate(
        [jnp.zeros((16, CTX), F32), tail, jnp.zeros((96, CTX), F32)], axis=0
    )
    made = split_dot(
        lambda a, b: lax.dot_general(a, b, (((0,), (1,)), ((), ())), preferred_element_type=F32),
        padded, sio_s[...], 3,
    )
    rnd_s[pl.ds(1024, CTX), :] = (made + skip[...] * nctx[...]).astype(BF16)
    finals = [pltpu.make_async_copy(rnd_s, rnd_o, outs.at[0])]
    finals[0].start()

    for copy in loads[1:]:
        copy.wait()

    @pl.loop(0, 4)
    def _(at):
        cols = pl.ds(pl.multiple_of(at * 256, 256), 256)
        q_s[:, cols] = dot_nn(rnd_s[pl.ds(0, 1024), :], w_s[0, :, cols]).astype(BF16)
        event(2 * at)
        k_s[:, cols] = dot_nn(rnd_s[...], w_s[1, :, cols]).astype(BF16)
        v_s[:, cols] = dot_nn(rnd_s[...], w_s[2, :, cols]).astype(BF16)
        event(2 * at + 1)

    for i, (a, b) in enumerate(((q_s, q_o), (k_s, k_o), (v_s, v_o))):
        finals.append(pltpu.make_async_copy(a, b, outs.at[1 + i]))
        finals[-1].start()

    for half in range(2):
        pbuf[half] = jnp.zeros((BLK, CTX + BLK), BF16)

    def p_copy(slot, at):
        return pltpu.make_async_copy(pbuf.at[slot], p_o.at[at], psem.at[slot])

    for b in range(NBLK):

        @pl.loop(0, 8)
        def _(h, b=b):
            cols = pl.ds(pl.multiple_of(h * DH, DH), DH)
            slot = h % 2
            if b == 0:

                @pl.when(h >= 2)
                def _():
                    p_copy(slot, h).wait()
            else:
                p_copy(slot, h).wait()
            for i in range(2):
                span = (i + 1) * 256
                rows = pl.ds(b * BLK + i * 256, 256)
                queries = q_s[rows, cols]
                scores = dot_nt(queries, k_s[pl.ds(b * BLK, span), cols]) * SCALE
                ahead = lax.broadcasted_iota(jnp.int32, scores.shape, 0) + i * 256
                scores = jnp.where(
                    ahead >= lax.broadcasted_iota(jnp.int32, scores.shape, 1), scores, NEG
                )
                top = jnp.max(scores, axis=-1, keepdims=True)
                if b:
                    before = dot_nt(queries, k_s[pl.ds(1024, CTX), cols]) * SCALE
                    top = jnp.maximum(top, jnp.max(before, axis=-1, keepdims=True))
                expos = jnp.exp(scores - top)
                total = jnp.sum(expos, axis=-1, keepdims=True)
                if b:
                    expos_before = jnp.exp(before - top)
                    total = total + jnp.sum(expos_before, axis=-1, keepdims=True)
                share = 1.0 / total
                weights = (expos * share).astype(BF16)
                mixed = dot_nn(weights, v_s[pl.ds(b * BLK, span), cols])
                pbuf[slot, pl.ds(i * 256, 256), pl.ds(CTX, span)] = weights
                if b:
                    weights = (expos_before * share).astype(BF16)
                    mixed = mixed + dot_nn(weights, v_s[pl.ds(1024, CTX), cols])
                    pbuf[slot, pl.ds(i * 256, 256), pl.ds(0, CTX)] = weights
                att_s[rows, cols] = mixed.astype(BF16)
            p_copy(slot, b * 8 + h).start()

            @pl.when(h < 5)
            def _(b=b, h=h):
                event(8 + 5 * b + h)

    finals.append(pltpu.make_async_copy(att_s, att_o, outs.at[4]))
    finals[-1].start()

    @pl.loop(0, NC)
    def _(index):
        mate(3, index, block(0)).wait_recv()

    load = pltpu.make_async_copy(wall.at[3], w_s.at[3], loc.at[3])
    load.start()
    load.wait()

    @pl.loop(0, 4)
    def _(at):
        rows = pl.ds(pl.multiple_of(at * 256, 256), 256)
        residual = tok_s[rows, :].astype(F32) + dot_nn(att_s[rows, :], w_s[3])
        res_s[rows, :] = residual
        xhat, _ = norm_parts(residual)
        sec_s[rows, :] = (xhat * sg[...] + sb[...]).astype(BF16)
        pltpu.make_async_copy(res_s.at[rows], res_o.at[rows], outs.at[5 + at]).start()
        pltpu.make_async_copy(sec_s.at[rows], sec_o.at[rows], outs.at[9 + at]).start()
        event(18 + at)

    event(22)
    for copy in finals:
        copy.wait()
    for at in range(4):
        rows = pl.ds(at * 256, 256)
        pltpu.make_async_copy(res_s.at[rows], res_o.at[rows], outs.at[5 + at]).wait()
        pltpu.make_async_copy(sec_s.at[rows], sec_o.at[rows], outs.at[9 + at]).wait()
    for slot in range(2):
        p_copy(slot, slot).wait()

    serve_in(1, 1, 2)
    serve_in(1, 0, 3)

    @pl.loop(0, NC)
    def _(index):
        for which in range(4, 8):
            mate(which, index, block(0)).wait_recv()
        for which in range(8):
            mate(which, index, block(0)).wait_send()
        mate_small(index, block(0)).wait_send()

    @pl.loop(0, NC - 1)
    def _(index):
        hop = index // 2
        way = index % 2
        for slot in range(6):
            ring(slot, way, hop, 0, block(0)).wait_send()
        ring_small(way, hop, block(0)).wait_send()
        for turn in range(2):
            twin(turn, index, 0, block(0)).wait_send()


def column(row):
    wide = jnp.broadcast_to(row, (16, 16))
    same = lax.broadcasted_iota(jnp.int32, (16, 16), 0) == lax.broadcasted_iota(jnp.int32, (16, 16), 1)
    return jnp.sum(jnp.where(same, wide, 0.0), axis=1, keepdims=True)


def any_spec(n):
    return [pl.BlockSpec(memory_space=pl.ANY)] * n


def vmem_spec(n):
    return [pl.BlockSpec(memory_space=pltpu.VMEM)] * n


def run_forward(tok, wq, wk, wv, wo, wup, s_in, s_out, fg, fb, skip, sg, sb, decay):
    shape = jax.ShapeDtypeStruct
    dma = pltpu.SemaphoreType.DMA
    big = (1024, 1024)
    ext = (1024 + CTX, 1024)
    return pl.pallas_call(
        forward_kernel,
        name="forward_part",
        out_shape=(
            shape((8,) + big, BF16), shape((1024, 128), BF16), shape(ext, BF16), shape(big, BF16),
            shape(ext, BF16), shape(ext, BF16), shape(big, BF16), shape(big, F32),
            shape(big, BF16), shape((16, BLK, CTX + BLK), BF16), shape((16, BLK), F32),
            shape((16, BLK), F32),
        ),
        in_specs=any_spec(6) + vmem_spec(8),
        out_specs=any_spec(10) + vmem_spec(2),
        scratch_shapes=[
            pltpu.VMEM(big, BF16), pltpu.VMEM(ext, BF16), pltpu.VMEM((4,) + big, BF16),
            pltpu.VMEM(big, BF16), pltpu.VMEM(ext, BF16), pltpu.VMEM(ext, BF16),
            pltpu.VMEM(big, BF16), pltpu.VMEM(big, F32), pltpu.VMEM(big, BF16),
            pltpu.VMEM((2, BLK, CTX + BLK), BF16), pltpu.VMEM((CTX, 1024), F32),
            pltpu.VMEM((1024, 128), BF16),
            pltpu.VMEM((8, 64, 1024), BF16), pltpu.VMEM((64, 128), BF16),
            dma((10,)), dma((6, 2, 4)), dma((6, 2, 4)), dma((2, 4)), dma((2, 4)),
            dma((9, NC)), dma((9, NC)), dma((2, NC - 1)), dma((2, NC - 1)), dma((13,)), dma((2,)),
        ],
        compiler_params=pltpu.CompilerParams(
            collective_id=0, has_side_effects=True, vmem_limit_bytes=VMEM_LIMIT
        ),
    )(tok, wq, wk, wv, wo, wup, s_in, s_out, fg, fb, skip, sg, sb, decay)


GELU_C = math.sqrt(2.0 / math.pi)
GELU_A = 0.044715


def feed_kernel(
    sec, res, wall, wdn, cot, live, upb, dnb, sg,
    out_o, gatt_o, dwup_o, fin_o, finr_o, gdb_o, gub_o, gsg_o, gsb_o,
    sec_s, gb_s, wup_s, wd_s, br_s, gs_s, act_s, gh_s, a_s, b_s, prec, rrec, rsend, xsend, xrec,
    xfs, xfr, dwup_s, own_s, res_s,
    loc, ars, arr, axs, axr, cas, car, cxs, cxr, ps, pr, rs, rr, xs, xr, fs, fr, outs, dsem,
):
    net = Net()
    rep, core = net.rep, net.core
    rows_of = 256
    ring_rows = 192
    part = 64
    ahead, behind = net.along(1), net.along(-1)

    def ring_part(shard, j, first=rep):
        return pl.ds(pl.multiple_of(shard * rows_of + (first + j) * part, part), part)

    def sole_part(shard, of):
        return pl.ds(pl.multiple_of(shard * rows_of + 3 * of * part, part), part)

    def block(shard):
        return pl.ds(pl.multiple_of(shard * rows_of, rows_of), rows_of)

    def mine_at(step):
        return net.at(-(step + 1), core)

    def other_at(step):
        return net.at(step + 1, 1 - core)

    loads = [
        pltpu.make_async_copy(wdn, own_s, loc.at[0]),
        pltpu.make_async_copy(sec, sec_s, loc.at[1]),
        pltpu.make_async_copy(cot, gb_s, loc.at[2]),
    ]
    loads += [pltpu.make_async_copy(wall.at[4 + i], wup_s.at[i], loc.at[3 + i]) for i in range(4)]
    for load in loads:
        load.start()
    net.greet()
    loads[0].wait()

    def gather(j, hop, shard):
        ref = wd_s.at[ring_part(shard, j)]
        return rcopy(ref, ref, ars.at[j, hop], arr.at[j, hop], ahead)

    def gather_twin(hop, shard, of):
        ref = wd_s.at[sole_part(shard, of)]
        return rcopy(ref, ref, axs.at[hop], axr.at[hop], net.twin)

    def mate_ring(j, index, shard):
        ref = wd_s.at[ring_part(shard, j)]
        return rcopy(ref, ref, cas.at[j, index], car.at[j, index], net.mate)

    def mate_sole(index, shard, of):
        ref = wd_s.at[sole_part(shard, of)]
        return rcopy(ref, ref, cxs.at[index], cxr.at[index], net.mate)

    here = net.shard
    sole_own = own_s.at[pl.ds(pl.multiple_of(3 * (1 - rep) * part, part), part)]
    for j in range(3):
        ring_own = own_s.at[pl.ds(pl.multiple_of((rep + j) * part, part), part)]
        target = wd_s.at[ring_part(here, j)]
        rcopy(ring_own, target, ars.at[j, 0], arr.at[j, 0], ahead).start()
        rcopy(ring_own, target, cas.at[j, 0], car.at[j, 0], net.mate).start()
    rcopy(sole_own, wd_s.at[sole_part(here, 1 - rep)], cxs.at[0], cxr.at[0], net.mate).start()

    def serve(j, hop):
        shard = mine_at(hop)
        gather(j, hop, shard).wait_recv()

        @pl.when(hop < NC - 2)
        def _():
            gather(j, hop + 1, shard).start()

        @pl.when(j == 2 * rep)
        def _():
            gather_twin(hop, shard, rep).start()

        mate_ring(j, hop + 1, shard).start()

    def serve_twin(hop):
        shard = mine_at(hop)
        gather_twin(hop, shard, 1 - rep).wait_recv()
        mate_sole(hop + 1, shard, 1 - rep).start()

    for load in loads[1:3]:
        load.wait()

    wd_s[block(here), :] = own_s[...]

    @pl.loop(0, 4)
    def _(at):
        rows = pl.ds(pl.multiple_of(at * 256, 256), 256)
        when = lax.broadcasted_iota(jnp.int32, (256, 1024), 0) + at * 256
        kept = jnp.where(when < live[0], gb_s[rows, :].astype(F32), 0.0)
        gb_s[rows, :] = kept.astype(BF16)
        added = jnp.sum(kept, axis=0, keepdims=True)
        gdb_o[...] = jnp.where(at == 0, added, gdb_o[...] + added)
        br_s[rows, :] = jnp.zeros((256, 1024), F32)
        gs_s[rows, :] = jnp.zeros((256, 1024), F32)

    for j in range(3):
        serve((2 * rep + j) % 3, 0)
    for load in loads[3:]:
        load.wait()
    serve_twin(0)

    def to_mate(step):
        slot = step % 2
        return rcopy(b_s.at[slot], prec.at[step], ps.at[step], pr.at[step], net.mate)

    def to_ring(j, step):
        return rcopy(rsend.at[step % 2, j], rrec.at[step, j], rs.at[step, j], rr.at[step, j], ahead)

    def to_twin(step):
        return rcopy(xsend.at[step % 2], xrec.at[step], xs.at[step], xr.at[step], net.twin)

    def dwup_copy(slot, half, shard):
        cols = pl.ds(pl.multiple_of((shard % 4) * 256, 256), 256)
        return pltpu.make_async_copy(
            dwup_s.at[slot, half], dwup_o.at[shard // 4, :, cols], dsem.at[slot, half]
        )

    ring_local = pl.ds(pl.multiple_of(rep * part, part), ring_rows)
    sole_mine = pl.ds(pl.multiple_of(3 * rep * part, part), part)
    sole_theirs = pl.ds(pl.multiple_of(3 * (1 - rep) * part, part), part)

    def combine(step):
        slot = step % 2
        to_mate(step).wait_recv()
        a_s[slot] = a_s[slot] + prec[step].astype(F32)

        @pl.when(step >= 2)
        def _():
            to_twin(step - 2).wait_send()

        xsend[slot] = a_s[slot, sole_theirs, :].astype(BF16)
        to_twin(step).start()

    def forward(j, step):
        slot = step % 2
        rows = pl.ds(pl.multiple_of((rep + j) * part, part), part)

        @pl.when(j == 2 * rep)
        def _():
            to_twin(step).wait_recv()
            a_s[slot, rows, :] = a_s[slot, rows, :] + xrec[step].astype(F32)

        @pl.when(step >= 1)
        def _():
            to_ring(j, step - 1).wait_recv()
            a_s[slot, rows, :] = a_s[slot, rows, :] + rrec[step - 1, j].astype(F32)

        @pl.when((step >= 2) & (step < NC - 1))
        def _():
            to_ring(j, step - 2).wait_send()

        @pl.when(step < NC - 1)
        def _():
            rsend[slot, j] = a_s[slot, rows, :].astype(BF16)
            to_ring(j, step).start()

    @pl.loop(0, NC)
    def _(step):
        slot = step % 2
        a, b = mine_at(step), other_at(step)
        index = (step + 1) % NC

        @pl.when(step >= 1)
        def _():
            combine(step - 1)

        def up(shard):
            cols = pl.ds(pl.multiple_of((shard % 4) * 256, 256), 256)
            return wup_s[shard // 4, :, cols]

        def bias(shard):
            return upb[:, pl.ds(pl.multiple_of(shard * 256, 256), 256)]

        def middle(half, shard, at):
            for block_at in range(2):
                rows = pl.ds(pl.multiple_of(at * 512 + block_at * 256, 256), 256)
                cols = pl.ds(half * 256, 256)
                hidden = dot_nn(sec_s[rows, :], up(shard)) + bias(shard)
                grad = dot_nt(gb_s[rows, :], wd_s[block(shard), :])
                square = hidden * hidden
                bent = jnp.tanh(hidden * (GELU_C + (GELU_C * GELU_A) * square))
                half_up = 0.5 + 0.5 * bent
                act_s[rows, cols] = (hidden * half_up).astype(BF16)
                slope = half_up + (0.5 * hidden) * (1.0 - bent * bent) * (
                    GELU_C + (3.0 * GELU_C * GELU_A) * square
                )
                gh_s[rows, cols] = (grad * slope).astype(BF16)

        @pl.loop(0, 2)
        def _(at):
            @pl.when(step < NC - 2)
            def _():
                serve((2 * rep + at) % 3, step + 1)

            middle(0, a, at)

        for j in range(3):
            mate_ring(j, index, b).wait_recv()
        mate_sole(index, b, 1 - rep).wait_recv()

        @pl.loop(0, 2)
        def _(at):
            @pl.when((at == 0) & (step < NC - 2))
            def _():
                serve((2 * rep + 2) % 3, step + 1)

            middle(1, b, at)

        made = dot_tn(act_s[...], gb_s[...])

        @pl.when(step >= 2)
        def _():
            to_mate(step - 2).wait_send()

        a_s[slot] = made[0:256]
        b_s[slot] = made[256:512].astype(BF16)
        to_mate(step).start()

        rise_up = dot_tn(sec_s[...], gh_s[...]).astype(BF16)
        for half, shard in enumerate((a, b)):
            cols = pl.ds(pl.multiple_of(shard * 256, 256), 256)
            gub_o[:, cols] = jnp.sum(
                gh_s[:, half * 256 : half * 256 + 256].astype(F32), axis=0, keepdims=True
            )

            @pl.when(step >= 2)
            def _(half=half, shard=shard):
                dwup_copy(slot, half, shard).wait()

            dwup_s[slot, half] = rise_up[:, half * 256 : half * 256 + 256]
            dwup_copy(slot, half, shard).start()

        @pl.loop(0, 4)
        def _(at):
            rows = pl.ds(pl.multiple_of(at * 256, 256), 256)
            down = jnp.concatenate([wd_s[block(a), :], wd_s[block(b), :]], axis=0)
            br_s[rows, :] = br_s[rows, :] + dot_nn(act_s[rows, :], down)
            rise = jnp.concatenate([up(a), up(b)], axis=1)
            gs_s[rows, :] = gs_s[rows, :] + dot_nt(gh_s[rows, :], rise)

            @pl.when((at < 3) & (step >= 1))
            def _():
                forward((2 * rep + 1 + at) % 3, step - 1)

            @pl.when((at == 1) & (step < NC - 2))
            def _():
                serve_twin(step + 1)

    def residual_in(at):
        rows = pl.ds(at * 256, 256)
        return pltpu.make_async_copy(res.at[rows], res_s.at[rows], loc.at[at])

    for at in range(4):
        residual_in(at).start()
    combine(NC - 1)

    def leave(at, which):
        rows = pl.ds(pl.multiple_of(at * 256, 256), 256)
        source = (sec_s, gb_s)[which]
        return pltpu.make_async_copy(
            source.at[rows], (out_o, gatt_o)[which].at[rows], outs.at[which, at]
        )

    @pl.loop(0, 4)
    def _(at):
        residual_in(at).wait()
        rows = pl.ds(pl.multiple_of(at * 256, 256), 256)
        kept = res_s[rows, :]
        when = lax.broadcasted_iota(jnp.int32, (256, 1024), 0) + at * 256
        total = kept + br_s[rows, :] + dnb[...]
        sec_s[rows, :] = jnp.where(when < live[0], total, 0.0).astype(BF16)
        xhat, inverse = norm_parts(kept)
        grad = gs_s[rows, :]
        gain = jnp.sum(grad * xhat, axis=0, keepdims=True)
        shift = jnp.sum(grad, axis=0, keepdims=True)
        gsg_o[...] = jnp.where(at == 0, gain, gsg_o[...] + gain)
        gsb_o[...] = jnp.where(at == 0, shift, gsb_o[...] + shift)
        grad = grad * sg[...]
        grad = grad - jnp.mean(grad, axis=-1, keepdims=True) - xhat * jnp.mean(
            grad * xhat, axis=-1, keepdims=True
        )
        gb_s[rows, :] = (gb_s[rows, :].astype(F32) + inverse * grad).astype(BF16)
        for which in range(2):
            leave(at, which).start()

    for j in range(3):
        forward((2 * rep + 1 + j) % 3, NC - 1)
    last = (NC - 1) % 2
    xfs[...] = a_s[last, ring_local, :].astype(BF16)
    swap = rcopy(xfs, xfr, fs.at[0], fr.at[0], net.twin)
    swap.start()
    fin_o[...] = xfs[...]

    @pl.loop(0, NC - 1)
    def _(hop):
        for j in range(3):
            gather(j, hop, 0).wait_send()
        gather_twin(hop, 0, 0).wait_send()

    @pl.loop(0, NC)
    def _(index):
        for j in range(3):
            mate_ring(j, index, 0).wait_send()
        mate_sole(index, 0, 0).wait_send()

    for step in range(NC - 2, NC):
        to_mate(step).wait_send()
        to_twin(step).wait_send()
        for j in range(3):
            to_ring(j, step - 1).wait_send()
        for half in range(2):
            dwup_copy(step % 2, half, 0).wait()
    for at in range(4):
        for which in range(2):
            leave(at, which).wait()
    swap.wait()
    finr_o[...] = xfr[...]


def run_feed(sec, res, wall, wdn, cot, live, upb, dnb, sg):
    shape = jax.ShapeDtypeStruct
    dma = pltpu.SemaphoreType.DMA
    vmem = pltpu.VMEM
    big = (1024, 1024)
    return pl.pallas_call(
        feed_kernel,
        name="feed_part",
        out_shape=(
            shape(big, BF16), shape(big, BF16), shape((4,) + big, BF16),
            shape((192, 1024), BF16), shape((192, 1024), BF16), shape((1, 1024), F32), shape((1, 4096), F32),
            shape((1, 1024), F32), shape((1, 1024), F32),
        ),
        in_specs=any_spec(5) + [pl.BlockSpec(memory_space=pltpu.SMEM)] + vmem_spec(3),
        out_specs=any_spec(3) + vmem_spec(6),
        scratch_shapes=[
            vmem(big, BF16), vmem(big, BF16), vmem((4,) + big, BF16), vmem((4096, 1024), BF16),
            vmem(big, F32), vmem(big, F32), vmem((1024, 512), BF16), vmem((1024, 512), BF16),
            vmem((2, 256, 1024), F32), vmem((2, 256, 1024), BF16), vmem((NC, 256, 1024), BF16),
            vmem((NC - 1, 3, 64, 1024), BF16), vmem((2, 3, 64, 1024), BF16), vmem((2, 64, 1024), BF16),
            vmem((NC, 64, 1024), BF16), vmem((192, 1024), BF16), vmem((192, 1024), BF16),
            vmem((2, 2, 1024, 256), BF16), vmem((256, 1024), BF16), vmem(big, F32),
            dma((7,)), dma((3, NC - 1)), dma((3, NC - 1)), dma((NC - 1,)), dma((NC - 1,)),
            dma((3, NC)), dma((3, NC)), dma((NC,)), dma((NC,)), dma((NC,)), dma((NC,)),
            dma((NC - 1, 3)), dma((NC - 1, 3)), dma((NC,)), dma((NC,)), dma((1,)), dma((1,)),
            dma((2, 4)), dma((2, 2)),
        ],
        compiler_params=pltpu.CompilerParams(
            collective_id=1, has_side_effects=True, vmem_limit_bytes=VMEM_LIMIT
        ),
    )(sec, res, wall, wdn, cot, live, upb, dnb, sg)


def backward_kernel(
    dwup, gatt, att, wall, q, kx, vx, rnd, p, tok, sio, u_in, st_in, fg, fb, skip, decay,
    gsg, gsb, gdb, gub,
    gtok_o, finb_o, finrb_o, fing_o, finrg_o, sums_o,
    own_b, prec_b, rrec_b, xrec_b, fin_b, finr_b, acc_b,
    own_g, prec_g, rrec_g, xrec_g, fin_g, finr_g, acc_g, go_s,
    gatt_s, wo_s, att_s, ga_s, q_s, k_s, v_s, rnd_s, dk_s, dv_s, pbuf, ds_s, gres_s, nb_s,
    sio_s, gd_s, gctx_s, sum_s, got_s, part_s,
    loc, psem, gsem, osem, mbs, mbr, mgs, mgr, rbs, rbr, rgs, rgr, xbs, xbr, xgs, xgr,
    fbs, fbr, fgs, fgr, ts, tr, us, ur,
):
    net = Net()
    rep, core = net.rep, net.core
    theirs = 1 - core

    loads = [
        pltpu.make_async_copy(gatt, gatt_s, loc.at[0]),
        pltpu.make_async_copy(wall.at[3], wo_s, loc.at[1]),
        pltpu.make_async_copy(att, att_s, loc.at[2]),
        pltpu.make_async_copy(q, q_s, loc.at[3]),
        pltpu.make_async_copy(kx, k_s, loc.at[4]),
        pltpu.make_async_copy(vx, v_s, loc.at[5]),
        pltpu.make_async_copy(rnd, rnd_s, loc.at[6]),
        pltpu.make_async_copy(sio, sio_s, loc.at[7]),
    ]
    rises = [pltpu.make_async_copy(dwup.at[i, :, core], own_b.at[i], loc.at[8 + i]) for i in range(4)]
    for copy in rises:
        copy.start()
    for copy in loads:
        copy.start()
    fin_b[...] = jnp.zeros(fin_b.shape, BF16)
    finr_b[...] = jnp.zeros(finr_b.shape, BF16)
    fin_g[...] = jnp.zeros(fin_g.shape, BF16)
    finr_g[...] = jnp.zeros(finr_g.shape, BF16)
    barrier = pltpu.get_barrier_semaphore()
    me = rep * (2 * NC) + net.shard

    def device(away):
        other = (me + away) % (4 * NC)
        return other, (other // (2 * NC), other % (2 * NC))

    @pl.loop(1, 4 * NC)
    def _(away):
        pl.semaphore_signal(barrier, inc=1, device_id=device(away)[1], device_id_type=MESH)

    pl.semaphore_wait(barrier, 4 * NC - 1)

    def mate_big(which, source):
        return rcopy(source, prec_b.at[which], mbs.at[which], mbr.at[which], net.mate)

    def mate_group(g):
        return rcopy(own_g.at[g, :, theirs], prec_g.at[g], mgs.at[g], mgr.at[g], net.mate)

    for i in (1, 2, 3 * (1 - rep), 3 * rep):
        mate_big(i, dwup.at[i, :, theirs]).start()

    def chip_for(n):
        t, way = n // 2, n % 2
        hops = (4 - t) * (1 - way) + (t - 3) * way
        return chip_at((net.pos + net.step * hops + 4 * NC) % NC)

    class Stream:
        def __init__(self, own, prec, rrec, xrec, fin, finr, acc, sems):
            self.own, self.prec, self.rrec, self.xrec = own, prec, rrec, xrec
            self.fin, self.finr, self.acc = fin, finr, acc
            self.rs, self.rr, self.xs, self.xr, self.fs, self.fr = sems

        def ring(self, slot, which, n):
            source = self.prec.at[which, chip_for(n)]
            way = n % 2
            return rcopy(
                source, self.rrec.at[slot, n], self.rs.at[slot, n], self.rr.at[slot, n],
                net.along(1 - 2 * way),
            )

        def twin(self, which, n):
            chip = chip_for(n)
            return rcopy(
                self.prec.at[which, chip], self.xrec.at[chip], self.xs.at[n], self.xr.at[n], net.twin
            )

        def finish(self, which):
            return rcopy(
                self.fin.at[which], self.finr.at[which], self.fs.at[which], self.fr.at[which], net.twin
            )

        def give(self, which, n):
            chip = chip_for(n)
            self.prec[which, chip] = (
                self.own(which, chip).astype(F32) + self.prec[which, chip].astype(F32)
            ).astype(BF16)
            self.twin(which, n).start()

        def turn(self, slot, which, n, sole):
            chip = chip_for(n)
            self.acc[...] = self.own(which, chip).astype(F32) + self.prec[which, chip].astype(F32)

            @pl.when(sole)
            def _():
                self.twin(which, n).wait_recv()
                self.acc[...] = self.acc[...] + self.xrec[chip].astype(F32)

            @pl.when((n >= 2) & (n < 7))
            def _():
                self.ring(slot, which, n - 2).wait_recv()
                self.acc[...] = self.acc[...] + self.rrec[slot, n - 2].astype(F32)

            @pl.when(n < 7)
            def _():
                self.prec[which, chip] = self.acc[...].astype(BF16)
                self.ring(slot, which, n).start()

            @pl.when(n == 7)
            def _():
                self.ring(slot, which, 5).wait_recv()
                self.ring(slot, which, 6).wait_recv()
                total = self.acc[...] + self.rrec[slot, 5].astype(F32) + self.rrec[slot, 6].astype(F32)
                self.fin[which] = total.astype(BF16)
                self.finish(which).start()

    big = Stream(
        lambda which, chip: own_b[which, chip], prec_b, rrec_b, xrec_b, fin_b, finr_b, acc_b,
        (rbs, rbr, xbs, xbr, fbs, fbr),
    )
    group = Stream(
        lambda which, chip: own_g[which, chip, core], prec_g, rrec_g, xrec_g, fin_g, finr_g, acc_g,
        (rgs, rgr, xgs, xgr, fgs, fgr),
    )

    def tile(index):
        return (
            pl.ds(pl.multiple_of((index // 8) * 16, 16), 16),
            pl.ds(pl.multiple_of((index % 8) * 128, 128), 128),
        )

    def share(away):
        other, where = device(away)
        return rcopy(sum_s.at[tile(other)], got_s.at[away], ts.at[away], tr.at[away], where)

    def spread(away):
        return rcopy(part_s, sums_o.at[tile(me)], us.at[away], ur.at[away], device(away)[1])

    def each_device(act):
        @pl.loop(1, 4 * NC)
        def _(away):
            act(away)

    def big_at(e):
        k, j = e // 4, e % 4
        n = k - 2 * (j // 2) - j // 3
        which = (j + 1) * (1 - j // 2) + (j // 2) * (3 * rep * (1 - j // 3) + 4 * (j // 3))

        @pl.when((j >= 2) & (n == 0))
        def _():
            mate_big(which, dwup.at[0, :, theirs]).wait_recv()

        @pl.when((n >= 0) & (n <= 7))
        def _():
            big.turn(j, which, n, j == 2)

    def group_at(e):
        k, j = e // 3, e % 3
        n = k - 2 * (j // 2)
        which = rep * (1 - (j + 1) // 2) + (j + 1) * ((j + 1) // 2)

        @pl.when((j >= 1) & (n == 0))
        def _():
            mate_group(which).wait_recv()

        @pl.when((n >= 0) & (n <= 7))
        def _():
            group.turn(j, which, n, j == 0)

    def run(at, low, high):
        @pl.loop(low, high)
        def _(e):
            at(e)

    for i in range(2):
        loads[i].wait()

    def p_copy(slot, at):
        return pltpu.make_async_copy(p.at[at], pbuf.at[slot], psem.at[slot])

    p_copy(0, 0).start()

    @pl.loop(0, 4)
    def _(at):
        rows = pl.ds(pl.multiple_of(at * 256, 256), 256)
        ga_s[rows, :] = dot_nt(gatt_s[rows, :], wo_s[...]).astype(BF16)

    for copy in rises:
        copy.wait()
    for i in (1, 2):
        mate_big(i, dwup.at[i, :, theirs]).wait_recv()
    run(big_at, 0, 8)
    mate_big(3 * (1 - rep), dwup.at[0, :, theirs]).wait_recv()

    @pl.loop(0, NC)
    def _(n):
        big.give(3 * (1 - rep), n)

    loads[2].wait()

    @pl.loop(0, 4)
    def _(at):
        cols = pl.ds(pl.multiple_of(at * 256, 256), 256)
        made = dot_tn(att_s[...], gatt_s[:, cols]).reshape(NC, 2, 64, 256)
        own_b[4, :, :, cols] = jnp.where(core == 0, made[:, 0], made[:, 1]).astype(BF16)
        go_s[:, :, cols] = jnp.where(core == 0, made[:, 1], made[:, 0]).astype(BF16)

    mate_big(4, go_s).start()
    tok_load = pltpu.make_async_copy(tok, wo_s, loc.at[0])
    tok_load.start()
    for copy in loads[3:]:
        copy.wait()
    ds_s[...] = jnp.zeros(ds_s.shape, BF16)
    dq_s = gatt_s

    def weights_in(i):
        target = (q_s, k_s.at[pl.ds(0, 1024)], v_s.at[pl.ds(0, 1024)])[i]
        return pltpu.make_async_copy(wall.at[i], target, loc.at[1 + i])

    @pl.loop(0, 4)
    def _(g):
        for hh in range(2):
            for b in range(NBLK):
                i = 2 * hh + b
                m = 4 * g + i
                h = 2 * g + hh
                slot = i % 2
                cols = pl.ds(pl.multiple_of(h * DH, DH), DH)
                following = 2 * hh + b + 1
                nb, nh = following % 2, 2 * g + following // 2
                p_copy(slot, b * 8 + h).wait()
                if following < 4:
                    p_copy(1 - slot, nb * 8 + nh).start()
                else:

                    @pl.when(g < 3)
                    def _():
                        p_copy(1 - slot, nh).start()

                for part in range(2):
                    span = (part + 1) * 256
                    rows = pl.ds(b * BLK + part * 256, 256)
                    local = pl.ds(part * 256, 256)
                    grads = ga_s[rows, cols]
                    slope = dot_nt(grads, v_s[pl.ds(b * BLK, span), cols])
                    kept = pbuf[slot, local, pl.ds(CTX, span)].astype(F32)
                    both = jnp.sum(kept * slope, axis=-1, keepdims=True)
                    mass = jnp.sum(kept, axis=-1, keepdims=True)
                    if b:
                        slope_before = dot_nt(grads, v_s[pl.ds(1024, CTX), cols])
                        kept_before = pbuf[slot, local, pl.ds(0, CTX)].astype(F32)
                        both += jnp.sum(kept_before * slope_before, axis=-1, keepdims=True)
                        mass += jnp.sum(kept_before, axis=-1, keepdims=True)
                    both = both / mass
                    inner = (kept * (slope - both)).astype(BF16)
                    ds_s[local, pl.ds(CTX, span)] = inner
                    total = dot_nn(inner, k_s[pl.ds(b * BLK, span), cols])
                    if b:
                        inner = (kept_before * (slope_before - both)).astype(BF16)
                        ds_s[local, pl.ds(0, CTX)] = inner
                        total = total + dot_nn(inner, k_s[pl.ds(1024, CTX), cols])
                    dq_s[rows, cols] = (total * SCALE).astype(BF16)
                rows = pl.ds(b * BLK, BLK)
                first = 0 if b else CTX
                made_k = dot_tn(ds_s[:, first:], q_s[rows, cols]) * SCALE
                made_v = dot_tn(pbuf[slot, :, first:], ga_s[rows, cols])
                if b:
                    dk_s[pl.ds(1024, CTX), cols] = made_k[:CTX].astype(BF16)
                    dv_s[pl.ds(1024, CTX), cols] = made_v[:CTX].astype(BF16)
                    made_k, made_v = made_k[CTX:], made_v[CTX:]
                dk_s[rows, cols] = made_k.astype(BF16)
                dv_s[rows, cols] = made_v.astype(BF16)

                run(big_at, 8 + (9 * m) // 4, 8 + (9 * (m + 1)) // 4)

                @pl.when(m == 9)
                def _():
                    for each in range(2):
                        mate_group(each).wait_recv()

                @pl.when((m >= 9) & (m < 13))
                def _(m=m):
                    for e in range(2):
                        group.give(1 - rep, 2 * (m - 9) + e)

        @pl.when(g == 3)
        def _():
            for i in range(3):
                weights_in(i).start()

        cols = pl.ds(pl.multiple_of(g * 256, 256), 256)
        own_g[g, :, :, :, 0:256] = dot_tn(rnd_s[0:1024, :], dq_s[:, cols]).astype(BF16).reshape(NC, 2, 64, 256)
        own_g[g, :, :, :, 256:512] = dot_tn(rnd_s[...], dk_s[:, cols]).astype(BF16).reshape(NC, 2, 64, 256)
        own_g[g, :, :, :, 512:768] = dot_tn(rnd_s[...], dv_s[:, cols]).astype(BF16).reshape(NC, 2, 64, 256)
        mate_group(g).start()

    run(group_at, 0, 6)
    for i in range(3):
        weights_in(i).wait()
    tok_load.wait()

    def gres_in(at):
        rows = pl.ds(pl.multiple_of(at * 256, 256), 256)
        return pltpu.make_async_copy(gatt.at[rows], gres_s.at[at % 2], gsem.at[at % 2])

    gres_in(0).start()

    after = pl.ds(1024, CTX)
    gctx = dot_nt(dk_s[after, :], k_s[0:1024, :]) + dot_nt(dv_s[after, :], v_s[0:1024, :])
    gctx_s[...] = gctx
    xhat, _ = norm_parts(wo_s[pl.ds(BLK - CTX, CTX), :].astype(F32))
    sum_s[32:48, :] = jnp.zeros((16, 1024), F32)
    sum_s[34:35, :] = jnp.sum(gctx * (xhat * fg[...] + fb[...]), axis=0, keepdims=True)
    for at, vector in ((35, gsg), (36, gsb), (37, gdb)):
        sum_s[at : at + 1, :] = vector[...]
    for at in range(4):
        sum_s[38 + at : 39 + at, :] = gub[:, at * 1024 : (at + 1) * 1024]
    run(group_at, 6, 9)
    states, raw = st_in[...], u_in[...]
    factor = jnp.exp(-column(decay[...]))
    scale = jnp.sqrt(1.0 - factor * factor)
    sum_s[16:32, :] = lax.dot_general(
        states[:, BLK - CTX :], gctx, (((1,), (0,)), ((), ())),
        preferred_element_type=F32, precision=lax.Precision.HIGHEST,
    )
    back = split_dot(
        lambda a, b: lax.dot_general(b, a, (((0,), (1,)), ((), ())), preferred_element_type=F32),
        gctx, sio_s[...], 3,
    )
    seeds = jnp.concatenate([jnp.zeros((16, BLK - CTX), F32), back[16:32, :]], axis=1)
    lam = lane_scan(seeds, factor, True)
    lane = lax.broadcasted_iota(jnp.int32, lam.shape, 1)
    earlier = jnp.where(lane >= 1, pltpu.roll(states, 1, 1), 0.0)
    rates = -factor * jnp.sum(lam * (earlier - (factor / scale) * raw), axis=1, keepdims=True)
    sum_s[48:64, :] = jnp.broadcast_to(rates, (16, 1024))
    driven = scale * lam
    sum_s[0:16, :] = split_dot(dot_nn, driven, rnd_s[0:BLK, :], 3)
    gd_s[...] = jnp.zeros(gd_s.shape, F32)
    gd_s[0:16, 0:BLK] = driven

    def leave(at):
        rows = pl.ds(pl.multiple_of(at * 256, 256), 256)
        return pltpu.make_async_copy(rnd_s.at[rows], gtok_o.at[rows], osem.at[at])

    @pl.loop(0, 4)
    def _(at):
        rows = pl.ds(pl.multiple_of(at * 256, 256), 256)

        @pl.when(at < 3)
        def _():
            gres_in(at + 1).start()

        nb_s[...] = (
            dot_nt(dq_s[rows, :], q_s[...])
            + dot_nt(dk_s[rows, :], k_s[0:1024, :])
            + dot_nt(dv_s[rows, :], v_s[0:1024, :])
            + split_dot(
                lambda a, b: lax.dot_general(a, b, (((0,), (1,)), ((), ())), preferred_element_type=F32),
                gd_s[:, rows], sio_s[...], 3,
            )
        )

        @pl.when(at == 1)
        def _():
            half = pl.ds(128, CTX)
            nb_s[half, :] = nb_s[half, :] + skip[...] * gctx_s[...]

        run(group_at, 9 + 3 * at, 12 + 3 * at)

        xhat, inverse = norm_parts(wo_s[rows, :].astype(F32))
        grad = nb_s[...]
        gain = jnp.sum(grad * xhat, axis=0, keepdims=True)
        shift = jnp.sum(grad, axis=0, keepdims=True)
        sum_s[32:33, :] = sum_s[32:33, :] + gain
        sum_s[33:34, :] = sum_s[33:34, :] + shift
        grad = grad * fg[...]
        grad = grad - jnp.mean(grad, axis=-1, keepdims=True) - xhat * jnp.mean(
            grad * xhat, axis=-1, keepdims=True
        )
        gres_in(at).wait()
        rnd_s[rows, :] = (gres_s[at % 2].astype(F32) + inverse * grad).astype(BF16)
        leave(at).start()

    each_device(lambda away: share(away).start())
    part_s[...] = sum_s[tile(me)]
    run(group_at, 21, 24)

    def add_in(away):
        share(away).wait_recv()
        part_s[...] = part_s[...] + got_s[away]

    each_device(add_in)
    each_device(lambda away: spread(away).start())
    sums_o[tile(me)] = part_s[...]
    run(group_at, 24, 30)

    for which in (3 * rep, 1, 2, 4):
        big.finish(which).wait_send()
    for which in (rep, 2, 3):
        group.finish(which).wait_send()
    twin_rise = 3 * (1 - rep)
    for which in (twin_rise, 1, 2, 4):
        big.finish(which).wait_recv()
    for which in (1 - rep, 2, 3):
        group.finish(which).wait_recv()
    for source, target in ((fin_b, finb_o), (finr_b, finrb_o), (fin_g, fing_o), (finr_g, finrg_o)):
        target[...] = source[...]

    def settle(away):
        spread(away).wait()
        share(away).wait_send()

    each_device(settle)
    for i in range(4):
        mate_big(i, dwup.at[i, :, theirs]).wait_send()
        mate_group(i).wait_send()
        leave(i).wait()
    mate_big(4, go_s).wait_send()

    @pl.loop(0, NC)
    def _(n):
        big.twin(3 * (1 - rep), n).wait_send()
        group.twin(1 - rep, n).wait_send()

    @pl.loop(0, NC - 1)
    def _(n):
        for slot in range(4):
            big.ring(slot, 0, n).wait_send()
        for slot in range(3):
            group.ring(slot, 0, n).wait_send()


def run_backward(*operands):
    shape = jax.ShapeDtypeStruct
    dma = pltpu.SemaphoreType.DMA
    vmem = pltpu.VMEM
    full = (1024, 1024)
    ext = (1024 + CTX, 1024)
    part = (64, 1024)
    cut = (64, 768)
    return pl.pallas_call(
        backward_kernel,
        name="backward_part",
        out_shape=(
            shape(full, BF16), shape((5,) + part, BF16), shape((5,) + part, BF16),
            shape((4,) + cut, BF16), shape((4,) + cut, BF16), shape((64, 1024), F32),
        ),
        in_specs=any_spec(11) + vmem_spec(10),
        out_specs=any_spec(1) + vmem_spec(5),
        scratch_shapes=[
            vmem((5, NC) + part, BF16), vmem((5, NC) + part, BF16), vmem((4, NC - 1) + part, BF16),
            vmem((NC,) + part, BF16), vmem((5,) + part, BF16), vmem((5,) + part, BF16), vmem(part, F32),
            vmem((4, NC, 2) + cut, BF16), vmem((4, NC) + cut, BF16), vmem((3, NC - 1) + cut, BF16),
            vmem((NC,) + cut, BF16), vmem((4,) + cut, BF16), vmem((4,) + cut, BF16), vmem(cut, F32),
            vmem((NC,) + part, BF16),
            vmem(full, BF16), vmem(full, BF16), vmem(full, BF16), vmem(full, BF16), vmem(full, BF16),
            vmem(ext, BF16), vmem(ext, BF16), vmem(ext, BF16), vmem(ext, BF16), vmem(ext, BF16),
            vmem((2, BLK, CTX + BLK), BF16), vmem((BLK, CTX + BLK), BF16), vmem((2, 256, 1024), BF16),
            vmem((256, 1024), F32), vmem((1024, 128), BF16), vmem((128, 1024), F32), vmem((CTX, 1024), F32),
            vmem((64, 1024), F32), vmem((4 * NC, 16, 128), F32), vmem((16, 128), F32),
            dma((12,)), dma((2,)), dma((2,)), dma((4,)), dma((5,)), dma((5,)), dma((4,)), dma((4,)),
            dma((4, NC - 1)), dma((4, NC - 1)), dma((3, NC - 1)), dma((3, NC - 1)),
            dma((NC,)), dma((NC,)), dma((NC,)), dma((NC,)), dma((5,)), dma((5,)), dma((4,)), dma((4,)),
            dma((4 * NC,)), dma((4 * NC,)), dma((4 * NC,)), dma((4 * NC,)),
        ],
        compiler_params=pltpu.CompilerParams(
            collective_id=2, has_side_effects=True, vmem_limit_bytes=VMEM_LIMIT
        ),
    )(*operands)


def outputs_kernel(
    finb, finrb, fing, finrg, find, findr, sums,
    dup_o, do_o, dq_o, dk_o, dv_o, ddown_o, gfg_o, gfb_o, gskip_o, gsg_o, gsb_o, gdb_o, gub_o, grate_o,
    gsi_o, gso_o,
):
    rep, shard = lax.axis_index("rep"), lax.axis_index("shard")
    for i in range(4):
        dup_o[:, i * 1024 : (i + 1) * 1024] = finb[i].astype(F32) + finrb[i].astype(F32)
    do_o[...] = finb[4].astype(F32) + finrb[4].astype(F32)
    for g in range(4):
        for i, out in enumerate((dq_o, dk_o, dv_o)):
            cols = slice(i * 256, (i + 1) * 256)
            out[:, g * 256 : (g + 1) * 256] = fing[g, :, cols].astype(F32) + finrg[g, :, cols].astype(F32)
    mine = pl.ds(pl.multiple_of(rep * 64, 64), 192)
    theirs = pl.ds(pl.multiple_of((1 - rep) * 64, 64), 192)
    ddown_o[...] = jnp.zeros((256, 1024), F32)
    ddown_o[mine, :] = find[...].astype(F32)
    ddown_o[theirs, :] = ddown_o[theirs, :] + findr[...].astype(F32)
    for at, out in enumerate((gfg_o, gfb_o, gskip_o, gsg_o, gsb_o, gdb_o)):
        out[...] = sums[32 + at : 33 + at, :]
    for at in range(4):
        gub_o[:, at * 1024 : (at + 1) * 1024] = sums[38 + at : 39 + at, :]
    same = lax.broadcasted_iota(jnp.int32, (16, 128), 0) == lax.broadcasted_iota(jnp.int32, (16, 128), 1)
    grate_o[...] = jnp.sum(jnp.where(same, sums[48:64, 0:128], 0.0), axis=0, keepdims=True)
    shift = (1024 - 64 * shard) % 1024
    gsi_o[...] = pltpu.roll(sums[0:16, :], shift, 1)[:, 0:64]
    gso_o[...] = pltpu.roll(sums[16:32, :], shift, 1)[:, 0:64]


def run_outputs(*operands):
    shape = jax.ShapeDtypeStruct
    row = shape((1, 1024), F32)
    part = shape((64, 1024), F32)
    return pl.pallas_call(
        outputs_kernel,
        name="outputs_part",
        out_shape=(
            shape((64, 4096), F32), part, part, part, part, shape((256, 1024), F32),
            row, row, row, row, row, row, shape((1, 4096), F32), shape((1, 128), F32),
            shape((16, 64), F32), shape((16, 64), F32),
        ),
        in_specs=vmem_spec(7),
        out_specs=vmem_spec(16),
        compiler_params=pltpu.CompilerParams(vmem_limit_bytes=VMEM_LIMIT),
    )(*operands)


def fused_device(
    tokens, lengths, first_gain, first_bias, decay_rates, state_in, state_out, skip_gain,
    query_weight, key_weight, value_weight, output_weight, second_gain, second_bias,
    up_weight, up_bias, down_weight, down_bias, cotangent,
):
    tok = tokens.reshape(1024, 1024)
    cot = cotangent.reshape(1024, 1024)
    fg, fb, skip, sg, sb, dnb, upb, decay = (
        v.reshape(1, -1)
        for v in (
            first_gain, first_bias, skip_gain, second_gain, second_bias, down_bias, up_bias, decay_rates,
        )
    )
    wall, sio, rnd, q, kx, vx, att, res, sec, p, u, st = run_forward(
        tok, query_weight, key_weight, value_weight, output_weight, up_weight, state_in, state_out,
        fg, fb, skip, sg, sb, decay,
    )
    result, gatt, dwup, find, findr, gdb, gub, gsg, gsb = run_feed(
        sec, res, wall, down_weight, cot, lengths, upb, dnb, sg
    )
    gtok, finb, finrb, fing, finrg, sums = run_backward(
        dwup.reshape(4, NC, 2, 64, 1024), gatt, att, wall, q, kx, vx, rnd, p, tok, sio,
        u, st, fg, fb, skip, decay, gsg, gsb, gdb, gub,
    )
    dup, do, dq, dk, dv, ddown, *rest = run_outputs(finb, finrb, fing, finrg, find, findr, sums)
    gfg, gfb, gskip, gsg, gsb, gdb, gub, grate, gsi, gso = rest
    return (
        result.reshape(1, 1024, 1024), gtok.reshape(1, 1024, 1024), gfg[0], gfb[0],
        grate[0, 0:16], gsi, gso, gskip[0], dq, dk, dv, do, gsg[0], gsb[0], dup, gub[0], ddown, gdb[0],
    )


NORM_EPS = 1e-05
NEG_LARGE = -1e30
HIGHEST = lax.Precision.HIGHEST


def layer_norm(hidden, gain_vec, bias_vec):
    average = jnp.mean(hidden, axis=-1, keepdims=True)
    centred = hidden - average
    spread = jnp.mean(centred * centred, axis=-1, keepdims=True)
    return centred * lax.rsqrt(spread + NORM_EPS) * gain_vec + bias_vec


def state_context(driven_raw, normed, decay_rates, state_out, skip_gain):
    decay_factor = jnp.exp(-decay_rates)
    driven = driven_raw * jnp.sqrt(1.0 - decay_factor * decay_factor)
    factors = jnp.broadcast_to(decay_factor, driven.shape)

    def combine(earlier, subsequent):
        return (earlier[0] * subsequent[0], subsequent[0] * earlier[1] + subsequent[1])

    states = lax.associative_scan(combine, (factors, driven), axis=1)[1]
    seq_count = driven_raw.shape[0]
    state_width = driven_raw.shape[2]
    model_width = normed.shape[2]
    tail_states = states.reshape(seq_count, NBLK, BLK, state_width)[:, :, BLK - CTX :, :]
    skipped = normed.reshape(seq_count, NBLK, BLK, model_width)[:, :, BLK - CTX :, :]
    outputs = (
        jnp.einsum("sbcp,pd->sbcd", tail_states, state_out, precision=HIGHEST) + skip_gain * skipped
    )
    empty_ctx = jnp.zeros((seq_count, 1, CTX, model_width), jnp.float32)
    return jnp.concatenate([empty_ctx, outputs[:, : NBLK - 1]], axis=1)


def block_scores(queries, key_rows, ctx_keys, ctx_valid):
    row_count = queries.shape[0]
    head_count = queries.shape[1] // DH
    query_heads = queries.reshape(row_count, head_count, DH)
    key_heads = jnp.concatenate([ctx_keys, key_rows], 0).reshape(-1, head_count, DH)
    scores = jnp.einsum(
        "qhd,khd->hqk", query_heads, key_heads, preferred_element_type=jnp.float32
    ) * DH ** (-0.5)
    causal = lax.broadcasted_iota(jnp.int32, (row_count, row_count), 0) >= lax.broadcasted_iota(
        jnp.int32, (row_count, row_count), 1
    )
    allowed = jnp.concatenate(
        [jnp.broadcast_to(ctx_valid[None, :], (row_count, ctx_keys.shape[0])), causal], axis=1
    )
    return (jnp.where(allowed[None], scores, NEG_LARGE), query_heads, key_heads)


def attend_forward(block_item):
    queries, key_rows, value_rows, ctx_keys, ctx_values, ctx_valid = block_item
    scores, query_heads, key_heads = block_scores(queries, key_rows, ctx_keys, ctx_valid)
    row_max = jnp.max(scores, axis=-1, keepdims=True)
    expos = jnp.exp(scores - row_max)
    denominator = jnp.sum(expos, axis=-1, keepdims=True)
    weights = (expos / denominator).astype(jnp.bfloat16)
    value_heads = jnp.concatenate([ctx_values, value_rows], 0).reshape(key_heads.shape)
    attended = jnp.einsum("hqk,khd->qhd", weights, value_heads, preferred_element_type=jnp.float32)
    return (
        attended.reshape(queries.shape).astype(jnp.bfloat16),
        (row_max + jnp.log(denominator))[..., 0],
    )


def attend_backward(block_item):
    queries, key_rows, value_rows, ctx_keys, ctx_values, ctx_valid, log_total, grad_attended = (
        block_item
    )
    scores, query_heads, key_heads = block_scores(queries, key_rows, ctx_keys, ctx_valid)
    probs = jnp.exp(scores - log_total[..., None])
    value_heads = jnp.concatenate([ctx_values, value_rows], 0).reshape(key_heads.shape)
    grad_heads = grad_attended.reshape(query_heads.shape)
    grad_probs = jnp.einsum(
        "qhd,khd->hqk", grad_heads, value_heads, preferred_element_type=jnp.float32
    )
    grad_scores = (
        probs * (grad_probs - jnp.sum(probs * grad_probs, axis=-1, keepdims=True))
    ).astype(jnp.bfloat16)
    grad_values = jnp.einsum(
        "hqk,qhd->khd", probs.astype(jnp.bfloat16), grad_heads, preferred_element_type=jnp.float32
    )
    grad_queries = jnp.einsum(
        "hqk,khd->qhd", grad_scores, key_heads, preferred_element_type=jnp.float32
    ) * DH ** (-0.5)
    grad_keys = jnp.einsum(
        "hqk,qhd->khd", grad_scores, query_heads, preferred_element_type=jnp.float32
    ) * DH ** (-0.5)
    ctx_count = ctx_keys.shape[0]
    model_width = queries.shape[1]
    grad_keys = grad_keys.reshape(-1, model_width).astype(jnp.bfloat16)
    grad_values = grad_values.reshape(-1, model_width).astype(jnp.bfloat16)
    return (
        grad_queries.reshape(queries.shape).astype(jnp.bfloat16),
        grad_keys[ctx_count:],
        grad_values[ctx_count:],
        grad_keys[:ctx_count],
        grad_values[:ctx_count],
    )


def per_device(
    tokens,
    lengths,
    first_gain,
    first_bias,
    decay_rates,
    state_in,
    state_out,
    skip_gain,
    query_weight,
    key_weight,
    value_weight,
    output_weight,
    second_gain,
    second_bias,
    up_weight,
    up_bias,
    down_weight,
    down_bias,
    cotangent,
):
    full_query, full_key, full_value, full_output, full_up, full_down, full_in, full_out = (
        lax.all_gather(query_weight, "shard", axis=0, tiled=True),
        lax.all_gather(key_weight, "shard", axis=0, tiled=True),
        lax.all_gather(value_weight, "shard", axis=0, tiled=True),
        lax.all_gather(output_weight, "shard", axis=0, tiled=True),
        lax.all_gather(up_weight, "shard", axis=0, tiled=True),
        lax.all_gather(down_weight, "shard", axis=0, tiled=True),
        lax.all_gather(state_in, "shard", axis=1, tiled=True),
        lax.all_gather(state_out, "shard", axis=1, tiled=True),
    )
    seq_count, seq_len, model_width = tokens.shape
    row_count = seq_count * seq_len
    block_count = seq_count * NBLK
    positions = lax.broadcasted_iota(jnp.int32, (seq_count, seq_len), 1)
    row_mask = (positions < lengths[:, None]).astype(jnp.float32).reshape(row_count, 1)
    block_index = lax.broadcasted_iota(jnp.int32, (seq_count, NBLK, CTX), 1)
    ctx_valid = (block_index > 0).reshape(block_count, CTX)
    token_rows = tokens.astype(jnp.float32)
    normed, first_pullback = jax.vjp(layer_norm, token_rows, first_gain, first_bias)
    rounded = normed.astype(jnp.bfloat16)
    driven_raw = jnp.einsum("std,pd->stp", rounded, full_in, preferred_element_type=jnp.float32)
    context, state_pullback = jax.vjp(
        state_context, driven_raw, normed, decay_rates, full_out.astype(jnp.float32), skip_gain
    )
    ctx_rows = context.astype(jnp.bfloat16).reshape(block_count * CTX, model_width)
    flat_rounded = rounded.reshape(row_count, model_width)
    query_rows = jnp.dot(flat_rounded, full_query, preferred_element_type=jnp.float32).astype(
        jnp.bfloat16
    )
    key_rows = jnp.dot(flat_rounded, full_key, preferred_element_type=jnp.float32).astype(
        jnp.bfloat16
    )
    value_rows = jnp.dot(flat_rounded, full_value, preferred_element_type=jnp.float32).astype(
        jnp.bfloat16
    )
    ctx_keys = jnp.dot(ctx_rows, full_key, preferred_element_type=jnp.float32).astype(jnp.bfloat16)
    ctx_values = jnp.dot(ctx_rows, full_value, preferred_element_type=jnp.float32).astype(
        jnp.bfloat16
    )
    block_inputs = (
        query_rows.reshape(block_count, BLK, model_width),
        key_rows.reshape(block_count, BLK, model_width),
        value_rows.reshape(block_count, BLK, model_width),
        ctx_keys.reshape(block_count, CTX, model_width),
        ctx_values.reshape(block_count, CTX, model_width),
        ctx_valid,
    )
    attended, log_total = lax.map(attend_forward, block_inputs)
    attended_rows = attended.reshape(row_count, model_width)
    residual = token_rows.reshape(row_count, model_width) + jnp.dot(
        attended_rows, full_output, preferred_element_type=jnp.float32
    )
    second, second_pullback = jax.vjp(layer_norm, residual, second_gain, second_bias)
    second_rows = second.astype(jnp.bfloat16)
    hidden = jnp.dot(second_rows, full_up, preferred_element_type=jnp.float32) + up_bias
    active, gelu_pullback = jax.vjp(jax.nn.gelu, hidden)
    active_rows = active.astype(jnp.bfloat16)
    branch = jnp.dot(active_rows, full_down, preferred_element_type=jnp.float32) + down_bias
    result = (
        ((residual + branch) * row_mask)
        .astype(jnp.bfloat16)
        .reshape(seq_count, seq_len, model_width)
    )
    full_query, full_key, full_value, full_output, full_up, full_down, full_in, full_out = (
        lax.all_gather(query_weight, "shard", axis=0, tiled=True),
        lax.all_gather(key_weight, "shard", axis=0, tiled=True),
        lax.all_gather(value_weight, "shard", axis=0, tiled=True),
        lax.all_gather(output_weight, "shard", axis=0, tiled=True),
        lax.all_gather(up_weight, "shard", axis=0, tiled=True),
        lax.all_gather(down_weight, "shard", axis=0, tiled=True),
        lax.all_gather(state_in, "shard", axis=1, tiled=True),
        lax.all_gather(state_out, "shard", axis=1, tiled=True),
    )
    grad_branch = cotangent.reshape(row_count, model_width).astype(jnp.float32) * row_mask
    branch_rounded = grad_branch.astype(jnp.bfloat16)
    grad_down = jnp.einsum(
        "rf,rd->fd", active_rows, branch_rounded, preferred_element_type=jnp.float32
    )
    grad_down_bias = jnp.sum(grad_branch, axis=0)
    grad_active = jnp.einsum(
        "rd,fd->rf", branch_rounded, full_down, preferred_element_type=jnp.float32
    )
    (grad_hidden,) = gelu_pullback(grad_active)
    hidden_rounded = grad_hidden.astype(jnp.bfloat16)
    grad_up = jnp.einsum(
        "rd,rf->df", second_rows, hidden_rounded, preferred_element_type=jnp.float32
    )
    grad_up_bias = jnp.sum(hidden_rounded.astype(jnp.float32), axis=0)
    grad_second = jnp.einsum(
        "rf,df->rd", hidden_rounded, full_up, preferred_element_type=jnp.float32
    )
    grad_residual_part, grad_second_gain, grad_second_bias = second_pullback(grad_second)
    grad_residual = grad_branch + grad_residual_part
    residual_rounded = grad_residual.astype(jnp.bfloat16)
    grad_output = jnp.einsum(
        "rd,re->de", attended_rows, residual_rounded, preferred_element_type=jnp.float32
    )
    grad_attended = jnp.einsum(
        "re,de->rd", residual_rounded, full_output, preferred_element_type=jnp.float32
    ).astype(jnp.bfloat16)
    grad_query_rows, grad_key_rows, grad_value_rows, grad_ctx_keys, grad_ctx_values = lax.map(
        attend_backward,
        block_inputs + (log_total, grad_attended.reshape(block_count, BLK, model_width)),
    )
    grad_query_rows = grad_query_rows.reshape(row_count, model_width)
    grad_key_rows = grad_key_rows.reshape(row_count, model_width)
    grad_value_rows = grad_value_rows.reshape(row_count, model_width)
    grad_ctx_keys = grad_ctx_keys.reshape(block_count * CTX, model_width)
    grad_ctx_values = grad_ctx_values.reshape(block_count * CTX, model_width)
    grad_query = jnp.einsum(
        "rd,re->de", flat_rounded, grad_query_rows, preferred_element_type=jnp.float32
    )
    grad_key = jnp.einsum(
        "rd,re->de", flat_rounded, grad_key_rows, preferred_element_type=jnp.float32
    ) + jnp.einsum("rd,re->de", ctx_rows, grad_ctx_keys, preferred_element_type=jnp.float32)
    grad_value = jnp.einsum(
        "rd,re->de", flat_rounded, grad_value_rows, preferred_element_type=jnp.float32
    ) + jnp.einsum("rd,re->de", ctx_rows, grad_ctx_values, preferred_element_type=jnp.float32)
    grad_normed = (
        jnp.einsum("re,de->rd", grad_query_rows, full_query, preferred_element_type=jnp.float32)
        + jnp.einsum("re,de->rd", grad_key_rows, full_key, preferred_element_type=jnp.float32)
        + jnp.einsum("re,de->rd", grad_value_rows, full_value, preferred_element_type=jnp.float32)
    )
    grad_context = jnp.einsum(
        "re,de->rd", grad_ctx_keys, full_key, preferred_element_type=jnp.float32
    ) + jnp.einsum("re,de->rd", grad_ctx_values, full_value, preferred_element_type=jnp.float32)
    grad_context = grad_context.reshape(seq_count, NBLK, CTX, model_width)
    grad_driven, state_normed, grad_rates, grad_state_out, grad_skip = state_pullback(grad_context)
    grad_in = jnp.einsum(
        "stp,std->pd", grad_driven, rounded, precision=HIGHEST, preferred_element_type=jnp.float32
    )
    state_rounded = jnp.einsum(
        "stp,pd->std", grad_driven, full_in, precision=HIGHEST, preferred_element_type=jnp.float32
    )
    normed_total = (
        grad_normed.reshape(seq_count, seq_len, model_width) + state_rounded + state_normed
    )
    tokens_part, grad_first_gain, grad_first_bias = first_pullback(normed_total)
    grad_tokens = (tokens_part + grad_residual.reshape(seq_count, seq_len, model_width)).astype(
        jnp.bfloat16
    )
    piece_query, piece_key, piece_value, piece_output, piece_up, piece_down, piece_in, piece_out = (
        lax.psum_scatter(grad_query, "shard", scatter_dimension=0, tiled=True),
        lax.psum_scatter(grad_key, "shard", scatter_dimension=0, tiled=True),
        lax.psum_scatter(grad_value, "shard", scatter_dimension=0, tiled=True),
        lax.psum_scatter(grad_output, "shard", scatter_dimension=0, tiled=True),
        lax.psum_scatter(grad_up, "shard", scatter_dimension=0, tiled=True),
        lax.psum_scatter(grad_down, "shard", scatter_dimension=0, tiled=True),
        lax.psum_scatter(grad_in, "shard", scatter_dimension=1, tiled=True),
        lax.psum_scatter(grad_state_out, "shard", scatter_dimension=1, tiled=True),
    )
    piece_query, piece_key, piece_value, piece_output, piece_up, piece_down, piece_in, piece_out = (
        lax.psum(piece_query.astype(jnp.bfloat16), "rep").astype(jnp.float32),
        lax.psum(piece_key.astype(jnp.bfloat16), "rep").astype(jnp.float32),
        lax.psum(piece_value.astype(jnp.bfloat16), "rep").astype(jnp.float32),
        lax.psum(piece_output.astype(jnp.bfloat16), "rep").astype(jnp.float32),
        lax.psum(piece_up.astype(jnp.bfloat16), "rep").astype(jnp.float32),
        lax.psum(piece_down.astype(jnp.bfloat16), "rep").astype(jnp.float32),
        lax.psum(piece_in.astype(jnp.bfloat16), "rep").astype(jnp.float32),
        lax.psum(piece_out.astype(jnp.bfloat16), "rep").astype(jnp.float32),
    )
    (
        sum_first_gain,
        sum_first_bias,
        sum_rates,
        sum_skip,
        sum_second_gain,
        sum_second_bias,
        sum_up_bias,
        sum_down_bias,
    ) = lax.psum(
        (
            grad_first_gain,
            grad_first_bias,
            grad_rates,
            grad_skip,
            grad_second_gain,
            grad_second_bias,
            grad_up_bias,
            grad_down_bias,
        ),
        ("rep", "shard"),
    )
    return (
        result,
        grad_tokens,
        sum_first_gain,
        sum_first_bias,
        sum_rates,
        piece_in,
        piece_out,
        sum_skip,
        piece_query,
        piece_key,
        piece_value,
        piece_output,
        sum_second_gain,
        sum_second_bias,
        piece_up,
        sum_up_bias,
        piece_down,
        sum_down_bias,
    )


def solution(mesh):
    placed = (
        P(("rep", "shard"), None, None),
        P(("rep", "shard")),
        P(),
        P(),
        P(),
        P(None, "shard"),
        P(None, "shard"),
        P(),
        P("shard", None),
        P("shard", None),
        P("shard", None),
        P("shard", None),
        P(),
        P(),
        P("shard", None),
        P(),
        P("shard", None),
        P(),
        P(("rep", "shard"), None, None),
    )
    fused = mesh.shape["rep"] == 2 and mesh.shape["shard"] == 2 * NC
    return jax.shard_map(
        fused_device if fused else per_device,
        mesh=mesh,
        in_specs=placed,
        out_specs=(
            P(("rep", "shard"), None, None),
            P(("rep", "shard"), None, None),
            P(),
            P(),
            P(),
            P(None, "shard"),
            P(None, "shard"),
            P(),
            P("shard", None),
            P("shard", None),
            P("shard", None),
            P("shard", None),
            P(),
            P(),
            P("shard", None),
            P(),
            P("shard", None),
            P(),
        ),
        check_vma=False,
    )
```

```python
import functools
import math

import jax
import jax.numpy as jnp
from jax import lax
from jax.experimental import pallas as pl
from jax.experimental.pallas import tpu as pltpu
from jax.sharding import PartitionSpec as P

DH = 128
BLK = 512
CTX = 128
NBLK = 2
EPS = 1e-05
NEG = -1e30
SCALE = DH ** (-0.5)
MESH = pl.DeviceIdType.MESH
F32 = jnp.float32
BF16 = jnp.bfloat16
VMEM_LIMIT = 66_000_000
NC = 8


def chip_at(pos):
    turned = pos // 4
    return (1 - turned) * (2 * pos) + turned * (2 * (7 - pos) + 1)


class Net:
    def __init__(self):
        self.rep = lax.axis_index("rep")
        self.shard = lax.axis_index("shard")
        self.core = self.shard % 2
        chip = self.shard // 2
        z, y = chip // 2, chip % 2
        self.pos = (1 - y) * z + y * (7 - z)
        self.step = 1 - 2 * self.core
        self.mate = (self.rep, 2 * chip + 1 - self.core)
        self.twin = (1 - self.rep, self.shard)

    def at(self, hops, core):
        return 2 * chip_at((self.pos + self.step * hops + 4 * NC) % NC) + core

    def along(self, hops):
        return (self.rep, self.at(hops, self.core))

    def greet(self):
        barrier = pltpu.get_barrier_semaphore()
        for device in (self.along(1), self.along(-1), self.mate, self.twin):
            pl.semaphore_signal(barrier, inc=1, device_id=device, device_id_type=MESH)
        pl.semaphore_wait(barrier, 4)


def rcopy(src, dst, send, recv, device):
    return pltpu.make_async_remote_copy(
        src_ref=src, dst_ref=dst, send_sem=send, recv_sem=recv, device_id=device, device_id_type=MESH
    )


def dot_nn(a, b):
    return lax.dot_general(a, b, (((1,), (0,)), ((), ())), preferred_element_type=F32)


def dot_nt(a, b):
    return lax.dot_general(a, b, (((1,), (1,)), ((), ())), preferred_element_type=F32)


def dot_tn(a, b):
    return lax.dot_general(a, b, (((0,), (0,)), ((), ())), preferred_element_type=F32)


def norm_parts(rows):
    centred = rows - jnp.mean(rows, axis=-1, keepdims=True)
    spread = jnp.mean(centred * centred, axis=-1, keepdims=True)
    inverse = lax.rsqrt(spread + EPS)
    return centred * inverse, inverse


def split_dot(dot, left, right, narrow):
    total = None
    rest = left
    for _ in range(narrow):
        term = rest.astype(BF16)
        part = dot(term, right)
        total = part if total is None else total + part
        rest = rest - term.astype(F32)
    return total


def lane_scan(values, factor, reverse):
    width = values.shape[1]
    lane = lax.broadcasted_iota(jnp.int32, values.shape, 1)
    shift = 1
    power = factor
    while shift < width:
        if reverse:
            moved = pltpu.roll(values, width - shift, 1)
            moved = jnp.where(lane < width - shift, moved, 0.0)
        else:
            moved = pltpu.roll(values, shift, 1)
            moved = jnp.where(lane >= shift, moved, 0.0)
        values = values + power * moved
        power = power * power
        shift *= 2
    return values


def forward_kernel(
    tok, wq, wk, wv, wo, wup, wdn, s_in, s_out, fg, fb, skip, sg, sb, decay,
    wall, wdpre, sio_all, rnd_o, q_o, k_o, v_o, att_o, res_o, sec_o, p_o, u_o, st_o,
    tok_s, rnd_s, w_s, q_s, k_s, v_s, att_s, res_s, sec_s, pbuf, nctx, sio_s,
    own_s, sio_own, loc, rs, rr, ss, sr, cs, cr, xs, xr, outs, psem, ds, dr,
):
    net = Net()
    rep, core = net.rep, net.core
    rows_of = 64
    width = 1024

    def block(shard):
        return pl.ds(pl.multiple_of(shard * rows_of, rows_of), rows_of)

    mine = block(net.shard)
    own = [wq, wk, wv, wo]
    copies = [pltpu.make_async_copy(own[i], own_s.at[i], loc.at[i]) for i in range(4)]
    copies += [
        pltpu.make_async_copy(wup.at[:, pl.ds(i * width, width)], own_s.at[4 + i], loc.at[4 + i])
        for i in range(4)
    ]
    small = pltpu.make_async_copy(sio_own, sio_all.at[mine], loc.at[8])
    arrive = pltpu.make_async_copy(tok, tok_s, loc.at[9])
    for copy in copies:
        copy.start()
    arrive.start()
    packed = jnp.concatenate(
        [s_in[...].astype(F32), s_out[...].astype(F32), jnp.zeros((96, rows_of), F32)], axis=0
    )
    sio_own[...] = packed.T.astype(BF16)
    small.start()
    net.greet()
    for copy in copies:
        copy.wait()

    def piece(slot):
        if isinstance(slot, int) and slot < 2:
            return 1 if slot else 2 * rep
        later = slot - 2
        return 3 + later + (1 + 3 * rep) * ((3 - later) // 3) - (later % 2) * (3 - later) // 2

    def ring(slot, way, hop, which, where):
        ref = wall.at[which, where]
        sems = rs.at[slot, way, hop], rr.at[slot, way, hop]
        return rcopy(ref, ref, *sems, net.along(1 - 2 * way))

    def ring_own(slot, way):
        which = piece(slot)
        sems = rs.at[slot, way, 0], rr.at[slot, way, 0]
        ref = wall.at[which, mine]
        rcopy(own_s.at[which], ref, *sems, net.along(1 - 2 * way)).start()

    def ring_small(way, hop, where):
        ref = sio_all.at[where]
        return rcopy(ref, ref, ss.at[way, hop], sr.at[way, hop], net.along(1 - 2 * way))

    def mate(which, index, where):
        ref = wall.at[which, where]
        return rcopy(ref, ref, cs.at[which, index], cr.at[which, index], net.mate)

    def mate_small(index, where):
        ref = sio_all.at[where]
        return rcopy(ref, ref, cs.at[8, index], cr.at[8, index], net.mate)

    def twin(turn, index, which, where):
        ref = wall.at[which, where]
        return rcopy(ref, ref, xs.at[turn, index], xr.at[turn, index], net.twin)

    hand = rcopy(wdn, wdpre.at[0], ds.at[0], dr.at[0], net.along(1))
    hand_on = rcopy(wdpre.at[0], wdpre.at[1], ds.at[1], dr.at[1], net.mate)

    def source(way, hop):
        return block(net.at((2 * way - 1) * (hop + 1), core))

    def serve(slot, way, hop):
        which = piece(slot)
        where = source(way, hop)
        ring(slot, way, hop, which, where).wait_recv()

        @pl.when(hop < 3 - way)
        def _():
            ring(slot, way, hop + 1, which, where).start()

        mate(which, 1 + 2 * hop + way, where).start()

    def serve_out(slot, turn, way, hop):
        twin(turn, 2 * hop + way, piece(slot), source(way, hop)).start()

    def serve_in(turn, way, hop):
        where = source(way, hop)
        which = 2 * (1 - rep) if turn == 0 else 7 - 3 * rep
        twin(turn, 2 * hop + way, which, where).wait_recv()
        mate(which, 1 + 2 * hop + way, where).start()

    for slot in range(2):
        for way in range(2):
            ring_own(slot, way)
    small.wait()
    for way in range(2):
        ring_small(way, 0, mine).start()
    mate_small(0, mine).start()
    for which in range(8):
        rcopy(own_s.at[which], wall.at[which, mine], cs.at[which, 0], cr.at[which, 0], net.mate).start()
    keep = [pltpu.make_async_copy(own_s.at[i], wall.at[i, mine], loc.at[i]) for i in range(8)]
    for copy in keep:
        copy.start()
    arrive.wait()

    def first_norm(at):
        rows = pl.ds(pl.multiple_of(at * 128, 128), 128)
        xhat, _ = norm_parts(tok_s[rows, :].astype(F32))
        normed = xhat * fg[...] + fb[...]
        rnd_s[rows, :] = normed.astype(BF16)

    order = [
        (hop, slot, way) for hop in range(4) for slot in range(2) for way in range(2) if hop < 4 - way
    ]
    owed = []
    for n, (hop, slot, way) in enumerate(order):
        if n % 2 == 0:
            first_norm(n // 2)
        serve(slot, way, hop)
        if slot == 0:
            serve_out(0, 0, way, hop)
            owed.append((n, way, hop))
        else:
            where = source(way, hop)
            ring_small(way, hop, where).wait_recv()
            if hop < 3 - way:
                ring_small(way, hop + 1, where).start()
            mate_small(1 + 2 * hop + way, where).start()
        if n in (10, 12):
            for later in range(2):
                for each in range(2):
                    ring_own(n - 8 + later, each)
        if owed and n - owed[0][0] >= 6:
            serve_in(0, *owed.pop(0)[1:])
    first_norm(7)
    for each in owed:
        serve_in(0, *each[1:])

    def event(m):
        half, place = m // 14, m % 14
        late = place // 12
        hop = place // 4
        index = ((place % 4) // 2) * (1 - late) + (place - 12) * late
        way = (place % 2) * (1 - late)
        slot = 2 + 2 * half + index
        serve(slot, way, hop)

        @pl.when(slot == 2)
        def _():
            serve_out(2, 1, way, hop)

        @pl.when(m == 10)
        def _():
            hand.start()

        @pl.when((m >= 8) & (m <= 20) & (m % 4 < 2))
        def _():
            serve_in(1, m % 2, (m - 8) // 4)

    xhat, _ = norm_parts(tok_s[pl.ds(BLK - CTX, CTX), :].astype(F32))
    nctx[...] = xhat * fg[...] + fb[...]

    @pl.loop(0, NC)
    def _(index):
        where = block(0)
        mate_small(index, where).wait_recv()
        for which in range(3):
            mate(which, index, where).wait_recv()

    for copy in keep:
        copy.wait()
    loads = [pltpu.make_async_copy(sio_all, sio_s, loc.at[8])]
    loads += [pltpu.make_async_copy(wall.at[i], w_s.at[i], loc.at[i]) for i in range(3)]
    for copy in loads:
        copy.start()
    loads[0].wait()
    u_all = lax.dot_general(
        sio_s[...], rnd_s[pl.ds(0, BLK), :], (((0,), (1,)), ((), ())), preferred_element_type=F32
    )
    factor = jnp.exp(-column(decay[...]))
    raw = u_all[0:16, :]
    u_o[...] = raw
    states = lane_scan(raw * jnp.sqrt(1.0 - factor * factor), factor, False)
    st_o[...] = states
    tail = states[:, BLK - CTX :]
    padded = jnp.concatenate(
        [jnp.zeros((16, CTX), F32), tail, jnp.zeros((96, CTX), F32)], axis=0
    )
    made = split_dot(
        lambda a, b: lax.dot_general(a, b, (((0,), (1,)), ((), ())), preferred_element_type=F32),
        padded, sio_s[...], 3,
    )
    rnd_s[pl.ds(1024, CTX), :] = (made + skip[...] * nctx[...]).astype(BF16)
    finals = [pltpu.make_async_copy(rnd_s, rnd_o, outs.at[0])]
    finals[0].start()

    for copy in loads[1:]:
        copy.wait()

    @pl.loop(0, 4)
    def _(at):
        cols = pl.ds(pl.multiple_of(at * 256, 256), 256)
        q_s[:, cols] = dot_nn(rnd_s[pl.ds(0, 1024), :], w_s[0, :, cols]).astype(BF16)
        event(2 * at)
        k_s[:, cols] = dot_nn(rnd_s[...], w_s[1, :, cols]).astype(BF16)
        v_s[:, cols] = dot_nn(rnd_s[...], w_s[2, :, cols]).astype(BF16)
        event(2 * at + 1)

    for i, (a, b) in enumerate(((q_s, q_o), (k_s, k_o), (v_s, v_o))):
        finals.append(pltpu.make_async_copy(a, b, outs.at[1 + i]))
        finals[-1].start()

    for half in range(2):
        pbuf[half] = jnp.zeros((BLK, CTX + BLK), BF16)

    def p_copy(slot, at):
        return pltpu.make_async_copy(pbuf.at[slot], p_o.at[at], psem.at[slot])

    for b in range(NBLK):

        @pl.loop(0, 8)
        def _(h, b=b):
            cols = pl.ds(pl.multiple_of(h * DH, DH), DH)
            slot = h % 2
            if b == 0:

                @pl.when(h >= 2)
                def _():
                    p_copy(slot, h).wait()
            else:
                p_copy(slot, h).wait()
            for i in range(2):
                span = (i + 1) * 256
                rows = pl.ds(b * BLK + i * 256, 256)
                queries = q_s[rows, cols]
                scores = dot_nt(queries, k_s[pl.ds(b * BLK, span), cols]) * SCALE
                ahead = lax.broadcasted_iota(jnp.int32, scores.shape, 0) + i * 256
                scores = jnp.where(
                    ahead >= lax.broadcasted_iota(jnp.int32, scores.shape, 1), scores, NEG
                )
                top = jnp.max(scores, axis=-1, keepdims=True)
                if b:
                    before = dot_nt(queries, k_s[pl.ds(1024, CTX), cols]) * SCALE
                    top = jnp.maximum(top, jnp.max(before, axis=-1, keepdims=True))
                expos = jnp.exp(scores - top)
                total = jnp.sum(expos, axis=-1, keepdims=True)
                if b:
                    expos_before = jnp.exp(before - top)
                    total = total + jnp.sum(expos_before, axis=-1, keepdims=True)
                share = 1.0 / total
                weights = (expos * share).astype(BF16)
                mixed = dot_nn(weights, v_s[pl.ds(b * BLK, span), cols])
                pbuf[slot, pl.ds(i * 256, 256), pl.ds(CTX, span)] = weights
                if b:
                    weights = (expos_before * share).astype(BF16)
                    mixed = mixed + dot_nn(weights, v_s[pl.ds(1024, CTX), cols])
                    pbuf[slot, pl.ds(i * 256, 256), pl.ds(0, CTX)] = weights
                att_s[rows, cols] = mixed.astype(BF16)
            p_copy(slot, b * 8 + h).start()

            event(8 + 8 * b + h)

    finals.append(pltpu.make_async_copy(att_s, att_o, outs.at[4]))
    finals[-1].start()

    @pl.loop(0, NC)
    def _(index):
        mate(3, index, block(0)).wait_recv()

    load = pltpu.make_async_copy(wall.at[3], w_s.at[3], loc.at[3])
    load.start()
    load.wait()

    @pl.loop(0, 4)
    def _(at):
        rows = pl.ds(pl.multiple_of(at * 256, 256), 256)
        residual = tok_s[rows, :].astype(F32) + dot_nn(att_s[rows, :], w_s[3])
        res_s[rows, :] = residual
        xhat, _ = norm_parts(residual)
        sec_s[rows, :] = (xhat * sg[...] + sb[...]).astype(BF16)
        pltpu.make_async_copy(res_s.at[rows], res_o.at[rows], outs.at[5 + at]).start()
        pltpu.make_async_copy(sec_s.at[rows], sec_o.at[rows], outs.at[9 + at]).start()
        event(24 + at)

        @pl.when(at == 0)
        def _():
            hand.wait_recv()
            hand_on.start()

    for copy in finals:
        copy.wait()
    for at in range(4):
        rows = pl.ds(at * 256, 256)
        pltpu.make_async_copy(res_s.at[rows], res_o.at[rows], outs.at[5 + at]).wait()
        pltpu.make_async_copy(sec_s.at[rows], sec_o.at[rows], outs.at[9 + at]).wait()
    for slot in range(2):
        p_copy(slot, slot).wait()

    hand.wait_send()
    hand_on.wait()

    @pl.loop(0, NC)
    def _(index):
        for which in range(4, 8):
            mate(which, index, block(0)).wait_recv()
        for which in range(8):
            mate(which, index, block(0)).wait_send()
        mate_small(index, block(0)).wait_send()

    @pl.loop(0, NC - 1)
    def _(index):
        hop = index // 2
        way = index % 2
        for slot in range(6):
            ring(slot, way, hop, 0, block(0)).wait_send()
        ring_small(way, hop, block(0)).wait_send()
        for turn in range(2):
            twin(turn, index, 0, block(0)).wait_send()


def column(row):
    wide = jnp.broadcast_to(row, (16, 16))
    same = lax.broadcasted_iota(jnp.int32, (16, 16), 0) == lax.broadcasted_iota(jnp.int32, (16, 16), 1)
    return jnp.sum(jnp.where(same, wide, 0.0), axis=1, keepdims=True)


def any_spec(n):
    return [pl.BlockSpec(memory_space=pl.ANY)] * n


def vmem_spec(n):
    return [pl.BlockSpec(memory_space=pltpu.VMEM)] * n


def run_forward(tok, wq, wk, wv, wo, wup, wdn, s_in, s_out, fg, fb, skip, sg, sb, decay):
    shape = jax.ShapeDtypeStruct
    dma = pltpu.SemaphoreType.DMA
    big = (1024, 1024)
    ext = (1024 + CTX, 1024)
    return pl.pallas_call(
        forward_kernel,
        name="forward_part",
        out_shape=(
            shape((8,) + big, BF16), shape((2, 256, 1024), BF16), shape((1024, 128), BF16),
            shape(ext, BF16), shape(big, BF16),
            shape(ext, BF16), shape(ext, BF16), shape(big, BF16), shape(big, F32),
            shape(big, BF16), shape((16, BLK, CTX + BLK), BF16), shape((16, BLK), F32),
            shape((16, BLK), F32),
        ),
        in_specs=any_spec(7) + vmem_spec(8),
        out_specs=any_spec(11) + vmem_spec(2),
        scratch_shapes=[
            pltpu.VMEM(big, BF16), pltpu.VMEM(ext, BF16), pltpu.VMEM((4,) + big, BF16),
            pltpu.VMEM(big, BF16), pltpu.VMEM(ext, BF16), pltpu.VMEM(ext, BF16),
            pltpu.VMEM(big, BF16), pltpu.VMEM(big, F32), pltpu.VMEM(big, BF16),
            pltpu.VMEM((2, BLK, CTX + BLK), BF16), pltpu.VMEM((CTX, 1024), F32),
            pltpu.VMEM((1024, 128), BF16),
            pltpu.VMEM((8, 64, 1024), BF16), pltpu.VMEM((64, 128), BF16),
            dma((10,)), dma((6, 2, 4)), dma((6, 2, 4)), dma((2, 4)), dma((2, 4)),
            dma((9, NC)), dma((9, NC)), dma((2, NC - 1)), dma((2, NC - 1)), dma((13,)), dma((2,)), dma((2,)), dma((2,)),
        ],
        compiler_params=pltpu.CompilerParams(
            collective_id=0, has_side_effects=True, vmem_limit_bytes=VMEM_LIMIT
        ),
    )(tok, wq, wk, wv, wo, wup, wdn, s_in, s_out, fg, fb, skip, sg, sb, decay)


GELU_C = math.sqrt(2.0 / math.pi)
GELU_A = 0.044715


def feed_kernel(
    sec, res, wall, wdn, wdpre, cot, live, upb, dnb, sg,
    out_o, gatt_o, dwown_o, dwmate_o, fin_o, gdb_o, gub_o, gsg_o, gsb_o,
    sec_s, gb_s, wup_s, wd_s, br_s, gs_s, act_s, gh_s, a_s, b_s, prec, rrec, rsend, xsend, xrec,
    dwup_s, own_s, res_s,
    loc, ars, arr, axs, axr, cas, car, cxs, cxr, ps, pr, rs, rr, xs, xr, outs, dsem, dms, dmr,
):
    net = Net()
    rep, core = net.rep, net.core
    rows_of = 256
    ring_rows = 192
    part = 64
    ahead, behind = net.along(1), net.along(-1)

    def ring_part(shard, j, first=rep):
        return pl.ds(pl.multiple_of(shard * rows_of + (first + j) * part, part), part)

    def sole_part(shard, of):
        return pl.ds(pl.multiple_of(shard * rows_of + 3 * of * part, part), part)

    def block(shard):
        return pl.ds(pl.multiple_of(shard * rows_of, rows_of), rows_of)

    def mine_at(step):
        return net.at(-(step + 1), core)

    def other_at(step):
        return net.at(step + 1, 1 - core)

    loads = [
        pltpu.make_async_copy(wdn, own_s, loc.at[0]),
        pltpu.make_async_copy(sec, sec_s, loc.at[1]),
        pltpu.make_async_copy(cot, gb_s, loc.at[2]),
        pltpu.make_async_copy(wdpre.at[0], wd_s.at[block(mine_at(0))], loc.at[7]),
        pltpu.make_async_copy(wdpre.at[1], wd_s.at[block(other_at(0))], loc.at[8]),
    ]
    loads += [pltpu.make_async_copy(wall.at[4 + i], wup_s.at[i], loc.at[3 + i]) for i in range(4)]
    for load in loads:
        load.start()
    net.greet()
    loads[0].wait()
    loads[3].wait()

    def gather(j, hop, shard):
        ref = wd_s.at[ring_part(shard, j)]
        return rcopy(ref, ref, ars.at[j, hop], arr.at[j, hop], ahead)

    def gather_twin(hop, shard, of):
        ref = wd_s.at[sole_part(shard, of)]
        return rcopy(ref, ref, axs.at[hop], axr.at[hop], net.twin)

    def mate_ring(j, index, shard):
        ref = wd_s.at[ring_part(shard, j)]
        return rcopy(ref, ref, cas.at[j, index], car.at[j, index], net.mate)

    def mate_sole(index, shard, of):
        ref = wd_s.at[sole_part(shard, of)]
        return rcopy(ref, ref, cxs.at[index], cxr.at[index], net.mate)

    here = net.shard
    sole_own = own_s.at[pl.ds(pl.multiple_of(3 * (1 - rep) * part, part), part)]
    for j in range(3):
        ring_own = own_s.at[pl.ds(pl.multiple_of((rep + j) * part, part), part)]
        target = wd_s.at[ring_part(here, j)]
        gather(j, 1, mine_at(0)).start()
        rcopy(ring_own, target, cas.at[j, 0], car.at[j, 0], net.mate).start()
    rcopy(sole_own, wd_s.at[sole_part(here, 1 - rep)], cxs.at[0], cxr.at[0], net.mate).start()

    def serve(j, hop):
        shard = mine_at(hop)
        gather(j, hop, shard).wait_recv()

        @pl.when(hop < NC - 2)
        def _():
            gather(j, hop + 1, shard).start()

        @pl.when(j == 2 * rep)
        def _():
            gather_twin(hop, shard, rep).start()

        mate_ring(j, hop + 1, shard).start()

    def serve_twin(hop):
        shard = mine_at(hop)
        gather_twin(hop, shard, 1 - rep).wait_recv()
        mate_sole(hop + 1, shard, 1 - rep).start()

    for load in loads[1:3]:
        load.wait()

    wd_s[block(here), :] = own_s[...]

    @pl.loop(0, 4)
    def _(at):
        rows = pl.ds(pl.multiple_of(at * 256, 256), 256)
        when = lax.broadcasted_iota(jnp.int32, (256, 1024), 0) + at * 256
        kept = jnp.where(when < live[0], gb_s[rows, :].astype(F32), 0.0)
        gb_s[rows, :] = kept.astype(BF16)
        added = jnp.sum(kept, axis=0, keepdims=True)
        gdb_o[...] = jnp.where(at == 0, added, gdb_o[...] + added)
        br_s[rows, :] = jnp.zeros((256, 1024), F32)
        gs_s[rows, :] = jnp.zeros((256, 1024), F32)

    for load in loads[4:]:
        load.wait()

    def to_mate(step):
        slot = step % 2
        return rcopy(b_s.at[slot], prec.at[step], ps.at[step], pr.at[step], net.mate)

    def to_ring(j, step):
        return rcopy(rsend.at[step % 2, j], rrec.at[step, j], rs.at[step, j], rr.at[step, j], ahead)

    def to_twin(step):
        return rcopy(xsend.at[step % 2], xrec.at[step], xs.at[step], xr.at[step], net.twin)

    def dwup_at(target, shard):
        cols = pl.ds(pl.multiple_of((shard % 4) * 256, 256), 256)
        return target.at[shard // 4, :, :, cols]

    def dwup_copy(slot, half, shard):
        return pltpu.make_async_copy(
            dwup_s.at[slot, half, :, core], dwup_at(dwown_o, shard), dsem.at[slot, half]
        )

    def dwup_mate(step, half, shard):
        return rcopy(
            dwup_s.at[step % 2, half, :, 1 - core], dwup_at(dwmate_o, shard),
            dms.at[step, half], dmr.at[step, half], net.mate,
        )

    ring_local = pl.ds(pl.multiple_of(rep * part, part), ring_rows)
    sole_mine = pl.ds(pl.multiple_of(3 * rep * part, part), part)
    sole_theirs = pl.ds(pl.multiple_of(3 * (1 - rep) * part, part), part)

    def combine(step):
        slot = step % 2
        to_mate(step).wait_recv()
        a_s[slot] = a_s[slot] + prec[step].astype(F32)

        @pl.when(step >= 2)
        def _():
            to_twin(step - 2).wait_send()

        xsend[slot] = a_s[slot, sole_theirs, :].astype(BF16)
        to_twin(step).start()

    def forward(j, step):
        slot = step % 2
        rows = pl.ds(pl.multiple_of((rep + j) * part, part), part)

        @pl.when(j == 2 * rep)
        def _():
            to_twin(step).wait_recv()
            a_s[slot, rows, :] = a_s[slot, rows, :] + xrec[step].astype(F32)

        @pl.when(step >= 1)
        def _():
            to_ring(j, step - 1).wait_recv()
            a_s[slot, rows, :] = a_s[slot, rows, :] + rrec[step - 1, j].astype(F32)

        @pl.when((step >= 2) & (step < NC - 1))
        def _():
            to_ring(j, step - 2).wait_send()

        @pl.when(step < NC - 1)
        def _():
            rsend[slot, j] = a_s[slot, rows, :].astype(BF16)
            to_ring(j, step).start()

    @pl.loop(0, NC)
    def _(step):
        slot = step % 2
        a, b = mine_at(step), other_at(step)
        index = (step + 1) % NC

        @pl.when(step >= 1)
        def _():
            combine(step - 1)

        def up(shard):
            cols = pl.ds(pl.multiple_of((shard % 4) * 256, 256), 256)
            return wup_s[shard // 4, :, cols]

        def bias(shard):
            return upb[:, pl.ds(pl.multiple_of(shard * 256, 256), 256)]

        def middle(half, shard, at):
            for block_at in range(2):
                rows = pl.ds(pl.multiple_of(at * 512 + block_at * 256, 256), 256)
                cols = pl.ds(half * 256, 256)
                hidden = dot_nn(sec_s[rows, :], up(shard)) + bias(shard)
                grad = dot_nt(gb_s[rows, :], wd_s[block(shard), :])
                square = hidden * hidden
                bent = jnp.tanh(hidden * (GELU_C + (GELU_C * GELU_A) * square))
                half_up = 0.5 + 0.5 * bent
                act_s[rows, cols] = (hidden * half_up).astype(BF16)
                slope = half_up + (0.5 * hidden) * (1.0 - bent * bent) * (
                    GELU_C + (3.0 * GELU_C * GELU_A) * square
                )
                gh_s[rows, cols] = (grad * slope).astype(BF16)

        @pl.loop(0, 2)
        def _(at):
            middle(0, a, at)

        @pl.when(step < NC - 2)
        def _():
            serve(2 * rep, step + 1)

        @pl.when(step >= 1)
        def _():
            for j in range(3):
                mate_ring(j, index, b).wait_recv()
            mate_sole(index, b, 1 - rep).wait_recv()

        @pl.loop(0, 2)
        def _(at):
            middle(1, b, at)

            @pl.when(step < NC - 2)
            def _():
                serve((2 * rep + 1 + at) % 3, step + 1)

        made = dot_tn(act_s[...], gb_s[...])

        @pl.when(step >= 2)
        def _():
            to_mate(step - 2).wait_send()

        a_s[slot] = made[0:256]
        b_s[slot] = made[256:512].astype(BF16)
        to_mate(step).start()

        rise_up = dot_tn(sec_s[...], gh_s[...]).astype(BF16)
        for half, shard in enumerate((a, b)):
            cols = pl.ds(pl.multiple_of(shard * 256, 256), 256)
            gub_o[:, cols] = jnp.sum(
                gh_s[:, half * 256 : half * 256 + 256].astype(F32), axis=0, keepdims=True
            )

            @pl.when(step >= 2)
            def _(half=half, shard=shard):
                dwup_copy(slot, half, shard).wait()
                dwup_mate(step - 2, half, shard).wait_send()

            dwup_s[slot, half] = rise_up[:, half * 256 : half * 256 + 256].reshape(NC, 2, 64, 256)
            dwup_copy(slot, half, shard).start()
            dwup_mate(step, half, shard).start()

        @pl.loop(0, 4)
        def _(at):
            rows = pl.ds(pl.multiple_of(at * 256, 256), 256)
            down = jnp.concatenate([wd_s[block(a), :], wd_s[block(b), :]], axis=0)
            br_s[rows, :] = br_s[rows, :] + dot_nn(act_s[rows, :], down)
            rise = jnp.concatenate([up(a), up(b)], axis=1)
            gs_s[rows, :] = gs_s[rows, :] + dot_nt(gh_s[rows, :], rise)

            @pl.when((at < 3) & (step >= 1))
            def _():
                forward((2 * rep + 1 + at) % 3, step - 1)

            @pl.when((at == 1) & (step < NC - 2))
            def _():
                serve_twin(step + 1)

    def residual_in(at):
        rows = pl.ds(at * 256, 256)
        return pltpu.make_async_copy(res.at[rows], res_s.at[rows], loc.at[at])

    for at in range(4):
        residual_in(at).start()
    combine(NC - 1)

    def leave(at, which):
        rows = pl.ds(pl.multiple_of(at * 256, 256), 256)
        source = (sec_s, gb_s)[which]
        return pltpu.make_async_copy(
            source.at[rows], (out_o, gatt_o)[which].at[rows], outs.at[which, at]
        )

    @pl.loop(0, 4)
    def _(at):
        residual_in(at).wait()
        rows = pl.ds(pl.multiple_of(at * 256, 256), 256)
        kept = res_s[rows, :]
        when = lax.broadcasted_iota(jnp.int32, (256, 1024), 0) + at * 256
        total = kept + br_s[rows, :] + dnb[...]
        sec_s[rows, :] = jnp.where(when < live[0], total, 0.0).astype(BF16)
        xhat, inverse = norm_parts(kept)
        grad = gs_s[rows, :]
        gain = jnp.sum(grad * xhat, axis=0, keepdims=True)
        shift = jnp.sum(grad, axis=0, keepdims=True)
        gsg_o[...] = jnp.where(at == 0, gain, gsg_o[...] + gain)
        gsb_o[...] = jnp.where(at == 0, shift, gsb_o[...] + shift)
        grad = grad * sg[...]
        grad = grad - jnp.mean(grad, axis=-1, keepdims=True) - xhat * jnp.mean(
            grad * xhat, axis=-1, keepdims=True
        )
        gb_s[rows, :] = (gb_s[rows, :].astype(F32) + inverse * grad).astype(BF16)
        for which in range(2):
            leave(at, which).start()

    for j in range(3):
        forward((2 * rep + 1 + j) % 3, NC - 1)
    last = (NC - 1) % 2
    fin_o[...] = a_s[last, ring_local, :].astype(BF16)

    @pl.loop(1, NC - 1)
    def _(hop):
        for j in range(3):
            gather(j, hop, 0).wait_send()
        gather_twin(hop, 0, 0).wait_send()

    @pl.loop(1, NC)
    def _(later):
        index = (later + 1) % NC
        for j in range(3):
            mate_ring(j, index, 0).wait_send()
        mate_sole(index, 0, 0).wait_send()

    for step in range(NC - 2, NC):
        to_mate(step).wait_send()
        to_twin(step).wait_send()
        for j in range(3):
            to_ring(j, step - 1).wait_send()
        for half in range(2):
            dwup_copy(step % 2, half, 0).wait()
            dwup_mate(step, half, 0).wait_send()
    for at in range(4):
        for which in range(2):
            leave(at, which).wait()

    @pl.loop(0, NC)
    def _(step):
        for half in range(2):
            dwup_mate(step, half, 0).wait_recv()


def run_feed(sec, res, wall, wdn, wdpre, cot, live, upb, dnb, sg):
    shape = jax.ShapeDtypeStruct
    dma = pltpu.SemaphoreType.DMA
    vmem = pltpu.VMEM
    big = (1024, 1024)
    return pl.pallas_call(
        feed_kernel,
        name="feed_part",
        out_shape=(
            shape(big, BF16), shape(big, BF16), shape((4, NC, 64, 1024), BF16),
            shape((4, NC, 64, 1024), BF16), shape((192, 1024), BF16), shape((1, 1024), F32), shape((1, 4096), F32),
            shape((1, 1024), F32), shape((1, 1024), F32),
        ),
        in_specs=any_spec(6) + [pl.BlockSpec(memory_space=pltpu.SMEM)] + vmem_spec(3),
        out_specs=any_spec(4) + vmem_spec(5),
        scratch_shapes=[
            vmem(big, BF16), vmem(big, BF16), vmem((4,) + big, BF16), vmem((4096, 1024), BF16),
            vmem(big, F32), vmem(big, F32), vmem((1024, 512), BF16), vmem((1024, 512), BF16),
            vmem((2, 256, 1024), F32), vmem((2, 256, 1024), BF16), vmem((NC, 256, 1024), BF16),
            vmem((NC - 1, 3, 64, 1024), BF16), vmem((2, 3, 64, 1024), BF16), vmem((2, 64, 1024), BF16),
            vmem((NC, 64, 1024), BF16),
            vmem((2, 2, NC, 2, 64, 256), BF16), vmem((256, 1024), BF16), vmem(big, F32),
            dma((9,)), dma((3, NC - 1)), dma((3, NC - 1)), dma((NC - 1,)), dma((NC - 1,)),
            dma((3, NC)), dma((3, NC)), dma((NC,)), dma((NC,)), dma((NC,)), dma((NC,)),
            dma((NC - 1, 3)), dma((NC - 1, 3)), dma((NC,)), dma((NC,)),
            dma((2, 4)), dma((2, 2)), dma((NC, 2)), dma((NC, 2)),
        ],
        compiler_params=pltpu.CompilerParams(
            collective_id=1, has_side_effects=True, vmem_limit_bytes=VMEM_LIMIT
        ),
    )(sec, res, wall, wdn, wdpre, cot, live, upb, dnb, sg)


def backward_kernel(
    dwown, dwmate, find, gatt, att, wall, q, kx, vx, rnd, p, tok, sio, u_in, st_in, fg, fb, skip, decay,
    gsg, gsb, gdb, gub,
    gtok_o, findr_o, fin_b, finr_b, fin_g, finr_g, sums_o,
    own_b, prec_b, rrec_b, xrec_b, acc_b,
    own_g, prec_g, rrec_g, xrec_g, acc_g, go_s,
    gatt_s, wo_s, att_s, ga_s, q_s, k_s, v_s, rnd_s, dk_s, dv_s, pbuf, ds_s, gres_s, nb_s,
    sio_s, gd_s, gctx_s, sum_s, got_s, part_s,
    loc, psem, gsem, osem, mbs, mbr, mgs, mgr, rbs, rbr, rgs, rgr, xbs, xbr, xgs, xgr,
    fbs, fbr, fgs, fgr, ts, tr, us, ur, ds, dr,
):
    net = Net()
    rep, core = net.rep, net.core
    theirs = 1 - core

    loads = [
        pltpu.make_async_copy(gatt, gatt_s, loc.at[0]),
        pltpu.make_async_copy(wall.at[3], wo_s, loc.at[1]),
        pltpu.make_async_copy(att, att_s, loc.at[2]),
        pltpu.make_async_copy(q, q_s, loc.at[3]),
        pltpu.make_async_copy(kx, k_s, loc.at[4]),
        pltpu.make_async_copy(vx, v_s, loc.at[5]),
        pltpu.make_async_copy(rnd, rnd_s, loc.at[6]),
        pltpu.make_async_copy(sio, sio_s, loc.at[7]),
    ]
    rises = [
        pltpu.make_async_copy(dwown, own_b.at[pl.ds(0, 4)], loc.at[8]),
        pltpu.make_async_copy(dwmate, prec_b.at[pl.ds(0, 4)], loc.at[9]),
    ]
    for copy in rises:
        copy.start()
    for copy in loads:
        copy.start()
    fin_b[...] = jnp.zeros(fin_b.shape, BF16)
    finr_b[...] = jnp.zeros(finr_b.shape, BF16)
    fin_g[...] = jnp.zeros(fin_g.shape, BF16)
    finr_g[...] = jnp.zeros(finr_g.shape, BF16)
    barrier = pltpu.get_barrier_semaphore()
    me = rep * (2 * NC) + net.shard

    def device(away):
        other = (me + away) % (4 * NC)
        return other, (other // (2 * NC), other % (2 * NC))

    @pl.loop(1, 4 * NC)
    def _(away):
        pl.semaphore_signal(barrier, inc=1, device_id=device(away)[1], device_id_type=MESH)

    pl.semaphore_wait(barrier, 4 * NC - 1)

    mate_out = rcopy(go_s, prec_b.at[4], mbs.at[0], mbr.at[0], net.mate)

    def mate_group(g):
        return rcopy(own_g.at[g, :, theirs], prec_g.at[g], mgs.at[g], mgr.at[g], net.mate)

    swap = rcopy(find, findr_o, ds.at[0], dr.at[0], net.twin)
    swap.start()

    def chip_for(n):
        t, way = n // 2, n % 2
        hops = (4 - t) * (1 - way) + (t - 3) * way
        return chip_at((net.pos + net.step * hops + 4 * NC) % NC)

    class Stream:
        def __init__(self, own, prec, rrec, xrec, fin, finr, acc, sems):
            self.own, self.prec, self.rrec, self.xrec = own, prec, rrec, xrec
            self.fin, self.finr, self.acc = fin, finr, acc
            self.rs, self.rr, self.xs, self.xr, self.fs, self.fr = sems

        def ring(self, slot, which, n):
            source = self.prec.at[which, chip_for(n)]
            way = n % 2
            return rcopy(
                source, self.rrec.at[slot, n], self.rs.at[slot, n], self.rr.at[slot, n],
                net.along(1 - 2 * way),
            )

        def twin(self, which, n):
            chip = chip_for(n)
            return rcopy(
                self.prec.at[which, chip], self.xrec.at[chip], self.xs.at[n], self.xr.at[n], net.twin
            )

        def finish(self, which):
            return rcopy(
                self.fin.at[which], self.finr.at[which], self.fs.at[which], self.fr.at[which], net.twin
            )

        def give(self, which, n):
            chip = chip_for(n)
            self.prec[which, chip] = (
                self.own(which, chip).astype(F32) + self.prec[which, chip].astype(F32)
            ).astype(BF16)
            self.twin(which, n).start()

        def turn(self, slot, which, n, sole):
            chip = chip_for(n)
            self.acc[...] = self.own(which, chip).astype(F32) + self.prec[which, chip].astype(F32)

            @pl.when(sole)
            def _():
                self.twin(which, n).wait_recv()
                self.acc[...] = self.acc[...] + self.xrec[chip].astype(F32)

            @pl.when((n >= 2) & (n < 7))
            def _():
                self.ring(slot, which, n - 2).wait_recv()
                self.acc[...] = self.acc[...] + self.rrec[slot, n - 2].astype(F32)

            @pl.when(n < 7)
            def _():
                self.prec[which, chip] = self.acc[...].astype(BF16)
                self.ring(slot, which, n).start()

            @pl.when(n == 7)
            def _():
                self.ring(slot, which, 5).wait_recv()
                self.ring(slot, which, 6).wait_recv()
                total = self.acc[...] + self.rrec[slot, 5].astype(F32) + self.rrec[slot, 6].astype(F32)
                self.fin[which] = total.astype(BF16)
                self.finish(which).start()

    big = Stream(
        lambda which, chip: own_b[which, chip], prec_b, rrec_b, xrec_b, fin_b, finr_b, acc_b,
        (rbs, rbr, xbs, xbr, fbs, fbr),
    )
    group = Stream(
        lambda which, chip: own_g[which, chip, core], prec_g, rrec_g, xrec_g, fin_g, finr_g, acc_g,
        (rgs, rgr, xgs, xgr, fgs, fgr),
    )

    def tile(index):
        return (
            pl.ds(pl.multiple_of((index // 8) * 16, 16), 16),
            pl.ds(pl.multiple_of((index % 8) * 128, 128), 128),
        )

    def share(away):
        other, where = device(away)
        return rcopy(sum_s.at[tile(other)], got_s.at[away], ts.at[away], tr.at[away], where)

    def spread(away):
        return rcopy(part_s, sums_o.at[tile(me)], us.at[away], ur.at[away], device(away)[1])

    def each_device(act):
        for away in range(1, 4 * NC):
            act(away)

    def big_at(e):
        k, j = e // 4, e % 4
        n = k - 2 * (j // 2) - j // 3
        which = (j + 1) * (1 - j // 2) + (j // 2) * (3 * rep * (1 - j // 3) + 4 * (j // 3))

        @pl.when((j == 3) & (n == 0))
        def _():
            mate_out.wait_recv()

        @pl.when((n >= 0) & (n <= 7))
        def _():
            big.turn(j, which, n, j == 2)

    def group_at(e):
        k, j = e // 3, e % 3
        n = k - j // 2
        which = rep * (1 - (j + 1) // 2) + (j + 1) * ((j + 1) // 2)

        @pl.when((j >= 1) & (n == 0))
        def _():
            mate_group(which).wait_recv()

        @pl.when((n >= 0) & (n <= 7))
        def _():
            group.turn(j, which, n, j == 0)

    def run(at, low, high):
        @pl.loop(low, high)
        def _(e):
            at(e)

    for copy in rises:
        copy.wait()

    @pl.loop(0, NC)
    def _(n):
        big.give(3 * (1 - rep), n)

    run(big_at, 0, 4)
    for i in range(2):
        loads[i].wait()

    def p_copy(slot, at):
        return pltpu.make_async_copy(p.at[at], pbuf.at[slot], psem.at[slot])

    p_copy(0, 0).start()

    @pl.loop(0, 4)
    def _(at):
        rows = pl.ds(pl.multiple_of(at * 256, 256), 256)
        ga_s[rows, :] = dot_nt(gatt_s[rows, :], wo_s[...]).astype(BF16)

    run(big_at, 4, 8)
    loads[2].wait()

    @pl.loop(0, 4)
    def _(at):
        cols = pl.ds(pl.multiple_of(at * 256, 256), 256)
        made = dot_tn(att_s[...], gatt_s[:, cols]).reshape(NC, 2, 64, 256)
        own_b[4, :, :, cols] = jnp.where(core == 0, made[:, 0], made[:, 1]).astype(BF16)
        go_s[:, :, cols] = jnp.where(core == 0, made[:, 1], made[:, 0]).astype(BF16)

    mate_out.start()
    tok_load = pltpu.make_async_copy(tok, wo_s, loc.at[0])
    tok_load.start()
    for copy in loads[3:]:
        copy.wait()
    ds_s[...] = jnp.zeros(ds_s.shape, BF16)
    dq_s = gatt_s

    def weights_in(i):
        target = (q_s, k_s.at[pl.ds(0, 1024)], v_s.at[pl.ds(0, 1024)])[i]
        return pltpu.make_async_copy(wall.at[i], target, loc.at[1 + i])

    @pl.loop(0, 4)
    def _(g):
        for hh in range(2):
            for b in range(NBLK):
                i = 2 * hh + b
                m = 4 * g + i
                h = 2 * g + hh
                slot = i % 2
                cols = pl.ds(pl.multiple_of(h * DH, DH), DH)
                following = 2 * hh + b + 1
                nb, nh = following % 2, 2 * g + following // 2
                p_copy(slot, b * 8 + h).wait()
                if following < 4:
                    p_copy(1 - slot, nb * 8 + nh).start()
                else:

                    @pl.when(g < 3)
                    def _():
                        p_copy(1 - slot, nh).start()

                for part in range(2):
                    span = (part + 1) * 256
                    rows = pl.ds(b * BLK + part * 256, 256)
                    local = pl.ds(part * 256, 256)
                    grads = ga_s[rows, cols]
                    slope = dot_nt(grads, v_s[pl.ds(b * BLK, span), cols])
                    kept = pbuf[slot, local, pl.ds(CTX, span)].astype(F32)
                    both = jnp.sum(kept * slope, axis=-1, keepdims=True)
                    mass = jnp.sum(kept, axis=-1, keepdims=True)
                    if b:
                        slope_before = dot_nt(grads, v_s[pl.ds(1024, CTX), cols])
                        kept_before = pbuf[slot, local, pl.ds(0, CTX)].astype(F32)
                        both += jnp.sum(kept_before * slope_before, axis=-1, keepdims=True)
                        mass += jnp.sum(kept_before, axis=-1, keepdims=True)
                    both = both / mass
                    inner = (kept * (slope - both)).astype(BF16)
                    ds_s[local, pl.ds(CTX, span)] = inner
                    total = dot_nn(inner, k_s[pl.ds(b * BLK, span), cols])
                    if b:
                        inner = (kept_before * (slope_before - both)).astype(BF16)
                        ds_s[local, pl.ds(0, CTX)] = inner
                        total = total + dot_nn(inner, k_s[pl.ds(1024, CTX), cols])
                    dq_s[rows, cols] = (total * SCALE).astype(BF16)
                rows = pl.ds(b * BLK, BLK)
                first = 0 if b else CTX
                made_k = dot_tn(ds_s[:, first:], q_s[rows, cols]) * SCALE
                made_v = dot_tn(pbuf[slot, :, first:], ga_s[rows, cols])
                if b:
                    dk_s[pl.ds(1024, CTX), cols] = made_k[:CTX].astype(BF16)
                    dv_s[pl.ds(1024, CTX), cols] = made_v[:CTX].astype(BF16)
                    made_k, made_v = made_k[CTX:], made_v[CTX:]
                dk_s[rows, cols] = made_k.astype(BF16)
                dv_s[rows, cols] = made_v.astype(BF16)

                @pl.when(m < 15)
                def _(m=m):
                    run(big_at, 8 + (5 * m) // 2, 8 + (5 * m + 5) // 2)


                @pl.when(m == 9)
                def _():
                    for each in range(2):
                        mate_group(each).wait_recv()

                @pl.when((m >= 9) & (m < 13))
                def _(m=m):
                    for e in range(2):
                        group.give(1 - rep, 2 * (m - 9) + e)

        @pl.when(g == 3)
        def _():
            for i in range(3):
                weights_in(i).start()

        cols = pl.ds(pl.multiple_of(g * 256, 256), 256)
        own_g[g, :, :, :, 0:256] = dot_tn(rnd_s[0:1024, :], dq_s[:, cols]).astype(BF16).reshape(NC, 2, 64, 256)
        own_g[g, :, :, :, 256:512] = dot_tn(rnd_s[...], dk_s[:, cols]).astype(BF16).reshape(NC, 2, 64, 256)
        own_g[g, :, :, :, 512:768] = dot_tn(rnd_s[...], dv_s[:, cols]).astype(BF16).reshape(NC, 2, 64, 256)
        mate_group(g).start()

    run(group_at, 0, 3)
    for i in range(3):
        weights_in(i).wait()
    tok_load.wait()

    def gres_in(at):
        rows = pl.ds(pl.multiple_of(at * 256, 256), 256)
        return pltpu.make_async_copy(gatt.at[rows], gres_s.at[at % 2], gsem.at[at % 2])

    gres_in(0).start()

    after = pl.ds(1024, CTX)
    gctx = dot_nt(dk_s[after, :], k_s[0:1024, :]) + dot_nt(dv_s[after, :], v_s[0:1024, :])
    gctx_s[...] = gctx
    xhat, _ = norm_parts(wo_s[pl.ds(BLK - CTX, CTX), :].astype(F32))
    sum_s[32:48, :] = jnp.zeros((16, 1024), F32)
    sum_s[34:35, :] = jnp.sum(gctx * (xhat * fg[...] + fb[...]), axis=0, keepdims=True)
    for at, vector in ((35, gsg), (36, gsb), (37, gdb)):
        sum_s[at : at + 1, :] = vector[...]
    for at in range(4):
        sum_s[38 + at : 39 + at, :] = gub[:, at * 1024 : (at + 1) * 1024]
    run(group_at, 3, 6)
    states, raw = st_in[...], u_in[...]
    factor = jnp.exp(-column(decay[...]))
    scale = jnp.sqrt(1.0 - factor * factor)
    sum_s[16:32, :] = lax.dot_general(
        states[:, BLK - CTX :], gctx, (((1,), (0,)), ((), ())),
        preferred_element_type=F32, precision=lax.Precision.HIGHEST,
    )
    back = split_dot(
        lambda a, b: lax.dot_general(b, a, (((0,), (1,)), ((), ())), preferred_element_type=F32),
        gctx, sio_s[...], 3,
    )
    seeds = jnp.concatenate([jnp.zeros((16, BLK - CTX), F32), back[16:32, :]], axis=1)
    lam = lane_scan(seeds, factor, True)
    lane = lax.broadcasted_iota(jnp.int32, lam.shape, 1)
    earlier = jnp.where(lane >= 1, pltpu.roll(states, 1, 1), 0.0)
    rates = -factor * jnp.sum(lam * (earlier - (factor / scale) * raw), axis=1, keepdims=True)
    sum_s[48:64, :] = jnp.broadcast_to(rates, (16, 1024))
    driven = scale * lam
    sum_s[0:16, :] = split_dot(dot_nn, driven, rnd_s[0:BLK, :], 3)
    gd_s[...] = jnp.zeros(gd_s.shape, F32)
    gd_s[0:16, 0:BLK] = driven

    def add_in(away):
        share(away).wait_recv()
        part_s[...] = part_s[...] + got_s[away]

    def leave(at):
        rows = pl.ds(pl.multiple_of(at * 256, 256), 256)
        return pltpu.make_async_copy(rnd_s.at[rows], gtok_o.at[rows], osem.at[at])

    @pl.loop(0, 4)
    def _(at):
        rows = pl.ds(pl.multiple_of(at * 256, 256), 256)

        @pl.when(at < 3)
        def _():
            gres_in(at + 1).start()

        nb_s[...] = (
            dot_nt(dq_s[rows, :], q_s[...])
            + dot_nt(dk_s[rows, :], k_s[0:1024, :])
            + dot_nt(dv_s[rows, :], v_s[0:1024, :])
            + split_dot(
                lambda a, b: lax.dot_general(a, b, (((0,), (1,)), ((), ())), preferred_element_type=F32),
                gd_s[:, rows], sio_s[...], 3,
            )
        )

        @pl.when(at == 1)
        def _():
            half = pl.ds(128, CTX)
            nb_s[half, :] = nb_s[half, :] + skip[...] * gctx_s[...]

        run(group_at, 6 + 3 * at, 9 + 3 * at)

        xhat, inverse = norm_parts(wo_s[rows, :].astype(F32))
        grad = nb_s[...]
        gain = jnp.sum(grad * xhat, axis=0, keepdims=True)
        shift = jnp.sum(grad, axis=0, keepdims=True)
        sum_s[32:33, :] = sum_s[32:33, :] + gain
        sum_s[33:34, :] = sum_s[33:34, :] + shift
        grad = grad * fg[...]
        grad = grad - jnp.mean(grad, axis=-1, keepdims=True) - xhat * jnp.mean(
            grad * xhat, axis=-1, keepdims=True
        )
        gres_in(at).wait()
        rnd_s[rows, :] = (gres_s[at % 2].astype(F32) + inverse * grad).astype(BF16)
        leave(at).start()

    each_device(lambda away: share(away).start())
    part_s[...] = sum_s[tile(me)]
    run(group_at, 18, 21)
    each_device(add_in)
    each_device(lambda away: spread(away).start())
    sums_o[tile(me)] = part_s[...]
    run(group_at, 21, 27)

    for which in (3 * rep, 1, 2, 4):
        big.finish(which).wait_send()
    for which in (rep, 2, 3):
        group.finish(which).wait_send()
    twin_rise = 3 * (1 - rep)
    for which in (twin_rise, 1, 2, 4):
        big.finish(which).wait_recv()
    for which in (1 - rep, 2, 3):
        group.finish(which).wait_recv()
    def settle(away):
        spread(away).wait()
        share(away).wait_send()

    each_device(settle)
    for i in range(4):
        mate_group(i).wait_send()
        leave(i).wait()
    mate_out.wait_send()
    swap.wait()

    @pl.loop(0, NC)
    def _(n):
        big.twin(3 * (1 - rep), n).wait_send()
        group.twin(1 - rep, n).wait_send()

    @pl.loop(0, NC - 1)
    def _(n):
        for slot in range(4):
            big.ring(slot, 0, n).wait_send()
        for slot in range(3):
            group.ring(slot, 0, n).wait_send()


def run_backward(*operands):
    shape = jax.ShapeDtypeStruct
    dma = pltpu.SemaphoreType.DMA
    vmem = pltpu.VMEM
    full = (1024, 1024)
    ext = (1024 + CTX, 1024)
    part = (64, 1024)
    cut = (64, 768)
    return pl.pallas_call(
        backward_kernel,
        name="backward_part",
        out_shape=(
            shape(full, BF16), shape((192, 1024), BF16), shape((5,) + part, BF16), shape((5,) + part, BF16),
            shape((4,) + cut, BF16), shape((4,) + cut, BF16), shape((64, 1024), F32),
        ),
        in_specs=any_spec(13) + vmem_spec(10),
        out_specs=any_spec(2) + vmem_spec(5),
        scratch_shapes=[
            vmem((5, NC) + part, BF16), vmem((5, NC) + part, BF16), vmem((4, NC - 1) + part, BF16),
            vmem((NC,) + part, BF16), vmem(part, F32),
            vmem((4, NC, 2) + cut, BF16), vmem((4, NC) + cut, BF16), vmem((3, NC - 1) + cut, BF16),
            vmem((NC,) + cut, BF16), vmem(cut, F32),
            vmem((NC,) + part, BF16),
            vmem(full, BF16), vmem(full, BF16), vmem(full, BF16), vmem(full, BF16), vmem(full, BF16),
            vmem(ext, BF16), vmem(ext, BF16), vmem(ext, BF16), vmem(ext, BF16), vmem(ext, BF16),
            vmem((2, BLK, CTX + BLK), BF16), vmem((BLK, CTX + BLK), BF16), vmem((2, 256, 1024), BF16),
            vmem((256, 1024), F32), vmem((1024, 128), BF16), vmem((128, 1024), F32), vmem((CTX, 1024), F32), vmem((64, 1024), F32), vmem((4 * NC, 16, 128), F32), vmem((16, 128), F32),
            dma((10,)), dma((2,)), dma((2,)), dma((4,)), dma((1,)), dma((1,)), dma((4,)), dma((4,)),
            dma((4, NC - 1)), dma((4, NC - 1)), dma((3, NC - 1)), dma((3, NC - 1)),
            dma((NC,)), dma((NC,)), dma((NC,)), dma((NC,)), dma((5,)), dma((5,)), dma((4,)), dma((4,)),
            dma((4 * NC,)), dma((4 * NC,)), dma((4 * NC,)), dma((4 * NC,)), dma((1,)), dma((1,)),
        ],
        compiler_params=pltpu.CompilerParams(
            collective_id=2, has_side_effects=True, vmem_limit_bytes=VMEM_LIMIT
        ),
    )(*operands)


def outputs_kernel(
    finb, finrb, fing, finrg, find, findr, sums,
    dup_o, do_o, dq_o, dk_o, dv_o, ddown_o, gfg_o, gfb_o, gskip_o, gsg_o, gsb_o, gdb_o, gub_o, grate_o,
    gsi_o, gso_o,
):
    rep, shard = lax.axis_index("rep"), lax.axis_index("shard")
    for i in range(4):
        dup_o[:, i * 1024 : (i + 1) * 1024] = finb[i].astype(F32) + finrb[i].astype(F32)
    do_o[...] = finb[4].astype(F32) + finrb[4].astype(F32)
    for g in range(4):
        for i, out in enumerate((dq_o, dk_o, dv_o)):
            cols = slice(i * 256, (i + 1) * 256)
            out[:, g * 256 : (g + 1) * 256] = fing[g, :, cols].astype(F32) + finrg[g, :, cols].astype(F32)
    mine = pl.ds(pl.multiple_of(rep * 64, 64), 192)
    theirs = pl.ds(pl.multiple_of((1 - rep) * 64, 64), 192)
    ddown_o[...] = jnp.zeros((256, 1024), F32)
    ddown_o[mine, :] = find[...].astype(F32)
    ddown_o[theirs, :] = ddown_o[theirs, :] + findr[...].astype(F32)
    for at, out in enumerate((gfg_o, gfb_o, gskip_o, gsg_o, gsb_o, gdb_o)):
        out[...] = sums[32 + at : 33 + at, :]
    for at in range(4):
        gub_o[:, at * 1024 : (at + 1) * 1024] = sums[38 + at : 39 + at, :]
    same = lax.broadcasted_iota(jnp.int32, (16, 128), 0) == lax.broadcasted_iota(jnp.int32, (16, 128), 1)
    grate_o[...] = jnp.sum(jnp.where(same, sums[48:64, 0:128], 0.0), axis=0, keepdims=True)
    shift = (1024 - 64 * shard) % 1024
    gsi_o[...] = pltpu.roll(sums[0:16, :], shift, 1)[:, 0:64]
    gso_o[...] = pltpu.roll(sums[16:32, :], shift, 1)[:, 0:64]


def run_outputs(*operands):
    shape = jax.ShapeDtypeStruct
    row = shape((1, 1024), F32)
    part = shape((64, 1024), F32)
    return pl.pallas_call(
        outputs_kernel,
        name="outputs_part",
        out_shape=(
            shape((64, 4096), F32), part, part, part, part, shape((256, 1024), F32),
            row, row, row, row, row, row, shape((1, 4096), F32), shape((1, 128), F32),
            shape((16, 64), F32), shape((16, 64), F32),
        ),
        in_specs=vmem_spec(7),
        out_specs=vmem_spec(16),
        compiler_params=pltpu.CompilerParams(vmem_limit_bytes=VMEM_LIMIT),
    )(*operands)


def fused_device(
    tokens, lengths, first_gain, first_bias, decay_rates, state_in, state_out, skip_gain,
    query_weight, key_weight, value_weight, output_weight, second_gain, second_bias,
    up_weight, up_bias, down_weight, down_bias, cotangent,
):
    tok = tokens.reshape(1024, 1024)
    cot = cotangent.reshape(1024, 1024)
    fg, fb, skip, sg, sb, dnb, upb, decay = (
        v.reshape(1, -1)
        for v in (
            first_gain, first_bias, skip_gain, second_gain, second_bias, down_bias, up_bias, decay_rates,
        )
    )
    wall, wdpre, sio, rnd, q, kx, vx, att, res, sec, p, u, st = run_forward(
        tok, query_weight, key_weight, value_weight, output_weight, up_weight, down_weight, state_in, state_out,
        fg, fb, skip, sg, sb, decay,
    )
    result, gatt, dwown, dwmate, find, gdb, gub, gsg, gsb = run_feed(
        sec, res, wall, down_weight, wdpre, cot, lengths, upb, dnb, sg
    )
    gtok, findr, finb, finrb, fing, finrg, sums = run_backward(
        dwown, dwmate, find, gatt, att, wall, q, kx, vx, rnd, p, tok, sio,
        u, st, fg, fb, skip, decay, gsg, gsb, gdb, gub,
    )
    dup, do, dq, dk, dv, ddown, *rest = run_outputs(finb, finrb, fing, finrg, find, findr, sums)
    gfg, gfb, gskip, gsg, gsb, gdb, gub, grate, gsi, gso = rest
    return (
        result.reshape(1, 1024, 1024), gtok.reshape(1, 1024, 1024), gfg[0], gfb[0],
        grate[0, 0:16], gsi, gso, gskip[0], dq, dk, dv, do, gsg[0], gsb[0], dup, gub[0], ddown, gdb[0],
    )


NORM_EPS = 1e-05
NEG_LARGE = -1e30
HIGHEST = lax.Precision.HIGHEST


def layer_norm(hidden, gain_vec, bias_vec):
    average = jnp.mean(hidden, axis=-1, keepdims=True)
    centred = hidden - average
    spread = jnp.mean(centred * centred, axis=-1, keepdims=True)
    return centred * lax.rsqrt(spread + NORM_EPS) * gain_vec + bias_vec


def state_context(driven_raw, normed, decay_rates, state_out, skip_gain):
    decay_factor = jnp.exp(-decay_rates)
    driven = driven_raw * jnp.sqrt(1.0 - decay_factor * decay_factor)
    factors = jnp.broadcast_to(decay_factor, driven.shape)

    def combine(earlier, subsequent):
        return (earlier[0] * subsequent[0], subsequent[0] * earlier[1] + subsequent[1])

    states = lax.associative_scan(combine, (factors, driven), axis=1)[1]
    seq_count = driven_raw.shape[0]
    state_width = driven_raw.shape[2]
    model_width = normed.shape[2]
    tail_states = states.reshape(seq_count, NBLK, BLK, state_width)[:, :, BLK - CTX :, :]
    skipped = normed.reshape(seq_count, NBLK, BLK, model_width)[:, :, BLK - CTX :, :]
    outputs = (
        jnp.einsum("sbcp,pd->sbcd", tail_states, state_out, precision=HIGHEST) + skip_gain * skipped
    )
    empty_ctx = jnp.zeros((seq_count, 1, CTX, model_width), jnp.float32)
    return jnp.concatenate([empty_ctx, outputs[:, : NBLK - 1]], axis=1)


def block_scores(queries, key_rows, ctx_keys, ctx_valid):
    row_count = queries.shape[0]
    head_count = queries.shape[1] // DH
    query_heads = queries.reshape(row_count, head_count, DH)
    key_heads = jnp.concatenate([ctx_keys, key_rows], 0).reshape(-1, head_count, DH)
    scores = jnp.einsum(
        "qhd,khd->hqk", query_heads, key_heads, preferred_element_type=jnp.float32
    ) * DH ** (-0.5)
    causal = lax.broadcasted_iota(jnp.int32, (row_count, row_count), 0) >= lax.broadcasted_iota(
        jnp.int32, (row_count, row_count), 1
    )
    allowed = jnp.concatenate(
        [jnp.broadcast_to(ctx_valid[None, :], (row_count, ctx_keys.shape[0])), causal], axis=1
    )
    return (jnp.where(allowed[None], scores, NEG_LARGE), query_heads, key_heads)


def attend_forward(block_item):
    queries, key_rows, value_rows, ctx_keys, ctx_values, ctx_valid = block_item
    scores, query_heads, key_heads = block_scores(queries, key_rows, ctx_keys, ctx_valid)
    row_max = jnp.max(scores, axis=-1, keepdims=True)
    expos = jnp.exp(scores - row_max)
    denominator = jnp.sum(expos, axis=-1, keepdims=True)
    weights = (expos / denominator).astype(jnp.bfloat16)
    value_heads = jnp.concatenate([ctx_values, value_rows], 0).reshape(key_heads.shape)
    attended = jnp.einsum("hqk,khd->qhd", weights, value_heads, preferred_element_type=jnp.float32)
    return (
        attended.reshape(queries.shape).astype(jnp.bfloat16),
        (row_max + jnp.log(denominator))[..., 0],
    )


def attend_backward(block_item):
    queries, key_rows, value_rows, ctx_keys, ctx_values, ctx_valid, log_total, grad_attended = (
        block_item
    )
    scores, query_heads, key_heads = block_scores(queries, key_rows, ctx_keys, ctx_valid)
    probs = jnp.exp(scores - log_total[..., None])
    value_heads = jnp.concatenate([ctx_values, value_rows], 0).reshape(key_heads.shape)
    grad_heads = grad_attended.reshape(query_heads.shape)
    grad_probs = jnp.einsum(
        "qhd,khd->hqk", grad_heads, value_heads, preferred_element_type=jnp.float32
    )
    grad_scores = (
        probs * (grad_probs - jnp.sum(probs * grad_probs, axis=-1, keepdims=True))
    ).astype(jnp.bfloat16)
    grad_values = jnp.einsum(
        "hqk,qhd->khd", probs.astype(jnp.bfloat16), grad_heads, preferred_element_type=jnp.float32
    )
    grad_queries = jnp.einsum(
        "hqk,khd->qhd", grad_scores, key_heads, preferred_element_type=jnp.float32
    ) * DH ** (-0.5)
    grad_keys = jnp.einsum(
        "hqk,qhd->khd", grad_scores, query_heads, preferred_element_type=jnp.float32
    ) * DH ** (-0.5)
    ctx_count = ctx_keys.shape[0]
    model_width = queries.shape[1]
    grad_keys = grad_keys.reshape(-1, model_width).astype(jnp.bfloat16)
    grad_values = grad_values.reshape(-1, model_width).astype(jnp.bfloat16)
    return (
        grad_queries.reshape(queries.shape).astype(jnp.bfloat16),
        grad_keys[ctx_count:],
        grad_values[ctx_count:],
        grad_keys[:ctx_count],
        grad_values[:ctx_count],
    )


def per_device(
    tokens,
    lengths,
    first_gain,
    first_bias,
    decay_rates,
    state_in,
    state_out,
    skip_gain,
    query_weight,
    key_weight,
    value_weight,
    output_weight,
    second_gain,
    second_bias,
    up_weight,
    up_bias,
    down_weight,
    down_bias,
    cotangent,
):
    full_query, full_key, full_value, full_output, full_up, full_down, full_in, full_out = (
        lax.all_gather(query_weight, "shard", axis=0, tiled=True),
        lax.all_gather(key_weight, "shard", axis=0, tiled=True),
        lax.all_gather(value_weight, "shard", axis=0, tiled=True),
        lax.all_gather(output_weight, "shard", axis=0, tiled=True),
        lax.all_gather(up_weight, "shard", axis=0, tiled=True),
        lax.all_gather(down_weight, "shard", axis=0, tiled=True),
        lax.all_gather(state_in, "shard", axis=1, tiled=True),
        lax.all_gather(state_out, "shard", axis=1, tiled=True),
    )
    seq_count, seq_len, model_width = tokens.shape
    row_count = seq_count * seq_len
    block_count = seq_count * NBLK
    positions = lax.broadcasted_iota(jnp.int32, (seq_count, seq_len), 1)
    row_mask = (positions < lengths[:, None]).astype(jnp.float32).reshape(row_count, 1)
    block_index = lax.broadcasted_iota(jnp.int32, (seq_count, NBLK, CTX), 1)
    ctx_valid = (block_index > 0).reshape(block_count, CTX)
    token_rows = tokens.astype(jnp.float32)
    normed, first_pullback = jax.vjp(layer_norm, token_rows, first_gain, first_bias)
    rounded = normed.astype(jnp.bfloat16)
    driven_raw = jnp.einsum("std,pd->stp", rounded, full_in, preferred_element_type=jnp.float32)
    context, state_pullback = jax.vjp(
        state_context, driven_raw, normed, decay_rates, full_out.astype(jnp.float32), skip_gain
    )
    ctx_rows = context.astype(jnp.bfloat16).reshape(block_count * CTX, model_width)
    flat_rounded = rounded.reshape(row_count, model_width)
    query_rows = jnp.dot(flat_rounded, full_query, preferred_element_type=jnp.float32).astype(
        jnp.bfloat16
    )
    key_rows = jnp.dot(flat_rounded, full_key, preferred_element_type=jnp.float32).astype(
        jnp.bfloat16
    )
    value_rows = jnp.dot(flat_rounded, full_value, preferred_element_type=jnp.float32).astype(
        jnp.bfloat16
    )
    ctx_keys = jnp.dot(ctx_rows, full_key, preferred_element_type=jnp.float32).astype(jnp.bfloat16)
    ctx_values = jnp.dot(ctx_rows, full_value, preferred_element_type=jnp.float32).astype(
        jnp.bfloat16
    )
    block_inputs = (
        query_rows.reshape(block_count, BLK, model_width),
        key_rows.reshape(block_count, BLK, model_width),
        value_rows.reshape(block_count, BLK, model_width),
        ctx_keys.reshape(block_count, CTX, model_width),
        ctx_values.reshape(block_count, CTX, model_width),
        ctx_valid,
    )
    attended, log_total = lax.map(attend_forward, block_inputs)
    attended_rows = attended.reshape(row_count, model_width)
    residual = token_rows.reshape(row_count, model_width) + jnp.dot(
        attended_rows, full_output, preferred_element_type=jnp.float32
    )
    second, second_pullback = jax.vjp(layer_norm, residual, second_gain, second_bias)
    second_rows = second.astype(jnp.bfloat16)
    hidden = jnp.dot(second_rows, full_up, preferred_element_type=jnp.float32) + up_bias
    active, gelu_pullback = jax.vjp(jax.nn.gelu, hidden)
    active_rows = active.astype(jnp.bfloat16)
    branch = jnp.dot(active_rows, full_down, preferred_element_type=jnp.float32) + down_bias
    result = (
        ((residual + branch) * row_mask)
        .astype(jnp.bfloat16)
        .reshape(seq_count, seq_len, model_width)
    )
    full_query, full_key, full_value, full_output, full_up, full_down, full_in, full_out = (
        lax.all_gather(query_weight, "shard", axis=0, tiled=True),
        lax.all_gather(key_weight, "shard", axis=0, tiled=True),
        lax.all_gather(value_weight, "shard", axis=0, tiled=True),
        lax.all_gather(output_weight, "shard", axis=0, tiled=True),
        lax.all_gather(up_weight, "shard", axis=0, tiled=True),
        lax.all_gather(down_weight, "shard", axis=0, tiled=True),
        lax.all_gather(state_in, "shard", axis=1, tiled=True),
        lax.all_gather(state_out, "shard", axis=1, tiled=True),
    )
    grad_branch = cotangent.reshape(row_count, model_width).astype(jnp.float32) * row_mask
    branch_rounded = grad_branch.astype(jnp.bfloat16)
    grad_down = jnp.einsum(
        "rf,rd->fd", active_rows, branch_rounded, preferred_element_type=jnp.float32
    )
    grad_down_bias = jnp.sum(grad_branch, axis=0)
    grad_active = jnp.einsum(
        "rd,fd->rf", branch_rounded, full_down, preferred_element_type=jnp.float32
    )
    (grad_hidden,) = gelu_pullback(grad_active)
    hidden_rounded = grad_hidden.astype(jnp.bfloat16)
    grad_up = jnp.einsum(
        "rd,rf->df", second_rows, hidden_rounded, preferred_element_type=jnp.float32
    )
    grad_up_bias = jnp.sum(hidden_rounded.astype(jnp.float32), axis=0)
    grad_second = jnp.einsum(
        "rf,df->rd", hidden_rounded, full_up, preferred_element_type=jnp.float32
    )
    grad_residual_part, grad_second_gain, grad_second_bias = second_pullback(grad_second)
    grad_residual = grad_branch + grad_residual_part
    residual_rounded = grad_residual.astype(jnp.bfloat16)
    grad_output = jnp.einsum(
        "rd,re->de", attended_rows, residual_rounded, preferred_element_type=jnp.float32
    )
    grad_attended = jnp.einsum(
        "re,de->rd", residual_rounded, full_output, preferred_element_type=jnp.float32
    ).astype(jnp.bfloat16)
    grad_query_rows, grad_key_rows, grad_value_rows, grad_ctx_keys, grad_ctx_values = lax.map(
        attend_backward,
        block_inputs + (log_total, grad_attended.reshape(block_count, BLK, model_width)),
    )
    grad_query_rows = grad_query_rows.reshape(row_count, model_width)
    grad_key_rows = grad_key_rows.reshape(row_count, model_width)
    grad_value_rows = grad_value_rows.reshape(row_count, model_width)
    grad_ctx_keys = grad_ctx_keys.reshape(block_count * CTX, model_width)
    grad_ctx_values = grad_ctx_values.reshape(block_count * CTX, model_width)
    grad_query = jnp.einsum(
        "rd,re->de", flat_rounded, grad_query_rows, preferred_element_type=jnp.float32
    )
    grad_key = jnp.einsum(
        "rd,re->de", flat_rounded, grad_key_rows, preferred_element_type=jnp.float32
    ) + jnp.einsum("rd,re->de", ctx_rows, grad_ctx_keys, preferred_element_type=jnp.float32)
    grad_value = jnp.einsum(
        "rd,re->de", flat_rounded, grad_value_rows, preferred_element_type=jnp.float32
    ) + jnp.einsum("rd,re->de", ctx_rows, grad_ctx_values, preferred_element_type=jnp.float32)
    grad_normed = (
        jnp.einsum("re,de->rd", grad_query_rows, full_query, preferred_element_type=jnp.float32)
        + jnp.einsum("re,de->rd", grad_key_rows, full_key, preferred_element_type=jnp.float32)
        + jnp.einsum("re,de->rd", grad_value_rows, full_value, preferred_element_type=jnp.float32)
    )
    grad_context = jnp.einsum(
        "re,de->rd", grad_ctx_keys, full_key, preferred_element_type=jnp.float32
    ) + jnp.einsum("re,de->rd", grad_ctx_values, full_value, preferred_element_type=jnp.float32)
    grad_context = grad_context.reshape(seq_count, NBLK, CTX, model_width)
    grad_driven, state_normed, grad_rates, grad_state_out, grad_skip = state_pullback(grad_context)
    grad_in = jnp.einsum(
        "stp,std->pd", grad_driven, rounded, precision=HIGHEST, preferred_element_type=jnp.float32
    )
    state_rounded = jnp.einsum(
        "stp,pd->std", grad_driven, full_in, precision=HIGHEST, preferred_element_type=jnp.float32
    )
    normed_total = (
        grad_normed.reshape(seq_count, seq_len, model_width) + state_rounded + state_normed
    )
    tokens_part, grad_first_gain, grad_first_bias = first_pullback(normed_total)
    grad_tokens = (tokens_part + grad_residual.reshape(seq_count, seq_len, model_width)).astype(
        jnp.bfloat16
    )
    piece_query, piece_key, piece_value, piece_output, piece_up, piece_down, piece_in, piece_out = (
        lax.psum_scatter(grad_query, "shard", scatter_dimension=0, tiled=True),
        lax.psum_scatter(grad_key, "shard", scatter_dimension=0, tiled=True),
        lax.psum_scatter(grad_value, "shard", scatter_dimension=0, tiled=True),
        lax.psum_scatter(grad_output, "shard", scatter_dimension=0, tiled=True),
        lax.psum_scatter(grad_up, "shard", scatter_dimension=0, tiled=True),
        lax.psum_scatter(grad_down, "shard", scatter_dimension=0, tiled=True),
        lax.psum_scatter(grad_in, "shard", scatter_dimension=1, tiled=True),
        lax.psum_scatter(grad_state_out, "shard", scatter_dimension=1, tiled=True),
    )
    piece_query, piece_key, piece_value, piece_output, piece_up, piece_down, piece_in, piece_out = (
        lax.psum(piece_query.astype(jnp.bfloat16), "rep").astype(jnp.float32),
        lax.psum(piece_key.astype(jnp.bfloat16), "rep").astype(jnp.float32),
        lax.psum(piece_value.astype(jnp.bfloat16), "rep").astype(jnp.float32),
        lax.psum(piece_output.astype(jnp.bfloat16), "rep").astype(jnp.float32),
        lax.psum(piece_up.astype(jnp.bfloat16), "rep").astype(jnp.float32),
        lax.psum(piece_down.astype(jnp.bfloat16), "rep").astype(jnp.float32),
        lax.psum(piece_in.astype(jnp.bfloat16), "rep").astype(jnp.float32),
        lax.psum(piece_out.astype(jnp.bfloat16), "rep").astype(jnp.float32),
    )
    (
        sum_first_gain,
        sum_first_bias,
        sum_rates,
        sum_skip,
        sum_second_gain,
        sum_second_bias,
        sum_up_bias,
        sum_down_bias,
    ) = lax.psum(
        (
            grad_first_gain,
            grad_first_bias,
            grad_rates,
            grad_skip,
            grad_second_gain,
            grad_second_bias,
            grad_up_bias,
            grad_down_bias,
        ),
        ("rep", "shard"),
    )
    return (
        result,
        grad_tokens,
        sum_first_gain,
        sum_first_bias,
        sum_rates,
        piece_in,
        piece_out,
        sum_skip,
        piece_query,
        piece_key,
        piece_value,
        piece_output,
        sum_second_gain,
        sum_second_bias,
        piece_up,
        sum_up_bias,
        piece_down,
        sum_down_bias,
    )


def solution(mesh):
    placed = (
        P(("rep", "shard"), None, None),
        P(("rep", "shard")),
        P(),
        P(),
        P(),
        P(None, "shard"),
        P(None, "shard"),
        P(),
        P("shard", None),
        P("shard", None),
        P("shard", None),
        P("shard", None),
        P(),
        P(),
        P("shard", None),
        P(),
        P("shard", None),
        P(),
        P(("rep", "shard"), None, None),
    )
    fused = mesh.shape["rep"] == 2 and mesh.shape["shard"] == 2 * NC
    return jax.shard_map(
        fused_device if fused else per_device,
        mesh=mesh,
        in_specs=placed,
        out_specs=(
            P(("rep", "shard"), None, None),
            P(("rep", "shard"), None, None),
            P(),
            P(),
            P(),
            P(None, "shard"),
            P(None, "shard"),
            P(),
            P("shard", None),
            P("shard", None),
            P("shard", None),
            P("shard", None),
            P(),
            P(),
            P("shard", None),
            P(),
            P("shard", None),
            P(),
        ),
        check_vma=False,
    )
```

```python
import functools
import math

import jax
import jax.numpy as jnp
from jax import lax
from jax.experimental import pallas as pl
from jax.experimental.pallas import tpu as pltpu
from jax.sharding import PartitionSpec as P

DH = 128
BLK = 512
CTX = 128
NBLK = 2
EPS = 1e-05
NEG = -1e30
SCALE = DH ** (-0.5)
MESH = pl.DeviceIdType.MESH
F32 = jnp.float32
BF16 = jnp.bfloat16
VMEM_LIMIT = 66_000_000
NC = 8


def chip_at(pos):
    turned = pos // 4
    return (1 - turned) * (2 * pos) + turned * (2 * (7 - pos) + 1)


class Net:
    def __init__(self):
        self.rep = lax.axis_index("rep")
        self.shard = lax.axis_index("shard")
        self.core = self.shard % 2
        chip = self.shard // 2
        z, y = chip // 2, chip % 2
        self.pos = (1 - y) * z + y * (7 - z)
        self.step = 1 - 2 * self.core
        self.mate = (self.rep, 2 * chip + 1 - self.core)
        self.twin = (1 - self.rep, self.shard)

    def at(self, hops, core):
        return 2 * chip_at((self.pos + self.step * hops + 4 * NC) % NC) + core

    def along(self, hops):
        return (self.rep, self.at(hops, self.core))

    def greet(self):
        barrier = pltpu.get_barrier_semaphore()
        for device in (self.along(1), self.along(-1), self.mate, self.twin):
            pl.semaphore_signal(barrier, inc=1, device_id=device, device_id_type=MESH)
        pl.semaphore_wait(barrier, 4)


def rcopy(src, dst, send, recv, device):
    return pltpu.make_async_remote_copy(
        src_ref=src, dst_ref=dst, send_sem=send, recv_sem=recv, device_id=device, device_id_type=MESH
    )


def dot_nn(a, b):
    return lax.dot_general(a, b, (((1,), (0,)), ((), ())), preferred_element_type=F32)


def dot_nt(a, b):
    return lax.dot_general(a, b, (((1,), (1,)), ((), ())), preferred_element_type=F32)


def dot_tn(a, b):
    return lax.dot_general(a, b, (((0,), (0,)), ((), ())), preferred_element_type=F32)


def norm_parts(rows):
    centred = rows - jnp.mean(rows, axis=-1, keepdims=True)
    spread = jnp.mean(centred * centred, axis=-1, keepdims=True)
    inverse = lax.rsqrt(spread + EPS)
    return centred * inverse, inverse


def split_dot(dot, left, right, narrow):
    total = None
    rest = left
    for _ in range(narrow):
        term = rest.astype(BF16)
        part = dot(term, right)
        total = part if total is None else total + part
        rest = rest - term.astype(F32)
    return total


def lane_scan(values, factor, reverse):
    width = values.shape[1]
    lane = lax.broadcasted_iota(jnp.int32, values.shape, 1)
    shift = 1
    power = factor
    while shift < width:
        if reverse:
            moved = pltpu.roll(values, width - shift, 1)
            moved = jnp.where(lane < width - shift, moved, 0.0)
        else:
            moved = pltpu.roll(values, shift, 1)
            moved = jnp.where(lane >= shift, moved, 0.0)
        values = values + power * moved
        power = power * power
        shift *= 2
    return values


def forward_kernel(
    tok, wq, wk, wv, wo, wup, wdn, s_in, s_out, fg, fb, skip, sg, sb, decay,
    wall, wdpre, sio_all, rnd_o, q_o, k_o, v_o, att_o, res_o, sec_o, p_o, u_o, st_o,
    tok_s, rnd_s, w_s, q_s, k_s, v_s, att_s, res_s, sec_s, pbuf, nctx, sio_s,
    own_s, sio_own, loc, rs, rr, ss, sr, cs, cr, xs, xr, outs, psem, ds, dr,
):
    net = Net()
    rep, core = net.rep, net.core
    rows_of = 64
    width = 1024

    def block(shard):
        return pl.ds(pl.multiple_of(shard * rows_of, rows_of), rows_of)

    mine = block(net.shard)
    own = [wq, wk, wv, wo]
    copies = [pltpu.make_async_copy(own[i], own_s.at[i], loc.at[i]) for i in range(4)]
    copies += [
        pltpu.make_async_copy(wup.at[:, pl.ds(i * width, width)], own_s.at[4 + i], loc.at[4 + i])
        for i in range(4)
    ]
    small = pltpu.make_async_copy(sio_own, sio_all.at[mine], loc.at[8])
    arrive = pltpu.make_async_copy(tok, tok_s, loc.at[9])
    for copy in copies:
        copy.start()
    arrive.start()
    packed = jnp.concatenate(
        [s_in[...].astype(F32), s_out[...].astype(F32), jnp.zeros((96, rows_of), F32)], axis=0
    )
    sio_own[...] = packed.T.astype(BF16)
    small.start()
    net.greet()
    for copy in copies:
        copy.wait()

    def piece(slot):
        if isinstance(slot, int) and slot < 2:
            return 1 if slot else 2 * rep
        later = slot - 2
        return 3 + later + (1 + 3 * rep) * ((3 - later) // 3) - (later % 2) * (3 - later) // 2

    def ring(slot, way, hop, which, where):
        ref = wall.at[which, where]
        sems = rs.at[slot, way, hop], rr.at[slot, way, hop]
        return rcopy(ref, ref, *sems, net.along(1 - 2 * way))

    def ring_own(slot, way):
        which = piece(slot)
        sems = rs.at[slot, way, 0], rr.at[slot, way, 0]
        ref = wall.at[which, mine]
        rcopy(own_s.at[which], ref, *sems, net.along(1 - 2 * way)).start()

    def ring_small(way, hop, where):
        ref = sio_all.at[where]
        return rcopy(ref, ref, ss.at[way, hop], sr.at[way, hop], net.along(1 - 2 * way))

    def mate(which, index, where):
        ref = wall.at[which, where]
        return rcopy(ref, ref, cs.at[which, index], cr.at[which, index], net.mate)

    def mate_small(index, where):
        ref = sio_all.at[where]
        return rcopy(ref, ref, cs.at[8, index], cr.at[8, index], net.mate)

    def twin(turn, index, which, where):
        ref = wall.at[which, where]
        return rcopy(ref, ref, xs.at[turn, index], xr.at[turn, index], net.twin)

    hand = rcopy(wdn, wdpre.at[0], ds.at[0], dr.at[0], net.along(1))
    hand_on = rcopy(wdpre.at[0], wdpre.at[1], ds.at[1], dr.at[1], net.mate)

    def source(way, hop):
        return block(net.at((2 * way - 1) * (hop + 1), core))

    def serve(slot, way, hop):
        which = piece(slot)
        where = source(way, hop)
        ring(slot, way, hop, which, where).wait_recv()

        @pl.when(hop < 3 - way)
        def _():
            ring(slot, way, hop + 1, which, where).start()

        mate(which, 1 + 2 * hop + way, where).start()

    def serve_out(slot, turn, way, hop):
        twin(turn, 2 * hop + way, piece(slot), source(way, hop)).start()

    def serve_in(turn, way, hop):
        where = source(way, hop)
        which = 2 * (1 - rep) if turn == 0 else 7 - 3 * rep
        twin(turn, 2 * hop + way, which, where).wait_recv()
        mate(which, 1 + 2 * hop + way, where).start()

    for slot in range(2):
        for way in range(2):
            ring_own(slot, way)
    small.wait()
    for way in range(2):
        ring_small(way, 0, mine).start()
    mate_small(0, mine).start()
    for which in range(8):
        rcopy(own_s.at[which], wall.at[which, mine], cs.at[which, 0], cr.at[which, 0], net.mate).start()
    keep = [pltpu.make_async_copy(own_s.at[i], wall.at[i, mine], loc.at[i]) for i in range(8)]
    for copy in keep:
        copy.start()
    arrive.wait()

    def first_norm(at):
        rows = pl.ds(pl.multiple_of(at * 128, 128), 128)
        xhat, _ = norm_parts(tok_s[rows, :].astype(F32))
        normed = xhat * fg[...] + fb[...]
        rnd_s[rows, :] = normed.astype(BF16)

    order = [
        (hop, slot, way) for hop in range(4) for slot in range(2) for way in range(2) if hop < 4 - way
    ]
    owed = []
    for n, (hop, slot, way) in enumerate(order):
        if n % 2 == 0:
            first_norm(n // 2)
        serve(slot, way, hop)
        if slot == 0:
            serve_out(0, 0, way, hop)
            owed.append((n, way, hop))
        else:
            where = source(way, hop)
            ring_small(way, hop, where).wait_recv()
            if hop < 3 - way:
                ring_small(way, hop + 1, where).start()
            mate_small(1 + 2 * hop + way, where).start()
        if n in (12, 13):
            for later in range(2):
                for each in range(2):
                    ring_own((2 if n == 12 else 4) + later, each)
        if owed and n - owed[0][0] >= 6:
            serve_in(0, *owed.pop(0)[1:])
    first_norm(7)
    for each in owed:
        serve_in(0, *each[1:])

    def event(m):
        half, place = m // 14, m % 14
        late = place // 12
        hop = place // 4
        index = ((place % 4) // 2) * (1 - late) + (place - 12) * late
        way = (place % 2) * (1 - late)
        slot = 2 + 2 * half + index
        serve(slot, way, hop)

        @pl.when(slot == 2)
        def _():
            serve_out(2, 1, way, hop)

        @pl.when(m == 10)
        def _():
            hand.start()

        @pl.when((m >= 8) & (m <= 20) & (m % 4 < 2))
        def _():
            serve_in(1, m % 2, (m - 8) // 4)

    xhat, _ = norm_parts(tok_s[pl.ds(BLK - CTX, CTX), :].astype(F32))
    nctx[...] = xhat * fg[...] + fb[...]

    @pl.loop(0, NC)
    def _(index):
        where = block(0)
        mate_small(index, where).wait_recv()
        for which in range(3):
            mate(which, index, where).wait_recv()

    for copy in keep:
        copy.wait()
    loads = [pltpu.make_async_copy(sio_all, sio_s, loc.at[8])]
    loads += [pltpu.make_async_copy(wall.at[i], w_s.at[i], loc.at[i]) for i in range(3)]
    for copy in loads:
        copy.start()
    loads[0].wait()
    u_all = lax.dot_general(
        sio_s[...], rnd_s[pl.ds(0, BLK), :], (((0,), (1,)), ((), ())), preferred_element_type=F32
    )
    factor = jnp.exp(-column(decay[...]))
    raw = u_all[0:16, :]
    u_o[...] = raw
    states = lane_scan(raw * jnp.sqrt(1.0 - factor * factor), factor, False)
    st_o[...] = states
    tail = states[:, BLK - CTX :]
    padded = jnp.concatenate(
        [jnp.zeros((16, CTX), F32), tail, jnp.zeros((96, CTX), F32)], axis=0
    )
    made = split_dot(
        lambda a, b: lax.dot_general(a, b, (((0,), (1,)), ((), ())), preferred_element_type=F32),
        padded, sio_s[...], 3,
    )
    rnd_s[pl.ds(1024, CTX), :] = (made + skip[...] * nctx[...]).astype(BF16)
    finals = [pltpu.make_async_copy(rnd_s, rnd_o, outs.at[0])]
    finals[0].start()

    for copy in loads[1:]:
        copy.wait()

    @pl.loop(0, 4)
    def _(at):
        cols = pl.ds(pl.multiple_of(at * 256, 256), 256)
        q_s[:, cols] = dot_nn(rnd_s[pl.ds(0, 1024), :], w_s[0, :, cols]).astype(BF16)
        event(2 * at)
        k_s[:, cols] = dot_nn(rnd_s[...], w_s[1, :, cols]).astype(BF16)
        v_s[:, cols] = dot_nn(rnd_s[...], w_s[2, :, cols]).astype(BF16)
        event(2 * at + 1)

    for i, (a, b) in enumerate(((q_s, q_o), (k_s, k_o), (v_s, v_o))):
        finals.append(pltpu.make_async_copy(a, b, outs.at[1 + i]))
        finals[-1].start()

    for half in range(2):
        pbuf[half] = jnp.zeros((BLK, CTX + BLK), BF16)

    def p_copy(slot, at):
        return pltpu.make_async_copy(pbuf.at[slot], p_o.at[at], psem.at[slot])

    for b in range(NBLK):

        @pl.loop(0, 8)
        def _(h, b=b):
            cols = pl.ds(pl.multiple_of(h * DH, DH), DH)
            slot = h % 2
            if b == 0:

                @pl.when(h >= 2)
                def _():
                    p_copy(slot, h).wait()
            else:
                p_copy(slot, h).wait()
            for i in range(2):
                span = (i + 1) * 256
                rows = pl.ds(b * BLK + i * 256, 256)
                queries = q_s[rows, cols]
                scores = dot_nt(queries, k_s[pl.ds(b * BLK, span), cols]) * SCALE
                ahead = lax.broadcasted_iota(jnp.int32, scores.shape, 0) + i * 256
                scores = jnp.where(
                    ahead >= lax.broadcasted_iota(jnp.int32, scores.shape, 1), scores, NEG
                )
                top = jnp.max(scores, axis=-1, keepdims=True)
                if b:
                    before = dot_nt(queries, k_s[pl.ds(1024, CTX), cols]) * SCALE
                    top = jnp.maximum(top, jnp.max(before, axis=-1, keepdims=True))
                expos = jnp.exp(scores - top)
                total = jnp.sum(expos, axis=-1, keepdims=True)
                if b:
                    expos_before = jnp.exp(before - top)
                    total = total + jnp.sum(expos_before, axis=-1, keepdims=True)
                share = 1.0 / total
                weights = (expos * share).astype(BF16)
                mixed = dot_nn(weights, v_s[pl.ds(b * BLK, span), cols])
                pbuf[slot, pl.ds(i * 256, 256), pl.ds(CTX, span)] = weights
                if b:
                    weights = (expos_before * share).astype(BF16)
                    mixed = mixed + dot_nn(weights, v_s[pl.ds(1024, CTX), cols])
                    pbuf[slot, pl.ds(i * 256, 256), pl.ds(0, CTX)] = weights
                att_s[rows, cols] = mixed.astype(BF16)
            p_copy(slot, b * 8 + h).start()

            event(8 + 8 * b + h)

    finals.append(pltpu.make_async_copy(att_s, att_o, outs.at[4]))
    finals[-1].start()

    @pl.loop(0, NC)
    def _(index):
        mate(3, index, block(0)).wait_recv()

    load = pltpu.make_async_copy(wall.at[3], w_s.at[3], loc.at[3])
    load.start()
    load.wait()

    @pl.loop(0, 4)
    def _(at):
        rows = pl.ds(pl.multiple_of(at * 256, 256), 256)
        residual = tok_s[rows, :].astype(F32) + dot_nn(att_s[rows, :], w_s[3])
        res_s[rows, :] = residual
        xhat, _ = norm_parts(residual)
        sec_s[rows, :] = (xhat * sg[...] + sb[...]).astype(BF16)
        pltpu.make_async_copy(res_s.at[rows], res_o.at[rows], outs.at[5 + at]).start()
        pltpu.make_async_copy(sec_s.at[rows], sec_o.at[rows], outs.at[9 + at]).start()
        event(24 + at)

        @pl.when(at == 0)
        def _():
            hand.wait_recv()
            hand_on.start()

    for copy in finals:
        copy.wait()
    for at in range(4):
        rows = pl.ds(at * 256, 256)
        pltpu.make_async_copy(res_s.at[rows], res_o.at[rows], outs.at[5 + at]).wait()
        pltpu.make_async_copy(sec_s.at[rows], sec_o.at[rows], outs.at[9 + at]).wait()
    for slot in range(2):
        p_copy(slot, slot).wait()

    hand.wait_send()
    hand_on.wait()

    @pl.loop(0, NC)
    def _(index):
        for which in range(4, 8):
            mate(which, index, block(0)).wait_recv()
        for which in range(8):
            mate(which, index, block(0)).wait_send()
        mate_small(index, block(0)).wait_send()

    @pl.loop(0, NC - 1)
    def _(index):
        hop = index // 2
        way = index % 2
        for slot in range(6):
            ring(slot, way, hop, 0, block(0)).wait_send()
        ring_small(way, hop, block(0)).wait_send()
        for turn in range(2):
            twin(turn, index, 0, block(0)).wait_send()


def column(row):
    wide = jnp.broadcast_to(row, (16, 16))
    same = lax.broadcasted_iota(jnp.int32, (16, 16), 0) == lax.broadcasted_iota(jnp.int32, (16, 16), 1)
    return jnp.sum(jnp.where(same, wide, 0.0), axis=1, keepdims=True)


def any_spec(n):
    return [pl.BlockSpec(memory_space=pl.ANY)] * n


def vmem_spec(n):
    return [pl.BlockSpec(memory_space=pltpu.VMEM)] * n


def run_forward(tok, wq, wk, wv, wo, wup, wdn, s_in, s_out, fg, fb, skip, sg, sb, decay):
    shape = jax.ShapeDtypeStruct
    dma = pltpu.SemaphoreType.DMA
    big = (1024, 1024)
    ext = (1024 + CTX, 1024)
    return pl.pallas_call(
        forward_kernel,
        name="forward_part",
        out_shape=(
            shape((8,) + big, BF16), shape((2, 256, 1024), BF16), shape((1024, 128), BF16),
            shape(ext, BF16), shape(big, BF16),
            shape(ext, BF16), shape(ext, BF16), shape(big, BF16), shape(big, F32),
            shape(big, BF16), shape((16, BLK, CTX + BLK), BF16), shape((16, BLK), F32),
            shape((16, BLK), F32),
        ),
        in_specs=any_spec(7) + vmem_spec(8),
        out_specs=any_spec(11) + vmem_spec(2),
        scratch_shapes=[
            pltpu.VMEM(big, BF16), pltpu.VMEM(ext, BF16), pltpu.VMEM((4,) + big, BF16),
            pltpu.VMEM(big, BF16), pltpu.VMEM(ext, BF16), pltpu.VMEM(ext, BF16),
            pltpu.VMEM(big, BF16), pltpu.VMEM(big, F32), pltpu.VMEM(big, BF16),
            pltpu.VMEM((2, BLK, CTX + BLK), BF16), pltpu.VMEM((CTX, 1024), F32),
            pltpu.VMEM((1024, 128), BF16),
            pltpu.VMEM((8, 64, 1024), BF16), pltpu.VMEM((64, 128), BF16),
            dma((10,)), dma((6, 2, 4)), dma((6, 2, 4)), dma((2, 4)), dma((2, 4)),
            dma((9, NC)), dma((9, NC)), dma((2, NC - 1)), dma((2, NC - 1)), dma((13,)), dma((2,)), dma((2,)), dma((2,)),
        ],
        compiler_params=pltpu.CompilerParams(
            collective_id=0, has_side_effects=True, vmem_limit_bytes=VMEM_LIMIT
        ),
    )(tok, wq, wk, wv, wo, wup, wdn, s_in, s_out, fg, fb, skip, sg, sb, decay)


GELU_C = math.sqrt(2.0 / math.pi)
GELU_A = 0.044715


def feed_kernel(
    sec, res, wall, wdn, wdpre, cot, live, upb, dnb, sg,
    out_o, gatt_o, dwown_o, dwmate_o, fin_o, gdb_o, gub_o, gsg_o, gsb_o,
    sec_s, gb_s, wup_s, wd_s, br_s, gs_s, act_s, gh_s, a_s, b_s, prec, rrec, rsend, xsend, xrec,
    dwup_s, own_s, res_s,
    loc, ars, arr, axs, axr, cas, car, cxs, cxr, ps, pr, rs, rr, xs, xr, outs, dsem, dms, dmr,
):
    net = Net()
    rep, core = net.rep, net.core
    rows_of = 256
    ring_rows = 192
    part = 64
    ahead, behind = net.along(1), net.along(-1)

    def ring_part(shard, j, first=rep):
        return pl.ds(pl.multiple_of(shard * rows_of + (first + j) * part, part), part)

    def sole_part(shard, of):
        return pl.ds(pl.multiple_of(shard * rows_of + 3 * of * part, part), part)

    def block(shard):
        return pl.ds(pl.multiple_of(shard * rows_of, rows_of), rows_of)

    def mine_at(step):
        return net.at(-(step + 1), core)

    def other_at(step):
        return net.at(step + 1, 1 - core)

    loads = [
        pltpu.make_async_copy(wdn, own_s, loc.at[0]),
        pltpu.make_async_copy(sec, sec_s, loc.at[1]),
        pltpu.make_async_copy(cot, gb_s, loc.at[2]),
        pltpu.make_async_copy(wdpre.at[0], wd_s.at[block(mine_at(0))], loc.at[7]),
        pltpu.make_async_copy(wdpre.at[1], wd_s.at[block(other_at(0))], loc.at[8]),
    ]
    loads += [pltpu.make_async_copy(wall.at[4 + i], wup_s.at[i], loc.at[3 + i]) for i in range(4)]
    for load in loads:
        load.start()
    net.greet()
    loads[0].wait()
    loads[3].wait()

    def gather(j, hop, shard):
        ref = wd_s.at[ring_part(shard, j)]
        return rcopy(ref, ref, ars.at[j, hop], arr.at[j, hop], ahead)

    def gather_twin(hop, shard, of):
        ref = wd_s.at[sole_part(shard, of)]
        return rcopy(ref, ref, axs.at[hop], axr.at[hop], net.twin)

    def mate_ring(j, index, shard):
        ref = wd_s.at[ring_part(shard, j)]
        return rcopy(ref, ref, cas.at[j, index], car.at[j, index], net.mate)

    def mate_sole(index, shard, of):
        ref = wd_s.at[sole_part(shard, of)]
        return rcopy(ref, ref, cxs.at[index], cxr.at[index], net.mate)

    here = net.shard
    sole_own = own_s.at[pl.ds(pl.multiple_of(3 * (1 - rep) * part, part), part)]
    for j in range(3):
        ring_own = own_s.at[pl.ds(pl.multiple_of((rep + j) * part, part), part)]
        target = wd_s.at[ring_part(here, j)]
        gather(j, 1, mine_at(0)).start()
        rcopy(ring_own, target, cas.at[j, 0], car.at[j, 0], net.mate).start()
    rcopy(sole_own, wd_s.at[sole_part(here, 1 - rep)], cxs.at[0], cxr.at[0], net.mate).start()

    def serve(j, hop):
        shard = mine_at(hop)
        gather(j, hop, shard).wait_recv()

        @pl.when(hop < NC - 2)
        def _():
            gather(j, hop + 1, shard).start()

        @pl.when(j == 2 * rep)
        def _():
            gather_twin(hop, shard, rep).start()

        mate_ring(j, hop + 1, shard).start()

    def serve_twin(hop):
        shard = mine_at(hop)
        gather_twin(hop, shard, 1 - rep).wait_recv()
        mate_sole(hop + 1, shard, 1 - rep).start()

    for load in loads[1:3]:
        load.wait()

    wd_s[block(here), :] = own_s[...]

    @pl.loop(0, 4)
    def _(at):
        rows = pl.ds(pl.multiple_of(at * 256, 256), 256)
        when = lax.broadcasted_iota(jnp.int32, (256, 1024), 0) + at * 256
        kept = jnp.where(when < live[0], gb_s[rows, :].astype(F32), 0.0)
        gb_s[rows, :] = kept.astype(BF16)
        added = jnp.sum(kept, axis=0, keepdims=True)
        gdb_o[...] = jnp.where(at == 0, added, gdb_o[...] + added)
        br_s[rows, :] = jnp.zeros((256, 1024), F32)
        gs_s[rows, :] = jnp.zeros((256, 1024), F32)

    for load in loads[4:]:
        load.wait()

    def to_mate(step):
        slot = step % 2
        return rcopy(b_s.at[slot], prec.at[step], ps.at[step], pr.at[step], net.mate)

    def to_ring(j, step):
        return rcopy(rsend.at[step % 2, j], rrec.at[step, j], rs.at[step, j], rr.at[step, j], ahead)

    def to_twin(step):
        return rcopy(xsend.at[step % 2], xrec.at[step], xs.at[step], xr.at[step], net.twin)

    def dwup_at(target, shard):
        cols = pl.ds(pl.multiple_of((shard % 4) * 256, 256), 256)
        return target.at[shard // 4, :, :, cols]

    def dwup_copy(slot, half, shard):
        return pltpu.make_async_copy(
            dwup_s.at[slot, half, :, core], dwup_at(dwown_o, shard), dsem.at[slot, half]
        )

    def dwup_mate(step, half, shard):
        return rcopy(
            dwup_s.at[step % 2, half, :, 1 - core], dwup_at(dwmate_o, shard),
            dms.at[step, half], dmr.at[step, half], net.mate,
        )

    ring_local = pl.ds(pl.multiple_of(rep * part, part), ring_rows)
    sole_mine = pl.ds(pl.multiple_of(3 * rep * part, part), part)
    sole_theirs = pl.ds(pl.multiple_of(3 * (1 - rep) * part, part), part)

    def combine(step):
        slot = step % 2
        to_mate(step).wait_recv()
        a_s[slot] = a_s[slot] + prec[step].astype(F32)

        @pl.when(step >= 2)
        def _():
            to_twin(step - 2).wait_send()

        xsend[slot] = a_s[slot, sole_theirs, :].astype(BF16)
        to_twin(step).start()

    def forward(j, step):
        slot = step % 2
        rows = pl.ds(pl.multiple_of((rep + j) * part, part), part)

        @pl.when(j == 2 * rep)
        def _():
            to_twin(step).wait_recv()
            a_s[slot, rows, :] = a_s[slot, rows, :] + xrec[step].astype(F32)

        @pl.when(step >= 1)
        def _():
            to_ring(j, step - 1).wait_recv()
            a_s[slot, rows, :] = a_s[slot, rows, :] + rrec[step - 1, j].astype(F32)

        @pl.when((step >= 2) & (step < NC - 1))
        def _():
            to_ring(j, step - 2).wait_send()

        @pl.when(step < NC - 1)
        def _():
            rsend[slot, j] = a_s[slot, rows, :].astype(BF16)
            to_ring(j, step).start()

    @pl.loop(0, NC)
    def _(step):
        slot = step % 2
        a, b = mine_at(step), other_at(step)
        index = (step + 1) % NC

        @pl.when(step >= 1)
        def _():
            combine(step - 1)

        def up(shard):
            cols = pl.ds(pl.multiple_of((shard % 4) * 256, 256), 256)
            return wup_s[shard // 4, :, cols]

        def bias(shard):
            return upb[:, pl.ds(pl.multiple_of(shard * 256, 256), 256)]

        def middle(half, shard, at):
            for block_at in range(1):
                rows = pl.ds(pl.multiple_of(at * 512 + block_at * 256, 256), 512)
                cols = pl.ds(half * 256, 256)
                hidden = dot_nn(sec_s[rows, :], up(shard)) + bias(shard)
                grad = dot_nt(gb_s[rows, :], wd_s[block(shard), :])
                square = hidden * hidden
                bent = jnp.tanh(hidden * (GELU_C + (GELU_C * GELU_A) * square))
                half_up = 0.5 + 0.5 * bent
                act_s[rows, cols] = (hidden * half_up).astype(BF16)
                slope = half_up + (0.5 * hidden) * (1.0 - bent * bent) * (
                    GELU_C + (3.0 * GELU_C * GELU_A) * square
                )
                gh_s[rows, cols] = (grad * slope).astype(BF16)

        @pl.loop(0, 2)
        def _(at):
            middle(0, a, at)

        @pl.when(step < NC - 2)
        def _():
            serve(2 * rep, step + 1)

        @pl.when(step >= 1)
        def _():
            for j in range(3):
                mate_ring(j, index, b).wait_recv()
            mate_sole(index, b, 1 - rep).wait_recv()

        @pl.loop(0, 2)
        def _(at):
            middle(1, b, at)

            @pl.when(step < NC - 2)
            def _():
                serve((2 * rep + 1 + at) % 3, step + 1)

        made = dot_tn(act_s[...], gb_s[...])

        @pl.when(step >= 2)
        def _():
            to_mate(step - 2).wait_send()

        a_s[slot] = made[0:256]
        b_s[slot] = made[256:512].astype(BF16)
        to_mate(step).start()

        rise_up = dot_tn(sec_s[...], gh_s[...]).astype(BF16)
        for half, shard in enumerate((a, b)):
            cols = pl.ds(pl.multiple_of(shard * 256, 256), 256)
            gub_o[:, cols] = jnp.sum(
                gh_s[:, half * 256 : half * 256 + 256].astype(F32), axis=0, keepdims=True
            )

            @pl.when(step >= 2)
            def _(half=half, shard=shard):
                dwup_copy(slot, half, shard).wait()
                dwup_mate(step - 2, half, shard).wait_send()

            dwup_s[slot, half] = rise_up[:, half * 256 : half * 256 + 256].reshape(NC, 2, 64, 256)
            dwup_copy(slot, half, shard).start()
            dwup_mate(step, half, shard).start()

        @pl.loop(0, 2)
        def _(at):
            rows = pl.ds(pl.multiple_of(at * 512, 512), 512)
            down = jnp.concatenate([wd_s[block(a), :], wd_s[block(b), :]], axis=0)
            br_s[rows, :] = br_s[rows, :] + dot_nn(act_s[rows, :], down)
            rise = jnp.concatenate([up(a), up(b)], axis=1)
            gs_s[rows, :] = gs_s[rows, :] + dot_nt(gh_s[rows, :], rise)

            @pl.when(step >= 1)
            def _():
                forward((2 * rep + 1 + at) % 3, step - 1)

            @pl.when((at == 1) & (step < NC - 2))
            def _():
                serve_twin(step + 1)

        @pl.when(step >= 1)
        def _():
            forward((2 * rep + 3) % 3, step - 1)

    def residual_in(at):
        rows = pl.ds(at * 256, 256)
        return pltpu.make_async_copy(res.at[rows], res_s.at[rows], loc.at[at])

    for at in range(4):
        residual_in(at).start()
    combine(NC - 1)

    def leave(at, which):
        rows = pl.ds(pl.multiple_of(at * 256, 256), 256)
        source = (sec_s, gb_s)[which]
        return pltpu.make_async_copy(
            source.at[rows], (out_o, gatt_o)[which].at[rows], outs.at[which, at]
        )

    @pl.loop(0, 4)
    def _(at):
        residual_in(at).wait()
        rows = pl.ds(pl.multiple_of(at * 256, 256), 256)
        kept = res_s[rows, :]
        when = lax.broadcasted_iota(jnp.int32, (256, 1024), 0) + at * 256
        total = kept + br_s[rows, :] + dnb[...]
        sec_s[rows, :] = jnp.where(when < live[0], total, 0.0).astype(BF16)
        xhat, inverse = norm_parts(kept)
        grad = gs_s[rows, :]
        gain = jnp.sum(grad * xhat, axis=0, keepdims=True)
        shift = jnp.sum(grad, axis=0, keepdims=True)
        gsg_o[...] = jnp.where(at == 0, gain, gsg_o[...] + gain)
        gsb_o[...] = jnp.where(at == 0, shift, gsb_o[...] + shift)
        grad = grad * sg[...]
        grad = grad - jnp.mean(grad, axis=-1, keepdims=True) - xhat * jnp.mean(
            grad * xhat, axis=-1, keepdims=True
        )
        gb_s[rows, :] = (gb_s[rows, :].astype(F32) + inverse * grad).astype(BF16)
        for which in range(2):
            leave(at, which).start()

    for j in range(3):
        forward((2 * rep + 1 + j) % 3, NC - 1)
    last = (NC - 1) % 2
    fin_o[...] = a_s[last, ring_local, :].astype(BF16)

    @pl.loop(1, NC - 1)
    def _(hop):
        for j in range(3):
            gather(j, hop, 0).wait_send()
        gather_twin(hop, 0, 0).wait_send()

    @pl.loop(1, NC)
    def _(later):
        index = (later + 1) % NC
        for j in range(3):
            mate_ring(j, index, 0).wait_send()
        mate_sole(index, 0, 0).wait_send()

    for step in range(NC - 2, NC):
        to_mate(step).wait_send()
        to_twin(step).wait_send()
        for j in range(3):
            to_ring(j, step - 1).wait_send()
        for half in range(2):
            dwup_copy(step % 2, half, 0).wait()
            dwup_mate(step, half, 0).wait_send()
    for at in range(4):
        for which in range(2):
            leave(at, which).wait()

    @pl.loop(0, NC)
    def _(step):
        for half in range(2):
            dwup_mate(step, half, 0).wait_recv()


def run_feed(sec, res, wall, wdn, wdpre, cot, live, upb, dnb, sg):
    shape = jax.ShapeDtypeStruct
    dma = pltpu.SemaphoreType.DMA
    vmem = pltpu.VMEM
    big = (1024, 1024)
    return pl.pallas_call(
        feed_kernel,
        name="feed_part",
        out_shape=(
            shape(big, BF16), shape(big, BF16), shape((4, NC, 64, 1024), BF16),
            shape((4, NC, 64, 1024), BF16), shape((192, 1024), BF16), shape((1, 1024), F32), shape((1, 4096), F32),
            shape((1, 1024), F32), shape((1, 1024), F32),
        ),
        in_specs=any_spec(6) + [pl.BlockSpec(memory_space=pltpu.SMEM)] + vmem_spec(3),
        out_specs=any_spec(4) + vmem_spec(5),
        scratch_shapes=[
            vmem(big, BF16), vmem(big, BF16), vmem((4,) + big, BF16), vmem((4096, 1024), BF16),
            vmem(big, F32), vmem(big, F32), vmem((1024, 512), BF16), vmem((1024, 512), BF16),
            vmem((2, 256, 1024), F32), vmem((2, 256, 1024), BF16), vmem((NC, 256, 1024), BF16),
            vmem((NC - 1, 3, 64, 1024), BF16), vmem((2, 3, 64, 1024), BF16), vmem((2, 64, 1024), BF16),
            vmem((NC, 64, 1024), BF16),
            vmem((2, 2, NC, 2, 64, 256), BF16), vmem((256, 1024), BF16), vmem(big, F32),
            dma((9,)), dma((3, NC - 1)), dma((3, NC - 1)), dma((NC - 1,)), dma((NC - 1,)),
            dma((3, NC)), dma((3, NC)), dma((NC,)), dma((NC,)), dma((NC,)), dma((NC,)),
            dma((NC - 1, 3)), dma((NC - 1, 3)), dma((NC,)), dma((NC,)),
            dma((2, 4)), dma((2, 2)), dma((NC, 2)), dma((NC, 2)),
        ],
        compiler_params=pltpu.CompilerParams(
            collective_id=1, has_side_effects=True, vmem_limit_bytes=VMEM_LIMIT
        ),
    )(sec, res, wall, wdn, wdpre, cot, live, upb, dnb, sg)


def backward_kernel(
    dwown, dwmate, find, gatt, att, wall, q, kx, vx, rnd, p, tok, sio, u_in, st_in, fg, fb, skip, decay,
    gsg, gsb, gdb, gub,
    gtok_o, findr_o, fin_b, finr_b, fin_g, finr_g, sums_o,
    own_b, prec_b, rrec_b, xrec_b, acc_b,
    own_g, prec_g, rrec_g, xrec_g, acc_g, go_s,
    gatt_s, wo_s, att_s, ga_s, q_s, k_s, v_s, rnd_s, dk_s, dv_s, pbuf, ds_s, gres_s, nb_s,
    sio_s, gd_s, gctx_s, sum_s, got_s, part_s,
    loc, psem, gsem, osem, mbs, mbr, mgs, mgr, rbs, rbr, rgs, rgr, xbs, xbr, xgs, xgr,
    fbs, fbr, fgs, fgr, ts, tr, us, ur, ds, dr,
):
    net = Net()
    rep, core = net.rep, net.core
    theirs = 1 - core

    loads = [
        pltpu.make_async_copy(gatt, gatt_s, loc.at[0]),
        pltpu.make_async_copy(wall.at[3], wo_s, loc.at[1]),
        pltpu.make_async_copy(att, att_s, loc.at[2]),
        pltpu.make_async_copy(q, q_s, loc.at[3]),
        pltpu.make_async_copy(kx, k_s, loc.at[4]),
        pltpu.make_async_copy(vx, v_s, loc.at[5]),
        pltpu.make_async_copy(rnd, rnd_s, loc.at[6]),
        pltpu.make_async_copy(sio, sio_s, loc.at[7]),
    ]
    rises = [
        pltpu.make_async_copy(dwown, own_b.at[pl.ds(0, 4)], loc.at[8]),
        pltpu.make_async_copy(dwmate, prec_b.at[pl.ds(0, 4)], loc.at[9]),
    ]
    for copy in rises:
        copy.start()
    for copy in loads:
        copy.start()
    fin_b[...] = jnp.zeros(fin_b.shape, BF16)
    finr_b[...] = jnp.zeros(finr_b.shape, BF16)
    fin_g[...] = jnp.zeros(fin_g.shape, BF16)
    finr_g[...] = jnp.zeros(finr_g.shape, BF16)
    barrier = pltpu.get_barrier_semaphore()
    me = rep * (2 * NC) + net.shard

    def device(away):
        other = (me + away) % (4 * NC)
        return other, (other // (2 * NC), other % (2 * NC))

    @pl.loop(1, 4 * NC)
    def _(away):
        pl.semaphore_signal(barrier, inc=1, device_id=device(away)[1], device_id_type=MESH)

    pl.semaphore_wait(barrier, 4 * NC - 1)

    mate_out = rcopy(go_s, prec_b.at[4], mbs.at[0], mbr.at[0], net.mate)

    def mate_group(g):
        return rcopy(own_g.at[g, :, theirs], prec_g.at[g], mgs.at[g], mgr.at[g], net.mate)

    swap = rcopy(find, findr_o, ds.at[0], dr.at[0], net.twin)
    swap.start()

    def chip_for(n):
        t, way = n // 2, n % 2
        hops = (4 - t) * (1 - way) + (t - 3) * way
        return chip_at((net.pos + net.step * hops + 4 * NC) % NC)

    class Stream:
        def __init__(self, own, prec, rrec, xrec, fin, finr, acc, sems):
            self.own, self.prec, self.rrec, self.xrec = own, prec, rrec, xrec
            self.fin, self.finr, self.acc = fin, finr, acc
            self.rs, self.rr, self.xs, self.xr, self.fs, self.fr = sems

        def ring(self, slot, which, n):
            source = self.prec.at[which, chip_for(n)]
            way = n % 2
            return rcopy(
                source, self.rrec.at[slot, n], self.rs.at[slot, n], self.rr.at[slot, n],
                net.along(1 - 2 * way),
            )

        def twin(self, which, n):
            chip = chip_for(n)
            return rcopy(
                self.prec.at[which, chip], self.xrec.at[chip], self.xs.at[n], self.xr.at[n], net.twin
            )

        def finish(self, which):
            return rcopy(
                self.fin.at[which], self.finr.at[which], self.fs.at[which], self.fr.at[which], net.twin
            )

        def give(self, which, n):
            chip = chip_for(n)
            self.prec[which, chip] = (
                self.own(which, chip).astype(F32) + self.prec[which, chip].astype(F32)
            ).astype(BF16)
            self.twin(which, n).start()

        def turn(self, slot, which, n, sole):
            chip = chip_for(n)
            self.acc[...] = self.own(which, chip).astype(F32) + self.prec[which, chip].astype(F32)

            @pl.when(sole)
            def _():
                self.twin(which, n).wait_recv()
                self.acc[...] = self.acc[...] + self.xrec[chip].astype(F32)

            @pl.when((n >= 2) & (n < 7))
            def _():
                self.ring(slot, which, n - 2).wait_recv()
                self.acc[...] = self.acc[...] + self.rrec[slot, n - 2].astype(F32)

            @pl.when(n < 7)
            def _():
                self.prec[which, chip] = self.acc[...].astype(BF16)
                self.ring(slot, which, n).start()

            @pl.when(n == 7)
            def _():
                self.ring(slot, which, 5).wait_recv()
                self.ring(slot, which, 6).wait_recv()
                total = self.acc[...] + self.rrec[slot, 5].astype(F32) + self.rrec[slot, 6].astype(F32)
                self.fin[which] = total.astype(BF16)
                self.finish(which).start()

    big = Stream(
        lambda which, chip: own_b[which, chip], prec_b, rrec_b, xrec_b, fin_b, finr_b, acc_b,
        (rbs, rbr, xbs, xbr, fbs, fbr),
    )
    group = Stream(
        lambda which, chip: own_g[which, chip, core], prec_g, rrec_g, xrec_g, fin_g, finr_g, acc_g,
        (rgs, rgr, xgs, xgr, fgs, fgr),
    )

    def tile(index):
        return (
            pl.ds(pl.multiple_of((index // 8) * 16, 16), 16),
            pl.ds(pl.multiple_of((index % 8) * 128, 128), 128),
        )

    def share(away):
        other, where = device(away)
        return rcopy(sum_s.at[tile(other)], got_s.at[away], ts.at[away], tr.at[away], where)

    def spread(away):
        return rcopy(part_s, sums_o.at[tile(me)], us.at[away], ur.at[away], device(away)[1])

    def each_device(act):
        for away in range(1, 4 * NC):
            act(away)

    def big_at(e):
        k, j = e // 4, e % 4
        n = k - j - (j // 2) * (1 - 2 * (j // 3))
        which = (j + 1) * (1 - j // 2) + (j // 2) * (3 * rep * (1 - j // 3) + 4 * (j // 3))

        @pl.when((j == 3) & (n == 0))
        def _():
            mate_out.wait_recv()

        @pl.when((n >= 0) & (n <= 7))
        def _():
            big.turn(j, which, n, j == 2)

    def group_at(e):
        k, j = e // 3, e % 3
        n = k
        which = rep * (1 - (j + 1) // 2) + (j + 1) * ((j + 1) // 2)

        @pl.when((j >= 1) & (n == 0))
        def _():
            mate_group(which).wait_recv()

        @pl.when((n >= 0) & (n <= 7))
        def _():
            group.turn(j, which, n, j == 0)

    def run(at, low, high):
        @pl.loop(low, high)
        def _(e):
            at(e)

    for copy in rises:
        copy.wait()

    @pl.loop(0, NC)
    def _(n):
        big.give(3 * (1 - rep), n)

    run(big_at, 0, 4)
    for i in range(2):
        loads[i].wait()

    def p_copy(slot, at):
        return pltpu.make_async_copy(p.at[at], pbuf.at[slot], psem.at[slot])

    p_copy(0, 0).start()

    @pl.loop(0, 2)
    def _(at):
        rows = pl.ds(pl.multiple_of(at * 512, 512), 512)
        ga_s[rows, :] = dot_nt(gatt_s[rows, :], wo_s[...]).astype(BF16)

    run(big_at, 4, 8)
    loads[2].wait()

    @pl.loop(0, 2)
    def _(at):
        cols = pl.ds(pl.multiple_of(at * 512, 512), 512)
        made = dot_tn(att_s[...], gatt_s[:, cols]).reshape(NC, 2, 64, 512)
        own_b[4, :, :, cols] = jnp.where(core == 0, made[:, 0], made[:, 1]).astype(BF16)
        go_s[:, :, cols] = jnp.where(core == 0, made[:, 1], made[:, 0]).astype(BF16)

    mate_out.start()
    tok_load = pltpu.make_async_copy(tok, wo_s, loc.at[0])
    tok_load.start()
    for copy in loads[3:]:
        copy.wait()
    ds_s[...] = jnp.zeros(ds_s.shape, BF16)
    dq_s = gatt_s

    def weights_in(i):
        target = (q_s, k_s.at[pl.ds(0, 1024)], v_s.at[pl.ds(0, 1024)])[i]
        return pltpu.make_async_copy(wall.at[i], target, loc.at[1 + i])

    @pl.loop(0, 4)
    def _(g):
        for hh in range(2):
            for b in range(NBLK):
                i = 2 * hh + b
                m = 4 * g + i
                h = 2 * g + hh
                slot = i % 2
                cols = pl.ds(pl.multiple_of(h * DH, DH), DH)
                following = 2 * hh + b + 1
                nb, nh = following % 2, 2 * g + following // 2
                p_copy(slot, b * 8 + h).wait()
                if following < 4:
                    p_copy(1 - slot, nb * 8 + nh).start()
                else:

                    @pl.when(g < 3)
                    def _():
                        p_copy(1 - slot, nh).start()

                for part in range(2):
                    span = (part + 1) * 256
                    rows = pl.ds(b * BLK + part * 256, 256)
                    local = pl.ds(part * 256, 256)
                    grads = ga_s[rows, cols]
                    slope = dot_nt(grads, v_s[pl.ds(b * BLK, span), cols])
                    kept = pbuf[slot, local, pl.ds(CTX, span)].astype(F32)
                    both = jnp.sum(kept * slope, axis=-1, keepdims=True)
                    mass = jnp.sum(kept, axis=-1, keepdims=True)
                    if b:
                        slope_before = dot_nt(grads, v_s[pl.ds(1024, CTX), cols])
                        kept_before = pbuf[slot, local, pl.ds(0, CTX)].astype(F32)
                        both += jnp.sum(kept_before * slope_before, axis=-1, keepdims=True)
                        mass += jnp.sum(kept_before, axis=-1, keepdims=True)
                    both = both / mass
                    inner = (kept * (slope - both)).astype(BF16)
                    ds_s[local, pl.ds(CTX, span)] = inner
                    total = dot_nn(inner, k_s[pl.ds(b * BLK, span), cols])
                    if b:
                        inner = (kept_before * (slope_before - both)).astype(BF16)
                        ds_s[local, pl.ds(0, CTX)] = inner
                        total = total + dot_nn(inner, k_s[pl.ds(1024, CTX), cols])
                    dq_s[rows, cols] = (total * SCALE).astype(BF16)
                rows = pl.ds(b * BLK, BLK)
                first = 0 if b else CTX
                made_k = dot_tn(ds_s[:, first:], q_s[rows, cols]) * SCALE
                made_v = dot_tn(pbuf[slot, :, first:], ga_s[rows, cols])
                if b:
                    dk_s[pl.ds(1024, CTX), cols] = made_k[:CTX].astype(BF16)
                    dv_s[pl.ds(1024, CTX), cols] = made_v[:CTX].astype(BF16)
                    made_k, made_v = made_k[CTX:], made_v[CTX:]
                dk_s[rows, cols] = made_k.astype(BF16)
                dv_s[rows, cols] = made_v.astype(BF16)

                run(big_at, 8 + 2 * m, 10 + 2 * m)


                @pl.when(m == 10)
                def _():
                    for each in range(2):
                        mate_group(each).wait_recv()

                @pl.when((m >= 10) & (m < 14))
                def _(m=m):
                    for e in range(2):
                        group.give(1 - rep, 2 * (m - 10) + e)

        @pl.when(g == 3)
        def _():
            for i in range(3):
                weights_in(i).start()

        cols = pl.ds(pl.multiple_of(g * 256, 256), 256)
        own_g[g, :, :, :, 0:256] = dot_tn(rnd_s[0:1024, :], dq_s[:, cols]).astype(BF16).reshape(NC, 2, 64, 256)
        own_g[g, :, :, :, 256:512] = dot_tn(rnd_s[...], dk_s[:, cols]).astype(BF16).reshape(NC, 2, 64, 256)
        own_g[g, :, :, :, 512:768] = dot_tn(rnd_s[...], dv_s[:, cols]).astype(BF16).reshape(NC, 2, 64, 256)
        mate_group(g).start()

    run(big_at, 40, 44)
    run(group_at, 0, 2)
    for i in range(3):
        weights_in(i).wait()
    tok_load.wait()

    def gres_in(at):
        rows = pl.ds(pl.multiple_of(at * 256, 256), 256)
        return pltpu.make_async_copy(gatt.at[rows], gres_s.at[at % 2], gsem.at[at % 2])

    gres_in(0).start()

    after = pl.ds(1024, CTX)
    gctx = dot_nt(dk_s[after, :], k_s[0:1024, :]) + dot_nt(dv_s[after, :], v_s[0:1024, :])
    gctx_s[...] = gctx
    xhat, _ = norm_parts(wo_s[pl.ds(BLK - CTX, CTX), :].astype(F32))
    sum_s[32:48, :] = jnp.zeros((16, 1024), F32)
    sum_s[34:35, :] = jnp.sum(gctx * (xhat * fg[...] + fb[...]), axis=0, keepdims=True)
    for at, vector in ((35, gsg), (36, gsb), (37, gdb)):
        sum_s[at : at + 1, :] = vector[...]
    for at in range(4):
        sum_s[38 + at : 39 + at, :] = gub[:, at * 1024 : (at + 1) * 1024]
    run(group_at, 2, 5)
    states, raw = st_in[...], u_in[...]
    factor = jnp.exp(-column(decay[...]))
    scale = jnp.sqrt(1.0 - factor * factor)
    sum_s[16:32, :] = lax.dot_general(
        states[:, BLK - CTX :], gctx, (((1,), (0,)), ((), ())),
        preferred_element_type=F32, precision=lax.Precision.HIGHEST,
    )
    back = split_dot(
        lambda a, b: lax.dot_general(b, a, (((0,), (1,)), ((), ())), preferred_element_type=F32),
        gctx, sio_s[...], 3,
    )
    seeds = jnp.concatenate([jnp.zeros((16, BLK - CTX), F32), back[16:32, :]], axis=1)
    lam = lane_scan(seeds, factor, True)
    lane = lax.broadcasted_iota(jnp.int32, lam.shape, 1)
    earlier = jnp.where(lane >= 1, pltpu.roll(states, 1, 1), 0.0)
    rates = -factor * jnp.sum(lam * (earlier - (factor / scale) * raw), axis=1, keepdims=True)
    sum_s[48:64, :] = jnp.broadcast_to(rates, (16, 1024))
    driven = scale * lam
    sum_s[0:16, :] = split_dot(dot_nn, driven, rnd_s[0:BLK, :], 3)
    gd_s[...] = jnp.zeros(gd_s.shape, F32)
    gd_s[0:16, 0:BLK] = driven

    def add_in(away):
        share(away).wait_recv()
        part_s[...] = part_s[...] + got_s[away]

    def leave(at):
        rows = pl.ds(pl.multiple_of(at * 256, 256), 256)
        return pltpu.make_async_copy(rnd_s.at[rows], gtok_o.at[rows], osem.at[at])

    @pl.loop(0, 4)
    def _(at):
        rows = pl.ds(pl.multiple_of(at * 256, 256), 256)

        @pl.when(at < 3)
        def _():
            gres_in(at + 1).start()

        xhat, inverse = norm_parts(wo_s[rows, :].astype(F32))
        nb_s[...] = (
            dot_nt(dq_s[rows, :], q_s[...])
            + dot_nt(dk_s[rows, :], k_s[0:1024, :])
            + dot_nt(dv_s[rows, :], v_s[0:1024, :])
        )

        @pl.when(at < 2)
        def _():
            nb_s[...] = nb_s[...] + split_dot(
                lambda a, b: lax.dot_general(a, b, (((0,), (1,)), ((), ())), preferred_element_type=F32),
                gd_s[:, rows], sio_s[...], 3,
            )

        @pl.when(at == 1)
        def _():
            half = pl.ds(128, CTX)
            nb_s[half, :] = nb_s[half, :] + skip[...] * gctx_s[...]

        run(group_at, 5 + 3 * at, 8 + 3 * at)

        grad = nb_s[...]
        gain = jnp.sum(grad * xhat, axis=0, keepdims=True)
        shift = jnp.sum(grad, axis=0, keepdims=True)
        sum_s[32:33, :] = sum_s[32:33, :] + gain
        sum_s[33:34, :] = sum_s[33:34, :] + shift
        grad = grad * fg[...]
        grad = grad - jnp.mean(grad, axis=-1, keepdims=True) - xhat * jnp.mean(
            grad * xhat, axis=-1, keepdims=True
        )
        gres_in(at).wait()
        rnd_s[rows, :] = (gres_s[at % 2].astype(F32) + inverse * grad).astype(BF16)
        leave(at).start()

    each_device(lambda away: share(away).start())
    part_s[...] = sum_s[tile(me)]
    run(group_at, 17, 20)
    each_device(add_in)
    each_device(lambda away: spread(away).start())
    sums_o[tile(me)] = part_s[...]
    run(group_at, 20, 24)

    for which in (3 * rep, 1, 2, 4):
        big.finish(which).wait_send()
    for which in (rep, 2, 3):
        group.finish(which).wait_send()
    twin_rise = 3 * (1 - rep)
    for which in (twin_rise, 1, 2, 4):
        big.finish(which).wait_recv()
    for which in (1 - rep, 2, 3):
        group.finish(which).wait_recv()
    def settle(away):
        spread(away).wait()
        share(away).wait_send()

    each_device(settle)
    for i in range(4):
        mate_group(i).wait_send()
        leave(i).wait()
    mate_out.wait_send()
    swap.wait()

    @pl.loop(0, NC)
    def _(n):
        big.twin(3 * (1 - rep), n).wait_send()
        group.twin(1 - rep, n).wait_send()

    @pl.loop(0, NC - 1)
    def _(n):
        for slot in range(4):
            big.ring(slot, 0, n).wait_send()
        for slot in range(3):
            group.ring(slot, 0, n).wait_send()


def run_backward(*operands):
    shape = jax.ShapeDtypeStruct
    dma = pltpu.SemaphoreType.DMA
    vmem = pltpu.VMEM
    full = (1024, 1024)
    ext = (1024 + CTX, 1024)
    part = (64, 1024)
    cut = (64, 768)
    return pl.pallas_call(
        backward_kernel,
        name="backward_part",
        out_shape=(
            shape(full, BF16), shape((192, 1024), BF16), shape((5,) + part, BF16), shape((5,) + part, BF16),
            shape((4,) + cut, BF16), shape((4,) + cut, BF16), shape((64, 1024), F32),
        ),
        in_specs=any_spec(13) + vmem_spec(10),
        out_specs=any_spec(2) + vmem_spec(5),
        scratch_shapes=[
            vmem((5, NC) + part, BF16), vmem((5, NC) + part, BF16), vmem((4, NC - 1) + part, BF16),
            vmem((NC,) + part, BF16), vmem(part, F32),
            vmem((4, NC, 2) + cut, BF16), vmem((4, NC) + cut, BF16), vmem((3, NC - 1) + cut, BF16),
            vmem((NC,) + cut, BF16), vmem(cut, F32),
            vmem((NC,) + part, BF16),
            vmem(full, BF16), vmem(full, BF16), vmem(full, BF16), vmem(full, BF16), vmem(full, BF16),
            vmem(ext, BF16), vmem(ext, BF16), vmem(ext, BF16), vmem(ext, BF16), vmem(ext, BF16),
            vmem((2, BLK, CTX + BLK), BF16), vmem((BLK, CTX + BLK), BF16), vmem((2, 256, 1024), BF16),
            vmem((256, 1024), F32), vmem((1024, 128), BF16), vmem((128, 1024), F32), vmem((CTX, 1024), F32), vmem((64, 1024), F32), vmem((4 * NC, 16, 128), F32), vmem((16, 128), F32),
            dma((10,)), dma((2,)), dma((2,)), dma((4,)), dma((1,)), dma((1,)), dma((4,)), dma((4,)),
            dma((4, NC - 1)), dma((4, NC - 1)), dma((3, NC - 1)), dma((3, NC - 1)),
            dma((NC,)), dma((NC,)), dma((NC,)), dma((NC,)), dma((5,)), dma((5,)), dma((4,)), dma((4,)),
            dma((4 * NC,)), dma((4 * NC,)), dma((4 * NC,)), dma((4 * NC,)), dma((1,)), dma((1,)),
        ],
        compiler_params=pltpu.CompilerParams(
            collective_id=2, has_side_effects=True, vmem_limit_bytes=VMEM_LIMIT
        ),
    )(*operands)


def outputs_kernel(
    result, gtok, finb, finrb, fing, finrg, find, findr, sums,
    result_o, gtok_o, dup_o, do_o, dq_o, dk_o, dv_o, ddown_o, gfg_o, gfb_o, gskip_o, gsg_o, gsb_o, gdb_o, gub_o, grate_o,
    gsi_o, gso_o, held, came, left,
):
    rep, shard = lax.axis_index("rep"), lax.axis_index("shard")
    pairs = ((result, result_o), (gtok, gtok_o))

    def take(which, at):
        rows = pl.ds(at * 256, 256)
        return pltpu.make_async_copy(pairs[which][0].at[rows], held.at[which, rows], came.at[which, at])

    def give(which, at):
        rows = pl.ds(at * 256, 256)
        return pltpu.make_async_copy(held.at[which, rows], pairs[which][1].at[rows], left.at[which, at])

    every = [(which, at) for which in range(2) for at in range(4)]
    for each in every:
        take(*each).start()
    for each in every:
        take(*each).wait()
        give(*each).start()
    for i in range(4):
        dup_o[:, i * 1024 : (i + 1) * 1024] = finb[i].astype(F32) + finrb[i].astype(F32)
    do_o[...] = finb[4].astype(F32) + finrb[4].astype(F32)
    for g in range(4):
        for i, out in enumerate((dq_o, dk_o, dv_o)):
            cols = slice(i * 256, (i + 1) * 256)
            out[:, g * 256 : (g + 1) * 256] = fing[g, :, cols].astype(F32) + finrg[g, :, cols].astype(F32)
    mine = pl.ds(pl.multiple_of(rep * 64, 64), 192)
    theirs = pl.ds(pl.multiple_of((1 - rep) * 64, 64), 192)
    ddown_o[...] = jnp.zeros((256, 1024), F32)
    ddown_o[mine, :] = find[...].astype(F32)
    ddown_o[theirs, :] = ddown_o[theirs, :] + findr[...].astype(F32)
    for at, out in enumerate((gfg_o, gfb_o, gskip_o, gsg_o, gsb_o, gdb_o)):
        out[...] = sums[32 + at : 33 + at, :]
    for at in range(4):
        gub_o[:, at * 1024 : (at + 1) * 1024] = sums[38 + at : 39 + at, :]
    same = lax.broadcasted_iota(jnp.int32, (16, 128), 0) == lax.broadcasted_iota(jnp.int32, (16, 128), 1)
    grate_o[...] = jnp.sum(jnp.where(same, sums[48:64, 0:128], 0.0), axis=0)[0:16]
    shift = (1024 - 64 * shard) % 1024
    gsi_o[...] = pltpu.roll(sums[0:16, :], shift, 1)[:, 0:64]
    gso_o[...] = pltpu.roll(sums[16:32, :], shift, 1)[:, 0:64]
    for each in every:
        give(*each).wait()


def run_outputs(*operands):
    shape = jax.ShapeDtypeStruct
    row = shape((1, 1024), F32)
    part = shape((64, 1024), F32)
    return pl.pallas_call(
        outputs_kernel,
        name="outputs_part",
        out_shape=(
            shape((1024, 1024), BF16), shape((1024, 1024), BF16),
            shape((64, 4096), F32), part, part, part, part, shape((256, 1024), F32),
            row, row, row, row, row, row, shape((1, 4096), F32), shape((16,), F32),
            shape((16, 64), F32), shape((16, 64), F32),
        ),
        in_specs=any_spec(2) + vmem_spec(7),
        out_specs=any_spec(2) + vmem_spec(16),
        scratch_shapes=[
            pltpu.VMEM((2, 1024, 1024), BF16),
            pltpu.SemaphoreType.DMA((2, 4)), pltpu.SemaphoreType.DMA((2, 4)),
        ],
        compiler_params=pltpu.CompilerParams(vmem_limit_bytes=VMEM_LIMIT),
    )(*operands)


def fused_device(
    tokens, lengths, first_gain, first_bias, decay_rates, state_in, state_out, skip_gain,
    query_weight, key_weight, value_weight, output_weight, second_gain, second_bias,
    up_weight, up_bias, down_weight, down_bias, cotangent,
):
    tok = tokens.reshape(1024, 1024)
    cot = cotangent.reshape(1024, 1024)
    fg, fb, skip, sg, sb, dnb, upb, decay = (
        v.reshape(1, -1)
        for v in (
            first_gain, first_bias, skip_gain, second_gain, second_bias, down_bias, up_bias, decay_rates,
        )
    )
    wall, wdpre, sio, rnd, q, kx, vx, att, res, sec, p, u, st = run_forward(
        tok, query_weight, key_weight, value_weight, output_weight, up_weight, down_weight, state_in, state_out,
        fg, fb, skip, sg, sb, decay,
    )
    result, gatt, dwown, dwmate, find, gdb, gub, gsg, gsb = run_feed(
        sec, res, wall, down_weight, wdpre, cot, lengths, upb, dnb, sg
    )
    gtok, findr, finb, finrb, fing, finrg, sums = run_backward(
        dwown, dwmate, find, gatt, att, wall, q, kx, vx, rnd, p, tok, sio,
        u, st, fg, fb, skip, decay, gsg, gsb, gdb, gub,
    )
    result, gtok, dup, do, dq, dk, dv, ddown, *rest = run_outputs(
        result, gtok, finb, finrb, fing, finrg, find, findr, sums
    )
    gfg, gfb, gskip, gsg, gsb, gdb, gub, grate, gsi, gso = rest
    return (
        result.reshape(1, 1024, 1024), gtok.reshape(1, 1024, 1024), gfg[0], gfb[0],
        grate, gsi, gso, gskip[0], dq, dk, dv, do, gsg[0], gsb[0], dup, gub[0], ddown, gdb[0],
    )


NORM_EPS = 1e-05
NEG_LARGE = -1e30
HIGHEST = lax.Precision.HIGHEST


def layer_norm(hidden, gain_vec, bias_vec):
    average = jnp.mean(hidden, axis=-1, keepdims=True)
    centred = hidden - average
    spread = jnp.mean(centred * centred, axis=-1, keepdims=True)
    return centred * lax.rsqrt(spread + NORM_EPS) * gain_vec + bias_vec


def state_context(driven_raw, normed, decay_rates, state_out, skip_gain):
    decay_factor = jnp.exp(-decay_rates)
    driven = driven_raw * jnp.sqrt(1.0 - decay_factor * decay_factor)
    factors = jnp.broadcast_to(decay_factor, driven.shape)

    def combine(earlier, subsequent):
        return (earlier[0] * subsequent[0], subsequent[0] * earlier[1] + subsequent[1])

    states = lax.associative_scan(combine, (factors, driven), axis=1)[1]
    seq_count = driven_raw.shape[0]
    state_width = driven_raw.shape[2]
    model_width = normed.shape[2]
    tail_states = states.reshape(seq_count, NBLK, BLK, state_width)[:, :, BLK - CTX :, :]
    skipped = normed.reshape(seq_count, NBLK, BLK, model_width)[:, :, BLK - CTX :, :]
    outputs = (
        jnp.einsum("sbcp,pd->sbcd", tail_states, state_out, precision=HIGHEST) + skip_gain * skipped
    )
    empty_ctx = jnp.zeros((seq_count, 1, CTX, model_width), jnp.float32)
    return jnp.concatenate([empty_ctx, outputs[:, : NBLK - 1]], axis=1)


def block_scores(queries, key_rows, ctx_keys, ctx_valid):
    row_count = queries.shape[0]
    head_count = queries.shape[1] // DH
    query_heads = queries.reshape(row_count, head_count, DH)
    key_heads = jnp.concatenate([ctx_keys, key_rows], 0).reshape(-1, head_count, DH)
    scores = jnp.einsum(
        "qhd,khd->hqk", query_heads, key_heads, preferred_element_type=jnp.float32
    ) * DH ** (-0.5)
    causal = lax.broadcasted_iota(jnp.int32, (row_count, row_count), 0) >= lax.broadcasted_iota(
        jnp.int32, (row_count, row_count), 1
    )
    allowed = jnp.concatenate(
        [jnp.broadcast_to(ctx_valid[None, :], (row_count, ctx_keys.shape[0])), causal], axis=1
    )
    return (jnp.where(allowed[None], scores, NEG_LARGE), query_heads, key_heads)


def attend_forward(block_item):
    queries, key_rows, value_rows, ctx_keys, ctx_values, ctx_valid = block_item
    scores, query_heads, key_heads = block_scores(queries, key_rows, ctx_keys, ctx_valid)
    row_max = jnp.max(scores, axis=-1, keepdims=True)
    expos = jnp.exp(scores - row_max)
    denominator = jnp.sum(expos, axis=-1, keepdims=True)
    weights = (expos / denominator).astype(jnp.bfloat16)
    value_heads = jnp.concatenate([ctx_values, value_rows], 0).reshape(key_heads.shape)
    attended = jnp.einsum("hqk,khd->qhd", weights, value_heads, preferred_element_type=jnp.float32)
    return (
        attended.reshape(queries.shape).astype(jnp.bfloat16),
        (row_max + jnp.log(denominator))[..., 0],
    )


def attend_backward(block_item):
    queries, key_rows, value_rows, ctx_keys, ctx_values, ctx_valid, log_total, grad_attended = (
        block_item
    )
    scores, query_heads, key_heads = block_scores(queries, key_rows, ctx_keys, ctx_valid)
    probs = jnp.exp(scores - log_total[..., None])
    value_heads = jnp.concatenate([ctx_values, value_rows], 0).reshape(key_heads.shape)
    grad_heads = grad_attended.reshape(query_heads.shape)
    grad_probs = jnp.einsum(
        "qhd,khd->hqk", grad_heads, value_heads, preferred_element_type=jnp.float32
    )
    grad_scores = (
        probs * (grad_probs - jnp.sum(probs * grad_probs, axis=-1, keepdims=True))
    ).astype(jnp.bfloat16)
    grad_values = jnp.einsum(
        "hqk,qhd->khd", probs.astype(jnp.bfloat16), grad_heads, preferred_element_type=jnp.float32
    )
    grad_queries = jnp.einsum(
        "hqk,khd->qhd", grad_scores, key_heads, preferred_element_type=jnp.float32
    ) * DH ** (-0.5)
    grad_keys = jnp.einsum(
        "hqk,qhd->khd", grad_scores, query_heads, preferred_element_type=jnp.float32
    ) * DH ** (-0.5)
    ctx_count = ctx_keys.shape[0]
    model_width = queries.shape[1]
    grad_keys = grad_keys.reshape(-1, model_width).astype(jnp.bfloat16)
    grad_values = grad_values.reshape(-1, model_width).astype(jnp.bfloat16)
    return (
        grad_queries.reshape(queries.shape).astype(jnp.bfloat16),
        grad_keys[ctx_count:],
        grad_values[ctx_count:],
        grad_keys[:ctx_count],
        grad_values[:ctx_count],
    )


def per_device(
    tokens,
    lengths,
    first_gain,
    first_bias,
    decay_rates,
    state_in,
    state_out,
    skip_gain,
    query_weight,
    key_weight,
    value_weight,
    output_weight,
    second_gain,
    second_bias,
    up_weight,
    up_bias,
    down_weight,
    down_bias,
    cotangent,
):
    full_query, full_key, full_value, full_output, full_up, full_down, full_in, full_out = (
        lax.all_gather(query_weight, "shard", axis=0, tiled=True),
        lax.all_gather(key_weight, "shard", axis=0, tiled=True),
        lax.all_gather(value_weight, "shard", axis=0, tiled=True),
        lax.all_gather(output_weight, "shard", axis=0, tiled=True),
        lax.all_gather(up_weight, "shard", axis=0, tiled=True),
        lax.all_gather(down_weight, "shard", axis=0, tiled=True),
        lax.all_gather(state_in, "shard", axis=1, tiled=True),
        lax.all_gather(state_out, "shard", axis=1, tiled=True),
    )
    seq_count, seq_len, model_width = tokens.shape
    row_count = seq_count * seq_len
    block_count = seq_count * NBLK
    positions = lax.broadcasted_iota(jnp.int32, (seq_count, seq_len), 1)
    row_mask = (positions < lengths[:, None]).astype(jnp.float32).reshape(row_count, 1)
    block_index = lax.broadcasted_iota(jnp.int32, (seq_count, NBLK, CTX), 1)
    ctx_valid = (block_index > 0).reshape(block_count, CTX)
    token_rows = tokens.astype(jnp.float32)
    normed, first_pullback = jax.vjp(layer_norm, token_rows, first_gain, first_bias)
    rounded = normed.astype(jnp.bfloat16)
    driven_raw = jnp.einsum("std,pd->stp", rounded, full_in, preferred_element_type=jnp.float32)
    context, state_pullback = jax.vjp(
        state_context, driven_raw, normed, decay_rates, full_out.astype(jnp.float32), skip_gain
    )
    ctx_rows = context.astype(jnp.bfloat16).reshape(block_count * CTX, model_width)
    flat_rounded = rounded.reshape(row_count, model_width)
    query_rows = jnp.dot(flat_rounded, full_query, preferred_element_type=jnp.float32).astype(
        jnp.bfloat16
    )
    key_rows = jnp.dot(flat_rounded, full_key, preferred_element_type=jnp.float32).astype(
        jnp.bfloat16
    )
    value_rows = jnp.dot(flat_rounded, full_value, preferred_element_type=jnp.float32).astype(
        jnp.bfloat16
    )
    ctx_keys = jnp.dot(ctx_rows, full_key, preferred_element_type=jnp.float32).astype(jnp.bfloat16)
    ctx_values = jnp.dot(ctx_rows, full_value, preferred_element_type=jnp.float32).astype(
        jnp.bfloat16
    )
    block_inputs = (
        query_rows.reshape(block_count, BLK, model_width),
        key_rows.reshape(block_count, BLK, model_width),
        value_rows.reshape(block_count, BLK, model_width),
        ctx_keys.reshape(block_count, CTX, model_width),
        ctx_values.reshape(block_count, CTX, model_width),
        ctx_valid,
    )
    attended, log_total = lax.map(attend_forward, block_inputs)
    attended_rows = attended.reshape(row_count, model_width)
    residual = token_rows.reshape(row_count, model_width) + jnp.dot(
        attended_rows, full_output, preferred_element_type=jnp.float32
    )
    second, second_pullback = jax.vjp(layer_norm, residual, second_gain, second_bias)
    second_rows = second.astype(jnp.bfloat16)
    hidden = jnp.dot(second_rows, full_up, preferred_element_type=jnp.float32) + up_bias
    active, gelu_pullback = jax.vjp(jax.nn.gelu, hidden)
    active_rows = active.astype(jnp.bfloat16)
    branch = jnp.dot(active_rows, full_down, preferred_element_type=jnp.float32) + down_bias
    result = (
        ((residual + branch) * row_mask)
        .astype(jnp.bfloat16)
        .reshape(seq_count, seq_len, model_width)
    )
    full_query, full_key, full_value, full_output, full_up, full_down, full_in, full_out = (
        lax.all_gather(query_weight, "shard", axis=0, tiled=True),
        lax.all_gather(key_weight, "shard", axis=0, tiled=True),
        lax.all_gather(value_weight, "shard", axis=0, tiled=True),
        lax.all_gather(output_weight, "shard", axis=0, tiled=True),
        lax.all_gather(up_weight, "shard", axis=0, tiled=True),
        lax.all_gather(down_weight, "shard", axis=0, tiled=True),
        lax.all_gather(state_in, "shard", axis=1, tiled=True),
        lax.all_gather(state_out, "shard", axis=1, tiled=True),
    )
    grad_branch = cotangent.reshape(row_count, model_width).astype(jnp.float32) * row_mask
    branch_rounded = grad_branch.astype(jnp.bfloat16)
    grad_down = jnp.einsum(
        "rf,rd->fd", active_rows, branch_rounded, preferred_element_type=jnp.float32
    )
    grad_down_bias = jnp.sum(grad_branch, axis=0)
    grad_active = jnp.einsum(
        "rd,fd->rf", branch_rounded, full_down, preferred_element_type=jnp.float32
    )
    (grad_hidden,) = gelu_pullback(grad_active)
    hidden_rounded = grad_hidden.astype(jnp.bfloat16)
    grad_up = jnp.einsum(
        "rd,rf->df", second_rows, hidden_rounded, preferred_element_type=jnp.float32
    )
    grad_up_bias = jnp.sum(hidden_rounded.astype(jnp.float32), axis=0)
    grad_second = jnp.einsum(
        "rf,df->rd", hidden_rounded, full_up, preferred_element_type=jnp.float32
    )
    grad_residual_part, grad_second_gain, grad_second_bias = second_pullback(grad_second)
    grad_residual = grad_branch + grad_residual_part
    residual_rounded = grad_residual.astype(jnp.bfloat16)
    grad_output = jnp.einsum(
        "rd,re->de", attended_rows, residual_rounded, preferred_element_type=jnp.float32
    )
    grad_attended = jnp.einsum(
        "re,de->rd", residual_rounded, full_output, preferred_element_type=jnp.float32
    ).astype(jnp.bfloat16)
    grad_query_rows, grad_key_rows, grad_value_rows, grad_ctx_keys, grad_ctx_values = lax.map(
        attend_backward,
        block_inputs + (log_total, grad_attended.reshape(block_count, BLK, model_width)),
    )
    grad_query_rows = grad_query_rows.reshape(row_count, model_width)
    grad_key_rows = grad_key_rows.reshape(row_count, model_width)
    grad_value_rows = grad_value_rows.reshape(row_count, model_width)
    grad_ctx_keys = grad_ctx_keys.reshape(block_count * CTX, model_width)
    grad_ctx_values = grad_ctx_values.reshape(block_count * CTX, model_width)
    grad_query = jnp.einsum(
        "rd,re->de", flat_rounded, grad_query_rows, preferred_element_type=jnp.float32
    )
    grad_key = jnp.einsum(
        "rd,re->de", flat_rounded, grad_key_rows, preferred_element_type=jnp.float32
    ) + jnp.einsum("rd,re->de", ctx_rows, grad_ctx_keys, preferred_element_type=jnp.float32)
    grad_value = jnp.einsum(
        "rd,re->de", flat_rounded, grad_value_rows, preferred_element_type=jnp.float32
    ) + jnp.einsum("rd,re->de", ctx_rows, grad_ctx_values, preferred_element_type=jnp.float32)
    grad_normed = (
        jnp.einsum("re,de->rd", grad_query_rows, full_query, preferred_element_type=jnp.float32)
        + jnp.einsum("re,de->rd", grad_key_rows, full_key, preferred_element_type=jnp.float32)
        + jnp.einsum("re,de->rd", grad_value_rows, full_value, preferred_element_type=jnp.float32)
    )
    grad_context = jnp.einsum(
        "re,de->rd", grad_ctx_keys, full_key, preferred_element_type=jnp.float32
    ) + jnp.einsum("re,de->rd", grad_ctx_values, full_value, preferred_element_type=jnp.float32)
    grad_context = grad_context.reshape(seq_count, NBLK, CTX, model_width)
    grad_driven, state_normed, grad_rates, grad_state_out, grad_skip = state_pullback(grad_context)
    grad_in = jnp.einsum(
        "stp,std->pd", grad_driven, rounded, precision=HIGHEST, preferred_element_type=jnp.float32
    )
    state_rounded = jnp.einsum(
        "stp,pd->std", grad_driven, full_in, precision=HIGHEST, preferred_element_type=jnp.float32
    )
    normed_total = (
        grad_normed.reshape(seq_count, seq_len, model_width) + state_rounded + state_normed
    )
    tokens_part, grad_first_gain, grad_first_bias = first_pullback(normed_total)
    grad_tokens = (tokens_part + grad_residual.reshape(seq_count, seq_len, model_width)).astype(
        jnp.bfloat16
    )
    piece_query, piece_key, piece_value, piece_output, piece_up, piece_down, piece_in, piece_out = (
        lax.psum_scatter(grad_query, "shard", scatter_dimension=0, tiled=True),
        lax.psum_scatter(grad_key, "shard", scatter_dimension=0, tiled=True),
        lax.psum_scatter(grad_value, "shard", scatter_dimension=0, tiled=True),
        lax.psum_scatter(grad_output, "shard", scatter_dimension=0, tiled=True),
        lax.psum_scatter(grad_up, "shard", scatter_dimension=0, tiled=True),
        lax.psum_scatter(grad_down, "shard", scatter_dimension=0, tiled=True),
        lax.psum_scatter(grad_in, "shard", scatter_dimension=1, tiled=True),
        lax.psum_scatter(grad_state_out, "shard", scatter_dimension=1, tiled=True),
    )
    piece_query, piece_key, piece_value, piece_output, piece_up, piece_down, piece_in, piece_out = (
        lax.psum(piece_query.astype(jnp.bfloat16), "rep").astype(jnp.float32),
        lax.psum(piece_key.astype(jnp.bfloat16), "rep").astype(jnp.float32),
        lax.psum(piece_value.astype(jnp.bfloat16), "rep").astype(jnp.float32),
        lax.psum(piece_output.astype(jnp.bfloat16), "rep").astype(jnp.float32),
        lax.psum(piece_up.astype(jnp.bfloat16), "rep").astype(jnp.float32),
        lax.psum(piece_down.astype(jnp.bfloat16), "rep").astype(jnp.float32),
        lax.psum(piece_in.astype(jnp.bfloat16), "rep").astype(jnp.float32),
        lax.psum(piece_out.astype(jnp.bfloat16), "rep").astype(jnp.float32),
    )
    (
        sum_first_gain,
        sum_first_bias,
        sum_rates,
        sum_skip,
        sum_second_gain,
        sum_second_bias,
        sum_up_bias,
        sum_down_bias,
    ) = lax.psum(
        (
            grad_first_gain,
            grad_first_bias,
            grad_rates,
            grad_skip,
            grad_second_gain,
            grad_second_bias,
            grad_up_bias,
            grad_down_bias,
        ),
        ("rep", "shard"),
    )
    return (
        result,
        grad_tokens,
        sum_first_gain,
        sum_first_bias,
        sum_rates,
        piece_in,
        piece_out,
        sum_skip,
        piece_query,
        piece_key,
        piece_value,
        piece_output,
        sum_second_gain,
        sum_second_bias,
        piece_up,
        sum_up_bias,
        piece_down,
        sum_down_bias,
    )


def solution(mesh):
    placed = (
        P(("rep", "shard"), None, None),
        P(("rep", "shard")),
        P(),
        P(),
        P(),
        P(None, "shard"),
        P(None, "shard"),
        P(),
        P("shard", None),
        P("shard", None),
        P("shard", None),
        P("shard", None),
        P(),
        P(),
        P("shard", None),
        P(),
        P("shard", None),
        P(),
        P(("rep", "shard"), None, None),
    )
    fused = mesh.shape["rep"] == 2 and mesh.shape["shard"] == 2 * NC
    return jax.shard_map(
        fused_device if fused else per_device,
        mesh=mesh,
        in_specs=placed,
        out_specs=(
            P(("rep", "shard"), None, None),
            P(("rep", "shard"), None, None),
            P(),
            P(),
            P(),
            P(None, "shard"),
            P(None, "shard"),
            P(),
            P("shard", None),
            P("shard", None),
            P("shard", None),
            P("shard", None),
            P(),
            P(),
            P("shard", None),
            P(),
            P("shard", None),
            P(),
        ),
        check_vma=False,
    )
```

```python
import functools
import math

import jax
import jax.numpy as jnp
from jax import lax
from jax.experimental import pallas as pl
from jax.experimental.pallas import tpu as pltpu
from jax.sharding import PartitionSpec as P

DH = 128
BLK = 512
CTX = 128
NBLK = 2
EPS = 1e-05
NEG = -1e30
SCALE = DH ** (-0.5)
MESH = pl.DeviceIdType.MESH
F32 = jnp.float32
BF16 = jnp.bfloat16
VMEM_LIMIT = 66_000_000
NC = 8


def chip_at(pos):
    turned = pos // 4
    return (1 - turned) * (2 * pos) + turned * (2 * (7 - pos) + 1)


class Net:
    def __init__(self):
        self.rep = lax.axis_index("rep")
        self.shard = lax.axis_index("shard")
        self.core = self.shard % 2
        chip = self.shard // 2
        z, y = chip // 2, chip % 2
        self.pos = (1 - y) * z + y * (7 - z)
        self.step = 1 - 2 * self.core
        self.mate = (self.rep, 2 * chip + 1 - self.core)
        self.twin = (1 - self.rep, self.shard)

    def at(self, hops, core):
        return 2 * chip_at((self.pos + self.step * hops + 4 * NC) % NC) + core

    def along(self, hops):
        return (self.rep, self.at(hops, self.core))

    def greet(self):
        barrier = pltpu.get_barrier_semaphore()
        for device in (self.along(1), self.along(-1), self.mate, self.twin):
            pl.semaphore_signal(barrier, inc=1, device_id=device, device_id_type=MESH)
        pl.semaphore_wait(barrier, 4)


def rcopy(src, dst, send, recv, device):
    return pltpu.make_async_remote_copy(
        src_ref=src, dst_ref=dst, send_sem=send, recv_sem=recv, device_id=device, device_id_type=MESH
    )


def dot_nn(a, b):
    return lax.dot_general(a, b, (((1,), (0,)), ((), ())), preferred_element_type=F32)


def dot_nt(a, b):
    return lax.dot_general(a, b, (((1,), (1,)), ((), ())), preferred_element_type=F32)


def dot_tn(a, b):
    return lax.dot_general(a, b, (((0,), (0,)), ((), ())), preferred_element_type=F32)


def norm_parts(rows):
    centred = rows - jnp.mean(rows, axis=-1, keepdims=True)
    spread = jnp.mean(centred * centred, axis=-1, keepdims=True)
    inverse = lax.rsqrt(spread + EPS)
    return centred * inverse, inverse


def split_dot(dot, left, right, narrow):
    total = None
    rest = left
    for _ in range(narrow):
        term = rest.astype(BF16)
        part = dot(term, right)
        total = part if total is None else total + part
        rest = rest - term.astype(F32)
    return total


def lane_scan(values, factor, reverse):
    width = values.shape[1]
    lane = lax.broadcasted_iota(jnp.int32, values.shape, 1)
    shift = 1
    power = factor
    while shift < width:
        if reverse:
            moved = pltpu.roll(values, width - shift, 1)
            moved = jnp.where(lane < width - shift, moved, 0.0)
        else:
            moved = pltpu.roll(values, shift, 1)
            moved = jnp.where(lane >= shift, moved, 0.0)
        values = values + power * moved
        power = power * power
        shift *= 2
    return values


def forward_kernel(
    tok, wq, wk, wv, wo, wup, wdn, s_in, s_out, fg, fb, skip, sg, sb, decay,
    wall, wdpre, sio_all, rnd_o, q_o, k_o, v_o, att_o, res_o, sec_o, p_o, u_o, st_o,
    tok_s, rnd_s, w_s, q_s, k_s, v_s, att_s, res_s, sec_s, pbuf, nctx, sio_s,
    own_s, sio_own, loc, rs, rr, ss, sr, cs, cr, xs, xr, outs, psem, ds, dr,
):
    net = Net()
    rep, core = net.rep, net.core
    rows_of = 64
    width = 1024

    def block(shard):
        return pl.ds(pl.multiple_of(shard * rows_of, rows_of), rows_of)

    mine = block(net.shard)
    own = [wq, wk, wv, wo]
    copies = [pltpu.make_async_copy(own[i], own_s.at[i], loc.at[i]) for i in range(4)]
    copies += [
        pltpu.make_async_copy(wup.at[:, pl.ds(i * width, width)], own_s.at[4 + i], loc.at[4 + i])
        for i in range(4)
    ]
    small = pltpu.make_async_copy(sio_own, sio_all.at[mine], loc.at[8])
    arrive = pltpu.make_async_copy(tok, tok_s, loc.at[9])
    for copy in copies:
        copy.start()
    arrive.start()
    packed = jnp.concatenate(
        [s_in[...].astype(F32), s_out[...].astype(F32), jnp.zeros((96, rows_of), F32)], axis=0
    )
    sio_own[...] = packed.T.astype(BF16)
    small.start()
    net.greet()
    for copy in copies:
        copy.wait()

    def piece(slot):
        if isinstance(slot, int) and slot < 2:
            return 1 if slot else 2 * rep
        later = slot - 2
        return 3 + later + (1 + 3 * rep) * ((3 - later) // 3) - (later % 2) * (3 - later) // 2

    def ring(slot, way, hop, which, where):
        ref = wall.at[which, where]
        sems = rs.at[slot, way, hop], rr.at[slot, way, hop]
        return rcopy(ref, ref, *sems, net.along(1 - 2 * way))

    def ring_own(slot, way):
        which = piece(slot)
        sems = rs.at[slot, way, 0], rr.at[slot, way, 0]
        ref = wall.at[which, mine]
        rcopy(own_s.at[which], ref, *sems, net.along(1 - 2 * way)).start()

    def ring_small(way, hop, where):
        ref = sio_all.at[where]
        return rcopy(ref, ref, ss.at[way, hop], sr.at[way, hop], net.along(1 - 2 * way))

    def mate(which, index, where):
        ref = wall.at[which, where]
        return rcopy(ref, ref, cs.at[which, index], cr.at[which, index], net.mate)

    def mate_small(index, where):
        ref = sio_all.at[where]
        return rcopy(ref, ref, cs.at[8, index], cr.at[8, index], net.mate)

    def twin(turn, index, which, where):
        ref = wall.at[which, where]
        return rcopy(ref, ref, xs.at[turn, index], xr.at[turn, index], net.twin)

    hand = rcopy(wdn, wdpre.at[0], ds.at[0], dr.at[0], net.along(1))
    hand_on = rcopy(wdpre.at[0], wdpre.at[1], ds.at[1], dr.at[1], net.mate)

    def source(way, hop):
        return block(net.at((2 * way - 1) * (hop + 1), core))

    def serve(slot, way, hop):
        which = piece(slot)
        where = source(way, hop)
        ring(slot, way, hop, which, where).wait_recv()

        @pl.when(hop < 3 - way)
        def _():
            ring(slot, way, hop + 1, which, where).start()

        mate(which, 1 + 2 * hop + way, where).start()

    def serve_out(slot, turn, way, hop):
        twin(turn, 2 * hop + way, piece(slot), source(way, hop)).start()

    def serve_in(turn, way, hop):
        where = source(way, hop)
        which = 2 * (1 - rep) if turn == 0 else 7 - 3 * rep
        twin(turn, 2 * hop + way, which, where).wait_recv()
        mate(which, 1 + 2 * hop + way, where).start()

    for slot in range(2):
        for way in range(2):
            ring_own(slot, way)
    small.wait()
    for way in range(2):
        ring_small(way, 0, mine).start()
    mate_small(0, mine).start()
    for which in range(8):
        rcopy(own_s.at[which], wall.at[which, mine], cs.at[which, 0], cr.at[which, 0], net.mate).start()
    keep = [pltpu.make_async_copy(own_s.at[i], wall.at[i, mine], loc.at[i]) for i in range(8)]
    for copy in keep:
        copy.start()
    arrive.wait()

    def first_norm(at):
        rows = pl.ds(pl.multiple_of(at * 128, 128), 128)
        xhat, _ = norm_parts(tok_s[rows, :].astype(F32))
        normed = xhat * fg[...] + fb[...]
        rnd_s[rows, :] = normed.astype(BF16)

    order = [
        (hop, slot, way) for hop in range(4) for slot in range(2) for way in range(2) if hop < 4 - way
    ]
    owed = []
    for n, (hop, slot, way) in enumerate(order):
        if n % 2 == 0:
            first_norm(n // 2)
        serve(slot, way, hop)
        if slot == 0:
            serve_out(0, 0, way, hop)
            owed.append((n, way, hop))
        else:
            where = source(way, hop)
            ring_small(way, hop, where).wait_recv()
            if hop < 3 - way:
                ring_small(way, hop + 1, where).start()
            mate_small(1 + 2 * hop + way, where).start()
        if n in (12, 13):
            for later in range(2):
                for each in range(2):
                    ring_own((2 if n == 12 else 4) + later, each)
        if owed and n - owed[0][0] >= 4:
            serve_in(0, *owed.pop(0)[1:])
    first_norm(7)
    for each in owed:
        serve_in(0, *each[1:])

    def event(m):
        half, place = m // 14, m % 14
        late = place // 12
        hop = place // 4
        index = ((place % 4) // 2) * (1 - late) + (place - 12) * late
        way = (place % 2) * (1 - late)
        slot = 2 + 2 * half + index
        serve(slot, way, hop)

        @pl.when(slot == 2)
        def _():
            serve_out(2, 1, way, hop)

        @pl.when(m == 10)
        def _():
            hand.start()

        @pl.when((m >= 8) & (m <= 20) & (m % 4 < 2))
        def _():
            serve_in(1, m % 2, (m - 8) // 4)

    xhat, _ = norm_parts(tok_s[pl.ds(BLK - CTX, CTX), :].astype(F32))
    nctx[...] = xhat * fg[...] + fb[...]

    @pl.loop(0, NC)
    def _(index):
        where = block(0)
        mate_small(index, where).wait_recv()
        for which in range(3):
            mate(which, index, where).wait_recv()

    for copy in keep:
        copy.wait()
    loads = [pltpu.make_async_copy(sio_all, sio_s, loc.at[8])]
    loads += [pltpu.make_async_copy(wall.at[i], w_s.at[i], loc.at[i]) for i in range(3)]
    for copy in loads:
        copy.start()
    loads[0].wait()
    u_all = lax.dot_general(
        sio_s[...], rnd_s[pl.ds(0, BLK), :], (((0,), (1,)), ((), ())), preferred_element_type=F32
    )
    factor = jnp.exp(-column(decay[...]))
    raw = u_all[0:16, :]
    u_o[...] = raw
    states = lane_scan(raw * jnp.sqrt(1.0 - factor * factor), factor, False)
    st_o[...] = states
    tail = states[:, BLK - CTX :]
    padded = jnp.concatenate(
        [jnp.zeros((16, CTX), F32), tail, jnp.zeros((96, CTX), F32)], axis=0
    )
    made = split_dot(
        lambda a, b: lax.dot_general(a, b, (((0,), (1,)), ((), ())), preferred_element_type=F32),
        padded, sio_s[...], 3,
    )
    rnd_s[pl.ds(1024, CTX), :] = (made + skip[...] * nctx[...]).astype(BF16)
    finals = [pltpu.make_async_copy(rnd_s, rnd_o, outs.at[0])]
    finals[0].start()

    for copy in loads[1:]:
        copy.wait()

    @pl.loop(0, 4)
    def _(at):
        cols = pl.ds(pl.multiple_of(at * 256, 256), 256)
        q_s[:, cols] = dot_nn(rnd_s[pl.ds(0, 1024), :], w_s[0, :, cols]).astype(BF16)
        event(2 * at)
        k_s[:, cols] = dot_nn(rnd_s[...], w_s[1, :, cols]).astype(BF16)
        v_s[:, cols] = dot_nn(rnd_s[...], w_s[2, :, cols]).astype(BF16)
        event(2 * at + 1)

    for i, (a, b) in enumerate(((q_s, q_o), (k_s, k_o), (v_s, v_o))):
        finals.append(pltpu.make_async_copy(a, b, outs.at[1 + i]))
        finals[-1].start()

    for half in range(2):
        pbuf[half] = jnp.zeros((BLK, CTX + BLK), BF16)

    def p_copy(slot, at):
        return pltpu.make_async_copy(pbuf.at[slot], p_o.at[at], psem.at[slot])

    for b in range(NBLK):

        @pl.loop(0, 8)
        def _(h, b=b):
            cols = pl.ds(pl.multiple_of(h * DH, DH), DH)
            slot = h % 2
            if b == 0:

                @pl.when(h >= 2)
                def _():
                    p_copy(slot, h).wait()
            else:
                p_copy(slot, h).wait()
            for i in range(2):
                span = (i + 1) * 256
                rows = pl.ds(b * BLK + i * 256, 256)
                queries = q_s[rows, cols]
                scores = dot_nt(queries, k_s[pl.ds(b * BLK, span), cols]) * SCALE
                ahead = lax.broadcasted_iota(jnp.int32, scores.shape, 0) + i * 256
                scores = jnp.where(
                    ahead >= lax.broadcasted_iota(jnp.int32, scores.shape, 1), scores, NEG
                )
                top = jnp.max(scores, axis=-1, keepdims=True)
                if b:
                    before = dot_nt(queries, k_s[pl.ds(1024, CTX), cols]) * SCALE
                    top = jnp.maximum(top, jnp.max(before, axis=-1, keepdims=True))
                expos = jnp.exp(scores - top)
                total = jnp.sum(expos, axis=-1, keepdims=True)
                if b:
                    expos_before = jnp.exp(before - top)
                    total = total + jnp.sum(expos_before, axis=-1, keepdims=True)
                share = 1.0 / total
                weights = (expos * share).astype(BF16)
                mixed = dot_nn(weights, v_s[pl.ds(b * BLK, span), cols])
                pbuf[slot, pl.ds(i * 256, 256), pl.ds(CTX, span)] = weights
                if b:
                    weights = (expos_before * share).astype(BF16)
                    mixed = mixed + dot_nn(weights, v_s[pl.ds(1024, CTX), cols])
                    pbuf[slot, pl.ds(i * 256, 256), pl.ds(0, CTX)] = weights
                att_s[rows, cols] = mixed.astype(BF16)
            p_copy(slot, b * 8 + h).start()

            event(8 + 8 * b + h)

    finals.append(pltpu.make_async_copy(att_s, att_o, outs.at[4]))
    finals[-1].start()

    @pl.loop(0, NC)
    def _(index):
        mate(3, index, block(0)).wait_recv()

    load = pltpu.make_async_copy(wall.at[3], w_s.at[3], loc.at[3])
    load.start()
    load.wait()

    @pl.loop(0, 4)
    def _(at):
        rows = pl.ds(pl.multiple_of(at * 256, 256), 256)
        residual = tok_s[rows, :].astype(F32) + dot_nn(att_s[rows, :], w_s[3])
        res_s[rows, :] = residual
        xhat, _ = norm_parts(residual)
        sec_s[rows, :] = (xhat * sg[...] + sb[...]).astype(BF16)
        pltpu.make_async_copy(res_s.at[rows], res_o.at[rows], outs.at[5 + at]).start()
        pltpu.make_async_copy(sec_s.at[rows], sec_o.at[rows], outs.at[9 + at]).start()
        event(24 + at)

        @pl.when(at == 0)
        def _():
            hand.wait_recv()
            hand_on.start()

    for copy in finals:
        copy.wait()
    for at in range(4):
        rows = pl.ds(at * 256, 256)
        pltpu.make_async_copy(res_s.at[rows], res_o.at[rows], outs.at[5 + at]).wait()
        pltpu.make_async_copy(sec_s.at[rows], sec_o.at[rows], outs.at[9 + at]).wait()
    for slot in range(2):
        p_copy(slot, slot).wait()

    hand.wait_send()
    hand_on.wait()

    @pl.loop(0, NC)
    def _(index):
        for which in range(4, 8):
            mate(which, index, block(0)).wait_recv()
        for which in range(8):
            mate(which, index, block(0)).wait_send()
        mate_small(index, block(0)).wait_send()

    @pl.loop(0, NC - 1)
    def _(index):
        hop = index // 2
        way = index % 2
        for slot in range(6):
            ring(slot, way, hop, 0, block(0)).wait_send()
        ring_small(way, hop, block(0)).wait_send()
        for turn in range(2):
            twin(turn, index, 0, block(0)).wait_send()


def column(row):
    wide = jnp.broadcast_to(row, (16, 16))
    same = lax.broadcasted_iota(jnp.int32, (16, 16), 0) == lax.broadcasted_iota(jnp.int32, (16, 16), 1)
    return jnp.sum(jnp.where(same, wide, 0.0), axis=1, keepdims=True)


def any_spec(n):
    return [pl.BlockSpec(memory_space=pl.ANY)] * n


def vmem_spec(n):
    return [pl.BlockSpec(memory_space=pltpu.VMEM)] * n


def run_forward(tok, wq, wk, wv, wo, wup, wdn, s_in, s_out, fg, fb, skip, sg, sb, decay):
    shape = jax.ShapeDtypeStruct
    dma = pltpu.SemaphoreType.DMA
    big = (1024, 1024)
    ext = (1024 + CTX, 1024)
    return pl.pallas_call(
        forward_kernel,
        name="forward_part",
        out_shape=(
            shape((8,) + big, BF16), shape((2, 256, 1024), BF16), shape((1024, 128), BF16),
            shape(ext, BF16), shape(big, BF16),
            shape(ext, BF16), shape(ext, BF16), shape(big, BF16), shape(big, F32),
            shape(big, BF16), shape((16, BLK, CTX + BLK), BF16), shape((16, BLK), F32),
            shape((16, BLK), F32),
        ),
        in_specs=any_spec(7) + vmem_spec(8),
        out_specs=any_spec(11) + vmem_spec(2),
        scratch_shapes=[
            pltpu.VMEM(big, BF16), pltpu.VMEM(ext, BF16), pltpu.VMEM((4,) + big, BF16),
            pltpu.VMEM(big, BF16), pltpu.VMEM(ext, BF16), pltpu.VMEM(ext, BF16),
            pltpu.VMEM(big, BF16), pltpu.VMEM(big, F32), pltpu.VMEM(big, BF16),
            pltpu.VMEM((2, BLK, CTX + BLK), BF16), pltpu.VMEM((CTX, 1024), F32),
            pltpu.VMEM((1024, 128), BF16),
            pltpu.VMEM((8, 64, 1024), BF16), pltpu.VMEM((64, 128), BF16),
            dma((10,)), dma((6, 2, 4)), dma((6, 2, 4)), dma((2, 4)), dma((2, 4)),
            dma((9, NC)), dma((9, NC)), dma((2, NC - 1)), dma((2, NC - 1)), dma((13,)), dma((2,)), dma((2,)), dma((2,)),
        ],
        compiler_params=pltpu.CompilerParams(
            collective_id=0, has_side_effects=True, vmem_limit_bytes=VMEM_LIMIT
        ),
    )(tok, wq, wk, wv, wo, wup, wdn, s_in, s_out, fg, fb, skip, sg, sb, decay)


GELU_C = math.sqrt(2.0 / math.pi)
GELU_A = 0.044715


def feed_kernel(
    sec, res, wall, wdn, wdpre, cot, live, upb, dnb, sg,
    out_o, gatt_o, dwown_o, dwmate_o, fin_o, gdb_o, gub_o, gsg_o, gsb_o,
    sec_s, gb_s, wup_s, wd_s, br_s, gs_s, act_s, gh_s, a_s, b_s, prec, rrec, rsend, xsend, xrec,
    dwup_s, own_s, res_s,
    loc, ars, arr, axs, axr, cas, car, cxs, cxr, ps, pr, rs, rr, xs, xr, outs, dsem, dms, dmr,
):
    net = Net()
    rep, core = net.rep, net.core
    rows_of = 256
    ring_rows = 192
    part = 64
    ahead, behind = net.along(1), net.along(-1)

    def ring_part(shard, j, first=rep):
        return pl.ds(pl.multiple_of(shard * rows_of + (first + j) * part, part), part)

    def sole_part(shard, of):
        return pl.ds(pl.multiple_of(shard * rows_of + 3 * of * part, part), part)

    def block(shard):
        return pl.ds(pl.multiple_of(shard * rows_of, rows_of), rows_of)

    def mine_at(step):
        return net.at(-(step + 1), core)

    def other_at(step):
        return net.at(step + 1, 1 - core)

    loads = [
        pltpu.make_async_copy(wdn, own_s, loc.at[0]),
        pltpu.make_async_copy(sec, sec_s, loc.at[1]),
        pltpu.make_async_copy(cot, gb_s, loc.at[2]),
        pltpu.make_async_copy(wdpre.at[0], wd_s.at[block(mine_at(0))], loc.at[7]),
        pltpu.make_async_copy(wdpre.at[1], wd_s.at[block(other_at(0))], loc.at[8]),
    ]
    loads += [pltpu.make_async_copy(wall.at[4 + i], wup_s.at[i], loc.at[3 + i]) for i in range(4)]
    for load in loads:
        load.start()
    net.greet()
    loads[0].wait()
    loads[3].wait()

    def gather(j, hop, shard):
        ref = wd_s.at[ring_part(shard, j)]
        return rcopy(ref, ref, ars.at[j, hop], arr.at[j, hop], ahead)

    def gather_twin(hop, shard, of):
        ref = wd_s.at[sole_part(shard, of)]
        return rcopy(ref, ref, axs.at[hop], axr.at[hop], net.twin)

    def mate_ring(j, index, shard):
        ref = wd_s.at[ring_part(shard, j)]
        return rcopy(ref, ref, cas.at[j, index], car.at[j, index], net.mate)

    def mate_sole(index, shard, of):
        ref = wd_s.at[sole_part(shard, of)]
        return rcopy(ref, ref, cxs.at[index], cxr.at[index], net.mate)

    here = net.shard
    sole_own = own_s.at[pl.ds(pl.multiple_of(3 * (1 - rep) * part, part), part)]
    for j in range(3):
        ring_own = own_s.at[pl.ds(pl.multiple_of((rep + j) * part, part), part)]
        target = wd_s.at[ring_part(here, j)]
        gather(j, 1, mine_at(0)).start()
        rcopy(ring_own, target, cas.at[j, 0], car.at[j, 0], net.mate).start()
    rcopy(sole_own, wd_s.at[sole_part(here, 1 - rep)], cxs.at[0], cxr.at[0], net.mate).start()

    def serve(j, hop):
        shard = mine_at(hop)
        gather(j, hop, shard).wait_recv()

        @pl.when(hop < NC - 2)
        def _():
            gather(j, hop + 1, shard).start()

        @pl.when(j == 2 * rep)
        def _():
            gather_twin(hop, shard, rep).start()

        mate_ring(j, hop + 1, shard).start()

    def serve_twin(hop):
        shard = mine_at(hop)
        gather_twin(hop, shard, 1 - rep).wait_recv()
        mate_sole(hop + 1, shard, 1 - rep).start()

    for load in loads[1:3]:
        load.wait()

    wd_s[block(here), :] = own_s[...]

    @pl.loop(0, 4)
    def _(at):
        rows = pl.ds(pl.multiple_of(at * 256, 256), 256)
        when = lax.broadcasted_iota(jnp.int32, (256, 1024), 0) + at * 256
        kept = jnp.where(when < live[0], gb_s[rows, :].astype(F32), 0.0)
        gb_s[rows, :] = kept.astype(BF16)
        added = jnp.sum(kept, axis=0, keepdims=True)
        gdb_o[...] = jnp.where(at == 0, added, gdb_o[...] + added)
        br_s[rows, :] = jnp.zeros((256, 1024), F32)
        gs_s[rows, :] = jnp.zeros((256, 1024), F32)

    for load in loads[4:]:
        load.wait()

    def to_mate(step):
        slot = step % 2
        return rcopy(b_s.at[slot], prec.at[step], ps.at[step], pr.at[step], net.mate)

    def to_ring(j, step):
        return rcopy(rsend.at[step % 2, j], rrec.at[step, j], rs.at[step, j], rr.at[step, j], ahead)

    def to_twin(step):
        return rcopy(xsend.at[step % 2], xrec.at[step], xs.at[step], xr.at[step], net.twin)

    def dwup_at(target, shard):
        cols = pl.ds(pl.multiple_of((shard % 4) * 256, 256), 256)
        return target.at[shard // 4, :, :, cols]

    def dwup_copy(slot, half, shard):
        return pltpu.make_async_copy(
            dwup_s.at[slot, half, :, core], dwup_at(dwown_o, shard), dsem.at[slot, half]
        )

    def dwup_mate(step, half, shard):
        return rcopy(
            dwup_s.at[step % 2, half, :, 1 - core], dwup_at(dwmate_o, shard),
            dms.at[step, half], dmr.at[step, half], net.mate,
        )

    ring_local = pl.ds(pl.multiple_of(rep * part, part), ring_rows)
    sole_mine = pl.ds(pl.multiple_of(3 * rep * part, part), part)
    sole_theirs = pl.ds(pl.multiple_of(3 * (1 - rep) * part, part), part)

    def combine(step):
        slot = step % 2
        to_mate(step).wait_recv()
        a_s[slot] = a_s[slot] + prec[step].astype(F32)

        @pl.when(step >= 2)
        def _():
            to_twin(step - 2).wait_send()

        xsend[slot] = a_s[slot, sole_theirs, :].astype(BF16)
        to_twin(step).start()

    def forward(j, step):
        slot = step % 2
        rows = pl.ds(pl.multiple_of((rep + j) * part, part), part)

        @pl.when(j == 2 * rep)
        def _():
            to_twin(step).wait_recv()
            a_s[slot, rows, :] = a_s[slot, rows, :] + xrec[step].astype(F32)

        @pl.when(step >= 1)
        def _():
            to_ring(j, step - 1).wait_recv()
            a_s[slot, rows, :] = a_s[slot, rows, :] + rrec[step - 1, j].astype(F32)

        @pl.when((step >= 2) & (step < NC - 1))
        def _():
            to_ring(j, step - 2).wait_send()

        @pl.when(step < NC - 1)
        def _():
            rsend[slot, j] = a_s[slot, rows, :].astype(BF16)
            to_ring(j, step).start()

    @pl.loop(0, NC)
    def _(step):
        slot = step % 2
        a, b = mine_at(step), other_at(step)
        index = (step + 1) % NC

        @pl.when(step >= 1)
        def _():
            combine(step - 1)

        def up(shard):
            cols = pl.ds(pl.multiple_of((shard % 4) * 256, 256), 256)
            return wup_s[shard // 4, :, cols]

        def bias(shard):
            return upb[:, pl.ds(pl.multiple_of(shard * 256, 256), 256)]

        @pl.loop(0, 2)
        def _(half):
            @pl.when((half == 1) & (step >= 1))
            def _():
                for j in range(3):
                    mate_ring(j, index, b).wait_recv()
                mate_sole(index, b, 1 - rep).wait_recv()

            shard = a + half * (b - a)
            cols = pl.ds(pl.multiple_of(half * 256, 256), 256)
            hidden = dot_nn(sec_s[...], up(shard)) + bias(shard)
            grad = dot_nt(gb_s[...], wd_s[block(shard), :])
            square = hidden * hidden
            bent = jnp.tanh(hidden * (GELU_C + (GELU_C * GELU_A) * square))
            half_up = 0.5 + 0.5 * bent
            act_s[:, cols] = (hidden * half_up).astype(BF16)
            slope = half_up + (0.5 * hidden) * (1.0 - bent * bent) * (
                GELU_C + (3.0 * GELU_C * GELU_A) * square
            )
            gh_s[:, cols] = (grad * slope).astype(BF16)

            @pl.when(step < NC - 2)
            def _():
                serve((2 * rep + half) % 3, step + 1)

            @pl.when((half == 1) & (step < NC - 2))
            def _():
                serve((2 * rep + 2) % 3, step + 1)

        made = dot_tn(act_s[...], gb_s[...])

        @pl.when(step >= 2)
        def _():
            to_mate(step - 2).wait_send()

        a_s[slot] = made[0:256]
        b_s[slot] = made[256:512].astype(BF16)
        to_mate(step).start()

        rise_up = dot_tn(sec_s[...], gh_s[...]).astype(BF16)
        for half, shard in enumerate((a, b)):
            cols = pl.ds(pl.multiple_of(shard * 256, 256), 256)
            gub_o[:, cols] = jnp.sum(
                gh_s[:, half * 256 : half * 256 + 256].astype(F32), axis=0, keepdims=True
            )

            @pl.when(step >= 2)
            def _(half=half, shard=shard):
                dwup_copy(slot, half, shard).wait()
                dwup_mate(step - 2, half, shard).wait_send()

            dwup_s[slot, half] = rise_up[:, half * 256 : half * 256 + 256].reshape(NC, 2, 64, 256)
            dwup_copy(slot, half, shard).start()
            dwup_mate(step, half, shard).start()

        @pl.loop(0, 2)
        def _(at):
            rows = pl.ds(pl.multiple_of(at * 512, 512), 512)

            def rise_of(shard):
                cols = pl.ds(pl.multiple_of((shard % 4) * 256, 256), 256)
                return wup_s[shard // 4, rows, cols]

            down = jnp.concatenate([wd_s[block(a), rows], wd_s[block(b), rows]], axis=0)
            br_s[:, rows] = br_s[:, rows] + dot_nn(act_s[...], down)
            rise = jnp.concatenate([rise_of(a), rise_of(b)], axis=1)
            gs_s[:, rows] = gs_s[:, rows] + dot_nt(gh_s[...], rise)

            @pl.when(step >= 1)
            def _():
                forward((2 * rep + 1 + at) % 3, step - 1)

            @pl.when((at == 1) & (step < NC - 2))
            def _():
                serve_twin(step + 1)

        @pl.when(step >= 1)
        def _():
            forward((2 * rep + 3) % 3, step - 1)

    def residual_in(at):
        rows = pl.ds(at * 256, 256)
        return pltpu.make_async_copy(res.at[rows], res_s.at[rows], loc.at[at])

    for at in range(4):
        residual_in(at).start()
    combine(NC - 1)

    def leave(at, which):
        rows = pl.ds(pl.multiple_of(at * 256, 256), 256)
        source = (sec_s, gb_s)[which]
        return pltpu.make_async_copy(
            source.at[rows], (out_o, gatt_o)[which].at[rows], outs.at[which, at]
        )

    @pl.loop(0, 4)
    def _(at):
        residual_in(at).wait()
        rows = pl.ds(pl.multiple_of(at * 256, 256), 256)
        kept = res_s[rows, :]
        when = lax.broadcasted_iota(jnp.int32, (256, 1024), 0) + at * 256
        total = kept + br_s[rows, :] + dnb[...]
        sec_s[rows, :] = jnp.where(when < live[0], total, 0.0).astype(BF16)
        xhat, inverse = norm_parts(kept)
        grad = gs_s[rows, :]
        gain = jnp.sum(grad * xhat, axis=0, keepdims=True)
        shift = jnp.sum(grad, axis=0, keepdims=True)
        gsg_o[...] = jnp.where(at == 0, gain, gsg_o[...] + gain)
        gsb_o[...] = jnp.where(at == 0, shift, gsb_o[...] + shift)
        grad = grad * sg[...]
        grad = grad - jnp.mean(grad, axis=-1, keepdims=True) - xhat * jnp.mean(
            grad * xhat, axis=-1, keepdims=True
        )
        gb_s[rows, :] = (gb_s[rows, :].astype(F32) + inverse * grad).astype(BF16)
        for which in range(2):
            leave(at, which).start()

    for j in range(3):
        forward((2 * rep + 1 + j) % 3, NC - 1)
    last = (NC - 1) % 2
    fin_o[...] = a_s[last, ring_local, :].astype(BF16)

    @pl.loop(1, NC - 1)
    def _(hop):
        for j in range(3):
            gather(j, hop, 0).wait_send()
        gather_twin(hop, 0, 0).wait_send()

    @pl.loop(1, NC)
    def _(later):
        index = (later + 1) % NC
        for j in range(3):
            mate_ring(j, index, 0).wait_send()
        mate_sole(index, 0, 0).wait_send()

    for step in range(NC - 2, NC):
        to_mate(step).wait_send()
        to_twin(step).wait_send()
        for j in range(3):
            to_ring(j, step - 1).wait_send()
        for half in range(2):
            dwup_copy(step % 2, half, 0).wait()
            dwup_mate(step, half, 0).wait_send()
    for at in range(4):
        for which in range(2):
            leave(at, which).wait()

    @pl.loop(0, NC)
    def _(step):
        for half in range(2):
            dwup_mate(step, half, 0).wait_recv()


def run_feed(sec, res, wall, wdn, wdpre, cot, live, upb, dnb, sg):
    shape = jax.ShapeDtypeStruct
    dma = pltpu.SemaphoreType.DMA
    vmem = pltpu.VMEM
    big = (1024, 1024)
    return pl.pallas_call(
        feed_kernel,
        name="feed_part",
        out_shape=(
            shape(big, BF16), shape(big, BF16), shape((4, NC, 64, 1024), BF16),
            shape((4, NC, 64, 1024), BF16), shape((192, 1024), BF16), shape((1, 1024), F32), shape((1, 4096), F32),
            shape((1, 1024), F32), shape((1, 1024), F32),
        ),
        in_specs=any_spec(6) + [pl.BlockSpec(memory_space=pltpu.SMEM)] + vmem_spec(3),
        out_specs=any_spec(4) + vmem_spec(5),
        scratch_shapes=[
            vmem(big, BF16), vmem(big, BF16), vmem((4,) + big, BF16), vmem((4096, 1024), BF16),
            vmem(big, F32), vmem(big, F32), vmem((1024, 512), BF16), vmem((1024, 512), BF16),
            vmem((2, 256, 1024), F32), vmem((2, 256, 1024), BF16), vmem((NC, 256, 1024), BF16),
            vmem((NC - 1, 3, 64, 1024), BF16), vmem((2, 3, 64, 1024), BF16), vmem((2, 64, 1024), BF16),
            vmem((NC, 64, 1024), BF16),
            vmem((2, 2, NC, 2, 64, 256), BF16), vmem((256, 1024), BF16), vmem(big, F32),
            dma((9,)), dma((3, NC - 1)), dma((3, NC - 1)), dma((NC - 1,)), dma((NC - 1,)),
            dma((3, NC)), dma((3, NC)), dma((NC,)), dma((NC,)), dma((NC,)), dma((NC,)),
            dma((NC - 1, 3)), dma((NC - 1, 3)), dma((NC,)), dma((NC,)),
            dma((2, 4)), dma((2, 2)), dma((NC, 2)), dma((NC, 2)),
        ],
        compiler_params=pltpu.CompilerParams(
            collective_id=1, has_side_effects=True, vmem_limit_bytes=VMEM_LIMIT
        ),
    )(sec, res, wall, wdn, wdpre, cot, live, upb, dnb, sg)


def backward_kernel(
    dwown, dwmate, find, gatt, att, wall, q, kx, vx, rnd, p, tok, sio, u_in, st_in, fg, fb, skip, decay,
    gsg, gsb, gdb, gub,
    gtok_o, findr_o, fin_b, finr_b, fin_g, finr_g, sums_o,
    own_b, prec_b, rrec_b, xrec_b, acc_b,
    own_g, prec_g, rrec_g, xrec_g, acc_g, go_s,
    gatt_s, wo_s, att_s, ga_s, q_s, k_s, v_s, rnd_s, dk_s, dv_s, pbuf, ds_s, gres_s, nb_s,
    sio_s, gd_s, gctx_s, sum_s, got_s, part_s,
    loc, psem, gsem, osem, mbs, mbr, mgs, mgr, rbs, rbr, rgs, rgr, xbs, xbr, xgs, xgr,
    fbs, fbr, fgs, fgr, ts, tr, us, ur, ds, dr,
):
    net = Net()
    rep, core = net.rep, net.core
    theirs = 1 - core

    loads = [
        pltpu.make_async_copy(gatt, gatt_s, loc.at[0]),
        pltpu.make_async_copy(wall.at[3], wo_s, loc.at[1]),
        pltpu.make_async_copy(att, att_s, loc.at[2]),
        pltpu.make_async_copy(q, q_s, loc.at[3]),
        pltpu.make_async_copy(kx, k_s, loc.at[4]),
        pltpu.make_async_copy(vx, v_s, loc.at[5]),
        pltpu.make_async_copy(rnd, rnd_s, loc.at[6]),
        pltpu.make_async_copy(sio, sio_s, loc.at[7]),
    ]
    rises = [
        pltpu.make_async_copy(dwown, own_b.at[pl.ds(0, 4)], loc.at[8]),
        pltpu.make_async_copy(dwmate, prec_b.at[pl.ds(0, 4)], loc.at[9]),
    ]
    for copy in rises:
        copy.start()
    for copy in loads:
        copy.start()
    fin_b[...] = jnp.zeros(fin_b.shape, BF16)
    finr_b[...] = jnp.zeros(finr_b.shape, BF16)
    fin_g[...] = jnp.zeros(fin_g.shape, BF16)
    finr_g[...] = jnp.zeros(finr_g.shape, BF16)
    barrier = pltpu.get_barrier_semaphore()
    me = rep * (2 * NC) + net.shard

    def device(away):
        other = (me + away) % (4 * NC)
        return other, (other // (2 * NC), other % (2 * NC))

    @pl.loop(1, 4 * NC)
    def _(away):
        pl.semaphore_signal(barrier, inc=1, device_id=device(away)[1], device_id_type=MESH)

    pl.semaphore_wait(barrier, 4 * NC - 1)

    mate_out = rcopy(go_s, prec_b.at[4], mbs.at[0], mbr.at[0], net.mate)

    def mate_group(g):
        return rcopy(own_g.at[g, :, theirs], prec_g.at[g], mgs.at[g], mgr.at[g], net.mate)

    swap = rcopy(find, findr_o, ds.at[0], dr.at[0], net.twin)
    swap.start()

    def chip_for(n):
        t, way = n // 2, n % 2
        hops = (4 - t) * (1 - way) + (t - 3) * way
        return chip_at((net.pos + net.step * hops + 4 * NC) % NC)

    class Stream:
        def __init__(self, own, prec, rrec, xrec, fin, finr, acc, sems):
            self.own, self.prec, self.rrec, self.xrec = own, prec, rrec, xrec
            self.fin, self.finr, self.acc = fin, finr, acc
            self.rs, self.rr, self.xs, self.xr, self.fs, self.fr = sems

        def ring(self, slot, which, n):
            source = self.prec.at[which, chip_for(n)]
            way = n % 2
            return rcopy(
                source, self.rrec.at[slot, n], self.rs.at[slot, n], self.rr.at[slot, n],
                net.along(1 - 2 * way),
            )

        def twin(self, which, n):
            chip = chip_for(n)
            return rcopy(
                self.prec.at[which, chip], self.xrec.at[chip], self.xs.at[n], self.xr.at[n], net.twin
            )

        def finish(self, which):
            return rcopy(
                self.fin.at[which], self.finr.at[which], self.fs.at[which], self.fr.at[which], net.twin
            )

        def give(self, which, n):
            chip = chip_for(n)
            self.prec[which, chip] = (
                self.own(which, chip).astype(F32) + self.prec[which, chip].astype(F32)
            ).astype(BF16)
            self.twin(which, n).start()

        def turn(self, slot, which, n, sole):
            chip = chip_for(n)
            self.acc[...] = self.own(which, chip).astype(F32) + self.prec[which, chip].astype(F32)

            @pl.when(sole)
            def _():
                self.twin(which, n).wait_recv()
                self.acc[...] = self.acc[...] + self.xrec[chip].astype(F32)

            @pl.when((n >= 2) & (n < 7))
            def _():
                self.ring(slot, which, n - 2).wait_recv()
                self.acc[...] = self.acc[...] + self.rrec[slot, n - 2].astype(F32)

            @pl.when(n < 7)
            def _():
                self.prec[which, chip] = self.acc[...].astype(BF16)
                self.ring(slot, which, n).start()

            @pl.when(n == 7)
            def _():
                self.ring(slot, which, 5).wait_recv()
                self.ring(slot, which, 6).wait_recv()
                total = self.acc[...] + self.rrec[slot, 5].astype(F32) + self.rrec[slot, 6].astype(F32)
                self.fin[which] = total.astype(BF16)
                self.finish(which).start()

    big = Stream(
        lambda which, chip: own_b[which, chip], prec_b, rrec_b, xrec_b, fin_b, finr_b, acc_b,
        (rbs, rbr, xbs, xbr, fbs, fbr),
    )
    group = Stream(
        lambda which, chip: own_g[which, chip, core], prec_g, rrec_g, xrec_g, fin_g, finr_g, acc_g,
        (rgs, rgr, xgs, xgr, fgs, fgr),
    )

    def tile(index):
        return (
            pl.ds(pl.multiple_of((index // 8) * 16, 16), 16),
            pl.ds(pl.multiple_of((index % 8) * 128, 128), 128),
        )

    def share(away):
        other, where = device(away)
        return rcopy(sum_s.at[tile(other)], got_s.at[away], ts.at[away], tr.at[away], where)

    def spread(away):
        return rcopy(part_s, sums_o.at[tile(me)], us.at[away], ur.at[away], device(away)[1])

    def each_device(act):
        for away in range(1, 4 * NC):
            act(away)

    def big_at(e):
        k, j = e // 4, e % 4
        n = k - j - (j // 2) * (1 - 2 * (j // 3))
        which = (j + 1) * (1 - j // 2) + (j // 2) * (3 * rep * (1 - j // 3) + 4 * (j // 3))

        @pl.when((j == 3) & (n == 0))
        def _():
            mate_out.wait_recv()

        @pl.when((n >= 0) & (n <= 7))
        def _():
            big.turn(j, which, n, j == 2)

    def group_at(e):
        k, j = e // 3, e % 3
        n = k
        which = rep * (1 - (j + 1) // 2) + (j + 1) * ((j + 1) // 2)

        @pl.when((j >= 1) & (n == 0))
        def _():
            mate_group(which).wait_recv()

        @pl.when((n >= 0) & (n <= 7))
        def _():
            group.turn(j, which, n, j == 0)

    def run(at, low, high):
        @pl.loop(low, high)
        def _(e):
            at(e)

    for copy in rises:
        copy.wait()

    @pl.loop(0, NC)
    def _(n):
        big.give(3 * (1 - rep), n)

    run(big_at, 0, 4)
    for i in range(2):
        loads[i].wait()

    def p_copy(slot, at):
        return pltpu.make_async_copy(p.at[at], pbuf.at[slot], psem.at[slot])

    p_copy(0, 0).start()

    @pl.loop(0, 2)
    def _(at):
        rows = pl.ds(pl.multiple_of(at * 512, 512), 512)
        ga_s[rows, :] = dot_nt(gatt_s[rows, :], wo_s[...]).astype(BF16)

    run(big_at, 4, 8)
    loads[2].wait()

    @pl.loop(0, 2)
    def _(at):
        cols = pl.ds(pl.multiple_of(at * 512, 512), 512)
        made = dot_tn(att_s[...], gatt_s[:, cols]).reshape(NC, 2, 64, 512)
        own_b[4, :, :, cols] = jnp.where(core == 0, made[:, 0], made[:, 1]).astype(BF16)
        go_s[:, :, cols] = jnp.where(core == 0, made[:, 1], made[:, 0]).astype(BF16)

    mate_out.start()
    tok_load = pltpu.make_async_copy(tok, wo_s, loc.at[0])
    tok_load.start()
    for copy in loads[3:]:
        copy.wait()
    ds_s[...] = jnp.zeros(ds_s.shape, BF16)
    dq_s = gatt_s

    def weights_in(i):
        target = (q_s, k_s.at[pl.ds(0, 1024)], v_s.at[pl.ds(0, 1024)])[i]
        return pltpu.make_async_copy(wall.at[i], target, loc.at[1 + i])

    @pl.loop(0, 4)
    def _(g):
        for hh in range(2):
            for b in range(NBLK):
                i = 2 * hh + b
                m = 4 * g + i
                h = 2 * g + hh
                slot = i % 2
                cols = pl.ds(pl.multiple_of(h * DH, DH), DH)
                following = 2 * hh + b + 1
                nb, nh = following % 2, 2 * g + following // 2
                p_copy(slot, b * 8 + h).wait()
                if following < 4:
                    p_copy(1 - slot, nb * 8 + nh).start()
                else:

                    @pl.when(g < 3)
                    def _():
                        p_copy(1 - slot, nh).start()

                for part in range(2):
                    span = (part + 1) * 256
                    rows = pl.ds(b * BLK + part * 256, 256)
                    local = pl.ds(part * 256, 256)
                    grads = ga_s[rows, cols]
                    slope = dot_nt(grads, v_s[pl.ds(b * BLK, span), cols])
                    kept = pbuf[slot, local, pl.ds(CTX, span)].astype(F32)
                    both = jnp.sum(kept * slope, axis=-1, keepdims=True)
                    mass = jnp.sum(kept, axis=-1, keepdims=True)
                    if b:
                        slope_before = dot_nt(grads, v_s[pl.ds(1024, CTX), cols])
                        kept_before = pbuf[slot, local, pl.ds(0, CTX)].astype(F32)
                        both += jnp.sum(kept_before * slope_before, axis=-1, keepdims=True)
                        mass += jnp.sum(kept_before, axis=-1, keepdims=True)
                    both = both / mass
                    inner = (kept * (slope - both)).astype(BF16)
                    ds_s[local, pl.ds(CTX, span)] = inner
                    total = dot_nn(inner, k_s[pl.ds(b * BLK, span), cols])
                    if b:
                        inner = (kept_before * (slope_before - both)).astype(BF16)
                        ds_s[local, pl.ds(0, CTX)] = inner
                        total = total + dot_nn(inner, k_s[pl.ds(1024, CTX), cols])
                    dq_s[rows, cols] = (total * SCALE).astype(BF16)
                rows = pl.ds(b * BLK, BLK)
                first = 0 if b else CTX
                made_k = dot_tn(ds_s[:, first:], q_s[rows, cols]) * SCALE
                made_v = dot_tn(pbuf[slot, :, first:], ga_s[rows, cols])
                if b:
                    dk_s[pl.ds(1024, CTX), cols] = made_k[:CTX].astype(BF16)
                    dv_s[pl.ds(1024, CTX), cols] = made_v[:CTX].astype(BF16)
                    made_k, made_v = made_k[CTX:], made_v[CTX:]
                dk_s[rows, cols] = made_k.astype(BF16)
                dv_s[rows, cols] = made_v.astype(BF16)

                run(big_at, 8 + 2 * m, 10 + 2 * m)


                @pl.when(m == 10)
                def _():
                    for each in range(2):
                        mate_group(each).wait_recv()

                @pl.when((m >= 10) & (m < 14))
                def _(m=m):
                    for e in range(2):
                        group.give(1 - rep, 2 * (m - 10) + e)

        @pl.when(g == 3)
        def _():
            for i in range(3):
                weights_in(i).start()

        cols = pl.ds(pl.multiple_of(g * 256, 256), 256)
        own_g[g, :, :, :, 0:256] = dot_tn(rnd_s[0:1024, :], dq_s[:, cols]).astype(BF16).reshape(NC, 2, 64, 256)
        own_g[g, :, :, :, 256:512] = dot_tn(rnd_s[...], dk_s[:, cols]).astype(BF16).reshape(NC, 2, 64, 256)
        own_g[g, :, :, :, 512:768] = dot_tn(rnd_s[...], dv_s[:, cols]).astype(BF16).reshape(NC, 2, 64, 256)
        mate_group(g).start()

    run(big_at, 40, 44)
    run(group_at, 0, 2)
    for i in range(3):
        weights_in(i).wait()
    tok_load.wait()

    def gres_in(at):
        rows = pl.ds(pl.multiple_of(at * 256, 256), 256)
        return pltpu.make_async_copy(gatt.at[rows], gres_s.at[at % 2], gsem.at[at % 2])

    gres_in(0).start()

    after = pl.ds(1024, CTX)
    gctx = dot_nt(dk_s[after, :], k_s[0:1024, :]) + dot_nt(dv_s[after, :], v_s[0:1024, :])
    gctx_s[...] = gctx
    xhat, _ = norm_parts(wo_s[pl.ds(BLK - CTX, CTX), :].astype(F32))
    sum_s[32:48, :] = jnp.zeros((16, 1024), F32)
    sum_s[34:35, :] = jnp.sum(gctx * (xhat * fg[...] + fb[...]), axis=0, keepdims=True)
    for at, vector in ((35, gsg), (36, gsb), (37, gdb)):
        sum_s[at : at + 1, :] = vector[...]
    for at in range(4):
        sum_s[38 + at : 39 + at, :] = gub[:, at * 1024 : (at + 1) * 1024]
    run(group_at, 2, 5)
    states, raw = st_in[...], u_in[...]
    factor = jnp.exp(-column(decay[...]))
    scale = jnp.sqrt(1.0 - factor * factor)
    sum_s[16:32, :] = lax.dot_general(
        states[:, BLK - CTX :], gctx, (((1,), (0,)), ((), ())),
        preferred_element_type=F32, precision=lax.Precision.HIGHEST,
    )
    back = split_dot(
        lambda a, b: lax.dot_general(b, a, (((0,), (1,)), ((), ())), preferred_element_type=F32),
        gctx, sio_s[...], 3,
    )
    seeds = jnp.concatenate([jnp.zeros((16, BLK - CTX), F32), back[16:32, :]], axis=1)
    lam = lane_scan(seeds, factor, True)
    lane = lax.broadcasted_iota(jnp.int32, lam.shape, 1)
    earlier = jnp.where(lane >= 1, pltpu.roll(states, 1, 1), 0.0)
    rates = -factor * jnp.sum(lam * (earlier - (factor / scale) * raw), axis=1, keepdims=True)
    sum_s[48:64, :] = jnp.broadcast_to(rates, (16, 1024))
    driven = scale * lam
    sum_s[0:16, :] = split_dot(dot_nn, driven, rnd_s[0:BLK, :], 3)
    gd_s[...] = jnp.zeros(gd_s.shape, F32)
    gd_s[0:16, 0:BLK] = driven

    def add_in(away):
        share(away).wait_recv()
        part_s[...] = part_s[...] + got_s[away]

    def leave(at):
        rows = pl.ds(pl.multiple_of(at * 256, 256), 256)
        return pltpu.make_async_copy(rnd_s.at[rows], gtok_o.at[rows], osem.at[at])

    @pl.loop(0, 4)
    def _(at):
        rows = pl.ds(pl.multiple_of(at * 256, 256), 256)

        @pl.when(at < 3)
        def _():
            gres_in(at + 1).start()

        xhat, inverse = norm_parts(wo_s[rows, :].astype(F32))
        nb_s[...] = (
            dot_nt(dq_s[rows, :], q_s[...])
            + dot_nt(dk_s[rows, :], k_s[0:1024, :])
            + dot_nt(dv_s[rows, :], v_s[0:1024, :])
        )

        @pl.when(at < 2)
        def _():
            nb_s[...] = nb_s[...] + split_dot(
                lambda a, b: lax.dot_general(a, b, (((0,), (1,)), ((), ())), preferred_element_type=F32),
                gd_s[:, rows], sio_s[...], 3,
            )

        @pl.when(at == 1)
        def _():
            half = pl.ds(128, CTX)
            nb_s[half, :] = nb_s[half, :] + skip[...] * gctx_s[...]

        run(group_at, 5 + 3 * at, 8 + 3 * at)

        grad = nb_s[...]
        gain = jnp.sum(grad * xhat, axis=0, keepdims=True)
        shift = jnp.sum(grad, axis=0, keepdims=True)
        sum_s[32:33, :] = sum_s[32:33, :] + gain
        sum_s[33:34, :] = sum_s[33:34, :] + shift
        grad = grad * fg[...]
        grad = grad - jnp.mean(grad, axis=-1, keepdims=True) - xhat * jnp.mean(
            grad * xhat, axis=-1, keepdims=True
        )
        gres_in(at).wait()
        rnd_s[rows, :] = (gres_s[at % 2].astype(F32) + inverse * grad).astype(BF16)
        leave(at).start()

    each_device(lambda away: share(away).start())
    part_s[...] = sum_s[tile(me)]
    run(group_at, 17, 20)
    each_device(add_in)
    each_device(lambda away: spread(away).start())
    sums_o[tile(me)] = part_s[...]
    run(group_at, 20, 24)

    for which in (3 * rep, 1, 2, 4):
        big.finish(which).wait_send()
    for which in (rep, 2, 3):
        group.finish(which).wait_send()
    twin_rise = 3 * (1 - rep)
    for which in (twin_rise, 1, 2, 4):
        big.finish(which).wait_recv()
    for which in (1 - rep, 2, 3):
        group.finish(which).wait_recv()
    def settle(away):
        spread(away).wait()
        share(away).wait_send()

    each_device(settle)
    for i in range(4):
        mate_group(i).wait_send()
        leave(i).wait()
    mate_out.wait_send()
    swap.wait()

    @pl.loop(0, NC)
    def _(n):
        big.twin(3 * (1 - rep), n).wait_send()
        group.twin(1 - rep, n).wait_send()

    @pl.loop(0, NC - 1)
    def _(n):
        for slot in range(4):
            big.ring(slot, 0, n).wait_send()
        for slot in range(3):
            group.ring(slot, 0, n).wait_send()


def run_backward(*operands):
    shape = jax.ShapeDtypeStruct
    dma = pltpu.SemaphoreType.DMA
    vmem = pltpu.VMEM
    full = (1024, 1024)
    ext = (1024 + CTX, 1024)
    part = (64, 1024)
    cut = (64, 768)
    return pl.pallas_call(
        backward_kernel,
        name="backward_part",
        out_shape=(
            shape(full, BF16), shape((192, 1024), BF16), shape((5,) + part, BF16), shape((5,) + part, BF16),
            shape((4,) + cut, BF16), shape((4,) + cut, BF16), shape((64, 1024), F32),
        ),
        in_specs=any_spec(13) + vmem_spec(10),
        out_specs=any_spec(2) + vmem_spec(5),
        scratch_shapes=[
            vmem((5, NC) + part, BF16), vmem((5, NC) + part, BF16), vmem((4, NC - 1) + part, BF16),
            vmem((NC,) + part, BF16), vmem(part, F32),
            vmem((4, NC, 2) + cut, BF16), vmem((4, NC) + cut, BF16), vmem((3, NC - 1) + cut, BF16),
            vmem((NC,) + cut, BF16), vmem(cut, F32),
            vmem((NC,) + part, BF16),
            vmem(full, BF16), vmem(full, BF16), vmem(full, BF16), vmem(full, BF16), vmem(full, BF16),
            vmem(ext, BF16), vmem(ext, BF16), vmem(ext, BF16), vmem(ext, BF16), vmem(ext, BF16),
            vmem((2, BLK, CTX + BLK), BF16), vmem((BLK, CTX + BLK), BF16), vmem((2, 256, 1024), BF16),
            vmem((256, 1024), F32), vmem((1024, 128), BF16), vmem((128, 1024), F32), vmem((CTX, 1024), F32), vmem((64, 1024), F32), vmem((4 * NC, 16, 128), F32), vmem((16, 128), F32),
            dma((10,)), dma((2,)), dma((2,)), dma((4,)), dma((1,)), dma((1,)), dma((4,)), dma((4,)),
            dma((4, NC - 1)), dma((4, NC - 1)), dma((3, NC - 1)), dma((3, NC - 1)),
            dma((NC,)), dma((NC,)), dma((NC,)), dma((NC,)), dma((5,)), dma((5,)), dma((4,)), dma((4,)),
            dma((4 * NC,)), dma((4 * NC,)), dma((4 * NC,)), dma((4 * NC,)), dma((1,)), dma((1,)),
        ],
        compiler_params=pltpu.CompilerParams(
            collective_id=2, has_side_effects=True, vmem_limit_bytes=VMEM_LIMIT
        ),
    )(*operands)


def outputs_kernel(
    result, gtok, finb, finrb, fing, finrg, find, findr, sums,
    result_o, gtok_o, dup_o, do_o, dq_o, dk_o, dv_o, ddown_o, gfg_o, gfb_o, gskip_o, gsg_o, gsb_o, gdb_o, gub_o, grate_o,
    gsi_o, gso_o, held, came, left,
):
    rep, shard = lax.axis_index("rep"), lax.axis_index("shard")
    pairs = ((result, result_o), (gtok, gtok_o))

    def take(which, at):
        rows = pl.ds(at * 256, 256)
        return pltpu.make_async_copy(pairs[which][0].at[rows], held.at[which, rows], came.at[which, at])

    def give(which, at):
        rows = pl.ds(at * 256, 256)
        return pltpu.make_async_copy(held.at[which, rows], pairs[which][1].at[rows], left.at[which, at])

    every = [(which, at) for which in range(2) for at in range(4)]
    for each in every:
        take(*each).start()
    for i in range(4):
        dup_o[:, i * 1024 : (i + 1) * 1024] = finb[i].astype(F32) + finrb[i].astype(F32)
    for each in every:
        take(*each).wait()
        give(*each).start()
    do_o[...] = finb[4].astype(F32) + finrb[4].astype(F32)
    for g in range(4):
        for i, out in enumerate((dq_o, dk_o, dv_o)):
            cols = slice(i * 256, (i + 1) * 256)
            out[:, g * 256 : (g + 1) * 256] = fing[g, :, cols].astype(F32) + finrg[g, :, cols].astype(F32)
    mine = pl.ds(pl.multiple_of(rep * 64, 64), 192)
    theirs = pl.ds(pl.multiple_of((1 - rep) * 64, 64), 192)
    ddown_o[...] = jnp.zeros((256, 1024), F32)
    ddown_o[mine, :] = find[...].astype(F32)
    ddown_o[theirs, :] = ddown_o[theirs, :] + findr[...].astype(F32)
    for at, out in enumerate((gfg_o, gfb_o, gskip_o, gsg_o, gsb_o, gdb_o)):
        out[...] = sums[32 + at : 33 + at, :]
    for at in range(4):
        gub_o[:, at * 1024 : (at + 1) * 1024] = sums[38 + at : 39 + at, :]
    same = lax.broadcasted_iota(jnp.int32, (16, 128), 0) == lax.broadcasted_iota(jnp.int32, (16, 128), 1)
    grate_o[...] = jnp.sum(jnp.where(same, sums[48:64, 0:128], 0.0), axis=0)[0:16]
    shift = (1024 - 64 * shard) % 1024
    gsi_o[...] = pltpu.roll(sums[0:16, :], shift, 1)[:, 0:64]
    gso_o[...] = pltpu.roll(sums[16:32, :], shift, 1)[:, 0:64]
    for each in every:
        give(*each).wait()


def run_outputs(*operands):
    shape = jax.ShapeDtypeStruct
    row = shape((1, 1024), F32)
    part = shape((64, 1024), F32)
    return pl.pallas_call(
        outputs_kernel,
        name="outputs_part",
        out_shape=(
            shape((1024, 1024), BF16), shape((1024, 1024), BF16),
            shape((64, 4096), F32), part, part, part, part, shape((256, 1024), F32),
            row, row, row, row, row, row, shape((1, 4096), F32), shape((16,), F32),
            shape((16, 64), F32), shape((16, 64), F32),
        ),
        in_specs=any_spec(2) + vmem_spec(7),
        out_specs=any_spec(2) + vmem_spec(16),
        scratch_shapes=[
            pltpu.VMEM((2, 1024, 1024), BF16),
            pltpu.SemaphoreType.DMA((2, 4)), pltpu.SemaphoreType.DMA((2, 4)),
        ],
        compiler_params=pltpu.CompilerParams(vmem_limit_bytes=VMEM_LIMIT),
    )(*operands)


def fused_device(
    tokens, lengths, first_gain, first_bias, decay_rates, state_in, state_out, skip_gain,
    query_weight, key_weight, value_weight, output_weight, second_gain, second_bias,
    up_weight, up_bias, down_weight, down_bias, cotangent,
):
    tok = tokens.reshape(1024, 1024)
    cot = cotangent.reshape(1024, 1024)
    fg, fb, skip, sg, sb, dnb, upb, decay = (
        v.reshape(1, -1)
        for v in (
            first_gain, first_bias, skip_gain, second_gain, second_bias, down_bias, up_bias, decay_rates,
        )
    )
    wall, wdpre, sio, rnd, q, kx, vx, att, res, sec, p, u, st = run_forward(
        tok, query_weight, key_weight, value_weight, output_weight, up_weight, down_weight, state_in, state_out,
        fg, fb, skip, sg, sb, decay,
    )
    result, gatt, dwown, dwmate, find, gdb, gub, gsg, gsb = run_feed(
        sec, res, wall, down_weight, wdpre, cot, lengths, upb, dnb, sg
    )
    gtok, findr, finb, finrb, fing, finrg, sums = run_backward(
        dwown, dwmate, find, gatt, att, wall, q, kx, vx, rnd, p, tok, sio,
        u, st, fg, fb, skip, decay, gsg, gsb, gdb, gub,
    )
    result, gtok, dup, do, dq, dk, dv, ddown, *rest = run_outputs(
        result, gtok, finb, finrb, fing, finrg, find, findr, sums
    )
    gfg, gfb, gskip, gsg, gsb, gdb, gub, grate, gsi, gso = rest
    return (
        result.reshape(1, 1024, 1024), gtok.reshape(1, 1024, 1024), gfg[0], gfb[0],
        grate, gsi, gso, gskip[0], dq, dk, dv, do, gsg[0], gsb[0], dup, gub[0], ddown, gdb[0],
    )


NORM_EPS = 1e-05
NEG_LARGE = -1e30
HIGHEST = lax.Precision.HIGHEST


def layer_norm(hidden, gain_vec, bias_vec):
    average = jnp.mean(hidden, axis=-1, keepdims=True)
    centred = hidden - average
    spread = jnp.mean(centred * centred, axis=-1, keepdims=True)
    return centred * lax.rsqrt(spread + NORM_EPS) * gain_vec + bias_vec


def state_context(driven_raw, normed, decay_rates, state_out, skip_gain):
    decay_factor = jnp.exp(-decay_rates)
    driven = driven_raw * jnp.sqrt(1.0 - decay_factor * decay_factor)
    factors = jnp.broadcast_to(decay_factor, driven.shape)

    def combine(earlier, subsequent):
        return (earlier[0] * subsequent[0], subsequent[0] * earlier[1] + subsequent[1])

    states = lax.associative_scan(combine, (factors, driven), axis=1)[1]
    seq_count = driven_raw.shape[0]
    state_width = driven_raw.shape[2]
    model_width = normed.shape[2]
    tail_states = states.reshape(seq_count, NBLK, BLK, state_width)[:, :, BLK - CTX :, :]
    skipped = normed.reshape(seq_count, NBLK, BLK, model_width)[:, :, BLK - CTX :, :]
    outputs = (
        jnp.einsum("sbcp,pd->sbcd", tail_states, state_out, precision=HIGHEST) + skip_gain * skipped
    )
    empty_ctx = jnp.zeros((seq_count, 1, CTX, model_width), jnp.float32)
    return jnp.concatenate([empty_ctx, outputs[:, : NBLK - 1]], axis=1)


def block_scores(queries, key_rows, ctx_keys, ctx_valid):
    row_count = queries.shape[0]
    head_count = queries.shape[1] // DH
    query_heads = queries.reshape(row_count, head_count, DH)
    key_heads = jnp.concatenate([ctx_keys, key_rows], 0).reshape(-1, head_count, DH)
    scores = jnp.einsum(
        "qhd,khd->hqk", query_heads, key_heads, preferred_element_type=jnp.float32
    ) * DH ** (-0.5)
    causal = lax.broadcasted_iota(jnp.int32, (row_count, row_count), 0) >= lax.broadcasted_iota(
        jnp.int32, (row_count, row_count), 1
    )
    allowed = jnp.concatenate(
        [jnp.broadcast_to(ctx_valid[None, :], (row_count, ctx_keys.shape[0])), causal], axis=1
    )
    return (jnp.where(allowed[None], scores, NEG_LARGE), query_heads, key_heads)


def attend_forward(block_item):
    queries, key_rows, value_rows, ctx_keys, ctx_values, ctx_valid = block_item
    scores, query_heads, key_heads = block_scores(queries, key_rows, ctx_keys, ctx_valid)
    row_max = jnp.max(scores, axis=-1, keepdims=True)
    expos = jnp.exp(scores - row_max)
    denominator = jnp.sum(expos, axis=-1, keepdims=True)
    weights = (expos / denominator).astype(jnp.bfloat16)
    value_heads = jnp.concatenate([ctx_values, value_rows], 0).reshape(key_heads.shape)
    attended = jnp.einsum("hqk,khd->qhd", weights, value_heads, preferred_element_type=jnp.float32)
    return (
        attended.reshape(queries.shape).astype(jnp.bfloat16),
        (row_max + jnp.log(denominator))[..., 0],
    )


def attend_backward(block_item):
    queries, key_rows, value_rows, ctx_keys, ctx_values, ctx_valid, log_total, grad_attended = (
        block_item
    )
    scores, query_heads, key_heads = block_scores(queries, key_rows, ctx_keys, ctx_valid)
    probs = jnp.exp(scores - log_total[..., None])
    value_heads = jnp.concatenate([ctx_values, value_rows], 0).reshape(key_heads.shape)
    grad_heads = grad_attended.reshape(query_heads.shape)
    grad_probs = jnp.einsum(
        "qhd,khd->hqk", grad_heads, value_heads, preferred_element_type=jnp.float32
    )
    grad_scores = (
        probs * (grad_probs - jnp.sum(probs * grad_probs, axis=-1, keepdims=True))
    ).astype(jnp.bfloat16)
    grad_values = jnp.einsum(
        "hqk,qhd->khd", probs.astype(jnp.bfloat16), grad_heads, preferred_element_type=jnp.float32
    )
    grad_queries = jnp.einsum(
        "hqk,khd->qhd", grad_scores, key_heads, preferred_element_type=jnp.float32
    ) * DH ** (-0.5)
    grad_keys = jnp.einsum(
        "hqk,qhd->khd", grad_scores, query_heads, preferred_element_type=jnp.float32
    ) * DH ** (-0.5)
    ctx_count = ctx_keys.shape[0]
    model_width = queries.shape[1]
    grad_keys = grad_keys.reshape(-1, model_width).astype(jnp.bfloat16)
    grad_values = grad_values.reshape(-1, model_width).astype(jnp.bfloat16)
    return (
        grad_queries.reshape(queries.shape).astype(jnp.bfloat16),
        grad_keys[ctx_count:],
        grad_values[ctx_count:],
        grad_keys[:ctx_count],
        grad_values[:ctx_count],
    )


def per_device(
    tokens,
    lengths,
    first_gain,
    first_bias,
    decay_rates,
    state_in,
    state_out,
    skip_gain,
    query_weight,
    key_weight,
    value_weight,
    output_weight,
    second_gain,
    second_bias,
    up_weight,
    up_bias,
    down_weight,
    down_bias,
    cotangent,
):
    full_query, full_key, full_value, full_output, full_up, full_down, full_in, full_out = (
        lax.all_gather(query_weight, "shard", axis=0, tiled=True),
        lax.all_gather(key_weight, "shard", axis=0, tiled=True),
        lax.all_gather(value_weight, "shard", axis=0, tiled=True),
        lax.all_gather(output_weight, "shard", axis=0, tiled=True),
        lax.all_gather(up_weight, "shard", axis=0, tiled=True),
        lax.all_gather(down_weight, "shard", axis=0, tiled=True),
        lax.all_gather(state_in, "shard", axis=1, tiled=True),
        lax.all_gather(state_out, "shard", axis=1, tiled=True),
    )
    seq_count, seq_len, model_width = tokens.shape
    row_count = seq_count * seq_len
    block_count = seq_count * NBLK
    positions = lax.broadcasted_iota(jnp.int32, (seq_count, seq_len), 1)
    row_mask = (positions < lengths[:, None]).astype(jnp.float32).reshape(row_count, 1)
    block_index = lax.broadcasted_iota(jnp.int32, (seq_count, NBLK, CTX), 1)
    ctx_valid = (block_index > 0).reshape(block_count, CTX)
    token_rows = tokens.astype(jnp.float32)
    normed, first_pullback = jax.vjp(layer_norm, token_rows, first_gain, first_bias)
    rounded = normed.astype(jnp.bfloat16)
    driven_raw = jnp.einsum("std,pd->stp", rounded, full_in, preferred_element_type=jnp.float32)
    context, state_pullback = jax.vjp(
        state_context, driven_raw, normed, decay_rates, full_out.astype(jnp.float32), skip_gain
    )
    ctx_rows = context.astype(jnp.bfloat16).reshape(block_count * CTX, model_width)
    flat_rounded = rounded.reshape(row_count, model_width)
    query_rows = jnp.dot(flat_rounded, full_query, preferred_element_type=jnp.float32).astype(
        jnp.bfloat16
    )
    key_rows = jnp.dot(flat_rounded, full_key, preferred_element_type=jnp.float32).astype(
        jnp.bfloat16
    )
    value_rows = jnp.dot(flat_rounded, full_value, preferred_element_type=jnp.float32).astype(
        jnp.bfloat16
    )
    ctx_keys = jnp.dot(ctx_rows, full_key, preferred_element_type=jnp.float32).astype(jnp.bfloat16)
    ctx_values = jnp.dot(ctx_rows, full_value, preferred_element_type=jnp.float32).astype(
        jnp.bfloat16
    )
    block_inputs = (
        query_rows.reshape(block_count, BLK, model_width),
        key_rows.reshape(block_count, BLK, model_width),
        value_rows.reshape(block_count, BLK, model_width),
        ctx_keys.reshape(block_count, CTX, model_width),
        ctx_values.reshape(block_count, CTX, model_width),
        ctx_valid,
    )
    attended, log_total = lax.map(attend_forward, block_inputs)
    attended_rows = attended.reshape(row_count, model_width)
    residual = token_rows.reshape(row_count, model_width) + jnp.dot(
        attended_rows, full_output, preferred_element_type=jnp.float32
    )
    second, second_pullback = jax.vjp(layer_norm, residual, second_gain, second_bias)
    second_rows = second.astype(jnp.bfloat16)
    hidden = jnp.dot(second_rows, full_up, preferred_element_type=jnp.float32) + up_bias
    active, gelu_pullback = jax.vjp(jax.nn.gelu, hidden)
    active_rows = active.astype(jnp.bfloat16)
    branch = jnp.dot(active_rows, full_down, preferred_element_type=jnp.float32) + down_bias
    result = (
        ((residual + branch) * row_mask)
        .astype(jnp.bfloat16)
        .reshape(seq_count, seq_len, model_width)
    )
    full_query, full_key, full_value, full_output, full_up, full_down, full_in, full_out = (
        lax.all_gather(query_weight, "shard", axis=0, tiled=True),
        lax.all_gather(key_weight, "shard", axis=0, tiled=True),
        lax.all_gather(value_weight, "shard", axis=0, tiled=True),
        lax.all_gather(output_weight, "shard", axis=0, tiled=True),
        lax.all_gather(up_weight, "shard", axis=0, tiled=True),
        lax.all_gather(down_weight, "shard", axis=0, tiled=True),
        lax.all_gather(state_in, "shard", axis=1, tiled=True),
        lax.all_gather(state_out, "shard", axis=1, tiled=True),
    )
    grad_branch = cotangent.reshape(row_count, model_width).astype(jnp.float32) * row_mask
    branch_rounded = grad_branch.astype(jnp.bfloat16)
    grad_down = jnp.einsum(
        "rf,rd->fd", active_rows, branch_rounded, preferred_element_type=jnp.float32
    )
    grad_down_bias = jnp.sum(grad_branch, axis=0)
    grad_active = jnp.einsum(
        "rd,fd->rf", branch_rounded, full_down, preferred_element_type=jnp.float32
    )
    (grad_hidden,) = gelu_pullback(grad_active)
    hidden_rounded = grad_hidden.astype(jnp.bfloat16)
    grad_up = jnp.einsum(
        "rd,rf->df", second_rows, hidden_rounded, preferred_element_type=jnp.float32
    )
    grad_up_bias = jnp.sum(hidden_rounded.astype(jnp.float32), axis=0)
    grad_second = jnp.einsum(
        "rf,df->rd", hidden_rounded, full_up, preferred_element_type=jnp.float32
    )
    grad_residual_part, grad_second_gain, grad_second_bias = second_pullback(grad_second)
    grad_residual = grad_branch + grad_residual_part
    residual_rounded = grad_residual.astype(jnp.bfloat16)
    grad_output = jnp.einsum(
        "rd,re->de", attended_rows, residual_rounded, preferred_element_type=jnp.float32
    )
    grad_attended = jnp.einsum(
        "re,de->rd", residual_rounded, full_output, preferred_element_type=jnp.float32
    ).astype(jnp.bfloat16)
    grad_query_rows, grad_key_rows, grad_value_rows, grad_ctx_keys, grad_ctx_values = lax.map(
        attend_backward,
        block_inputs + (log_total, grad_attended.reshape(block_count, BLK, model_width)),
    )
    grad_query_rows = grad_query_rows.reshape(row_count, model_width)
    grad_key_rows = grad_key_rows.reshape(row_count, model_width)
    grad_value_rows = grad_value_rows.reshape(row_count, model_width)
    grad_ctx_keys = grad_ctx_keys.reshape(block_count * CTX, model_width)
    grad_ctx_values = grad_ctx_values.reshape(block_count * CTX, model_width)
    grad_query = jnp.einsum(
        "rd,re->de", flat_rounded, grad_query_rows, preferred_element_type=jnp.float32
    )
    grad_key = jnp.einsum(
        "rd,re->de", flat_rounded, grad_key_rows, preferred_element_type=jnp.float32
    ) + jnp.einsum("rd,re->de", ctx_rows, grad_ctx_keys, preferred_element_type=jnp.float32)
    grad_value = jnp.einsum(
        "rd,re->de", flat_rounded, grad_value_rows, preferred_element_type=jnp.float32
    ) + jnp.einsum("rd,re->de", ctx_rows, grad_ctx_values, preferred_element_type=jnp.float32)
    grad_normed = (
        jnp.einsum("re,de->rd", grad_query_rows, full_query, preferred_element_type=jnp.float32)
        + jnp.einsum("re,de->rd", grad_key_rows, full_key, preferred_element_type=jnp.float32)
        + jnp.einsum("re,de->rd", grad_value_rows, full_value, preferred_element_type=jnp.float32)
    )
    grad_context = jnp.einsum(
        "re,de->rd", grad_ctx_keys, full_key, preferred_element_type=jnp.float32
    ) + jnp.einsum("re,de->rd", grad_ctx_values, full_value, preferred_element_type=jnp.float32)
    grad_context = grad_context.reshape(seq_count, NBLK, CTX, model_width)
    grad_driven, state_normed, grad_rates, grad_state_out, grad_skip = state_pullback(grad_context)
    grad_in = jnp.einsum(
        "stp,std->pd", grad_driven, rounded, precision=HIGHEST, preferred_element_type=jnp.float32
    )
    state_rounded = jnp.einsum(
        "stp,pd->std", grad_driven, full_in, precision=HIGHEST, preferred_element_type=jnp.float32
    )
    normed_total = (
        grad_normed.reshape(seq_count, seq_len, model_width) + state_rounded + state_normed
    )
    tokens_part, grad_first_gain, grad_first_bias = first_pullback(normed_total)
    grad_tokens = (tokens_part + grad_residual.reshape(seq_count, seq_len, model_width)).astype(
        jnp.bfloat16
    )
    piece_query, piece_key, piece_value, piece_output, piece_up, piece_down, piece_in, piece_out = (
        lax.psum_scatter(grad_query, "shard", scatter_dimension=0, tiled=True),
        lax.psum_scatter(grad_key, "shard", scatter_dimension=0, tiled=True),
        lax.psum_scatter(grad_value, "shard", scatter_dimension=0, tiled=True),
        lax.psum_scatter(grad_output, "shard", scatter_dimension=0, tiled=True),
        lax.psum_scatter(grad_up, "shard", scatter_dimension=0, tiled=True),
        lax.psum_scatter(grad_down, "shard", scatter_dimension=0, tiled=True),
        lax.psum_scatter(grad_in, "shard", scatter_dimension=1, tiled=True),
        lax.psum_scatter(grad_state_out, "shard", scatter_dimension=1, tiled=True),
    )
    piece_query, piece_key, piece_value, piece_output, piece_up, piece_down, piece_in, piece_out = (
        lax.psum(piece_query.astype(jnp.bfloat16), "rep").astype(jnp.float32),
        lax.psum(piece_key.astype(jnp.bfloat16), "rep").astype(jnp.float32),
        lax.psum(piece_value.astype(jnp.bfloat16), "rep").astype(jnp.float32),
        lax.psum(piece_output.astype(jnp.bfloat16), "rep").astype(jnp.float32),
        lax.psum(piece_up.astype(jnp.bfloat16), "rep").astype(jnp.float32),
        lax.psum(piece_down.astype(jnp.bfloat16), "rep").astype(jnp.float32),
        lax.psum(piece_in.astype(jnp.bfloat16), "rep").astype(jnp.float32),
        lax.psum(piece_out.astype(jnp.bfloat16), "rep").astype(jnp.float32),
    )
    (
        sum_first_gain,
        sum_first_bias,
        sum_rates,
        sum_skip,
        sum_second_gain,
        sum_second_bias,
        sum_up_bias,
        sum_down_bias,
    ) = lax.psum(
        (
            grad_first_gain,
            grad_first_bias,
            grad_rates,
            grad_skip,
            grad_second_gain,
            grad_second_bias,
            grad_up_bias,
            grad_down_bias,
        ),
        ("rep", "shard"),
    )
    return (
        result,
        grad_tokens,
        sum_first_gain,
        sum_first_bias,
        sum_rates,
        piece_in,
        piece_out,
        sum_skip,
        piece_query,
        piece_key,
        piece_value,
        piece_output,
        sum_second_gain,
        sum_second_bias,
        piece_up,
        sum_up_bias,
        piece_down,
        sum_down_bias,
    )


def solution(mesh):
    placed = (
        P(("rep", "shard"), None, None),
        P(("rep", "shard")),
        P(),
        P(),
        P(),
        P(None, "shard"),
        P(None, "shard"),
        P(),
        P("shard", None),
        P("shard", None),
        P("shard", None),
        P("shard", None),
        P(),
        P(),
        P("shard", None),
        P(),
        P("shard", None),
        P(),
        P(("rep", "shard"), None, None),
    )
    fused = mesh.shape["rep"] == 2 and mesh.shape["shard"] == 2 * NC
    return jax.shard_map(
        fused_device if fused else per_device,
        mesh=mesh,
        in_specs=placed,
        out_specs=(
            P(("rep", "shard"), None, None),
            P(("rep", "shard"), None, None),
            P(),
            P(),
            P(),
            P(None, "shard"),
            P(None, "shard"),
            P(),
            P("shard", None),
            P("shard", None),
            P("shard", None),
            P("shard", None),
            P(),
            P(),
            P("shard", None),
            P(),
            P("shard", None),
            P(),
        ),
        check_vma=False,
    )
```

```python
import functools
import math

import jax
import jax.numpy as jnp
from jax import lax
from jax.experimental import pallas as pl
from jax.experimental.pallas import tpu as pltpu
from jax.sharding import PartitionSpec as P

DH = 128
BLK = 512
CTX = 128
NBLK = 2
EPS = 1e-05
NEG = -1e30
SCALE = DH ** (-0.5)
MESH = pl.DeviceIdType.MESH
F32 = jnp.float32
BF16 = jnp.bfloat16
VMEM_LIMIT = 66_000_000
NC = 8


def chip_at(pos):
    turned = pos // 4
    return (1 - turned) * (2 * pos) + turned * (2 * (7 - pos) + 1)


class Net:
    def __init__(self):
        self.rep = lax.axis_index("rep")
        self.shard = lax.axis_index("shard")
        self.core = self.shard % 2
        chip = self.shard // 2
        z, y = chip // 2, chip % 2
        self.pos = (1 - y) * z + y * (7 - z)
        self.step = 1 - 2 * self.core
        self.mate = (self.rep, 2 * chip + 1 - self.core)
        self.twin = (1 - self.rep, self.shard)

    def at(self, hops, core):
        return 2 * chip_at((self.pos + self.step * hops + 4 * NC) % NC) + core

    def along(self, hops):
        return (self.rep, self.at(hops, self.core))

    def greet(self):
        barrier = pltpu.get_barrier_semaphore()
        for device in (self.along(1), self.along(-1), self.mate, self.twin):
            pl.semaphore_signal(barrier, inc=1, device_id=device, device_id_type=MESH)
        pl.semaphore_wait(barrier, 4)


def rcopy(src, dst, send, recv, device):
    return pltpu.make_async_remote_copy(
        src_ref=src, dst_ref=dst, send_sem=send, recv_sem=recv, device_id=device, device_id_type=MESH
    )


def dot_nn(a, b):
    return lax.dot_general(a, b, (((1,), (0,)), ((), ())), preferred_element_type=F32)


def dot_nt(a, b):
    return lax.dot_general(a, b, (((1,), (1,)), ((), ())), preferred_element_type=F32)


def dot_tn(a, b):
    return lax.dot_general(a, b, (((0,), (0,)), ((), ())), preferred_element_type=F32)


def norm_parts(rows):
    centred = rows - jnp.mean(rows, axis=-1, keepdims=True)
    spread = jnp.mean(centred * centred, axis=-1, keepdims=True)
    inverse = lax.rsqrt(spread + EPS)
    return centred * inverse, inverse


def split_dot(dot, left, right, narrow):
    total = None
    rest = left
    for _ in range(narrow):
        term = rest.astype(BF16)
        part = dot(term, right)
        total = part if total is None else total + part
        rest = rest - term.astype(F32)
    return total


def lane_scan(values, factor, reverse):
    width = values.shape[1]
    lane = lax.broadcasted_iota(jnp.int32, values.shape, 1)
    shift = 1
    power = factor
    while shift < width:
        if reverse:
            moved = pltpu.roll(values, width - shift, 1)
            moved = jnp.where(lane < width - shift, moved, 0.0)
        else:
            moved = pltpu.roll(values, shift, 1)
            moved = jnp.where(lane >= shift, moved, 0.0)
        values = values + power * moved
        power = power * power
        shift *= 2
    return values


def forward_kernel(
    tok, wq, wk, wv, wo, wup, wdn, s_in, s_out, fg, fb, skip, sg, sb, decay,
    wall, wdpre, sio_all, rnd_o, q_o, k_o, v_o, att_o, res_o, sec_o, p_o, u_o, st_o,
    tok_s, rnd_s, w_s, q_s, k_s, v_s, att_s, res_s, sec_s, pbuf, nctx, sio_s,
    own_s, sio_own, loc, rs, rr, ss, sr, cs, cr, xs, xr, outs, psem, ds, dr,
):
    net = Net()
    rep, core = net.rep, net.core
    rows_of = 64
    width = 1024

    def block(shard):
        return pl.ds(pl.multiple_of(shard * rows_of, rows_of), rows_of)

    mine = block(net.shard)
    own = [wq, wk, wv, wo]
    copies = [pltpu.make_async_copy(own[i], own_s.at[i], loc.at[i]) for i in range(4)]
    copies += [
        pltpu.make_async_copy(wup.at[:, pl.ds(i * width, width)], own_s.at[4 + i], loc.at[4 + i])
        for i in range(4)
    ]
    small = pltpu.make_async_copy(sio_own, sio_all.at[mine], loc.at[8])
    arrive = pltpu.make_async_copy(tok, tok_s, loc.at[9])
    for copy in copies:
        copy.start()
    arrive.start()
    packed = jnp.concatenate(
        [s_in[...].astype(F32), s_out[...].astype(F32), jnp.zeros((96, rows_of), F32)], axis=0
    )
    sio_own[...] = packed.T.astype(BF16)
    small.start()
    net.greet()
    for copy in copies:
        copy.wait()

    def piece(slot):
        if isinstance(slot, int) and slot < 2:
            return 1 if slot else 2 * rep
        later = slot - 2
        return 3 + later + (1 + 3 * rep) * ((3 - later) // 3) - (later % 2) * (3 - later) // 2

    def ring(slot, way, hop, which, where):
        ref = wall.at[which, where]
        sems = rs.at[slot, way, hop], rr.at[slot, way, hop]
        return rcopy(ref, ref, *sems, net.along(1 - 2 * way))

    def ring_own(slot, way):
        which = piece(slot)
        sems = rs.at[slot, way, 0], rr.at[slot, way, 0]
        ref = wall.at[which, mine]
        rcopy(own_s.at[which], ref, *sems, net.along(1 - 2 * way)).start()

    def ring_small(way, hop, where):
        ref = sio_all.at[where]
        return rcopy(ref, ref, ss.at[way, hop], sr.at[way, hop], net.along(1 - 2 * way))

    def mate(which, index, where):
        ref = wall.at[which, where]
        return rcopy(ref, ref, cs.at[which, index], cr.at[which, index], net.mate)

    def mate_small(index, where):
        ref = sio_all.at[where]
        return rcopy(ref, ref, cs.at[8, index], cr.at[8, index], net.mate)

    def twin(turn, index, which, where):
        ref = wall.at[which, where]
        return rcopy(ref, ref, xs.at[turn, index], xr.at[turn, index], net.twin)

    hand = rcopy(wdn, wdpre.at[0], ds.at[0], dr.at[0], net.along(1))
    hand_on = rcopy(wdpre.at[0], wdpre.at[1], ds.at[1], dr.at[1], net.mate)

    def source(way, hop):
        return block(net.at((2 * way - 1) * (hop + 1), core))

    def serve(slot, way, hop):
        which = piece(slot)
        where = source(way, hop)
        ring(slot, way, hop, which, where).wait_recv()

        @pl.when(hop < 3 - way)
        def _():
            ring(slot, way, hop + 1, which, where).start()

        mate(which, 1 + 2 * hop + way, where).start()

    def serve_out(slot, turn, way, hop):
        twin(turn, 2 * hop + way, piece(slot), source(way, hop)).start()

    def serve_in(turn, way, hop):
        where = source(way, hop)
        which = 2 * (1 - rep) if turn == 0 else 7 - 3 * rep
        twin(turn, 2 * hop + way, which, where).wait_recv()
        mate(which, 1 + 2 * hop + way, where).start()

    for slot in range(2):
        for way in range(2):
            ring_own(slot, way)
    small.wait()
    for way in range(2):
        ring_small(way, 0, mine).start()
    mate_small(0, mine).start()
    for which in range(8):
        rcopy(own_s.at[which], wall.at[which, mine], cs.at[which, 0], cr.at[which, 0], net.mate).start()
    keep = [pltpu.make_async_copy(own_s.at[i], wall.at[i, mine], loc.at[i]) for i in range(8)]
    for copy in keep:
        copy.start()
    arrive.wait()

    def first_norm(at):
        rows = pl.ds(pl.multiple_of(at * 128, 128), 128)
        xhat, _ = norm_parts(tok_s[rows, :].astype(F32))
        normed = xhat * fg[...] + fb[...]
        rnd_s[rows, :] = normed.astype(BF16)

    order = [
        (hop, slot, way) for hop in range(4) for slot in range(2) for way in range(2) if hop < 4 - way
    ]
    owed = []
    for n, (hop, slot, way) in enumerate(order):
        if n % 2 == 0:
            first_norm(n // 2)
        serve(slot, way, hop)
        if slot == 0:
            serve_out(0, 0, way, hop)
            owed.append((n, way, hop))
        else:
            where = source(way, hop)
            ring_small(way, hop, where).wait_recv()
            if hop < 3 - way:
                ring_small(way, hop + 1, where).start()
            mate_small(1 + 2 * hop + way, where).start()
        if n in (12, 13):
            for later in range(2):
                for each in range(2):
                    ring_own((2 if n == 12 else 4) + later, each)
        if owed and n - owed[0][0] >= 4:
            serve_in(0, *owed.pop(0)[1:])
    first_norm(7)
    for each in owed:
        serve_in(0, *each[1:])

    def event(m):
        half, place = m // 14, m % 14
        late = place // 12
        hop = place // 4
        index = ((place % 4) // 2) * (1 - late) + (place - 12) * late
        way = (place % 2) * (1 - late)
        slot = 2 + 2 * half + index
        serve(slot, way, hop)

        @pl.when(slot == 2)
        def _():
            serve_out(2, 1, way, hop)

        @pl.when(m == 10)
        def _():
            hand.start()

        @pl.when((m >= 8) & (m <= 20) & (m % 4 < 2))
        def _():
            serve_in(1, m % 2, (m - 8) // 4)

    xhat, _ = norm_parts(tok_s[pl.ds(BLK - CTX, CTX), :].astype(F32))
    nctx[...] = xhat * fg[...] + fb[...]

    @pl.loop(0, NC)
    def _(index):
        where = block(0)
        mate_small(index, where).wait_recv()
        for which in range(3):
            mate(which, index, where).wait_recv()

    for copy in keep:
        copy.wait()
    loads = [pltpu.make_async_copy(sio_all, sio_s, loc.at[8])]
    loads += [pltpu.make_async_copy(wall.at[i], w_s.at[i], loc.at[i]) for i in range(3)]
    for copy in loads:
        copy.start()
    loads[0].wait()
    u_all = lax.dot_general(
        sio_s[...], rnd_s[pl.ds(0, BLK), :], (((0,), (1,)), ((), ())), preferred_element_type=F32
    )
    factor = jnp.exp(-column(decay[...]))
    raw = u_all[0:16, :]
    u_o[...] = raw
    states = lane_scan(raw * jnp.sqrt(1.0 - factor * factor), factor, False)
    st_o[...] = states
    tail = states[:, BLK - CTX :]
    padded = jnp.concatenate(
        [jnp.zeros((16, CTX), F32), tail, jnp.zeros((96, CTX), F32)], axis=0
    )
    made = split_dot(
        lambda a, b: lax.dot_general(a, b, (((0,), (1,)), ((), ())), preferred_element_type=F32),
        padded, sio_s[...], 3,
    )
    rnd_s[pl.ds(1024, CTX), :] = (made + skip[...] * nctx[...]).astype(BF16)
    finals = [pltpu.make_async_copy(rnd_s, rnd_o, outs.at[0])]
    finals[0].start()

    for copy in loads[1:]:
        copy.wait()

    @pl.loop(0, 4)
    def _(at):
        cols = pl.ds(pl.multiple_of(at * 256, 256), 256)
        q_s[:, cols] = dot_nn(rnd_s[pl.ds(0, 1024), :], w_s[0, :, cols]).astype(BF16)
        event(2 * at)
        k_s[:, cols] = dot_nn(rnd_s[...], w_s[1, :, cols]).astype(BF16)
        v_s[:, cols] = dot_nn(rnd_s[...], w_s[2, :, cols]).astype(BF16)
        event(2 * at + 1)

    for i, (a, b) in enumerate(((q_s, q_o), (k_s, k_o), (v_s, v_o))):
        finals.append(pltpu.make_async_copy(a, b, outs.at[1 + i]))
        finals[-1].start()

    for half in range(2):
        pbuf[half] = jnp.zeros((BLK, CTX + BLK), BF16)

    def p_copy(slot, at):
        return pltpu.make_async_copy(pbuf.at[slot], p_o.at[at], psem.at[slot])

    for b in range(NBLK):

        @pl.loop(0, 8)
        def _(h, b=b):
            cols = pl.ds(pl.multiple_of(h * DH, DH), DH)
            slot = h % 2
            if b == 0:

                @pl.when(h >= 2)
                def _():
                    p_copy(slot, h).wait()
            else:
                p_copy(slot, h).wait()
            for i in range(2):
                span = (i + 1) * 256
                rows = pl.ds(b * BLK + i * 256, 256)
                queries = q_s[rows, cols]
                scores = dot_nt(queries, k_s[pl.ds(b * BLK, span), cols]) * SCALE
                ahead = lax.broadcasted_iota(jnp.int32, scores.shape, 0) + i * 256
                scores = jnp.where(
                    ahead >= lax.broadcasted_iota(jnp.int32, scores.shape, 1), scores, NEG
                )
                top = jnp.max(scores, axis=-1, keepdims=True)
                if b:
                    before = dot_nt(queries, k_s[pl.ds(1024, CTX), cols]) * SCALE
                    top = jnp.maximum(top, jnp.max(before, axis=-1, keepdims=True))
                expos = jnp.exp(scores - top)
                total = jnp.sum(expos, axis=-1, keepdims=True)
                if b:
                    expos_before = jnp.exp(before - top)
                    total = total + jnp.sum(expos_before, axis=-1, keepdims=True)
                share = 1.0 / total
                weights = (expos * share).astype(BF16)
                mixed = dot_nn(weights, v_s[pl.ds(b * BLK, span), cols])
                pbuf[slot, pl.ds(i * 256, 256), pl.ds(CTX, span)] = weights
                if b:
                    weights = (expos_before * share).astype(BF16)
                    mixed = mixed + dot_nn(weights, v_s[pl.ds(1024, CTX), cols])
                    pbuf[slot, pl.ds(i * 256, 256), pl.ds(0, CTX)] = weights
                att_s[rows, cols] = mixed.astype(BF16)
            p_copy(slot, b * 8 + h).start()

            event(8 + 8 * b + h)

    finals.append(pltpu.make_async_copy(att_s, att_o, outs.at[4]))
    finals[-1].start()

    @pl.loop(0, NC)
    def _(index):
        mate(3, index, block(0)).wait_recv()

    load = pltpu.make_async_copy(wall.at[3], w_s.at[3], loc.at[3])
    load.start()
    load.wait()

    @pl.loop(0, 4)
    def _(at):
        rows = pl.ds(pl.multiple_of(at * 256, 256), 256)
        residual = tok_s[rows, :].astype(F32) + dot_nn(att_s[rows, :], w_s[3])
        res_s[rows, :] = residual
        xhat, _ = norm_parts(residual)
        sec_s[rows, :] = (xhat * sg[...] + sb[...]).astype(BF16)
        pltpu.make_async_copy(res_s.at[rows], res_o.at[rows], outs.at[5 + at]).start()
        pltpu.make_async_copy(sec_s.at[rows], sec_o.at[rows], outs.at[9 + at]).start()
        event(24 + at)

        @pl.when(at == 0)
        def _():
            hand.wait_recv()
            hand_on.start()

    for copy in finals:
        copy.wait()
    for at in range(4):
        rows = pl.ds(at * 256, 256)
        pltpu.make_async_copy(res_s.at[rows], res_o.at[rows], outs.at[5 + at]).wait()
        pltpu.make_async_copy(sec_s.at[rows], sec_o.at[rows], outs.at[9 + at]).wait()
    for slot in range(2):
        p_copy(slot, slot).wait()

    hand.wait_send()
    hand_on.wait()

    @pl.loop(0, NC)
    def _(index):
        for which in range(4, 8):
            mate(which, index, block(0)).wait_recv()
        for which in range(8):
            mate(which, index, block(0)).wait_send()
        mate_small(index, block(0)).wait_send()

    @pl.loop(0, NC - 1)
    def _(index):
        hop = index // 2
        way = index % 2
        for slot in range(6):
            ring(slot, way, hop, 0, block(0)).wait_send()
        ring_small(way, hop, block(0)).wait_send()
        for turn in range(2):
            twin(turn, index, 0, block(0)).wait_send()


def column(row):
    wide = jnp.broadcast_to(row, (16, 16))
    same = lax.broadcasted_iota(jnp.int32, (16, 16), 0) == lax.broadcasted_iota(jnp.int32, (16, 16), 1)
    return jnp.sum(jnp.where(same, wide, 0.0), axis=1, keepdims=True)


def any_spec(n):
    return [pl.BlockSpec(memory_space=pl.ANY)] * n


def vmem_spec(n):
    return [pl.BlockSpec(memory_space=pltpu.VMEM)] * n


def run_forward(tok, wq, wk, wv, wo, wup, wdn, s_in, s_out, fg, fb, skip, sg, sb, decay):
    shape = jax.ShapeDtypeStruct
    dma = pltpu.SemaphoreType.DMA
    big = (1024, 1024)
    ext = (1024 + CTX, 1024)
    return pl.pallas_call(
        forward_kernel,
        name="forward_part",
        out_shape=(
            shape((8,) + big, BF16), shape((2, 256, 1024), BF16), shape((1024, 128), BF16),
            shape(ext, BF16), shape(big, BF16),
            shape(ext, BF16), shape(ext, BF16), shape(big, BF16), shape(big, F32),
            shape(big, BF16), shape((16, BLK, CTX + BLK), BF16), shape((16, BLK), F32),
            shape((16, BLK), F32),
        ),
        in_specs=any_spec(7) + vmem_spec(8),
        out_specs=any_spec(11) + vmem_spec(2),
        scratch_shapes=[
            pltpu.VMEM(big, BF16), pltpu.VMEM(ext, BF16), pltpu.VMEM((4,) + big, BF16),
            pltpu.VMEM(big, BF16), pltpu.VMEM(ext, BF16), pltpu.VMEM(ext, BF16),
            pltpu.VMEM(big, BF16), pltpu.VMEM(big, F32), pltpu.VMEM(big, BF16),
            pltpu.VMEM((2, BLK, CTX + BLK), BF16), pltpu.VMEM((CTX, 1024), F32),
            pltpu.VMEM((1024, 128), BF16),
            pltpu.VMEM((8, 64, 1024), BF16), pltpu.VMEM((64, 128), BF16),
            dma((10,)), dma((6, 2, 4)), dma((6, 2, 4)), dma((2, 4)), dma((2, 4)),
            dma((9, NC)), dma((9, NC)), dma((2, NC - 1)), dma((2, NC - 1)), dma((13,)), dma((2,)), dma((2,)), dma((2,)),
        ],
        compiler_params=pltpu.CompilerParams(
            collective_id=0, has_side_effects=True, vmem_limit_bytes=VMEM_LIMIT
        ),
    )(tok, wq, wk, wv, wo, wup, wdn, s_in, s_out, fg, fb, skip, sg, sb, decay)


GELU_C = math.sqrt(2.0 / math.pi)
GELU_A = 0.044715


def feed_kernel(
    sec, res, wall, wdn, wdpre, cot, live, upb, dnb, sg,
    out_o, gatt_o, dwown_o, dwmate_o, fin_o, gdb_o, gub_o, gsg_o, gsb_o,
    sec_s, gb_s, wup_s, wd_s, br_s, gs_s, act_s, gh_s, a_s, b_s, prec, rrec, rsend, xsend, xrec,
    dwup_s, own_s, res_s,
    loc, ars, arr, axs, axr, cas, car, cxs, cxr, ps, pr, rs, rr, xs, xr, outs, dsem, dms, dmr,
):
    net = Net()
    rep, core = net.rep, net.core
    rows_of = 256
    ring_rows = 192
    part = 64
    ahead, behind = net.along(1), net.along(-1)

    def ring_part(shard, j, first=rep):
        return pl.ds(pl.multiple_of(shard * rows_of + (first + j) * part, part), part)

    def sole_part(shard, of):
        return pl.ds(pl.multiple_of(shard * rows_of + 3 * of * part, part), part)

    def block(shard):
        return pl.ds(pl.multiple_of(shard * rows_of, rows_of), rows_of)

    def mine_at(step):
        return net.at(-(step + 1), core)

    def other_at(step):
        return net.at(step + 1, 1 - core)

    loads = [
        pltpu.make_async_copy(wdn, own_s, loc.at[0]),
        pltpu.make_async_copy(sec, sec_s, loc.at[1]),
        pltpu.make_async_copy(cot, gb_s, loc.at[2]),
        pltpu.make_async_copy(wdpre.at[0], wd_s.at[block(mine_at(0))], loc.at[7]),
        pltpu.make_async_copy(wdpre.at[1], wd_s.at[block(other_at(0))], loc.at[8]),
    ]
    loads += [pltpu.make_async_copy(wall.at[4 + i], wup_s.at[i], loc.at[3 + i]) for i in range(4)]
    for load in loads:
        load.start()
    net.greet()
    loads[0].wait()
    loads[3].wait()

    def gather(j, hop, shard):
        ref = wd_s.at[ring_part(shard, j)]
        return rcopy(ref, ref, ars.at[j, hop], arr.at[j, hop], ahead)

    def gather_twin(hop, shard, of):
        ref = wd_s.at[sole_part(shard, of)]
        return rcopy(ref, ref, axs.at[hop], axr.at[hop], net.twin)

    def mate_ring(j, index, shard):
        ref = wd_s.at[ring_part(shard, j)]
        return rcopy(ref, ref, cas.at[j, index], car.at[j, index], net.mate)

    def mate_sole(index, shard, of):
        ref = wd_s.at[sole_part(shard, of)]
        return rcopy(ref, ref, cxs.at[index], cxr.at[index], net.mate)

    here = net.shard
    sole_own = own_s.at[pl.ds(pl.multiple_of(3 * (1 - rep) * part, part), part)]
    for j in range(3):
        ring_own = own_s.at[pl.ds(pl.multiple_of((rep + j) * part, part), part)]
        target = wd_s.at[ring_part(here, j)]
        gather(j, 1, mine_at(0)).start()
        rcopy(ring_own, target, cas.at[j, 0], car.at[j, 0], net.mate).start()
    rcopy(sole_own, wd_s.at[sole_part(here, 1 - rep)], cxs.at[0], cxr.at[0], net.mate).start()

    def serve(j, hop):
        shard = mine_at(hop)
        gather(j, hop, shard).wait_recv()

        @pl.when(hop < NC - 2)
        def _():
            gather(j, hop + 1, shard).start()

        @pl.when(j == 2 * rep)
        def _():
            gather_twin(hop, shard, rep).start()

        mate_ring(j, hop + 1, shard).start()

    def serve_twin(hop):
        shard = mine_at(hop)
        gather_twin(hop, shard, 1 - rep).wait_recv()
        mate_sole(hop + 1, shard, 1 - rep).start()

    for load in loads[1:3]:
        load.wait()

    wd_s[block(here), :] = own_s[...]

    @pl.loop(0, 4)
    def _(at):
        rows = pl.ds(pl.multiple_of(at * 256, 256), 256)
        when = lax.broadcasted_iota(jnp.int32, (256, 1024), 0) + at * 256
        kept = jnp.where(when < live[0], gb_s[rows, :].astype(F32), 0.0)
        gb_s[rows, :] = kept.astype(BF16)
        added = jnp.sum(kept, axis=0, keepdims=True)
        gdb_o[...] = jnp.where(at == 0, added, gdb_o[...] + added)
        br_s[rows, :] = jnp.zeros((256, 1024), F32)
        gs_s[rows, :] = jnp.zeros((256, 1024), F32)

    for load in loads[4:]:
        load.wait()

    def to_mate(step):
        slot = step % 2
        return rcopy(b_s.at[slot], prec.at[step], ps.at[step], pr.at[step], net.mate)

    def to_ring(j, step):
        return rcopy(rsend.at[step % 2, j], rrec.at[step, j], rs.at[step, j], rr.at[step, j], ahead)

    def to_twin(step):
        return rcopy(xsend.at[step % 2], xrec.at[step], xs.at[step], xr.at[step], net.twin)

    def dwup_at(target, shard):
        cols = pl.ds(pl.multiple_of((shard % 4) * 256, 256), 256)
        return target.at[shard // 4, :, :, cols]

    def dwup_copy(slot, half, shard):
        return pltpu.make_async_copy(
            dwup_s.at[slot, half, :, core], dwup_at(dwown_o, shard), dsem.at[slot, half]
        )

    def dwup_mate(step, half, shard):
        return rcopy(
            dwup_s.at[step % 2, half, :, 1 - core], dwup_at(dwmate_o, shard),
            dms.at[step, half], dmr.at[step, half], net.mate,
        )

    ring_local = pl.ds(pl.multiple_of(rep * part, part), ring_rows)
    sole_mine = pl.ds(pl.multiple_of(3 * rep * part, part), part)
    sole_theirs = pl.ds(pl.multiple_of(3 * (1 - rep) * part, part), part)

    def combine(step):
        slot = step % 2
        to_mate(step).wait_recv()

        @pl.when(step >= 2)
        def _():
            to_twin(step - 2).wait_send()

        xsend[slot] = (a_s[slot, sole_theirs, :] + prec[step, sole_theirs, :].astype(F32)).astype(BF16)
        to_twin(step).start()

    def forward(j, step):
        slot = step % 2
        rows = pl.ds(pl.multiple_of((rep + j) * part, part), part)

        def both():
            return a_s[slot, rows, :] + prec[step, rows, :].astype(F32)

        def with_ring():
            return both() + rrec[step - 1, j].astype(F32)

        @pl.when(j == 2 * rep)
        def _():
            to_twin(step).wait_recv()
            a_s[slot, rows, :] = a_s[slot, rows, :] + xrec[step].astype(F32)

        @pl.when(step == 0)
        def _():
            rsend[slot, j] = both().astype(BF16)

        @pl.when(step >= 1)
        def _():
            to_ring(j, step - 1).wait_recv()

        @pl.when((step >= 2) & (step < NC - 1))
        def _():
            to_ring(j, step - 2).wait_send()

        @pl.when((step >= 1) & (step < NC - 1))
        def _():
            rsend[slot, j] = with_ring().astype(BF16)

        @pl.when(step < NC - 1)
        def _():
            to_ring(j, step).start()

        @pl.when(step == NC - 1)
        def _():
            a_s[slot, rows, :] = with_ring()

    @pl.loop(0, NC)
    def _(step):
        slot = step % 2
        a, b = mine_at(step), other_at(step)
        index = (step + 1) % NC

        @pl.when(step >= 1)
        def _():
            combine(step - 1)

        def up(shard):
            cols = pl.ds(pl.multiple_of((shard % 4) * 256, 256), 256)
            return wup_s[shard // 4, :, cols]

        def bias(shard):
            return upb[:, pl.ds(pl.multiple_of(shard * 256, 256), 256)]

        @pl.loop(0, 2)
        def _(half):
            @pl.when((half == 1) & (step >= 1))
            def _():
                for j in range(3):
                    mate_ring(j, index, b).wait_recv()
                mate_sole(index, b, 1 - rep).wait_recv()

            shard = a + half * (b - a)
            cols = pl.ds(pl.multiple_of(half * 256, 256), 256)
            hidden = dot_nn(sec_s[...], up(shard)) + bias(shard)
            grad = dot_nt(gb_s[...], wd_s[block(shard), :])
            square = hidden * hidden
            bent = jnp.tanh(hidden * (GELU_C + (GELU_C * GELU_A) * square))
            half_up = 0.5 + 0.5 * bent
            act_s[:, cols] = (hidden * half_up).astype(BF16)
            slope = half_up + (0.5 * hidden) * (1.0 - bent * bent) * (
                GELU_C + (3.0 * GELU_C * GELU_A) * square
            )
            gh_s[:, cols] = (grad * slope).astype(BF16)

            @pl.when(step < NC - 2)
            def _():
                serve((2 * rep + half) % 3, step + 1)

            @pl.when((half == 1) & (step < NC - 2))
            def _():
                serve((2 * rep + 2) % 3, step + 1)

        made = dot_tn(act_s[...], gb_s[...])

        @pl.when(step >= 2)
        def _():
            to_mate(step - 2).wait_send()

        a_s[slot] = made[0:256]
        b_s[slot] = made[256:512].astype(BF16)
        to_mate(step).start()

        rise_up = dot_tn(sec_s[...], gh_s[...]).astype(BF16)
        for half, shard in enumerate((a, b)):
            cols = pl.ds(pl.multiple_of(shard * 256, 256), 256)
            gub_o[:, cols] = jnp.sum(
                gh_s[:, half * 256 : half * 256 + 256].astype(F32), axis=0, keepdims=True
            )

            @pl.when(step >= 2)
            def _(half=half, shard=shard):
                dwup_copy(slot, half, shard).wait()
                dwup_mate(step - 2, half, shard).wait_send()

            dwup_s[slot, half] = rise_up[:, half * 256 : half * 256 + 256].reshape(NC, 2, 64, 256)
            dwup_copy(slot, half, shard).start()
            dwup_mate(step, half, shard).start()

        @pl.loop(0, 2)
        def _(at):
            rows = pl.ds(pl.multiple_of(at * 512, 512), 512)

            def rise_of(shard):
                cols = pl.ds(pl.multiple_of((shard % 4) * 256, 256), 256)
                return wup_s[shard // 4, rows, cols]

            down = jnp.concatenate([wd_s[block(a), rows], wd_s[block(b), rows]], axis=0)
            br_s[:, rows] = br_s[:, rows] + dot_nn(act_s[...], down)
            rise = jnp.concatenate([rise_of(a), rise_of(b)], axis=1)
            gs_s[:, rows] = gs_s[:, rows] + dot_nt(gh_s[...], rise)

            @pl.when(step >= 1)
            def _():
                forward((2 * rep + 1 + at) % 3, step - 1)

            @pl.when((at == 1) & (step < NC - 2))
            def _():
                serve_twin(step + 1)

        @pl.when(step >= 1)
        def _():
            forward((2 * rep + 3) % 3, step - 1)

    def residual_in(at):
        rows = pl.ds(at * 256, 256)
        return pltpu.make_async_copy(res.at[rows], res_s.at[rows], loc.at[at])

    for at in range(4):
        residual_in(at).start()
    combine(NC - 1)

    def leave(at, which):
        rows = pl.ds(pl.multiple_of(at * 256, 256), 256)
        source = (sec_s, gb_s)[which]
        return pltpu.make_async_copy(
            source.at[rows], (out_o, gatt_o)[which].at[rows], outs.at[which, at]
        )

    @pl.loop(0, 4)
    def _(at):
        residual_in(at).wait()
        rows = pl.ds(pl.multiple_of(at * 256, 256), 256)
        kept = res_s[rows, :]
        when = lax.broadcasted_iota(jnp.int32, (256, 1024), 0) + at * 256
        total = kept + br_s[rows, :] + dnb[...]
        sec_s[rows, :] = jnp.where(when < live[0], total, 0.0).astype(BF16)
        xhat, inverse = norm_parts(kept)
        grad = gs_s[rows, :]
        gain = jnp.sum(grad * xhat, axis=0, keepdims=True)
        shift = jnp.sum(grad, axis=0, keepdims=True)
        gsg_o[...] = jnp.where(at == 0, gain, gsg_o[...] + gain)
        gsb_o[...] = jnp.where(at == 0, shift, gsb_o[...] + shift)
        grad = grad * sg[...]
        grad = grad - jnp.mean(grad, axis=-1, keepdims=True) - xhat * jnp.mean(
            grad * xhat, axis=-1, keepdims=True
        )
        gb_s[rows, :] = (gb_s[rows, :].astype(F32) + inverse * grad).astype(BF16)
        for which in range(2):
            leave(at, which).start()

    for j in range(3):
        forward((2 * rep + 1 + j) % 3, NC - 1)
    last = (NC - 1) % 2
    fin_o[...] = a_s[last, ring_local, :].astype(BF16)

    @pl.loop(1, NC - 1)
    def _(hop):
        for j in range(3):
            gather(j, hop, 0).wait_send()
        gather_twin(hop, 0, 0).wait_send()

    @pl.loop(1, NC)
    def _(later):
        index = (later + 1) % NC
        for j in range(3):
            mate_ring(j, index, 0).wait_send()
        mate_sole(index, 0, 0).wait_send()

    for step in range(NC - 2, NC):
        to_mate(step).wait_send()
        to_twin(step).wait_send()
        for j in range(3):
            to_ring(j, step - 1).wait_send()
        for half in range(2):
            dwup_copy(step % 2, half, 0).wait()
            dwup_mate(step, half, 0).wait_send()
    for at in range(4):
        for which in range(2):
            leave(at, which).wait()

    @pl.loop(0, NC)
    def _(step):
        for half in range(2):
            dwup_mate(step, half, 0).wait_recv()


def run_feed(sec, res, wall, wdn, wdpre, cot, live, upb, dnb, sg):
    shape = jax.ShapeDtypeStruct
    dma = pltpu.SemaphoreType.DMA
    vmem = pltpu.VMEM
    big = (1024, 1024)
    return pl.pallas_call(
        feed_kernel,
        name="feed_part",
        out_shape=(
            shape(big, BF16), shape(big, BF16), shape((4, NC, 64, 1024), BF16),
            shape((4, NC, 64, 1024), BF16), shape((192, 1024), BF16), shape((1, 1024), F32), shape((1, 4096), F32),
            shape((1, 1024), F32), shape((1, 1024), F32),
        ),
        in_specs=any_spec(6) + [pl.BlockSpec(memory_space=pltpu.SMEM)] + vmem_spec(3),
        out_specs=any_spec(4) + vmem_spec(5),
        scratch_shapes=[
            vmem(big, BF16), vmem(big, BF16), vmem((4,) + big, BF16), vmem((4096, 1024), BF16),
            vmem(big, F32), vmem(big, F32), vmem((1024, 512), BF16), vmem((1024, 512), BF16),
            vmem((2, 256, 1024), F32), vmem((2, 256, 1024), BF16), vmem((NC, 256, 1024), BF16),
            vmem((NC - 1, 3, 64, 1024), BF16), vmem((2, 3, 64, 1024), BF16), vmem((2, 64, 1024), BF16),
            vmem((NC, 64, 1024), BF16),
            vmem((2, 2, NC, 2, 64, 256), BF16), vmem((256, 1024), BF16), vmem(big, F32),
            dma((9,)), dma((3, NC - 1)), dma((3, NC - 1)), dma((NC - 1,)), dma((NC - 1,)),
            dma((3, NC)), dma((3, NC)), dma((NC,)), dma((NC,)), dma((NC,)), dma((NC,)),
            dma((NC - 1, 3)), dma((NC - 1, 3)), dma((NC,)), dma((NC,)),
            dma((2, 4)), dma((2, 2)), dma((NC, 2)), dma((NC, 2)),
        ],
        compiler_params=pltpu.CompilerParams(
            collective_id=1, has_side_effects=True, vmem_limit_bytes=VMEM_LIMIT
        ),
    )(sec, res, wall, wdn, wdpre, cot, live, upb, dnb, sg)


def backward_kernel(
    dwown, dwmate, find, gatt, att, wall, q, kx, vx, rnd, p, tok, sio, u_in, st_in, fg, fb, skip, decay,
    gsg, gsb, gdb, gub,
    gtok_o, findr_o, fin_b, finr_b, fin_g, finr_g, sums_o,
    own_b, prec_b, rrec_b, xrec_b, acc_b,
    own_g, prec_g, rrec_g, xrec_g, acc_g, go_s,
    gatt_s, wo_s, att_s, ga_s, q_s, k_s, v_s, rnd_s, dk_s, dv_s, pbuf, ds_s, gres_s, nb_s,
    sio_s, gd_s, gctx_s, sum_s, got_s, part_s,
    loc, psem, gsem, osem, mbs, mbr, mgs, mgr, rbs, rbr, rgs, rgr, xbs, xbr, xgs, xgr,
    fbs, fbr, fgs, fgr, ts, tr, us, ur, ds, dr,
):
    net = Net()
    rep, core = net.rep, net.core
    theirs = 1 - core

    loads = [
        pltpu.make_async_copy(gatt, gatt_s, loc.at[0]),
        pltpu.make_async_copy(wall.at[3], wo_s, loc.at[1]),
        pltpu.make_async_copy(att, att_s, loc.at[2]),
        pltpu.make_async_copy(q, q_s, loc.at[3]),
        pltpu.make_async_copy(kx, k_s, loc.at[4]),
        pltpu.make_async_copy(vx, v_s, loc.at[5]),
        pltpu.make_async_copy(rnd, rnd_s, loc.at[6]),
        pltpu.make_async_copy(sio, sio_s, loc.at[7]),
    ]
    rises = [
        pltpu.make_async_copy(dwown, own_b.at[pl.ds(0, 4)], loc.at[8]),
        pltpu.make_async_copy(dwmate, prec_b.at[pl.ds(0, 4)], loc.at[9]),
    ]
    for copy in rises:
        copy.start()
    for copy in loads:
        copy.start()
    fin_b[...] = jnp.zeros(fin_b.shape, BF16)
    finr_b[...] = jnp.zeros(finr_b.shape, BF16)
    fin_g[...] = jnp.zeros(fin_g.shape, BF16)
    finr_g[...] = jnp.zeros(finr_g.shape, BF16)
    barrier = pltpu.get_barrier_semaphore()
    me = rep * (2 * NC) + net.shard

    def device(away):
        other = (me + away) % (4 * NC)
        return other, (other // (2 * NC), other % (2 * NC))

    @pl.loop(1, 4 * NC)
    def _(away):
        pl.semaphore_signal(barrier, inc=1, device_id=device(away)[1], device_id_type=MESH)

    pl.semaphore_wait(barrier, 4 * NC - 1)

    mate_out = rcopy(go_s, prec_b.at[4], mbs.at[0], mbr.at[0], net.mate)

    def mate_group(g):
        return rcopy(own_g.at[g, :, theirs], prec_g.at[g], mgs.at[g], mgr.at[g], net.mate)

    swap = rcopy(find, findr_o, ds.at[0], dr.at[0], net.twin)
    swap.start()

    def chip_for(n):
        t, way = n // 2, n % 2
        hops = (4 - t) * (1 - way) + (t - 3) * way
        return chip_at((net.pos + net.step * hops + 4 * NC) % NC)

    class Stream:
        def __init__(self, own, prec, rrec, xrec, fin, finr, acc, sems):
            self.own, self.prec, self.rrec, self.xrec = own, prec, rrec, xrec
            self.fin, self.finr, self.acc = fin, finr, acc
            self.rs, self.rr, self.xs, self.xr, self.fs, self.fr = sems

        def ring(self, slot, which, n):
            source = self.prec.at[which, chip_for(n)]
            way = n % 2
            return rcopy(
                source, self.rrec.at[slot, n], self.rs.at[slot, n], self.rr.at[slot, n],
                net.along(1 - 2 * way),
            )

        def twin(self, which, n):
            chip = chip_for(n)
            return rcopy(
                self.prec.at[which, chip], self.xrec.at[chip], self.xs.at[n], self.xr.at[n], net.twin
            )

        def finish(self, which):
            return rcopy(
                self.fin.at[which], self.finr.at[which], self.fs.at[which], self.fr.at[which], net.twin
            )

        def give(self, which, n):
            chip = chip_for(n)
            self.prec[which, chip] = (
                self.own(which, chip).astype(F32) + self.prec[which, chip].astype(F32)
            ).astype(BF16)
            self.twin(which, n).start()

        def turn(self, slot, which, n, sole):
            chip = chip_for(n)
            self.acc[...] = self.own(which, chip).astype(F32) + self.prec[which, chip].astype(F32)

            @pl.when(sole)
            def _():
                self.twin(which, n).wait_recv()
                self.acc[...] = self.acc[...] + self.xrec[chip].astype(F32)

            @pl.when((n >= 2) & (n < 7))
            def _():
                self.ring(slot, which, n - 2).wait_recv()
                self.acc[...] = self.acc[...] + self.rrec[slot, n - 2].astype(F32)

            @pl.when(n < 7)
            def _():
                self.prec[which, chip] = self.acc[...].astype(BF16)
                self.ring(slot, which, n).start()

            @pl.when(n == 7)
            def _():
                self.ring(slot, which, 5).wait_recv()
                self.ring(slot, which, 6).wait_recv()
                total = self.acc[...] + self.rrec[slot, 5].astype(F32) + self.rrec[slot, 6].astype(F32)
                self.fin[which] = total.astype(BF16)
                self.finish(which).start()

    big = Stream(
        lambda which, chip: own_b[which, chip], prec_b, rrec_b, xrec_b, fin_b, finr_b, acc_b,
        (rbs, rbr, xbs, xbr, fbs, fbr),
    )
    group = Stream(
        lambda which, chip: own_g[which, chip, core], prec_g, rrec_g, xrec_g, fin_g, finr_g, acc_g,
        (rgs, rgr, xgs, xgr, fgs, fgr),
    )

    def tile(index):
        return (
            pl.ds(pl.multiple_of((index // 8) * 16, 16), 16),
            pl.ds(pl.multiple_of((index % 8) * 128, 128), 128),
        )

    def share(away):
        other, where = device(away)
        return rcopy(sum_s.at[tile(other)], got_s.at[away], ts.at[away], tr.at[away], where)

    def spread(away):
        return rcopy(part_s, sums_o.at[tile(me)], us.at[away], ur.at[away], device(away)[1])

    def each_device(act):
        for away in range(1, 4 * NC):
            act(away)

    def big_at(e):
        k, j = e // 4, e % 4
        n = k - j - (j // 2) * (1 - 2 * (j // 3))
        which = (j + 1) * (1 - j // 2) + (j // 2) * (3 * rep * (1 - j // 3) + 4 * (j // 3))

        @pl.when((j == 3) & (n == 0))
        def _():
            mate_out.wait_recv()

        @pl.when((n >= 0) & (n <= 7))
        def _():
            big.turn(j, which, n, j == 2)

    def group_at(e):
        k, j = e // 3, e % 3
        n = k
        which = rep * (1 - (j + 1) // 2) + (j + 1) * ((j + 1) // 2)

        @pl.when((j >= 1) & (n == 0))
        def _():
            mate_group(which).wait_recv()

        @pl.when((n >= 0) & (n <= 7))
        def _():
            group.turn(j, which, n, j == 0)

    def run(at, low, high):
        @pl.loop(low, high)
        def _(e):
            at(e)

    for copy in rises:
        copy.wait()

    @pl.loop(0, NC)
    def _(n):
        big.give(3 * (1 - rep), n)

    run(big_at, 0, 4)
    for i in range(2):
        loads[i].wait()

    def p_copy(slot, at):
        return pltpu.make_async_copy(p.at[at], pbuf.at[slot], psem.at[slot])

    p_copy(0, 0).start()

    @pl.loop(0, 2)
    def _(at):
        rows = pl.ds(pl.multiple_of(at * 512, 512), 512)
        ga_s[rows, :] = dot_nt(gatt_s[rows, :], wo_s[...]).astype(BF16)

    run(big_at, 4, 8)
    loads[2].wait()

    @pl.loop(0, 2)
    def _(at):
        cols = pl.ds(pl.multiple_of(at * 512, 512), 512)
        made = dot_tn(att_s[...], gatt_s[:, cols]).reshape(NC, 2, 64, 512)
        own_b[4, :, :, cols] = jnp.where(core == 0, made[:, 0], made[:, 1]).astype(BF16)
        go_s[:, :, cols] = jnp.where(core == 0, made[:, 1], made[:, 0]).astype(BF16)

    mate_out.start()
    tok_load = pltpu.make_async_copy(tok, wo_s, loc.at[0])
    tok_load.start()
    for copy in loads[3:]:
        copy.wait()
    ds_s[...] = jnp.zeros(ds_s.shape, BF16)
    dq_s = gatt_s

    def weights_in(i):
        target = (q_s, k_s.at[pl.ds(0, 1024)], v_s.at[pl.ds(0, 1024)])[i]
        return pltpu.make_async_copy(wall.at[i], target, loc.at[1 + i])

    @pl.loop(0, 4)
    def _(g):
        for hh in range(2):
            for b in range(NBLK):
                i = 2 * hh + b
                m = 4 * g + i
                h = 2 * g + hh
                slot = i % 2
                cols = pl.ds(pl.multiple_of(h * DH, DH), DH)
                following = 2 * hh + b + 1
                nb, nh = following % 2, 2 * g + following // 2
                p_copy(slot, b * 8 + h).wait()
                if following < 4:
                    p_copy(1 - slot, nb * 8 + nh).start()
                else:

                    @pl.when(g < 3)
                    def _():
                        p_copy(1 - slot, nh).start()

                for part in range(2):
                    span = (part + 1) * 256
                    rows = pl.ds(b * BLK + part * 256, 256)
                    local = pl.ds(part * 256, 256)
                    grads = ga_s[rows, cols]
                    slope = dot_nt(grads, v_s[pl.ds(b * BLK, span), cols])
                    kept = pbuf[slot, local, pl.ds(CTX, span)].astype(F32)
                    both = jnp.sum(kept * slope, axis=-1, keepdims=True)
                    mass = jnp.sum(kept, axis=-1, keepdims=True)
                    if b:
                        slope_before = dot_nt(grads, v_s[pl.ds(1024, CTX), cols])
                        kept_before = pbuf[slot, local, pl.ds(0, CTX)].astype(F32)
                        both += jnp.sum(kept_before * slope_before, axis=-1, keepdims=True)
                        mass += jnp.sum(kept_before, axis=-1, keepdims=True)
                    both = both / mass
                    inner = (kept * (slope - both)).astype(BF16)
                    ds_s[local, pl.ds(CTX, span)] = inner
                    total = dot_nn(inner, k_s[pl.ds(b * BLK, span), cols])
                    if b:
                        inner = (kept_before * (slope_before - both)).astype(BF16)
                        ds_s[local, pl.ds(0, CTX)] = inner
                        total = total + dot_nn(inner, k_s[pl.ds(1024, CTX), cols])
                    dq_s[rows, cols] = (total * SCALE).astype(BF16)
                rows = pl.ds(b * BLK, BLK)
                first = 0 if b else CTX
                made_k = dot_tn(ds_s[:, first:], q_s[rows, cols]) * SCALE
                made_v = dot_tn(pbuf[slot, :, first:], ga_s[rows, cols])
                if b:
                    dk_s[pl.ds(1024, CTX), cols] = made_k[:CTX].astype(BF16)
                    dv_s[pl.ds(1024, CTX), cols] = made_v[:CTX].astype(BF16)
                    made_k, made_v = made_k[CTX:], made_v[CTX:]
                dk_s[rows, cols] = made_k.astype(BF16)
                dv_s[rows, cols] = made_v.astype(BF16)

                run(big_at, 8 + 2 * m, 10 + 2 * m)


                @pl.when(m == 10)
                def _():
                    for each in range(2):
                        mate_group(each).wait_recv()

                @pl.when((m >= 10) & (m < 14))
                def _(m=m):
                    for e in range(2):
                        group.give(1 - rep, 2 * (m - 10) + e)

        @pl.when(g == 3)
        def _():
            for i in range(3):
                weights_in(i).start()

        cols = pl.ds(pl.multiple_of(g * 256, 256), 256)
        own_g[g, :, :, :, 0:256] = dot_tn(rnd_s[0:1024, :], dq_s[:, cols]).astype(BF16).reshape(NC, 2, 64, 256)
        own_g[g, :, :, :, 256:512] = dot_tn(rnd_s[...], dk_s[:, cols]).astype(BF16).reshape(NC, 2, 64, 256)
        own_g[g, :, :, :, 512:768] = dot_tn(rnd_s[...], dv_s[:, cols]).astype(BF16).reshape(NC, 2, 64, 256)
        mate_group(g).start()

    run(big_at, 40, 44)
    run(group_at, 0, 2)
    for i in range(3):
        weights_in(i).wait()
    tok_load.wait()

    def gres_in(at):
        rows = pl.ds(pl.multiple_of(at * 256, 256), 256)
        return pltpu.make_async_copy(gatt.at[rows], gres_s.at[at % 2], gsem.at[at % 2])

    gres_in(0).start()

    after = pl.ds(1024, CTX)
    gctx = dot_nt(dk_s[after, :], k_s[0:1024, :]) + dot_nt(dv_s[after, :], v_s[0:1024, :])
    gctx_s[...] = gctx
    xhat, _ = norm_parts(wo_s[pl.ds(BLK - CTX, CTX), :].astype(F32))
    sum_s[32:48, :] = jnp.zeros((16, 1024), F32)
    sum_s[34:35, :] = jnp.sum(gctx * (xhat * fg[...] + fb[...]), axis=0, keepdims=True)
    for at, vector in ((35, gsg), (36, gsb), (37, gdb)):
        sum_s[at : at + 1, :] = vector[...]
    for at in range(4):
        sum_s[38 + at : 39 + at, :] = gub[:, at * 1024 : (at + 1) * 1024]
    run(group_at, 2, 5)
    states, raw = st_in[...], u_in[...]
    factor = jnp.exp(-column(decay[...]))
    scale = jnp.sqrt(1.0 - factor * factor)
    sum_s[16:32, :] = lax.dot_general(
        states[:, BLK - CTX :], gctx, (((1,), (0,)), ((), ())),
        preferred_element_type=F32, precision=lax.Precision.HIGHEST,
    )
    back = split_dot(
        lambda a, b: lax.dot_general(b, a, (((0,), (1,)), ((), ())), preferred_element_type=F32),
        gctx, sio_s[...], 3,
    )
    seeds = jnp.concatenate([jnp.zeros((16, BLK - CTX), F32), back[16:32, :]], axis=1)
    lam = lane_scan(seeds, factor, True)
    lane = lax.broadcasted_iota(jnp.int32, lam.shape, 1)
    earlier = jnp.where(lane >= 1, pltpu.roll(states, 1, 1), 0.0)
    rates = -factor * jnp.sum(lam * (earlier - (factor / scale) * raw), axis=1, keepdims=True)
    sum_s[48:64, :] = jnp.broadcast_to(rates, (16, 1024))
    driven = scale * lam
    sum_s[0:16, :] = split_dot(dot_nn, driven, rnd_s[0:BLK, :], 3)
    gd_s[...] = jnp.zeros(gd_s.shape, F32)
    gd_s[0:16, 0:BLK] = driven

    def add_in(away):
        share(away).wait_recv()
        part_s[...] = part_s[...] + got_s[away]

    def leave(at):
        rows = pl.ds(pl.multiple_of(at * 256, 256), 256)
        return pltpu.make_async_copy(rnd_s.at[rows], gtok_o.at[rows], osem.at[at])

    @pl.loop(0, 4)
    def _(at):
        rows = pl.ds(pl.multiple_of(at * 256, 256), 256)

        @pl.when(at < 3)
        def _():
            gres_in(at + 1).start()

        xhat, inverse = norm_parts(wo_s[rows, :].astype(F32))
        nb_s[...] = (
            dot_nt(dq_s[rows, :], q_s[...])
            + dot_nt(dk_s[rows, :], k_s[0:1024, :])
            + dot_nt(dv_s[rows, :], v_s[0:1024, :])
        )

        @pl.when(at < 2)
        def _():
            nb_s[...] = nb_s[...] + split_dot(
                lambda a, b: lax.dot_general(a, b, (((0,), (1,)), ((), ())), preferred_element_type=F32),
                gd_s[:, rows], sio_s[...], 3,
            )

        @pl.when(at == 1)
        def _():
            half = pl.ds(128, CTX)
            nb_s[half, :] = nb_s[half, :] + skip[...] * gctx_s[...]

        run(group_at, 5 + 3 * at, 8 + 3 * at)

        grad = nb_s[...]
        gain = jnp.sum(grad * xhat, axis=0, keepdims=True)
        shift = jnp.sum(grad, axis=0, keepdims=True)
        sum_s[32:33, :] = sum_s[32:33, :] + gain
        sum_s[33:34, :] = sum_s[33:34, :] + shift
        grad = grad * fg[...]
        grad = grad - jnp.mean(grad, axis=-1, keepdims=True) - xhat * jnp.mean(
            grad * xhat, axis=-1, keepdims=True
        )
        gres_in(at).wait()
        rnd_s[rows, :] = (gres_s[at % 2].astype(F32) + inverse * grad).astype(BF16)
        leave(at).start()

    each_device(lambda away: share(away).start())
    part_s[...] = sum_s[tile(me)]
    run(group_at, 17, 20)
    each_device(add_in)
    each_device(lambda away: spread(away).start())
    sums_o[tile(me)] = part_s[...]
    run(group_at, 20, 24)

    for which in (3 * rep, 1, 2, 4):
        big.finish(which).wait_send()
    for which in (rep, 2, 3):
        group.finish(which).wait_send()
    twin_rise = 3 * (1 - rep)
    for which in (twin_rise, 1, 2, 4):
        big.finish(which).wait_recv()
    for which in (1 - rep, 2, 3):
        group.finish(which).wait_recv()
    def settle(away):
        spread(away).wait()
        share(away).wait_send()

    each_device(settle)
    for i in range(4):
        mate_group(i).wait_send()
        leave(i).wait()
    mate_out.wait_send()
    swap.wait()

    @pl.loop(0, NC)
    def _(n):
        big.twin(3 * (1 - rep), n).wait_send()
        group.twin(1 - rep, n).wait_send()

    @pl.loop(0, NC - 1)
    def _(n):
        for slot in range(4):
            big.ring(slot, 0, n).wait_send()
        for slot in range(3):
            group.ring(slot, 0, n).wait_send()


def run_backward(*operands):
    shape = jax.ShapeDtypeStruct
    dma = pltpu.SemaphoreType.DMA
    vmem = pltpu.VMEM
    full = (1024, 1024)
    ext = (1024 + CTX, 1024)
    part = (64, 1024)
    cut = (64, 768)
    return pl.pallas_call(
        backward_kernel,
        name="backward_part",
        out_shape=(
            shape(full, BF16), shape((192, 1024), BF16), shape((5,) + part, BF16), shape((5,) + part, BF16),
            shape((4,) + cut, BF16), shape((4,) + cut, BF16), shape((64, 1024), F32),
        ),
        in_specs=any_spec(13) + vmem_spec(10),
        out_specs=any_spec(2) + vmem_spec(5),
        scratch_shapes=[
            vmem((5, NC) + part, BF16), vmem((5, NC) + part, BF16), vmem((4, NC - 1) + part, BF16),
            vmem((NC,) + part, BF16), vmem(part, F32),
            vmem((4, NC, 2) + cut, BF16), vmem((4, NC) + cut, BF16), vmem((3, NC - 1) + cut, BF16),
            vmem((NC,) + cut, BF16), vmem(cut, F32),
            vmem((NC,) + part, BF16),
            vmem(full, BF16), vmem(full, BF16), vmem(full, BF16), vmem(full, BF16), vmem(full, BF16),
            vmem(ext, BF16), vmem(ext, BF16), vmem(ext, BF16), vmem(ext, BF16), vmem(ext, BF16),
            vmem((2, BLK, CTX + BLK), BF16), vmem((BLK, CTX + BLK), BF16), vmem((2, 256, 1024), BF16),
            vmem((256, 1024), F32), vmem((1024, 128), BF16), vmem((128, 1024), F32), vmem((CTX, 1024), F32), vmem((64, 1024), F32), vmem((4 * NC, 16, 128), F32), vmem((16, 128), F32),
            dma((10,)), dma((2,)), dma((2,)), dma((4,)), dma((1,)), dma((1,)), dma((4,)), dma((4,)),
            dma((4, NC - 1)), dma((4, NC - 1)), dma((3, NC - 1)), dma((3, NC - 1)),
            dma((NC,)), dma((NC,)), dma((NC,)), dma((NC,)), dma((5,)), dma((5,)), dma((4,)), dma((4,)),
            dma((4 * NC,)), dma((4 * NC,)), dma((4 * NC,)), dma((4 * NC,)), dma((1,)), dma((1,)),
        ],
        compiler_params=pltpu.CompilerParams(
            collective_id=2, has_side_effects=True, vmem_limit_bytes=VMEM_LIMIT
        ),
    )(*operands)


def outputs_kernel(
    result, gtok, finb, finrb, fing, finrg, find, findr, sums,
    result_o, gtok_o, dup_o, do_o, dq_o, dk_o, dv_o, ddown_o, gfg_o, gfb_o, gskip_o, gsg_o, gsb_o, gdb_o, gub_o, grate_o,
    gsi_o, gso_o, held, came, left,
):
    rep, shard = lax.axis_index("rep"), lax.axis_index("shard")
    pairs = ((result, result_o), (gtok, gtok_o))

    def take(which, at):
        rows = pl.ds(at * 256, 256)
        return pltpu.make_async_copy(pairs[which][0].at[rows], held.at[which, rows], came.at[which, at])

    def give(which, at):
        rows = pl.ds(at * 256, 256)
        return pltpu.make_async_copy(held.at[which, rows], pairs[which][1].at[rows], left.at[which, at])

    every = [(which, at) for which in range(2) for at in range(4)]
    for each in every:
        take(*each).start()
    for i in range(4):
        dup_o[:, i * 1024 : (i + 1) * 1024] = finb[i].astype(F32) + finrb[i].astype(F32)
    for each in every:
        take(*each).wait()
        give(*each).start()
    do_o[...] = finb[4].astype(F32) + finrb[4].astype(F32)
    for g in range(4):
        for i, out in enumerate((dq_o, dk_o, dv_o)):
            cols = slice(i * 256, (i + 1) * 256)
            out[:, g * 256 : (g + 1) * 256] = fing[g, :, cols].astype(F32) + finrg[g, :, cols].astype(F32)
    mine = pl.ds(pl.multiple_of(rep * 64, 64), 192)
    theirs = pl.ds(pl.multiple_of((1 - rep) * 64, 64), 192)
    ddown_o[...] = jnp.zeros((256, 1024), F32)
    ddown_o[mine, :] = find[...].astype(F32)
    ddown_o[theirs, :] = ddown_o[theirs, :] + findr[...].astype(F32)
    for at, out in enumerate((gfg_o, gfb_o, gskip_o, gsg_o, gsb_o, gdb_o)):
        out[...] = sums[32 + at : 33 + at, :]
    for at in range(4):
        gub_o[:, at * 1024 : (at + 1) * 1024] = sums[38 + at : 39 + at, :]
    same = lax.broadcasted_iota(jnp.int32, (16, 128), 0) == lax.broadcasted_iota(jnp.int32, (16, 128), 1)
    grate_o[...] = jnp.sum(jnp.where(same, sums[48:64, 0:128], 0.0), axis=0)[0:16]
    shift = (1024 - 64 * shard) % 1024
    gsi_o[...] = pltpu.roll(sums[0:16, :], shift, 1)[:, 0:64]
    gso_o[...] = pltpu.roll(sums[16:32, :], shift, 1)[:, 0:64]
    for each in every:
        give(*each).wait()


def run_outputs(*operands):
    shape = jax.ShapeDtypeStruct
    row = shape((1, 1024), F32)
    part = shape((64, 1024), F32)
    return pl.pallas_call(
        outputs_kernel,
        name="outputs_part",
        out_shape=(
            shape((1024, 1024), BF16), shape((1024, 1024), BF16),
            shape((64, 4096), F32), part, part, part, part, shape((256, 1024), F32),
            row, row, row, row, row, row, shape((1, 4096), F32), shape((16,), F32),
            shape((16, 64), F32), shape((16, 64), F32),
        ),
        in_specs=any_spec(2) + vmem_spec(7),
        out_specs=any_spec(2) + vmem_spec(16),
        scratch_shapes=[
            pltpu.VMEM((2, 1024, 1024), BF16),
            pltpu.SemaphoreType.DMA((2, 4)), pltpu.SemaphoreType.DMA((2, 4)),
        ],
        compiler_params=pltpu.CompilerParams(vmem_limit_bytes=VMEM_LIMIT),
    )(*operands)


def fused_device(
    tokens, lengths, first_gain, first_bias, decay_rates, state_in, state_out, skip_gain,
    query_weight, key_weight, value_weight, output_weight, second_gain, second_bias,
    up_weight, up_bias, down_weight, down_bias, cotangent,
):
    tok = tokens.reshape(1024, 1024)
    cot = cotangent.reshape(1024, 1024)
    fg, fb, skip, sg, sb, dnb, upb, decay = (
        v.reshape(1, -1)
        for v in (
            first_gain, first_bias, skip_gain, second_gain, second_bias, down_bias, up_bias, decay_rates,
        )
    )
    wall, wdpre, sio, rnd, q, kx, vx, att, res, sec, p, u, st = run_forward(
        tok, query_weight, key_weight, value_weight, output_weight, up_weight, down_weight, state_in, state_out,
        fg, fb, skip, sg, sb, decay,
    )
    result, gatt, dwown, dwmate, find, gdb, gub, gsg, gsb = run_feed(
        sec, res, wall, down_weight, wdpre, cot, lengths, upb, dnb, sg
    )
    gtok, findr, finb, finrb, fing, finrg, sums = run_backward(
        dwown, dwmate, find, gatt, att, wall, q, kx, vx, rnd, p, tok, sio,
        u, st, fg, fb, skip, decay, gsg, gsb, gdb, gub,
    )
    result, gtok, dup, do, dq, dk, dv, ddown, *rest = run_outputs(
        result, gtok, finb, finrb, fing, finrg, find, findr, sums
    )
    gfg, gfb, gskip, gsg, gsb, gdb, gub, grate, gsi, gso = rest
    return (
        result.reshape(1, 1024, 1024), gtok.reshape(1, 1024, 1024), gfg[0], gfb[0],
        grate, gsi, gso, gskip[0], dq, dk, dv, do, gsg[0], gsb[0], dup, gub[0], ddown, gdb[0],
    )


NORM_EPS = 1e-05
NEG_LARGE = -1e30
HIGHEST = lax.Precision.HIGHEST


def layer_norm(hidden, gain_vec, bias_vec):
    average = jnp.mean(hidden, axis=-1, keepdims=True)
    centred = hidden - average
    spread = jnp.mean(centred * centred, axis=-1, keepdims=True)
    return centred * lax.rsqrt(spread + NORM_EPS) * gain_vec + bias_vec


def state_context(driven_raw, normed, decay_rates, state_out, skip_gain):
    decay_factor = jnp.exp(-decay_rates)
    driven = driven_raw * jnp.sqrt(1.0 - decay_factor * decay_factor)
    factors = jnp.broadcast_to(decay_factor, driven.shape)

    def combine(earlier, subsequent):
        return (earlier[0] * subsequent[0], subsequent[0] * earlier[1] + subsequent[1])

    states = lax.associative_scan(combine, (factors, driven), axis=1)[1]
    seq_count = driven_raw.shape[0]
    state_width = driven_raw.shape[2]
    model_width = normed.shape[2]
    tail_states = states.reshape(seq_count, NBLK, BLK, state_width)[:, :, BLK - CTX :, :]
    skipped = normed.reshape(seq_count, NBLK, BLK, model_width)[:, :, BLK - CTX :, :]
    outputs = (
        jnp.einsum("sbcp,pd->sbcd", tail_states, state_out, precision=HIGHEST) + skip_gain * skipped
    )
    empty_ctx = jnp.zeros((seq_count, 1, CTX, model_width), jnp.float32)
    return jnp.concatenate([empty_ctx, outputs[:, : NBLK - 1]], axis=1)


def block_scores(queries, key_rows, ctx_keys, ctx_valid):
    row_count = queries.shape[0]
    head_count = queries.shape[1] // DH
    query_heads = queries.reshape(row_count, head_count, DH)
    key_heads = jnp.concatenate([ctx_keys, key_rows], 0).reshape(-1, head_count, DH)
    scores = jnp.einsum(
        "qhd,khd->hqk", query_heads, key_heads, preferred_element_type=jnp.float32
    ) * DH ** (-0.5)
    causal = lax.broadcasted_iota(jnp.int32, (row_count, row_count), 0) >= lax.broadcasted_iota(
        jnp.int32, (row_count, row_count), 1
    )
    allowed = jnp.concatenate(
        [jnp.broadcast_to(ctx_valid[None, :], (row_count, ctx_keys.shape[0])), causal], axis=1
    )
    return (jnp.where(allowed[None], scores, NEG_LARGE), query_heads, key_heads)


def attend_forward(block_item):
    queries, key_rows, value_rows, ctx_keys, ctx_values, ctx_valid = block_item
    scores, query_heads, key_heads = block_scores(queries, key_rows, ctx_keys, ctx_valid)
    row_max = jnp.max(scores, axis=-1, keepdims=True)
    expos = jnp.exp(scores - row_max)
    denominator = jnp.sum(expos, axis=-1, keepdims=True)
    weights = (expos / denominator).astype(jnp.bfloat16)
    value_heads = jnp.concatenate([ctx_values, value_rows], 0).reshape(key_heads.shape)
    attended = jnp.einsum("hqk,khd->qhd", weights, value_heads, preferred_element_type=jnp.float32)
    return (
        attended.reshape(queries.shape).astype(jnp.bfloat16),
        (row_max + jnp.log(denominator))[..., 0],
    )


def attend_backward(block_item):
    queries, key_rows, value_rows, ctx_keys, ctx_values, ctx_valid, log_total, grad_attended = (
        block_item
    )
    scores, query_heads, key_heads = block_scores(queries, key_rows, ctx_keys, ctx_valid)
    probs = jnp.exp(scores - log_total[..., None])
    value_heads = jnp.concatenate([ctx_values, value_rows], 0).reshape(key_heads.shape)
    grad_heads = grad_attended.reshape(query_heads.shape)
    grad_probs = jnp.einsum(
        "qhd,khd->hqk", grad_heads, value_heads, preferred_element_type=jnp.float32
    )
    grad_scores = (
        probs * (grad_probs - jnp.sum(probs * grad_probs, axis=-1, keepdims=True))
    ).astype(jnp.bfloat16)
    grad_values = jnp.einsum(
        "hqk,qhd->khd", probs.astype(jnp.bfloat16), grad_heads, preferred_element_type=jnp.float32
    )
    grad_queries = jnp.einsum(
        "hqk,khd->qhd", grad_scores, key_heads, preferred_element_type=jnp.float32
    ) * DH ** (-0.5)
    grad_keys = jnp.einsum(
        "hqk,qhd->khd", grad_scores, query_heads, preferred_element_type=jnp.float32
    ) * DH ** (-0.5)
    ctx_count = ctx_keys.shape[0]
    model_width = queries.shape[1]
    grad_keys = grad_keys.reshape(-1, model_width).astype(jnp.bfloat16)
    grad_values = grad_values.reshape(-1, model_width).astype(jnp.bfloat16)
    return (
        grad_queries.reshape(queries.shape).astype(jnp.bfloat16),
        grad_keys[ctx_count:],
        grad_values[ctx_count:],
        grad_keys[:ctx_count],
        grad_values[:ctx_count],
    )


def per_device(
    tokens,
    lengths,
    first_gain,
    first_bias,
    decay_rates,
    state_in,
    state_out,
    skip_gain,
    query_weight,
    key_weight,
    value_weight,
    output_weight,
    second_gain,
    second_bias,
    up_weight,
    up_bias,
    down_weight,
    down_bias,
    cotangent,
):
    full_query, full_key, full_value, full_output, full_up, full_down, full_in, full_out = (
        lax.all_gather(query_weight, "shard", axis=0, tiled=True),
        lax.all_gather(key_weight, "shard", axis=0, tiled=True),
        lax.all_gather(value_weight, "shard", axis=0, tiled=True),
        lax.all_gather(output_weight, "shard", axis=0, tiled=True),
        lax.all_gather(up_weight, "shard", axis=0, tiled=True),
        lax.all_gather(down_weight, "shard", axis=0, tiled=True),
        lax.all_gather(state_in, "shard", axis=1, tiled=True),
        lax.all_gather(state_out, "shard", axis=1, tiled=True),
    )
    seq_count, seq_len, model_width = tokens.shape
    row_count = seq_count * seq_len
    block_count = seq_count * NBLK
    positions = lax.broadcasted_iota(jnp.int32, (seq_count, seq_len), 1)
    row_mask = (positions < lengths[:, None]).astype(jnp.float32).reshape(row_count, 1)
    block_index = lax.broadcasted_iota(jnp.int32, (seq_count, NBLK, CTX), 1)
    ctx_valid = (block_index > 0).reshape(block_count, CTX)
    token_rows = tokens.astype(jnp.float32)
    normed, first_pullback = jax.vjp(layer_norm, token_rows, first_gain, first_bias)
    rounded = normed.astype(jnp.bfloat16)
    driven_raw = jnp.einsum("std,pd->stp", rounded, full_in, preferred_element_type=jnp.float32)
    context, state_pullback = jax.vjp(
        state_context, driven_raw, normed, decay_rates, full_out.astype(jnp.float32), skip_gain
    )
    ctx_rows = context.astype(jnp.bfloat16).reshape(block_count * CTX, model_width)
    flat_rounded = rounded.reshape(row_count, model_width)
    query_rows = jnp.dot(flat_rounded, full_query, preferred_element_type=jnp.float32).astype(
        jnp.bfloat16
    )
    key_rows = jnp.dot(flat_rounded, full_key, preferred_element_type=jnp.float32).astype(
        jnp.bfloat16
    )
    value_rows = jnp.dot(flat_rounded, full_value, preferred_element_type=jnp.float32).astype(
        jnp.bfloat16
    )
    ctx_keys = jnp.dot(ctx_rows, full_key, preferred_element_type=jnp.float32).astype(jnp.bfloat16)
    ctx_values = jnp.dot(ctx_rows, full_value, preferred_element_type=jnp.float32).astype(
        jnp.bfloat16
    )
    block_inputs = (
        query_rows.reshape(block_count, BLK, model_width),
        key_rows.reshape(block_count, BLK, model_width),
        value_rows.reshape(block_count, BLK, model_width),
        ctx_keys.reshape(block_count, CTX, model_width),
        ctx_values.reshape(block_count, CTX, model_width),
        ctx_valid,
    )
    attended, log_total = lax.map(attend_forward, block_inputs)
    attended_rows = attended.reshape(row_count, model_width)
    residual = token_rows.reshape(row_count, model_width) + jnp.dot(
        attended_rows, full_output, preferred_element_type=jnp.float32
    )
    second, second_pullback = jax.vjp(layer_norm, residual, second_gain, second_bias)
    second_rows = second.astype(jnp.bfloat16)
    hidden = jnp.dot(second_rows, full_up, preferred_element_type=jnp.float32) + up_bias
    active, gelu_pullback = jax.vjp(jax.nn.gelu, hidden)
    active_rows = active.astype(jnp.bfloat16)
    branch = jnp.dot(active_rows, full_down, preferred_element_type=jnp.float32) + down_bias
    result = (
        ((residual + branch) * row_mask)
        .astype(jnp.bfloat16)
        .reshape(seq_count, seq_len, model_width)
    )
    full_query, full_key, full_value, full_output, full_up, full_down, full_in, full_out = (
        lax.all_gather(query_weight, "shard", axis=0, tiled=True),
        lax.all_gather(key_weight, "shard", axis=0, tiled=True),
        lax.all_gather(value_weight, "shard", axis=0, tiled=True),
        lax.all_gather(output_weight, "shard", axis=0, tiled=True),
        lax.all_gather(up_weight, "shard", axis=0, tiled=True),
        lax.all_gather(down_weight, "shard", axis=0, tiled=True),
        lax.all_gather(state_in, "shard", axis=1, tiled=True),
        lax.all_gather(state_out, "shard", axis=1, tiled=True),
    )
    grad_branch = cotangent.reshape(row_count, model_width).astype(jnp.float32) * row_mask
    branch_rounded = grad_branch.astype(jnp.bfloat16)
    grad_down = jnp.einsum(
        "rf,rd->fd", active_rows, branch_rounded, preferred_element_type=jnp.float32
    )
    grad_down_bias = jnp.sum(grad_branch, axis=0)
    grad_active = jnp.einsum(
        "rd,fd->rf", branch_rounded, full_down, preferred_element_type=jnp.float32
    )
    (grad_hidden,) = gelu_pullback(grad_active)
    hidden_rounded = grad_hidden.astype(jnp.bfloat16)
    grad_up = jnp.einsum(
        "rd,rf->df", second_rows, hidden_rounded, preferred_element_type=jnp.float32
    )
    grad_up_bias = jnp.sum(hidden_rounded.astype(jnp.float32), axis=0)
    grad_second = jnp.einsum(
        "rf,df->rd", hidden_rounded, full_up, preferred_element_type=jnp.float32
    )
    grad_residual_part, grad_second_gain, grad_second_bias = second_pullback(grad_second)
    grad_residual = grad_branch + grad_residual_part
    residual_rounded = grad_residual.astype(jnp.bfloat16)
    grad_output = jnp.einsum(
        "rd,re->de", attended_rows, residual_rounded, preferred_element_type=jnp.float32
    )
    grad_attended = jnp.einsum(
        "re,de->rd", residual_rounded, full_output, preferred_element_type=jnp.float32
    ).astype(jnp.bfloat16)
    grad_query_rows, grad_key_rows, grad_value_rows, grad_ctx_keys, grad_ctx_values = lax.map(
        attend_backward,
        block_inputs + (log_total, grad_attended.reshape(block_count, BLK, model_width)),
    )
    grad_query_rows = grad_query_rows.reshape(row_count, model_width)
    grad_key_rows = grad_key_rows.reshape(row_count, model_width)
    grad_value_rows = grad_value_rows.reshape(row_count, model_width)
    grad_ctx_keys = grad_ctx_keys.reshape(block_count * CTX, model_width)
    grad_ctx_values = grad_ctx_values.reshape(block_count * CTX, model_width)
    grad_query = jnp.einsum(
        "rd,re->de", flat_rounded, grad_query_rows, preferred_element_type=jnp.float32
    )
    grad_key = jnp.einsum(
        "rd,re->de", flat_rounded, grad_key_rows, preferred_element_type=jnp.float32
    ) + jnp.einsum("rd,re->de", ctx_rows, grad_ctx_keys, preferred_element_type=jnp.float32)
    grad_value = jnp.einsum(
        "rd,re->de", flat_rounded, grad_value_rows, preferred_element_type=jnp.float32
    ) + jnp.einsum("rd,re->de", ctx_rows, grad_ctx_values, preferred_element_type=jnp.float32)
    grad_normed = (
        jnp.einsum("re,de->rd", grad_query_rows, full_query, preferred_element_type=jnp.float32)
        + jnp.einsum("re,de->rd", grad_key_rows, full_key, preferred_element_type=jnp.float32)
        + jnp.einsum("re,de->rd", grad_value_rows, full_value, preferred_element_type=jnp.float32)
    )
    grad_context = jnp.einsum(
        "re,de->rd", grad_ctx_keys, full_key, preferred_element_type=jnp.float32
    ) + jnp.einsum("re,de->rd", grad_ctx_values, full_value, preferred_element_type=jnp.float32)
    grad_context = grad_context.reshape(seq_count, NBLK, CTX, model_width)
    grad_driven, state_normed, grad_rates, grad_state_out, grad_skip = state_pullback(grad_context)
    grad_in = jnp.einsum(
        "stp,std->pd", grad_driven, rounded, precision=HIGHEST, preferred_element_type=jnp.float32
    )
    state_rounded = jnp.einsum(
        "stp,pd->std", grad_driven, full_in, precision=HIGHEST, preferred_element_type=jnp.float32
    )
    normed_total = (
        grad_normed.reshape(seq_count, seq_len, model_width) + state_rounded + state_normed
    )
    tokens_part, grad_first_gain, grad_first_bias = first_pullback(normed_total)
    grad_tokens = (tokens_part + grad_residual.reshape(seq_count, seq_len, model_width)).astype(
        jnp.bfloat16
    )
    piece_query, piece_key, piece_value, piece_output, piece_up, piece_down, piece_in, piece_out = (
        lax.psum_scatter(grad_query, "shard", scatter_dimension=0, tiled=True),
        lax.psum_scatter(grad_key, "shard", scatter_dimension=0, tiled=True),
        lax.psum_scatter(grad_value, "shard", scatter_dimension=0, tiled=True),
        lax.psum_scatter(grad_output, "shard", scatter_dimension=0, tiled=True),
        lax.psum_scatter(grad_up, "shard", scatter_dimension=0, tiled=True),
        lax.psum_scatter(grad_down, "shard", scatter_dimension=0, tiled=True),
        lax.psum_scatter(grad_in, "shard", scatter_dimension=1, tiled=True),
        lax.psum_scatter(grad_state_out, "shard", scatter_dimension=1, tiled=True),
    )
    piece_query, piece_key, piece_value, piece_output, piece_up, piece_down, piece_in, piece_out = (
        lax.psum(piece_query.astype(jnp.bfloat16), "rep").astype(jnp.float32),
        lax.psum(piece_key.astype(jnp.bfloat16), "rep").astype(jnp.float32),
        lax.psum(piece_value.astype(jnp.bfloat16), "rep").astype(jnp.float32),
        lax.psum(piece_output.astype(jnp.bfloat16), "rep").astype(jnp.float32),
        lax.psum(piece_up.astype(jnp.bfloat16), "rep").astype(jnp.float32),
        lax.psum(piece_down.astype(jnp.bfloat16), "rep").astype(jnp.float32),
        lax.psum(piece_in.astype(jnp.bfloat16), "rep").astype(jnp.float32),
        lax.psum(piece_out.astype(jnp.bfloat16), "rep").astype(jnp.float32),
    )
    (
        sum_first_gain,
        sum_first_bias,
        sum_rates,
        sum_skip,
        sum_second_gain,
        sum_second_bias,
        sum_up_bias,
        sum_down_bias,
    ) = lax.psum(
        (
            grad_first_gain,
            grad_first_bias,
            grad_rates,
            grad_skip,
            grad_second_gain,
            grad_second_bias,
            grad_up_bias,
            grad_down_bias,
        ),
        ("rep", "shard"),
    )
    return (
        result,
        grad_tokens,
        sum_first_gain,
        sum_first_bias,
        sum_rates,
        piece_in,
        piece_out,
        sum_skip,
        piece_query,
        piece_key,
        piece_value,
        piece_output,
        sum_second_gain,
        sum_second_bias,
        piece_up,
        sum_up_bias,
        piece_down,
        sum_down_bias,
    )


def solution(mesh):
    placed = (
        P(("rep", "shard"), None, None),
        P(("rep", "shard")),
        P(),
        P(),
        P(),
        P(None, "shard"),
        P(None, "shard"),
        P(),
        P("shard", None),
        P("shard", None),
        P("shard", None),
        P("shard", None),
        P(),
        P(),
        P("shard", None),
        P(),
        P("shard", None),
        P(),
        P(("rep", "shard"), None, None),
    )
    fused = mesh.shape["rep"] == 2 and mesh.shape["shard"] == 2 * NC
    return jax.shard_map(
        fused_device if fused else per_device,
        mesh=mesh,
        in_specs=placed,
        out_specs=(
            P(("rep", "shard"), None, None),
            P(("rep", "shard"), None, None),
            P(),
            P(),
            P(),
            P(None, "shard"),
            P(None, "shard"),
            P(),
            P("shard", None),
            P("shard", None),
            P("shard", None),
            P("shard", None),
            P(),
            P(),
            P("shard", None),
            P(),
            P("shard", None),
            P(),
        ),
        check_vma=False,
    )
```
